32 devices in a mesh: dp: 4 (over x, core), ctx: 8 (over z, y).
Axes of the slice: x: 2, y: 2, z: 4, core: 2. Of those that a mesh axis runs over, the one named last changes fastest.
Arguments:
- tokens: bfloat16 [4, 4096, 512], P('dp', 'ctx'), may hold values from -6 to 6
- piece_starts: int32 [4, 4], P('dp'), may hold values from 0 to 3840, as said below
- qkv_weight: bfloat16 [786432], P(('dp', 'ctx')), may hold values from -0.375 to 0.375
- out_weight: bfloat16 [262144], P(('dp', 'ctx')), may hold values from -0.75 to 0.75
- up_weight: bfloat16 [1048576], P(('dp', 'ctx')), may hold values from -0.25 to 0.25
- down_weight: bfloat16 [1048576], P(('dp', 'ctx')), may hold values from -0.125 to 0.125
- biases: bfloat16 [4096], P(('dp', 'ctx')), may hold values from -2 to 2
- norms: bfloat16 [2048], P(('dp', 'ctx'))
- cotangent: bfloat16 [4, 4096, 512], P('dp', 'ctx'), may hold values from -6 to 6
Outputs:
- output: bfloat16 [4, 4096, 512], P('dp', 'ctx')
- grad_tokens: float32 [4, 4096, 512], P('dp', 'ctx')
- grad_qkv: float32 [786432], P(('dp', 'ctx'))
- grad_out: float32 [262144], P(('dp', 'ctx'))
- grad_up: float32 [1048576], P(('dp', 'ctx'))
- grad_down: float32 [1048576], P(('dp', 'ctx'))
- grad_biases: float32 [4096], P(('dp', 'ctx'))
- grad_norms: float32 [2048], P(('dp', 'ctx'))
The draws below stay inside these ranges and needn't reach their ends.
Inputs may be any that keep to these rules, and one draw needn't show every extreme that they name: `piece_starts`: each row holds 4 distinct multiples of 256 in increasing order; the first is 0 and the last 3840, so that every sequence opens and closes with a picture piece; a piece covers the 256 words from its start.
All inputs are finite; a program needn't handle non-finite values.
Results may differ from the reference program's by a relative error of at most 0.02.
Values may be sent and summed in bfloat16 or wider, within the bound.
A program may use at most 256 MiB of HBM per device.

```python
import jax
import jax.numpy as jnp
from jax import lax

D = 512
FF = 2048
HEADS = 8
PIECE = 256
SEQ_LEN = 4096
SEQS = 4
PIECES = 4


def draw_piece_starts(key, part):
    blocks_all = SEQ_LEN // PIECE

    def one_row(row_key):
        inner = jax.random.permutation(row_key, blocks_all - 2)[:PIECES - 2] + 1
        chosen = jnp.concatenate([jnp.zeros((1,), jnp.int32), jnp.sort(inner).astype(jnp.int32), jnp.full((1,), blocks_all - 1, jnp.int32)])
        return chosen * PIECE
    return jax.vmap(one_row)(jax.random.split(jax.random.fold_in(key, 11), SEQS))


def draw_norms(key, part):
    gain_key, shift_key = jax.random.split(jax.random.fold_in(key, 7))
    gains = 1.0 + 0.3 * jax.random.uniform(gain_key, (2, D), jnp.float32, -1.0, 1.0)
    shifts = 0.3 * jax.random.normal(shift_key, (2, D), jnp.float32)
    return jnp.concatenate([gains[0], shifts[0], gains[1], shifts[1]]).astype(jnp.bfloat16)


def level_of(stream_key, dims, cuts, smallest, high):
    level = 1.0
    for dim, parts in cuts:
        steps = jax.random.uniform(jax.random.fold_in(jax.random.fold_in(stream_key, 6), dim), (parts,), jnp.float32, smallest / len(cuts), high / len(cuts))
        level = level * jnp.repeat(jnp.exp(steps), dims[dim] // parts).reshape((-1,) + (1,) * (len(dims) - 1 - dim))
    return level


def gaussian(own_key, extent, width, limit, pieces=(), held_as=jnp.bfloat16):
    drawn = jax.random.normal(own_key, extent, jnp.float32) * width
    if len(pieces) > 0:
        drawn = level_of(own_key, extent, pieces, -0.22, 0.18) * drawn
    return jnp.clip(drawn, min=-limit, max=limit).astype(held_as)


def setup_inputs(seed: int = 0) -> dict:
    key_of = jax.random.split(jax.random.key(seed), 10)
    return {
        "tokens": gaussian(key_of[0], (SEQS, SEQ_LEN, D), 1.0, 6.0, ((0, 4), (1, 8))),
        "piece_starts": draw_piece_starts(jax.random.fold_in(key_of[9], 71), 0),
        "qkv_weight": gaussian(key_of[2], (3 * D * D,), (D // 2) ** -0.5, 0.375, ((0, 32),)),
        "out_weight": gaussian(key_of[3], (D * D,), (D // 8) ** -0.5, 0.75, ((0, 32),)),
        "up_weight": gaussian(key_of[4], (D * FF,), D ** -0.5, 0.25, ((0, 32),)),
        "down_weight": gaussian(key_of[5], (FF * D,), FF ** -0.5, 0.125, ((0, 32),)),
        "biases": gaussian(key_of[6], (4 * D + FF,), 0.3, 2.0, ((0, 32),)),
        "norms": draw_norms(jax.random.fold_in(key_of[9], 71), 0),
        "cotangent": gaussian(key_of[8], (SEQS, SEQ_LEN, D), 1.0, 6.0, ((0, 4), (1, 8))),
    }


@jax.custom_vjp
def low(v):
    return lax.optimization_barrier(v.astype(jnp.bfloat16)).astype(jnp.float32)

@jax.custom_vjp
def low_back(v):
    return v

def low_keep(v):
    return (low(v), None)

def low_pass(kept, grad):
    return (grad,)

def back_keep(v):
    return (v, None)

def back_low(kept, grad):
    return (low(grad),)
low.defvjp(low_keep, low_pass)
low_back.defvjp(back_keep, back_low)
highest = lax.Precision.HIGHEST
eps_norm = 1e-05

def matmul(left, right):
    return jnp.dot(left, right, precision=highest)

def layer_norm(values, gain, shift):
    center = lax.optimization_barrier(jnp.mean(values, axis=-1, keepdims=True))
    offsets = values - center
    spread = lax.optimization_barrier(jnp.mean(offsets * offsets, axis=-1, keepdims=True))
    return offsets * lax.rsqrt(spread + eps_norm) * gain + shift

def piece_flags(positions, starts_row):
    opening = positions // PIECE * PIECE
    return jnp.any(opening[:, None] == starts_row[None, :], axis=1)

def visible(query_pos, query_flag, key_pos):
    causal = key_pos[None, :] <= query_pos[:, None]
    same_piece = key_pos[None, :] // PIECE == query_pos[:, None] // PIECE
    return jnp.logical_or(causal, jnp.logical_and(same_piece, query_flag[:, None]))

def attention(queries, key_rows, value_rows, flags):
    length = queries.shape[0]
    model_width = queries.shape[1]
    head_dim = model_width // HEADS
    block_len = 512 if length % 512 == 0 else length
    key_heads = key_rows.reshape(length, HEADS, head_dim)
    value_heads = value_rows.reshape(length, HEADS, head_dim)
    key_pos = jnp.arange(length, dtype=jnp.int32)

    def one_block(position):
        begin = (position * block_len).astype(jnp.int32)
        query_block = lax.dynamic_slice_in_dim(queries, begin, block_len, 0).reshape(block_len, HEADS, head_dim)
        query_pos = begin + jnp.arange(block_len, dtype=jnp.int32)
        query_flag = lax.dynamic_slice_in_dim(flags, begin, block_len, 0)
        scores = jnp.einsum('qhd,khd->hqk', query_block, key_heads, precision=highest) * head_dim ** (-0.5)
        scores = low_back(scores)
        allowed = visible(query_pos, query_flag, key_pos)[None]
        scores = jnp.where(allowed, scores, -1e+30)
        softmax_p = low(jax.nn.softmax(scores, axis=-1))
        mixed = jnp.einsum('hqk,khd->qhd', softmax_p, value_heads, precision=highest)
        return mixed.reshape(block_len, model_width)
    blocks = lax.map(jax.checkpoint(one_block), jnp.arange(length // block_len, dtype=jnp.int32))
    return blocks.reshape(length, model_width)

def layer(tokens, qkv_weight, out_weight, up_weight, down_weight, biases, norms, flags):
    model_width = tokens.shape[1]
    hidden = up_weight.shape[0] // model_width
    qkv_mat = qkv_weight.reshape(model_width, 3 * model_width)
    out_mat = out_weight.reshape(model_width, model_width)
    up_mat = up_weight.reshape(model_width, hidden)
    down_mat = down_weight.reshape(hidden, model_width)
    bias_q = biases[:model_width]
    bias_v = biases[model_width:2 * model_width]
    bias_o = biases[2 * model_width:3 * model_width]
    bias_up = biases[3 * model_width:3 * model_width + hidden]
    bias_down = biases[3 * model_width + hidden:]
    gain_one = norms[:model_width]
    shift_one = norms[model_width:2 * model_width]
    gain_two = norms[2 * model_width:3 * model_width]
    shift_two = norms[3 * model_width:]
    first_in = low(layer_norm(tokens, gain_one, shift_one))
    projected = matmul(first_in, qkv_mat)
    queries = low(low_back(projected[:, :model_width] + bias_q))
    key_rows = low(low_back(projected[:, model_width:2 * model_width]))
    value_rows = low(low_back(projected[:, 2 * model_width:] + bias_v))
    mixed = low(low_back(attention(queries, key_rows, value_rows, flags)))
    after_attn = tokens + low_back(matmul(mixed, out_mat) + bias_o)
    second_in = low(layer_norm(after_attn, gain_two, shift_two))
    pre_act = low_back(matmul(second_in, up_mat) + bias_up)
    activated = low(jax.nn.gelu(pre_act, approximate=False))
    return after_attn + low_back(matmul(activated, down_mat) + bias_down)

def reference(tokens, piece_starts, qkv_weight, out_weight, up_weight, down_weight, biases, norms, cotangent):
    weights = (qkv_weight.astype(jnp.float32), out_weight.astype(jnp.float32), up_weight.astype(jnp.float32), down_weight.astype(jnp.float32), biases.astype(jnp.float32), norms.astype(jnp.float32))
    length = tokens.shape[1]
    positions = jnp.arange(length, dtype=jnp.int32)

    def one_sequence(totals, inputs):
        seq_tokens, seq_starts, seq_grad = inputs
        flags = piece_flags(positions, seq_starts)

        def local(seq_in, qkv_w, out_w, up_w, down_w, bias_w, norm_w):
            return layer(seq_in, qkv_w, out_w, up_w, down_w, bias_w, norm_w, flags)
        result, pullback = jax.vjp(local, seq_tokens.astype(jnp.float32), *weights)
        grads = pullback(seq_grad.astype(jnp.float32))
        new_totals = tuple((total + grad_part for total, grad_part in zip(totals, grads[1:])))
        return (new_totals, (result.astype(jnp.bfloat16), grads[0]))
    zeros_init = tuple((jnp.zeros_like(weight_in) for weight_in in weights))
    totals, (output, grad_tokens) = lax.scan(one_sequence, zeros_init, (tokens, piece_starts, cotangent))
    return (output, grad_tokens, totals[0], totals[1], totals[2], totals[3], totals[4], totals[5])
```

```python
import functools
import math

import jax
import jax.numpy as jnp
from jax import lax
from jax.experimental import pallas as pl
from jax.experimental.pallas import tpu as pltpu
from jax.sharding import PartitionSpec as P

HEADS = 8
PIECE = 256


eps_norm = 1e-05
masked_score = -1e30


def layer_norm(values, gain, shift):
    center = jnp.mean(values, axis=-1, keepdims=True)
    offsets = values - center
    spread = jnp.mean(offsets * offsets, axis=-1, keepdims=True)
    return offsets * lax.rsqrt(spread + eps_norm) * gain + shift


def gelu_exact(values):
    return jax.nn.gelu(values, approximate=False)


def piece_flags(positions, starts_row):
    opening = positions // PIECE * PIECE
    return jnp.any(opening[:, None] == starts_row[None, :], axis=1)


def visible(query_pos, query_flag, key_pos):
    causal = key_pos[None, :] <= query_pos[:, None]
    same_piece = key_pos[None, :] // PIECE == query_pos[:, None] // PIECE
    return jnp.logical_or(causal, jnp.logical_and(same_piece, query_flag[:, None]))


def to_blocks(arrays, shard_rows):
    block_len = 256
    block_count = shard_rows // block_len
    shaped = tuple((member.reshape(block_count, block_len, HEADS, -1) for member in arrays))
    return (block_len, block_count, shaped)


def keep_state(state):
    return state


def unpack(flats, model_width):
    qkv_flat, out_flat, up_flat, down_flat, bias_flat, norm_flat = flats
    hidden = up_flat.shape[0] // model_width
    return (
        qkv_flat.reshape(model_width, 3 * model_width),
        out_flat.reshape(model_width, model_width),
        up_flat.reshape(model_width, hidden),
        down_flat.reshape(hidden, model_width),
        bias_flat.astype(jnp.float32),
        norm_flat.astype(jnp.float32),
    )


def norm_back(values, gain, shift, upstream):
    _, pullback = jax.vjp(layer_norm, values, gain, shift)
    return pullback(upstream)


def column_sum(matrix):
    return jnp.sum(matrix.astype(jnp.float32), axis=0)


def query_terms(
    query_heads,
    grad_heads,
    own_lse,
    own_delta,
    query_pos,
    query_flag,
    key_block,
    value_block,
    key_pos,
    factor,
):
    scores = (
        jnp.einsum("qhd,khd->hqk", query_heads, key_block, preferred_element_type=jnp.float32)
        * factor
    )
    allowed = visible(query_pos, query_flag, key_pos)[None]
    softmax_p = jnp.where(allowed, jnp.exp(scores - own_lse[:, :, None]), 0.0)
    dprobs = jnp.einsum("qhd,khd->hqk", grad_heads, value_block, preferred_element_type=jnp.float32)
    dscores = (softmax_p * (dprobs - own_delta[:, :, None])).astype(jnp.bfloat16)
    return (
        jnp.einsum("hqk,khd->hqd", dscores, key_block, preferred_element_type=jnp.float32) * factor
    )


def key_terms(
    query_block,
    grad_block,
    lse_block,
    delta_block,
    remote_pos,
    remote_flag,
    key_heads,
    value_heads,
    key_pos,
    factor,
):
    scores = (
        jnp.einsum("qhd,khd->hqk", query_block, key_heads, preferred_element_type=jnp.float32)
        * factor
    )
    allowed = visible(remote_pos, remote_flag, key_pos)[None]
    softmax_p = jnp.where(allowed, jnp.exp(scores - lse_block[:, :, None]), 0.0)
    dprobs = jnp.einsum("qhd,khd->hqk", grad_block, value_heads, preferred_element_type=jnp.float32)
    dscores = (softmax_p * (dprobs - delta_block[:, :, None])).astype(jnp.bfloat16)
    grad_keys = (
        jnp.einsum("hqk,qhd->hkd", dscores, query_block, preferred_element_type=jnp.float32)
        * factor
    )
    grad_values = jnp.einsum(
        "hqk,qhd->hkd",
        softmax_p.astype(jnp.bfloat16),
        grad_block,
        preferred_element_type=jnp.float32,
    )
    return (grad_keys, grad_values)


def general_device(
    tokens, piece_starts, qkv_weight, out_weight, up_weight, down_weight, biases, norms, cotangent
):
    model_width = tokens.shape[2]
    seq_rows = tokens.shape[1]
    params = unpack(
        (
            lax.all_gather(qkv_weight, ("dp", "ctx"), axis=0, tiled=True),
            lax.all_gather(out_weight, ("dp", "ctx"), axis=0, tiled=True),
            lax.all_gather(up_weight, ("dp", "ctx"), axis=0, tiled=True),
            lax.all_gather(down_weight, ("dp", "ctx"), axis=0, tiled=True),
            lax.all_gather(biases, ("dp", "ctx"), axis=0, tiled=True),
            lax.all_gather(norms, ("dp", "ctx"), axis=0, tiled=True),
        ),
        model_width,
    )
    qkv_mat, out_mat, up_mat, down_mat, bias_all, norm_all = params
    hidden = up_mat.shape[1]
    head_dim = model_width // HEADS
    factor = head_dim ** (-0.5)
    first_row = lax.axis_index("ctx") * seq_rows
    last_row = first_row + seq_rows - 1
    query_pos = first_row + jnp.arange(seq_rows, dtype=jnp.int32)
    starts_row = piece_starts[0]
    query_flag = piece_flags(query_pos, starts_row)
    bias_q = bias_all[:model_width]
    bias_v = bias_all[model_width : 2 * model_width]
    bias_o = bias_all[2 * model_width : 3 * model_width]
    bias_up = bias_all[3 * model_width : 3 * model_width + hidden]
    bias_down = bias_all[3 * model_width + hidden :]
    gain_one = norm_all[:model_width]
    shift_one = norm_all[model_width : 2 * model_width]
    gain_two = norm_all[2 * model_width : 3 * model_width]
    shift_two = norm_all[3 * model_width :]
    inputs = tokens[0].astype(jnp.float32)
    first_in = layer_norm(inputs, gain_one, shift_one).astype(jnp.bfloat16)
    projected = jnp.dot(first_in, qkv_mat, preferred_element_type=jnp.float32)
    queries = (projected[:, :model_width] + bias_q).astype(jnp.bfloat16)
    key_rows = projected[:, model_width : 2 * model_width].astype(jnp.bfloat16)
    value_rows = (projected[:, 2 * model_width :] + bias_v).astype(jnp.bfloat16)
    query_heads = queries.reshape(seq_rows, HEADS, head_dim)
    key_heads = key_rows.reshape(seq_rows, HEADS, head_dim)
    value_heads = value_rows.reshape(seq_rows, HEADS, head_dim)
    start_state = (
        jnp.full((HEADS, seq_rows), masked_score, jnp.float32),
        jnp.zeros((HEADS, seq_rows), jnp.float32),
        jnp.zeros((HEADS, seq_rows, head_dim), jnp.float32),
    )
    shard = (
        lax.all_gather(key_rows, "ctx", axis=0, tiled=True),
        lax.all_gather(value_rows, "ctx", axis=0, tiled=True),
    )
    shard_rows = shard[0].shape[0]
    block_len, block_count, (key_blocks, value_blocks) = to_blocks(shard, shard_rows)

    def forward_one_block(state, block_in):
        running_max, running_sum, running_acc = state
        key_block, value_block, position = block_in
        key_pos = position * block_len + jnp.arange(block_len, dtype=jnp.int32)
        scores = (
            jnp.einsum("qhd,khd->hqk", query_heads, key_block, preferred_element_type=jnp.float32)
            * factor
        )
        allowed = visible(query_pos, query_flag, key_pos)[None]
        scores = jnp.where(allowed, scores, masked_score)
        new_max = jnp.maximum(running_max, jnp.max(scores, axis=-1))
        correction = jnp.exp(running_max - new_max)
        exp_scores = jnp.where(allowed, jnp.exp(scores - new_max[:, :, None]), 0.0)
        running_sum = running_sum * correction + jnp.sum(exp_scores, axis=-1)
        running_acc = running_acc * correction[:, :, None] + jnp.einsum(
            "hqk,khd->hqd",
            exp_scores.astype(jnp.bfloat16),
            value_block,
            preferred_element_type=jnp.float32,
        )
        return ((new_max, running_sum, running_acc), None)

    def forward_compute(state):
        return lax.scan(
            forward_one_block,
            state,
            (key_blocks, value_blocks, jnp.arange(block_count, dtype=jnp.int32)),
        )[0]

    run_max, run_sum, run_acc = lax.cond(
        jnp.int32(0) <= last_row, forward_compute, keep_state, start_state
    )
    mixed_heads = run_acc / run_sum[:, :, None]
    mixed_f = jnp.transpose(mixed_heads, (1, 0, 2)).reshape(seq_rows, model_width)
    mixed_b = mixed_f.astype(jnp.bfloat16)
    log_sum = run_max + jnp.log(run_sum)
    after_attn = inputs + jnp.dot(mixed_b, out_mat, preferred_element_type=jnp.float32) + bias_o
    second_in = layer_norm(after_attn, gain_two, shift_two).astype(jnp.bfloat16)
    pre_act = jnp.dot(second_in, up_mat, preferred_element_type=jnp.float32) + bias_up
    activated = gelu_exact(pre_act).astype(jnp.bfloat16)
    result = (
        after_attn + jnp.dot(activated, down_mat, preferred_element_type=jnp.float32) + bias_down
    )
    output = result.astype(jnp.bfloat16)[None]
    back = unpack(
        (
            lax.all_gather(qkv_weight, ("dp", "ctx"), axis=0, tiled=True),
            lax.all_gather(out_weight, ("dp", "ctx"), axis=0, tiled=True),
            lax.all_gather(up_weight, ("dp", "ctx"), axis=0, tiled=True),
            lax.all_gather(down_weight, ("dp", "ctx"), axis=0, tiled=True),
            lax.all_gather(biases, ("dp", "ctx"), axis=0, tiled=True),
            lax.all_gather(norms, ("dp", "ctx"), axis=0, tiled=True),
        ),
        model_width,
    )
    qkv_back, out_back, up_back, down_back, bias_back, norm_vec = back
    gain_one_b = norm_vec[:model_width]
    shift_one_b = norm_vec[model_width : 2 * model_width]
    gain_two_b = norm_vec[2 * model_width : 3 * model_width]
    shift_two_b = norm_vec[3 * model_width :]
    upstream = cotangent[0].astype(jnp.float32)
    grad_mlp = upstream.astype(jnp.bfloat16)
    grad_down_loc = jnp.einsum("ta,tb->ab", activated, grad_mlp, preferred_element_type=jnp.float32)
    grad_act = jnp.einsum("tb,ab->ta", grad_mlp, down_back, preferred_element_type=jnp.float32)
    _, gelu_pull = jax.vjp(gelu_exact, pre_act)
    grad_pre = gelu_pull(grad_act)[0].astype(jnp.bfloat16)
    grad_up_loc = jnp.einsum("ta,tb->ab", second_in, grad_pre, preferred_element_type=jnp.float32)
    grad_second = jnp.einsum("tb,ab->ta", grad_pre, up_back, preferred_element_type=jnp.float32)
    grad_after_part, grad_gain_two, grad_shift_two = norm_back(
        after_attn, gain_two_b, shift_two_b, grad_second
    )
    grad_after = upstream + grad_after_part
    grad_attn = grad_after.astype(jnp.bfloat16)
    grad_out_loc = jnp.einsum("ta,tb->ab", mixed_b, grad_attn, preferred_element_type=jnp.float32)
    grad_mixed = jnp.einsum(
        "tb,ab->ta", grad_attn, out_back, preferred_element_type=jnp.float32
    ).astype(jnp.bfloat16)
    grad_heads = grad_mixed.reshape(seq_rows, HEADS, head_dim)
    delta_rows = jnp.sum(
        grad_heads.astype(jnp.float32) * mixed_f.reshape(seq_rows, HEADS, head_dim), axis=-1
    )
    delta_heads = delta_rows.T
    stats = jnp.concatenate([log_sum.T, delta_rows], axis=1)
    all_stats = lax.all_gather(stats, "ctx", axis=0, tiled=True)
    zero_heads = jnp.zeros((HEADS, seq_rows, head_dim), jnp.float32)
    shard = (
        lax.all_gather(key_rows, "ctx", axis=0, tiled=True),
        lax.all_gather(value_rows, "ctx", axis=0, tiled=True),
    )
    shard_rows = shard[0].shape[0]
    query_block_len, query_block_count, (query_key_blocks, query_value_blocks) = to_blocks(
        shard, shard_rows
    )

    def query_one_block(total, block_in):
        key_block, value_block, position = block_in
        key_pos = position * query_block_len + jnp.arange(query_block_len, dtype=jnp.int32)
        term = query_terms(
            query_heads,
            grad_heads,
            log_sum,
            delta_heads,
            query_pos,
            query_flag,
            key_block,
            value_block,
            key_pos,
            factor,
        )
        return (total + term, None)

    def query_compute(total):
        return lax.scan(
            query_one_block,
            total,
            (query_key_blocks, query_value_blocks, jnp.arange(query_block_count, dtype=jnp.int32)),
        )[0]

    grad_q = lax.cond(jnp.int32(0) <= last_row, query_compute, keep_state, zero_heads)
    shard = (
        lax.all_gather(queries, "ctx", axis=0, tiled=True),
        lax.all_gather(grad_mixed, "ctx", axis=0, tiled=True),
    )
    shard_rows = shard[0].shape[0]
    key_block_len, key_block_count, (query_blocks, grad_blocks) = to_blocks(shard, shard_rows)

    def key_one_block(totals, block_in):
        query_block, grad_block, position = block_in
        begin = position * key_block_len
        remote_pos = begin + jnp.arange(key_block_len, dtype=jnp.int32)
        remote_flag = piece_flags(remote_pos, starts_row)
        stats_block = lax.dynamic_slice_in_dim(all_stats, begin, key_block_len, 0)
        lse_block = stats_block[:, :HEADS].T
        delta_block = stats_block[:, HEADS:].T
        grad_keys, grad_values = key_terms(
            query_block,
            grad_block,
            lse_block,
            delta_block,
            remote_pos,
            remote_flag,
            key_heads,
            value_heads,
            query_pos,
            factor,
        )
        return ((totals[0] + grad_keys, totals[1] + grad_values), None)

    def key_compute(totals):
        return lax.scan(
            key_one_block,
            totals,
            (query_blocks, grad_blocks, jnp.arange(key_block_count, dtype=jnp.int32)),
        )[0]

    grad_k, grad_v = lax.cond(
        jnp.int32(0) + shard_rows - 1 >= first_row,
        key_compute,
        keep_state,
        (zero_heads, zero_heads),
    )

    def merge_heads(grad_part):
        return (
            jnp.transpose(grad_part, (1, 0, 2)).reshape(seq_rows, model_width).astype(jnp.bfloat16)
        )

    grad_qkv_rows = jnp.concatenate(
        [merge_heads(grad_q), merge_heads(grad_k), merge_heads(grad_v)], axis=1
    )
    grad_qkv_loc = jnp.einsum(
        "ta,tb->ab", first_in, grad_qkv_rows, preferred_element_type=jnp.float32
    )
    grad_first = jnp.einsum(
        "tb,ab->ta", grad_qkv_rows, qkv_back, preferred_element_type=jnp.float32
    )
    grad_in_part, grad_gain_one, grad_shift_one = norm_back(
        inputs, gain_one_b, shift_one_b, grad_first
    )
    grad_tokens = (grad_after + grad_in_part)[None]
    grad_bias_loc = jnp.concatenate(
        [
            column_sum(grad_qkv_rows[:, :model_width]),
            column_sum(grad_qkv_rows[:, 2 * model_width :]),
            column_sum(grad_attn),
            column_sum(grad_pre),
            column_sum(grad_mlp),
        ]
    )
    grad_norm_loc = jnp.concatenate([grad_gain_one, grad_shift_one, grad_gain_two, grad_shift_two])
    summed = (
        lax.psum_scatter(grad_qkv_loc.reshape(-1), ("dp", "ctx"), scatter_dimension=0, tiled=True),
        lax.psum_scatter(grad_out_loc.reshape(-1), ("dp", "ctx"), scatter_dimension=0, tiled=True),
        lax.psum_scatter(grad_up_loc.reshape(-1), ("dp", "ctx"), scatter_dimension=0, tiled=True),
        lax.psum_scatter(grad_down_loc.reshape(-1), ("dp", "ctx"), scatter_dimension=0, tiled=True),
        lax.psum_scatter(grad_bias_loc, ("dp", "ctx"), scatter_dimension=0, tiled=True),
        lax.psum_scatter(grad_norm_loc, ("dp", "ctx"), scatter_dimension=0, tiled=True),
    )
    return (output, grad_tokens, summed[0], summed[1], summed[2], summed[3], summed[4], summed[5])


MESH = pl.DeviceIdType.MESH
BF16 = jnp.bfloat16
F32 = jnp.float32
VMEM_SPEC = pl.BlockSpec(memory_space=pltpu.VMEM)
SMEM_SPEC = pl.BlockSpec(memory_space=pltpu.SMEM)
ANY_SPEC = pl.BlockSpec(memory_space=pl.ANY)
HALF = 64
NT = (((1,), (1,)), ((), ()))
TN = (((0,), (0,)), ((), ()))
VMEM_LIMIT = 60 << 20


def params(cid=None):
    if cid is None:
        return pltpu.CompilerParams(vmem_limit_bytes=VMEM_LIMIT)
    return pltpu.CompilerParams(
        collective_id=cid, has_side_effects=True, vmem_limit_bytes=VMEM_LIMIT
    )


def place():
    dp = lax.axis_index("dp")
    ctx = lax.axis_index("ctx")
    return dp // 2, dp % 2, ctx // 2, ctx % 2


def device(x, core, z, y):
    return (x * 2 + core, z * 2 + y)


def greet(peers):
    barrier = pltpu.get_barrier_semaphore()
    for peer in peers:
        pl.semaphore_signal(barrier, inc=1, device_id=peer, device_id_type=MESH)
    pl.semaphore_wait(barrier, len(peers))


def remote(src, dst, send, recv, peer):
    return pltpu.make_async_remote_copy(
        src_ref=src,
        dst_ref=dst,
        send_sem=send,
        recv_sem=recv,
        device_id=peer,
        device_id_type=MESH,
    )


def gather_kernel(count, *refs):
    shards = refs[:count]
    outs = refs[count : 2 * count]
    own_sem, send, recv = refs[2 * count :]
    x, core, z, y = place()
    ox, oc, oy = 1 - x, 1 - core, 1 - y
    to_x = device(ox, core, z, y)
    to_y = device(x, core, z, oy)
    to_core = device(x, oc, z, y)
    others = [(z + j) % 4 for j in range(1, 4)]
    greet([device(x, core, other, y) for other in others] + [to_x, to_y, to_core])
    slot = 0

    def start(src, dst, peer, index):
        copy = remote(src, dst, send.at[index], recv.at[index], peer)
        copy.start()
        return copy

    own = []
    first = []
    for a in range(count):
        copy = pltpu.make_async_copy(shards[a], outs[a].at[x, core, z, y], own_sem.at[a])
        copy.start()
        own.append(copy)
        group = []
        for j, other in enumerate(others):
            group.append(
                start(
                    shards[a],
                    outs[a].at[x, core, z, y],
                    device(x, core, other, y),
                    a * 16 + j,
                )
            )
        first.append(group)
    second = []
    third = []
    fourth = []
    for a in range(count):
        own[a].wait()
        for copy in first[a]:
            copy.wait()
        part = outs[a].at[x, core, :, y]
        second.append(
            [
                start(part, part, to_x, a * 16 + 3),
                start(part, part, to_y, a * 16 + 4),
            ]
        )
        fourth.append(start(part, part, to_core, a * 16 + 5))
    for a in range(count):
        for copy in second[a]:
            copy.wait()
        from_x = outs[a].at[ox, core, :, y]
        from_y = outs[a].at[x, core, :, oy]
        low = outs[a].at[x, core, pl.ds(0, 2), oy]
        high = outs[a].at[ox, core, pl.ds(2, 2), y]
        third.append(
            [
                start(low, low, to_x, a * 16 + 6),
                start(high, high, to_y, a * 16 + 7),
            ]
        )
        fourth.append(start(from_x, from_x, to_core, a * 16 + 8))
        fourth.append(start(from_y, from_y, to_core, a * 16 + 9))
    for a in range(count):
        for copy in third[a]:
            copy.wait()
        part = outs[a].at[ox, core, :, oy]
        fourth.append(start(part, part, to_core, a * 16 + 10))
    for copy in fourth:
        copy.wait()


def gather_weights(shards, cid):
    count = len(shards)
    return pl.pallas_call(
        functools.partial(gather_kernel, count),
        out_shape=[jax.ShapeDtypeStruct((2, 2, 4, 2) + s.shape, s.dtype) for s in shards],
        in_specs=[ANY_SPEC] * count,
        out_specs=[ANY_SPEC] * count,
        scratch_shapes=[
            pltpu.SemaphoreType.DMA((count,)),
            pltpu.SemaphoreType.DMA((16 * count,)),
            pltpu.SemaphoreType.DMA((16 * count,)),
        ],
        compiler_params=params(cid),
    )(*shards)


def exchange_kernel(src_ref, out_ref, own_sem, send, recv):
    dp = lax.axis_index("dp")
    me = lax.axis_index("ctx")
    n = src_ref.shape[0]
    peers = [(me + i) % n for i in range(1, n)]
    greet([(dp, peer) for peer in peers])
    copies = []
    for i, peer in enumerate(peers):
        copy = remote(src_ref.at[peer], out_ref.at[me], send.at[i], recv.at[i], (dp, peer))
        copy.start()
        copies.append(copy)
    own = pltpu.make_async_copy(src_ref.at[me], out_ref.at[me], own_sem)
    own.start()
    own.wait()
    for copy in copies:
        copy.wait()


def exchange(blocks, cid):
    n = blocks.shape[0]
    return pl.pallas_call(
        exchange_kernel,
        out_shape=jax.ShapeDtypeStruct(blocks.shape, blocks.dtype),
        in_specs=[ANY_SPEC],
        out_specs=ANY_SPEC,
        scratch_shapes=[
            pltpu.SemaphoreType.DMA,
            pltpu.SemaphoreType.DMA((n - 1,)),
            pltpu.SemaphoreType.DMA((n - 1,)),
        ],
        compiler_params=params(cid),
    )(blocks)


def mm(a, b, dims=None):
    if dims is None:
        return jnp.dot(a, b, preferred_element_type=F32)
    return lax.dot_general(a, b, dims, preferred_element_type=F32)


def swap_halves(v):
    return jnp.concatenate([v[:, HALF:], v[:, :HALF]], axis=1)


def left_lanes(rows):
    return lax.broadcasted_iota(jnp.int32, (rows, 2 * HALF), 1) < HALF


def diagonal_mask(size, flags, first, transposed):
    row = lax.broadcasted_iota(jnp.int32, (size, size), 0)
    col = lax.broadcasted_iota(jnp.int32, (size, size), 1)
    key, query = (row, col) if transposed else (col, row)
    allowed = key <= query
    same = (key // PIECE) == (query // PIECE)
    for t in range(size // PIECE):
        inside = jnp.logical_and(same, (query // PIECE) == t)
        allowed = jnp.logical_or(allowed, jnp.logical_and(inside, flags[first + t] > 0))
    return allowed


def attend_kernel(rows, tile, flags, got, o2_ref, o_ref, lse_ref, q_s, k_s, v_s, m_s, acc_s):
    blocks = got.shape[0]
    half = rows // 2
    scale = math.log2(math.e) * HALF**-0.5
    left = left_lanes(rows)
    left_half = left_lanes(half)

    @pl.loop(0, blocks)
    def _(b):
        at = pl.multiple_of(b * rows, rows)
        pair = got[b, :rows]
        k_s[pl.ds(at, rows), :] = jnp.where(left, pair, 0).astype(BF16)
        v_s[pl.ds(at, rows), :] = jnp.where(left, 1, pair).astype(BF16)
        both = got[b, rows:]
        q_s[pl.ds(at, half), :] = jnp.where(left_half, both, 0).astype(BF16)
        q_s[pl.ds(at + half, half), :] = jnp.where(left_half, swap_halves(both), 0).astype(BF16)

    @pl.loop(0, blocks * rows // tile)
    def _(i):
        at = pl.multiple_of(i * tile, tile)
        q = q_s[pl.ds(at, tile), :]
        s = mm(q, k_s[pl.ds(at, tile), :], NT)
        allowed = diagonal_mask(tile, flags, i * (tile // PIECE), False)
        s = jnp.where(allowed, s, masked_score)
        m = jnp.max(s, axis=1, keepdims=True) * scale
        p = jnp.exp2(s * scale - m)
        m_s[...] = jnp.broadcast_to(m, m_s.shape)
        acc_s[...] = mm(p.astype(BF16), v_s[pl.ds(at, tile), :])

        @pl.loop(0, i)
        def _(j):
            start = pl.multiple_of(j * tile, tile)
            s = mm(q, k_s[pl.ds(start, tile), :], NT)
            old = m_s[...]
            new = jnp.maximum(old, jnp.max(s, axis=1, keepdims=True) * scale)
            p = jnp.exp2(s * scale - new[:, :1])
            m_s[...] = new
            acc_s[...] = acc_s[...] * jnp.exp2(old - new) + mm(
                p.astype(BF16), v_s[pl.ds(start, tile), :]
            )

        acc = acc_s[...]
        total = jnp.broadcast_to(acc[:, :1], acc.shape)
        o = acc / total
        o_ref[pl.ds(at, tile), :] = o
        lse = m_s[...] + jnp.log2(total)
        lse_ref[:, pl.ds(at, tile)] = jnp.transpose(lse)[:8]
        for t in range(tile // rows):
            top = o[t * rows : t * rows + half]
            low = o[t * rows + half : (t + 1) * rows]
            o2_ref[i * (tile // rows) + t] = jnp.where(left_half, swap_halves(top), low).astype(
                BF16
            )


def attend(flags, got, rows, tile):
    blocks = got.shape[0]
    length = blocks * rows
    return pl.pallas_call(
        functools.partial(attend_kernel, rows, tile),
        out_shape=[
            jax.ShapeDtypeStruct((blocks, rows // 2, 2 * HALF), BF16),
            jax.ShapeDtypeStruct((length, 2 * HALF), F32),
            jax.ShapeDtypeStruct((8, length), F32),
        ],
        in_specs=[SMEM_SPEC, VMEM_SPEC],
        out_specs=[VMEM_SPEC] * 3,
        scratch_shapes=[
            pltpu.VMEM((length, 2 * HALF), BF16),
            pltpu.VMEM((length, 2 * HALF), BF16),
            pltpu.VMEM((length, 2 * HALF), BF16),
            pltpu.VMEM((tile, 2 * HALF), F32),
            pltpu.VMEM((tile, 2 * HALF), F32),
        ],
        compiler_params=params(),
    )(flags, got)


def attend_back_kernel(
    rows, flags, got, do2_ref, o_ref, lse_ref, out_ref, qd_s, k_s, v_s, delta_s, dq_s, dk_s, dv_s
):
    blocks = got.shape[0]
    half = rows // 2
    scale = math.log2(math.e) * HALF**-0.5
    left = left_lanes(rows)
    left_half = left_lanes(half)

    @pl.loop(0, blocks)
    def _(b):
        at = pl.multiple_of(b * rows, rows)
        pair = got[b, :rows]
        k_s[pl.ds(at, rows), :] = jnp.where(left, pair, 0).astype(BF16)
        v_s[pl.ds(at, rows), :] = jnp.where(left, 0, pair).astype(BF16)
        both = got[b, rows:]
        grad = do2_ref[b]
        top = jnp.where(left_half, both, swap_halves(grad))
        low = jnp.where(left_half, swap_halves(both), grad)
        qd_s[pl.ds(at, half), :] = top
        qd_s[pl.ds(at + half, half), :] = low
        for part, begin in ((top, 0), (low, half)):
            product = jnp.where(
                left_half, 0.0, part.astype(F32) * o_ref[pl.ds(at + begin, half), :]
            )
            delta = jnp.sum(jnp.transpose(product), axis=0, keepdims=True)
            delta_s[:, pl.ds(at + begin, half)] = jnp.broadcast_to(delta, (8, half))
        dq_s[pl.ds(at, rows), :] = jnp.zeros((rows, 2 * HALF), F32)

    def tile(kj, qi, first):
        k0 = pl.multiple_of(kj * rows, rows)
        q0 = pl.multiple_of(qi * rows, rows)
        k = k_s[pl.ds(k0, rows), :]
        v = v_s[pl.ds(k0, rows), :]
        qd = qd_s[pl.ds(q0, rows), :]
        scores = mm(k, qd, NT)
        dprobs = mm(v, qd, NT)
        p = jnp.exp2(scores * scale - lse_ref[:1, pl.ds(q0, rows)])
        if first:
            allowed = diagonal_mask(rows, flags, kj * (rows // PIECE), True)
            p = jnp.where(allowed, p, 0.0)
        ds = (p * (dprobs - delta_s[:1, pl.ds(q0, rows)])).astype(BF16)
        dk = mm(ds, qd)
        dv = mm(p.astype(BF16), qd)
        if first:
            dk_s[...] = dk
            dv_s[...] = dv
        else:
            dk_s[...] += dk
            dv_s[...] += dv
        dq_s[pl.ds(q0, rows), :] += mm(ds, k, TN)

    @pl.loop(0, blocks)
    def _(kj):
        tile(kj, kj, True)

        @pl.loop(kj + 1, blocks)
        def _(qi):
            tile(kj, qi, False)

        factor = HALF**-0.5
        out_ref[kj, :rows] = jnp.where(left, dk_s[...] * factor, dv_s[...]).astype(BF16)
        at = pl.multiple_of(kj * rows, rows)
        top = dq_s[pl.ds(at, half), :]
        low = dq_s[pl.ds(at + half, half), :]
        out_ref[kj, rows:] = (jnp.where(left_half, top, swap_halves(low)) * factor).astype(BF16)


def attend_back(flags, got, do2, o, lse, rows):
    blocks = got.shape[0]
    length = blocks * rows
    return pl.pallas_call(
        functools.partial(attend_back_kernel, rows),
        out_shape=jax.ShapeDtypeStruct(got.shape, BF16),
        in_specs=[SMEM_SPEC] + [VMEM_SPEC] * 4,
        out_specs=VMEM_SPEC,
        scratch_shapes=[
            pltpu.VMEM((length, 2 * HALF), BF16),
            pltpu.VMEM((length, 2 * HALF), BF16),
            pltpu.VMEM((length, 2 * HALF), BF16),
            pltpu.VMEM((8, length), F32),
            pltpu.VMEM((length, 2 * HALF), F32),
            pltpu.VMEM((rows, 2 * HALF), F32),
            pltpu.VMEM((rows, 2 * HALF), F32),
        ],
        compiler_params=params(),
    )(flags, got, do2, o, lse)


def scatter_kernel(count, wires, *refs):
    parts = refs[:count]
    outs = refs[count : 2 * count]
    rest = refs[2 * count :]
    bufs = [rest[a * 11 : (a + 1) * 11] for a in range(count)]
    send, recv = rest[11 * count :]
    x, core, z, y = place()
    ox, oc, oy = 1 - x, 1 - core, 1 - y
    to_x = device(ox, core, z, y)
    to_y = device(x, core, z, oy)
    to_core = device(x, oc, z, y)
    others = [(z + j) % 4 for j in range(1, 4)]
    greet([device(x, core, other, y) for other in others] + [to_x, to_y, to_core])

    def start(src, dst, peer, index):
        copy = remote(src, dst, send.at[index], recv.at[index], peer)
        copy.start()
        return copy

    pend = []
    for a in range(count):
        s0, r0 = bufs[a][0], bufs[a][1]
        for xx in range(2):
            s0[xx] = parts[a][xx, oc].astype(wires[a])
        pend.append(start(s0, r0, to_core, a * 16))
    second = []
    for a in range(count):
        s0, r0, acc, s1x, r1x, s1y, r1y = bufs[a][:7]
        pend[a].wait()
        for xx in range(2):
            acc[xx] = parts[a][xx, core] + r0[xx].astype(F32)
        s1x[...] = acc[ox, pl.ds(0, 2)].astype(wires[a])
        group = [start(s1x, r1x, to_x, a * 16 + 1)]
        for xx in range(2):
            s1y[xx] = acc[xx, pl.ds(2, 2), oy].astype(wires[a])
        group.append(start(s1y, r1y, to_y, a * 16 + 2))
        second.append(group)
    third = []
    for a in range(count):
        s0, r0, acc, s1x, r1x, s1y, r1y, s2, r2, s3, r3 = bufs[a]
        for copy in second[a]:
            copy.wait()
        acc[x, pl.ds(0, 2)] += r1x[...].astype(F32)
        for xx in range(2):
            acc[xx, pl.ds(2, 2), y] += r1y[xx].astype(F32)
        s2[0] = acc[x, pl.ds(0, 2), oy].astype(wires[a])
        s2[1] = acc[ox, pl.ds(2, 2), y].astype(wires[a])
        third.append(
            [
                start(s2.at[0], r2.at[0], to_y, a * 16 + 3),
                start(s2.at[1], r2.at[1], to_x, a * 16 + 4),
            ]
        )
    last = []
    for a in range(count):
        s0, r0, acc, s1x, r1x, s1y, r1y, s2, r2, s3, r3 = bufs[a]
        for copy in third[a]:
            copy.wait()
        acc[x, pl.ds(0, 2), y] += r2[0].astype(F32)
        acc[x, pl.ds(2, 2), y] += r2[1].astype(F32)
        group = []
        for t in range(4):
            s3[t] = acc[x, t, y].astype(wires[a])
        for j, other in enumerate(others):
            group.append(
                start(
                    s3.at[other],
                    r3.at[j],
                    device(x, core, other, y),
                    a * 16 + 5 + j,
                )
            )
        last.append(group)
    for a in range(count):
        acc, r3 = bufs[a][2], bufs[a][10]
        for copy in last[a]:
            copy.wait()
        total = acc[x, z, y]
        for j in range(3):
            total = total + r3[j].astype(F32)
        outs[a][...] = total


def scatter_grads(parts, wires, cid):
    count = len(parts)
    scratch = []
    for part, wire in zip(parts, wires):
        r, w = part.shape[4:]
        scratch += [
            pltpu.VMEM((2, 4, 2, r, w), wire),
            pltpu.VMEM((2, 4, 2, r, w), wire),
            pltpu.VMEM((2, 4, 2, r, w), F32),
            pltpu.VMEM((2, 2, r, w), wire),
            pltpu.VMEM((2, 2, r, w), wire),
            pltpu.VMEM((2, 2, r, w), wire),
            pltpu.VMEM((2, 2, r, w), wire),
            pltpu.VMEM((2, 2, r, w), wire),
            pltpu.VMEM((2, 2, r, w), wire),
            pltpu.VMEM((4, r, w), wire),
            pltpu.VMEM((3, r, w), wire),
        ]
    return pl.pallas_call(
        functools.partial(scatter_kernel, count, wires),
        out_shape=[jax.ShapeDtypeStruct(p.shape[4:], F32) for p in parts],
        in_specs=[VMEM_SPEC] * count,
        out_specs=[VMEM_SPEC] * count,
        scratch_shapes=scratch
        + [pltpu.SemaphoreType.DMA((16 * count,)), pltpu.SemaphoreType.DMA((16 * count,))],
        compiler_params=params(cid),
    )(*parts)


def pair_rows(values, heads):
    rows = values.shape[0]
    shaped = values.reshape(2, rows // 2, heads, HALF)
    return jnp.transpose(shaped, (2, 1, 0, 3)).reshape(heads, rows // 2, 2 * HALF)


def unpair_rows(blocks):
    heads, half_rows, _ = blocks.shape
    shaped = blocks.reshape(heads, half_rows, 2, HALF)
    return jnp.transpose(shaped, (2, 1, 0, 3)).reshape(2 * half_rows, heads * HALF)


def fast_device(
    tokens, piece_starts, qkv_weight, out_weight, up_weight, down_weight, biases, norms, cotangent
):
    seq_rows, width = tokens.shape[1:]
    devices = 32
    length = seq_rows * HEADS
    hidden = up_weight.shape[0] * devices // width
    starts_row = piece_starts[0]
    openings = jnp.arange(length // PIECE, dtype=jnp.int32) * PIECE
    flags = jnp.any(openings[:, None] == starts_row[None, :], axis=1).astype(jnp.int32)

    bias_len = biases.shape[0]
    norm_len = norms.shape[0]
    small = jnp.zeros((16, 128), BF16)
    small = small.at[0, :bias_len].set(biases).at[1, :norm_len].set(norms)
    gathered = gather_weights(
        (
            small,
            qkv_weight.reshape(width // devices, 3 * width),
            out_weight.reshape(width // devices, width),
            up_weight.reshape(width // devices, hidden),
            down_weight.reshape(hidden // devices, width),
        ),
        1,
    )
    small_all = gathered[0].reshape(devices, 16, 128)
    bias_all = small_all[:, 0, :bias_len].reshape(-1).astype(F32)
    norm_all = small_all[:, 1, :norm_len].reshape(-1).astype(F32)
    qkv_mat = gathered[1].reshape(width, 3 * width)
    out_mat = gathered[2].reshape(width, width)
    up_mat = gathered[3].reshape(width, hidden)
    down_mat = gathered[4].reshape(hidden, width)
    bias_q = bias_all[:width]
    bias_v = bias_all[width : 2 * width]
    bias_o = bias_all[2 * width : 3 * width]
    bias_up = bias_all[3 * width : 3 * width + hidden]
    bias_down = bias_all[3 * width + hidden :]
    gain_one = norm_all[:width]
    shift_one = norm_all[width : 2 * width]
    gain_two = norm_all[2 * width : 3 * width]
    shift_two = norm_all[3 * width :]

    inputs = tokens[0].astype(F32)
    first_in = layer_norm(inputs, gain_one, shift_one).astype(BF16)
    projected = jnp.dot(first_in, qkv_mat, preferred_element_type=F32)
    queries = (projected[:, :width] + bias_q).astype(BF16)
    key_rows = projected[:, width : 2 * width].astype(BF16)
    value_rows = (projected[:, 2 * width :] + bias_v).astype(BF16)
    pairs = jnp.concatenate(
        [
            key_rows.reshape(seq_rows, HEADS, HALF),
            value_rows.reshape(seq_rows, HEADS, HALF),
        ],
        axis=2,
    )
    packed = jnp.concatenate(
        [jnp.transpose(pairs, (1, 0, 2)), pair_rows(queries, HEADS)], axis=1
    )
    got = exchange(packed, 2)
    o2, o_heads, lse = attend(flags, got, seq_rows, 2 * seq_rows)
    mixed_b = unpair_rows(exchange(o2, 3))
    after_attn = inputs + jnp.dot(mixed_b, out_mat, preferred_element_type=F32) + bias_o
    second_in = layer_norm(after_attn, gain_two, shift_two).astype(BF16)
    pre_act = jnp.dot(second_in, up_mat, preferred_element_type=F32) + bias_up
    activated = gelu_exact(pre_act).astype(BF16)
    result = after_attn + jnp.dot(activated, down_mat, preferred_element_type=F32) + bias_down
    output = result.astype(BF16)[None]

    upstream = cotangent[0].astype(F32)
    grad_mlp = cotangent[0]
    grad_down_loc = jnp.einsum("ta,tb->ab", activated, grad_mlp, preferred_element_type=F32)
    grad_act = jnp.einsum("tb,ab->ta", grad_mlp, down_mat, preferred_element_type=F32)
    _, gelu_pull = jax.vjp(gelu_exact, pre_act)
    grad_pre = gelu_pull(grad_act)[0].astype(BF16)
    grad_up_loc = jnp.einsum("ta,tb->ab", second_in, grad_pre, preferred_element_type=F32)
    grad_second = jnp.einsum("tb,ab->ta", grad_pre, up_mat, preferred_element_type=F32)
    grad_after_part, grad_gain_two, grad_shift_two = norm_back(
        after_attn, gain_two, shift_two, grad_second
    )
    grad_after = upstream + grad_after_part
    grad_attn = grad_after.astype(BF16)
    grad_out_loc = jnp.einsum("ta,tb->ab", mixed_b, grad_attn, preferred_element_type=F32)
    grad_mixed = jnp.einsum("tb,ab->ta", grad_attn, out_mat, preferred_element_type=F32).astype(
        BF16
    )
    do2 = exchange(pair_rows(grad_mixed, HEADS), 4)
    grads = exchange(attend_back(flags, got, do2, o_heads, lse, seq_rows), 5)
    grad_pairs = jnp.transpose(grads[:, :seq_rows], (1, 0, 2))
    grad_q = unpair_rows(grads[:, seq_rows:])
    grad_k = grad_pairs[:, :, :HALF].reshape(seq_rows, width)
    grad_v = grad_pairs[:, :, HALF:].reshape(seq_rows, width)
    grad_qkv_rows = jnp.concatenate([grad_q, grad_k, grad_v], axis=1)
    grad_qkv_loc = jnp.einsum("ta,tb->ab", first_in, grad_qkv_rows, preferred_element_type=F32)
    grad_first = jnp.einsum("tb,ab->ta", grad_qkv_rows, qkv_mat, preferred_element_type=F32)
    grad_in_part, grad_gain_one, grad_shift_one = norm_back(
        inputs, gain_one, shift_one, grad_first
    )
    grad_tokens = (grad_after + grad_in_part)[None]
    grad_bias_loc = jnp.concatenate(
        [
            column_sum(grad_q),
            column_sum(grad_v),
            column_sum(grad_attn),
            column_sum(grad_pre),
            column_sum(grad_mlp),
        ]
    )
    grad_norm_loc = jnp.concatenate([grad_gain_one, grad_shift_one, grad_gain_two, grad_shift_two])
    small_grad = jnp.concatenate(
        [
            grad_bias_loc.reshape(devices, 1, bias_len),
            jnp.pad(grad_norm_loc.reshape(devices, 1, norm_len), ((0, 0), (0, 0), (0, 128 - norm_len))),
            jnp.zeros((devices, 6, 128), F32),
        ],
        axis=1,
    )
    shape = (2, 2, 4, 2)
    summed = scatter_grads(
        (
            small_grad.reshape(shape + (8, 128)),
            grad_qkv_loc.reshape(shape + (width // devices, 3 * width)),
            grad_out_loc.reshape(shape + (width // devices, width)),
            grad_up_loc.reshape(shape + (width // devices, hidden)),
            grad_down_loc.reshape(shape + (hidden // devices, width)),
        ),
        (F32, BF16, BF16, BF16, BF16),
        6,
    )
    return (
        output,
        grad_tokens,
        summed[1].reshape(-1),
        summed[2].reshape(-1),
        summed[3].reshape(-1),
        summed[4].reshape(-1),
        summed[0][0, :bias_len],
        summed[0][1, :norm_len],
    )


def solution(mesh):
    flat = P(("dp", "ctx"))
    rows = P("dp", "ctx", None)
    fast = mesh.shape["dp"] == 4 and mesh.shape["ctx"] == HEADS
    return jax.shard_map(
        fast_device if fast else general_device,
        mesh=mesh,
        in_specs=(rows, P("dp", None), flat, flat, flat, flat, flat, flat, rows),
        out_specs=(rows, rows, flat, flat, flat, flat, flat, flat),
        check_vma=False,
    )
```

```python
import functools
import math

import jax
import jax.numpy as jnp
from jax import lax
from jax.experimental import pallas as pl
from jax.experimental.pallas import tpu as pltpu
from jax.sharding import PartitionSpec as P

HEADS = 8
PIECE = 256


eps_norm = 1e-05
masked_score = -1e30


def layer_norm(values, gain, shift):
    center = jnp.mean(values, axis=-1, keepdims=True)
    offsets = values - center
    spread = jnp.mean(offsets * offsets, axis=-1, keepdims=True)
    return offsets * lax.rsqrt(spread + eps_norm) * gain + shift


def gelu_exact(values):
    return jax.nn.gelu(values, approximate=False)


def piece_flags(positions, starts_row):
    opening = positions // PIECE * PIECE
    return jnp.any(opening[:, None] == starts_row[None, :], axis=1)


def visible(query_pos, query_flag, key_pos):
    causal = key_pos[None, :] <= query_pos[:, None]
    same_piece = key_pos[None, :] // PIECE == query_pos[:, None] // PIECE
    return jnp.logical_or(causal, jnp.logical_and(same_piece, query_flag[:, None]))


def to_blocks(arrays, shard_rows):
    block_len = 256
    block_count = shard_rows // block_len
    shaped = tuple((member.reshape(block_count, block_len, HEADS, -1) for member in arrays))
    return (block_len, block_count, shaped)


def keep_state(state):
    return state


def unpack(flats, model_width):
    qkv_flat, out_flat, up_flat, down_flat, bias_flat, norm_flat = flats
    hidden = up_flat.shape[0] // model_width
    return (
        qkv_flat.reshape(model_width, 3 * model_width),
        out_flat.reshape(model_width, model_width),
        up_flat.reshape(model_width, hidden),
        down_flat.reshape(hidden, model_width),
        bias_flat.astype(jnp.float32),
        norm_flat.astype(jnp.float32),
    )


def norm_back(values, gain, shift, upstream):
    _, pullback = jax.vjp(layer_norm, values, gain, shift)
    return pullback(upstream)


def column_sum(matrix):
    return jnp.sum(matrix.astype(jnp.float32), axis=0)


def query_terms(
    query_heads,
    grad_heads,
    own_lse,
    own_delta,
    query_pos,
    query_flag,
    key_block,
    value_block,
    key_pos,
    factor,
):
    scores = (
        jnp.einsum("qhd,khd->hqk", query_heads, key_block, preferred_element_type=jnp.float32)
        * factor
    )
    allowed = visible(query_pos, query_flag, key_pos)[None]
    softmax_p = jnp.where(allowed, jnp.exp(scores - own_lse[:, :, None]), 0.0)
    dprobs = jnp.einsum("qhd,khd->hqk", grad_heads, value_block, preferred_element_type=jnp.float32)
    dscores = (softmax_p * (dprobs - own_delta[:, :, None])).astype(jnp.bfloat16)
    return (
        jnp.einsum("hqk,khd->hqd", dscores, key_block, preferred_element_type=jnp.float32) * factor
    )


def key_terms(
    query_block,
    grad_block,
    lse_block,
    delta_block,
    remote_pos,
    remote_flag,
    key_heads,
    value_heads,
    key_pos,
    factor,
):
    scores = (
        jnp.einsum("qhd,khd->hqk", query_block, key_heads, preferred_element_type=jnp.float32)
        * factor
    )
    allowed = visible(remote_pos, remote_flag, key_pos)[None]
    softmax_p = jnp.where(allowed, jnp.exp(scores - lse_block[:, :, None]), 0.0)
    dprobs = jnp.einsum("qhd,khd->hqk", grad_block, value_heads, preferred_element_type=jnp.float32)
    dscores = (softmax_p * (dprobs - delta_block[:, :, None])).astype(jnp.bfloat16)
    grad_keys = (
        jnp.einsum("hqk,qhd->hkd", dscores, query_block, preferred_element_type=jnp.float32)
        * factor
    )
    grad_values = jnp.einsum(
        "hqk,qhd->hkd",
        softmax_p.astype(jnp.bfloat16),
        grad_block,
        preferred_element_type=jnp.float32,
    )
    return (grad_keys, grad_values)


def general_device(
    tokens, piece_starts, qkv_weight, out_weight, up_weight, down_weight, biases, norms, cotangent
):
    model_width = tokens.shape[2]
    seq_rows = tokens.shape[1]
    params = unpack(
        (
            lax.all_gather(qkv_weight, ("dp", "ctx"), axis=0, tiled=True),
            lax.all_gather(out_weight, ("dp", "ctx"), axis=0, tiled=True),
            lax.all_gather(up_weight, ("dp", "ctx"), axis=0, tiled=True),
            lax.all_gather(down_weight, ("dp", "ctx"), axis=0, tiled=True),
            lax.all_gather(biases, ("dp", "ctx"), axis=0, tiled=True),
            lax.all_gather(norms, ("dp", "ctx"), axis=0, tiled=True),
        ),
        model_width,
    )
    qkv_mat, out_mat, up_mat, down_mat, bias_all, norm_all = params
    hidden = up_mat.shape[1]
    head_dim = model_width // HEADS
    factor = head_dim ** (-0.5)
    first_row = lax.axis_index("ctx") * seq_rows
    last_row = first_row + seq_rows - 1
    query_pos = first_row + jnp.arange(seq_rows, dtype=jnp.int32)
    starts_row = piece_starts[0]
    query_flag = piece_flags(query_pos, starts_row)
    bias_q = bias_all[:model_width]
    bias_v = bias_all[model_width : 2 * model_width]
    bias_o = bias_all[2 * model_width : 3 * model_width]
    bias_up = bias_all[3 * model_width : 3 * model_width + hidden]
    bias_down = bias_all[3 * model_width + hidden :]
    gain_one = norm_all[:model_width]
    shift_one = norm_all[model_width : 2 * model_width]
    gain_two = norm_all[2 * model_width : 3 * model_width]
    shift_two = norm_all[3 * model_width :]
    inputs = tokens[0].astype(jnp.float32)
    first_in = layer_norm(inputs, gain_one, shift_one).astype(jnp.bfloat16)
    projected = jnp.dot(first_in, qkv_mat, preferred_element_type=jnp.float32)
    queries = (projected[:, :model_width] + bias_q).astype(jnp.bfloat16)
    key_rows = projected[:, model_width : 2 * model_width].astype(jnp.bfloat16)
    value_rows = (projected[:, 2 * model_width :] + bias_v).astype(jnp.bfloat16)
    query_heads = queries.reshape(seq_rows, HEADS, head_dim)
    key_heads = key_rows.reshape(seq_rows, HEADS, head_dim)
    value_heads = value_rows.reshape(seq_rows, HEADS, head_dim)
    start_state = (
        jnp.full((HEADS, seq_rows), masked_score, jnp.float32),
        jnp.zeros((HEADS, seq_rows), jnp.float32),
        jnp.zeros((HEADS, seq_rows, head_dim), jnp.float32),
    )
    shard = (
        lax.all_gather(key_rows, "ctx", axis=0, tiled=True),
        lax.all_gather(value_rows, "ctx", axis=0, tiled=True),
    )
    shard_rows = shard[0].shape[0]
    block_len, block_count, (key_blocks, value_blocks) = to_blocks(shard, shard_rows)

    def forward_one_block(state, block_in):
        running_max, running_sum, running_acc = state
        key_block, value_block, position = block_in
        key_pos = position * block_len + jnp.arange(block_len, dtype=jnp.int32)
        scores = (
            jnp.einsum("qhd,khd->hqk", query_heads, key_block, preferred_element_type=jnp.float32)
            * factor
        )
        allowed = visible(query_pos, query_flag, key_pos)[None]
        scores = jnp.where(allowed, scores, masked_score)
        new_max = jnp.maximum(running_max, jnp.max(scores, axis=-1))
        correction = jnp.exp(running_max - new_max)
        exp_scores = jnp.where(allowed, jnp.exp(scores - new_max[:, :, None]), 0.0)
        running_sum = running_sum * correction + jnp.sum(exp_scores, axis=-1)
        running_acc = running_acc * correction[:, :, None] + jnp.einsum(
            "hqk,khd->hqd",
            exp_scores.astype(jnp.bfloat16),
            value_block,
            preferred_element_type=jnp.float32,
        )
        return ((new_max, running_sum, running_acc), None)

    def forward_compute(state):
        return lax.scan(
            forward_one_block,
            state,
            (key_blocks, value_blocks, jnp.arange(block_count, dtype=jnp.int32)),
        )[0]

    run_max, run_sum, run_acc = lax.cond(
        jnp.int32(0) <= last_row, forward_compute, keep_state, start_state
    )
    mixed_heads = run_acc / run_sum[:, :, None]
    mixed_f = jnp.transpose(mixed_heads, (1, 0, 2)).reshape(seq_rows, model_width)
    mixed_b = mixed_f.astype(jnp.bfloat16)
    log_sum = run_max + jnp.log(run_sum)
    after_attn = inputs + jnp.dot(mixed_b, out_mat, preferred_element_type=jnp.float32) + bias_o
    second_in = layer_norm(after_attn, gain_two, shift_two).astype(jnp.bfloat16)
    pre_act = jnp.dot(second_in, up_mat, preferred_element_type=jnp.float32) + bias_up
    activated = gelu_exact(pre_act).astype(jnp.bfloat16)
    result = (
        after_attn + jnp.dot(activated, down_mat, preferred_element_type=jnp.float32) + bias_down
    )
    output = result.astype(jnp.bfloat16)[None]
    back = unpack(
        (
            lax.all_gather(qkv_weight, ("dp", "ctx"), axis=0, tiled=True),
            lax.all_gather(out_weight, ("dp", "ctx"), axis=0, tiled=True),
            lax.all_gather(up_weight, ("dp", "ctx"), axis=0, tiled=True),
            lax.all_gather(down_weight, ("dp", "ctx"), axis=0, tiled=True),
            lax.all_gather(biases, ("dp", "ctx"), axis=0, tiled=True),
            lax.all_gather(norms, ("dp", "ctx"), axis=0, tiled=True),
        ),
        model_width,
    )
    qkv_back, out_back, up_back, down_back, bias_back, norm_vec = back
    gain_one_b = norm_vec[:model_width]
    shift_one_b = norm_vec[model_width : 2 * model_width]
    gain_two_b = norm_vec[2 * model_width : 3 * model_width]
    shift_two_b = norm_vec[3 * model_width :]
    upstream = cotangent[0].astype(jnp.float32)
    grad_mlp = upstream.astype(jnp.bfloat16)
    grad_down_loc = jnp.einsum("ta,tb->ab", activated, grad_mlp, preferred_element_type=jnp.float32)
    grad_act = jnp.einsum("tb,ab->ta", grad_mlp, down_back, preferred_element_type=jnp.float32)
    _, gelu_pull = jax.vjp(gelu_exact, pre_act)
    grad_pre = gelu_pull(grad_act)[0].astype(jnp.bfloat16)
    grad_up_loc = jnp.einsum("ta,tb->ab", second_in, grad_pre, preferred_element_type=jnp.float32)
    grad_second = jnp.einsum("tb,ab->ta", grad_pre, up_back, preferred_element_type=jnp.float32)
    grad_after_part, grad_gain_two, grad_shift_two = norm_back(
        after_attn, gain_two_b, shift_two_b, grad_second
    )
    grad_after = upstream + grad_after_part
    grad_attn = grad_after.astype(jnp.bfloat16)
    grad_out_loc = jnp.einsum("ta,tb->ab", mixed_b, grad_attn, preferred_element_type=jnp.float32)
    grad_mixed = jnp.einsum(
        "tb,ab->ta", grad_attn, out_back, preferred_element_type=jnp.float32
    ).astype(jnp.bfloat16)
    grad_heads = grad_mixed.reshape(seq_rows, HEADS, head_dim)
    delta_rows = jnp.sum(
        grad_heads.astype(jnp.float32) * mixed_f.reshape(seq_rows, HEADS, head_dim), axis=-1
    )
    delta_heads = delta_rows.T
    stats = jnp.concatenate([log_sum.T, delta_rows], axis=1)
    all_stats = lax.all_gather(stats, "ctx", axis=0, tiled=True)
    zero_heads = jnp.zeros((HEADS, seq_rows, head_dim), jnp.float32)
    shard = (
        lax.all_gather(key_rows, "ctx", axis=0, tiled=True),
        lax.all_gather(value_rows, "ctx", axis=0, tiled=True),
    )
    shard_rows = shard[0].shape[0]
    query_block_len, query_block_count, (query_key_blocks, query_value_blocks) = to_blocks(
        shard, shard_rows
    )

    def query_one_block(total, block_in):
        key_block, value_block, position = block_in
        key_pos = position * query_block_len + jnp.arange(query_block_len, dtype=jnp.int32)
        term = query_terms(
            query_heads,
            grad_heads,
            log_sum,
            delta_heads,
            query_pos,
            query_flag,
            key_block,
            value_block,
            key_pos,
            factor,
        )
        return (total + term, None)

    def query_compute(total):
        return lax.scan(
            query_one_block,
            total,
            (query_key_blocks, query_value_blocks, jnp.arange(query_block_count, dtype=jnp.int32)),
        )[0]

    grad_q = lax.cond(jnp.int32(0) <= last_row, query_compute, keep_state, zero_heads)
    shard = (
        lax.all_gather(queries, "ctx", axis=0, tiled=True),
        lax.all_gather(grad_mixed, "ctx", axis=0, tiled=True),
    )
    shard_rows = shard[0].shape[0]
    key_block_len, key_block_count, (query_blocks, grad_blocks) = to_blocks(shard, shard_rows)

    def key_one_block(totals, block_in):
        query_block, grad_block, position = block_in
        begin = position * key_block_len
        remote_pos = begin + jnp.arange(key_block_len, dtype=jnp.int32)
        remote_flag = piece_flags(remote_pos, starts_row)
        stats_block = lax.dynamic_slice_in_dim(all_stats, begin, key_block_len, 0)
        lse_block = stats_block[:, :HEADS].T
        delta_block = stats_block[:, HEADS:].T
        grad_keys, grad_values = key_terms(
            query_block,
            grad_block,
            lse_block,
            delta_block,
            remote_pos,
            remote_flag,
            key_heads,
            value_heads,
            query_pos,
            factor,
        )
        return ((totals[0] + grad_keys, totals[1] + grad_values), None)

    def key_compute(totals):
        return lax.scan(
            key_one_block,
            totals,
            (query_blocks, grad_blocks, jnp.arange(key_block_count, dtype=jnp.int32)),
        )[0]

    grad_k, grad_v = lax.cond(
        jnp.int32(0) + shard_rows - 1 >= first_row,
        key_compute,
        keep_state,
        (zero_heads, zero_heads),
    )

    def merge_heads(grad_part):
        return (
            jnp.transpose(grad_part, (1, 0, 2)).reshape(seq_rows, model_width).astype(jnp.bfloat16)
        )

    grad_qkv_rows = jnp.concatenate(
        [merge_heads(grad_q), merge_heads(grad_k), merge_heads(grad_v)], axis=1
    )
    grad_qkv_loc = jnp.einsum(
        "ta,tb->ab", first_in, grad_qkv_rows, preferred_element_type=jnp.float32
    )
    grad_first = jnp.einsum(
        "tb,ab->ta", grad_qkv_rows, qkv_back, preferred_element_type=jnp.float32
    )
    grad_in_part, grad_gain_one, grad_shift_one = norm_back(
        inputs, gain_one_b, shift_one_b, grad_first
    )
    grad_tokens = (grad_after + grad_in_part)[None]
    grad_bias_loc = jnp.concatenate(
        [
            column_sum(grad_qkv_rows[:, :model_width]),
            column_sum(grad_qkv_rows[:, 2 * model_width :]),
            column_sum(grad_attn),
            column_sum(grad_pre),
            column_sum(grad_mlp),
        ]
    )
    grad_norm_loc = jnp.concatenate([grad_gain_one, grad_shift_one, grad_gain_two, grad_shift_two])
    summed = (
        lax.psum_scatter(grad_qkv_loc.reshape(-1), ("dp", "ctx"), scatter_dimension=0, tiled=True),
        lax.psum_scatter(grad_out_loc.reshape(-1), ("dp", "ctx"), scatter_dimension=0, tiled=True),
        lax.psum_scatter(grad_up_loc.reshape(-1), ("dp", "ctx"), scatter_dimension=0, tiled=True),
        lax.psum_scatter(grad_down_loc.reshape(-1), ("dp", "ctx"), scatter_dimension=0, tiled=True),
        lax.psum_scatter(grad_bias_loc, ("dp", "ctx"), scatter_dimension=0, tiled=True),
        lax.psum_scatter(grad_norm_loc, ("dp", "ctx"), scatter_dimension=0, tiled=True),
    )
    return (output, grad_tokens, summed[0], summed[1], summed[2], summed[3], summed[4], summed[5])


MESH = pl.DeviceIdType.MESH
BF16 = jnp.bfloat16
F32 = jnp.float32
VMEM_SPEC = pl.BlockSpec(memory_space=pltpu.VMEM)
SMEM_SPEC = pl.BlockSpec(memory_space=pltpu.SMEM)
ANY_SPEC = pl.BlockSpec(memory_space=pl.ANY)
HALF = 64
NT = (((1,), (1,)), ((), ()))
TN = (((0,), (0,)), ((), ()))
VMEM_LIMIT = 60 << 20


def params(cid=None):
    if cid is None:
        return pltpu.CompilerParams(vmem_limit_bytes=VMEM_LIMIT)
    return pltpu.CompilerParams(
        collective_id=cid, has_side_effects=True, vmem_limit_bytes=VMEM_LIMIT
    )


def place():
    dp = lax.axis_index("dp")
    ctx = lax.axis_index("ctx")
    return dp // 2, dp % 2, ctx // 2, ctx % 2


def device(x, core, z, y):
    return (x * 2 + core, z * 2 + y)


def greet(peers):
    barrier = pltpu.get_barrier_semaphore()
    for peer in peers:
        pl.semaphore_signal(barrier, inc=1, device_id=peer, device_id_type=MESH)
    pl.semaphore_wait(barrier, len(peers))


def remote(src, dst, send, recv, peer):
    return pltpu.make_async_remote_copy(
        src_ref=src,
        dst_ref=dst,
        send_sem=send,
        recv_sem=recv,
        device_id=peer,
        device_id_type=MESH,
    )


def mm(a, b, dims=None):
    if dims is None:
        return jnp.dot(a, b, preferred_element_type=F32)
    return lax.dot_general(a, b, dims, preferred_element_type=F32)


def swap_halves(v):
    return jnp.concatenate([v[:, HALF:], v[:, :HALF]], axis=1)


def left_lanes(rows):
    return lax.broadcasted_iota(jnp.int32, (rows, 2 * HALF), 1) < HALF


def diagonal_mask(size, flags, first, transposed):
    row = lax.broadcasted_iota(jnp.int32, (size, size), 0)
    col = lax.broadcasted_iota(jnp.int32, (size, size), 1)
    key, query = (row, col) if transposed else (col, row)
    allowed = key <= query
    same = (key // PIECE) == (query // PIECE)
    for t in range(size // PIECE):
        inside = jnp.logical_and(same, (query // PIECE) == t)
        allowed = jnp.logical_or(allowed, jnp.logical_and(inside, flags[first + t] > 0))
    return allowed


def xor8(a, b):
    return (
        (a // 4 + b // 4) % 2 * 4 + (a // 2 % 2 + b // 2 % 2) % 2 * 2 + (a % 2 + b % 2) % 2
    )


def unflatten(flat_ref, stage, rows, groups):
    count = rows * groups
    stage[pl.ds(0, count), :] = flat_ref[...].astype(F32)
    return [stage[pl.ds(j, rows, stride=groups), :] for j in range(groups)]


def forward_kernel(
    flags,
    tokens,
    small,
    qkv_flat,
    out_flat,
    up_flat,
    down_flat,
    a1_ref,
    got,
    mix,
    o_ref,
    lse_ref,
    vec_ref,
    qkv_all,
    ou_all,
    down_all,
    stage,
    qkv_own,
    ou_own,
    down_own,
    norm_s,
    packed,
    q_s,
    k_s,
    v_s,
    m_s,
    acc_s,
    o2_s,
    g_own,
    g_send,
    g_recv,
    x_send,
    x_recv,
    o_send,
    o_recv,
):
    x, core, z, y = place()
    ox, oc, oy = 1 - x, 1 - core, 1 - y
    me = z * 2 + y
    width = tokens.shape[1]
    rows = tokens.shape[0]
    half = rows // 2
    tile = 2 * rows
    groups = width // 128
    scale = math.log2(math.e) * HALF**-0.5
    left = left_lanes(rows)
    left_half = left_lanes(half)
    to_x = device(ox, core, z, y)
    to_y = device(x, core, z, oy)
    to_core = device(x, oc, z, y)
    others = [(z + j) % 4 for j in range(1, 4)]

    qkv = unflatten(qkv_flat, stage, 16, 3 * groups)
    left16 = left_lanes(16)
    for j in range(groups):
        k_pair, v_pair = qkv[groups + j], qkv[2 * groups + j]
        at = 128 * j
        qkv_own[:, at : at + 128] = qkv[j].astype(BF16)
        at = 128 * (groups + 2 * j)
        qkv_own[:, at : at + 128] = jnp.where(left16, k_pair, swap_halves(v_pair)).astype(BF16)
        at += 128
        qkv_own[:, at : at + 128] = jnp.where(left16, swap_halves(k_pair), v_pair).astype(BF16)
    qkv_own[:, 3 * width :] = small[...]
    greet(
        [device(x, core, z2, y2) for z2 in [z] + others for y2 in (y, oy)][1:] + [to_x, to_core]
    )

    arrays = ((qkv_own, qkv_all), (ou_own, ou_all), (down_own, down_all))

    def moves(phase, a):
        own, full = arrays[a]
        if phase == 1:
            mine = full.at[x, core, z, y]
            return [(own, mine, device(x, core, o, y), j) for j, o in enumerate(others)]
        if phase == 2:
            part = full.at[x, core, :, y]
            return [(part, part, to_x, 3), (part, part, to_y, 4), (part, part, to_core, 5)]
        if phase == 3:
            low = full.at[x, core, pl.ds(0, 2), oy]
            high = full.at[ox, core, pl.ds(2, 2), y]
            from_x = full.at[ox, core, :, y]
            from_y = full.at[x, core, :, oy]
            return [
                (low, low, to_x, 6),
                (high, high, to_y, 7),
                (from_x, from_x, to_core, 8),
                (from_y, from_y, to_core, 9),
            ]
        part = full.at[ox, core, :, oy]
        return [(part, part, to_core, 10)]

    def phase_copies(phase, a):
        copies = [
            remote(src, dst, g_send.at[a * 11 + n], g_recv.at[a * 11 + n], peer)
            for src, dst, peer, n in moves(phase, a)
        ]
        if phase == 1:
            own, full = arrays[a]
            copies.append(pltpu.make_async_copy(own, full.at[x, core, z, y], g_own.at[a]))
        return copies

    def launch(phase, a):
        for copy in phase_copies(phase, a):
            copy.start()

    def finish(phase, a):
        for copy in phase_copies(phase, a):
            copy.wait()

    launch(1, 0)
    out_parts = unflatten(out_flat, stage, 16, groups)
    for j in range(groups):
        ou_own[:, 128 * j : 128 * (j + 1)] = out_parts[j].astype(BF16)
    up_groups = up_flat.shape[0] // 16
    up_parts = unflatten(up_flat, stage, 16, up_groups)
    for j in range(up_groups):
        at = width + 128 * j
        ou_own[:, at : at + 128] = up_parts[j].astype(BF16)
    down_rows = down_flat.shape[0] // groups
    down_parts = unflatten(down_flat, stage, down_rows, groups)
    for j in range(groups):
        down_own[:, 128 * j : 128 * (j + 1)] = down_parts[j].astype(BF16)
    finish(1, 0)
    launch(2, 0)
    value = tokens[...].astype(F32)
    center = jnp.mean(value, axis=1, keepdims=True)
    offset = value - center
    spread = jnp.mean(offset * offset, axis=1, keepdims=True)
    norm_s[...] = offset * lax.rsqrt(spread + eps_norm)
    finish(2, 0)
    launch(3, 0)
    finish(3, 0)
    launch(4, 0)
    finish(4, 0)

    vec_ref[...] = jnp.zeros_like(vec_ref)
    devices = [(a, b, c, d) for a in range(2) for b in range(2) for c in range(4) for d in range(2)]
    norm_rows = []
    for n, (a, b, c, d) in enumerate(devices):
        piece = qkv_all[a, b, c, d, :, pl.ds(3 * width, 128)].astype(F32)
        vec_ref[0:1, 128 * n : 128 * (n + 1)] = piece[0:1]
        norm_rows.append(piece[1:2, :HALF])
    base = 128 * len(devices)
    for n in range(len(devices) // 2):
        pair = jnp.concatenate([norm_rows[2 * n], norm_rows[2 * n + 1]], axis=1)
        vec_ref[0:1, base + 128 * n : base + 128 * (n + 1)] = pair
    gain = vec_ref[0:1, base : base + width]
    shift = vec_ref[0:1, base + width : base + 2 * width]
    a1_ref[...] = (norm_s[...] * gain + shift).astype(BF16)

    hz = z // 2
    order = ((1 - hz) * 2 + z % 2, (1 - hz) * 2 + 1 - z % 2, hz * 2 + 1 - z % 2, z)
    marks = (4, 6, 2, 0)
    left1 = left_lanes(1)
    for tz, mark in zip(order, marks):
        a1 = a1_ref[...]
        at = pl.multiple_of(128 * tz, 128)
        w_q = qkv_all[:, :, :, :, :, pl.ds(at, 128)].reshape(width, 128)
        q = (mm(a1, w_q) + vec_ref[0:1, pl.ds(at, 128)]).astype(BF16)
        at_kv = pl.multiple_of(width + 256 * tz, 128)
        w_kv = qkv_all[:, :, :, :, :, pl.ds(at_kv, 256)].reshape(width, 256)
        bias = vec_ref[0:1, pl.ds(pl.multiple_of(width + 128 * tz, 128), 128)]
        kv = mm(a1, w_kv)
        even = kv[:, :128] + jnp.where(left1, 0.0, swap_halves(bias))
        odd = kv[:, 128:] + jnp.where(left1, 0.0, bias)
        packed[2 * tz, :rows] = even.astype(BF16)
        packed[2 * tz + 1, :rows] = odd.astype(BF16)
        top, low = q[:half], q[half:]
        packed[2 * tz, rows:] = jnp.where(left_half, top, swap_halves(low))
        packed[2 * tz + 1, rows:] = jnp.where(left_half, swap_halves(top), low)
        for step in range(2):
            ty = (y + step) % 2
            index = mark + step
            src = packed.at[2 * tz + ty]
            if index == 0:
                pltpu.make_async_copy(src, got.at[me], x_recv.at[0]).start()
            else:
                remote(
                    src, got.at[me], x_send.at[index], x_recv.at[index], device(x, core, tz, ty)
                ).start()
    launch(1, 1)
    launch(1, 2)

    def block_wait(sems, index, view):
        pltpu.make_async_copy(view, view, sems.at[index]).wait()

    @pl.loop(0, 4)
    def _(i):
        for t in range(2):
            b = 2 * i + t
            block_wait(x_recv, xor8(b, me), got.at[b])
            at = pl.multiple_of(b * rows, rows)
            pair = got[b, :rows]
            k_s[pl.ds(at, rows), :] = jnp.where(left, pair, 0).astype(BF16)
            v_s[pl.ds(at, rows), :] = jnp.where(left, 1, pair).astype(BF16)
            both = got[b, rows:]
            q_s[pl.ds(at, half), :] = jnp.where(left_half, both, 0).astype(BF16)
            q_s[pl.ds(at + half, half), :] = jnp.where(left_half, swap_halves(both), 0).astype(
                BF16
            )

        @pl.when(i == 1)
        def _():
            for a in (1, 2):
                finish(1, a)
                launch(2, a)

        @pl.when(i == 2)
        def _():
            for a in (1, 2):
                finish(2, a)
                launch(3, a)

        @pl.when(i == 3)
        def _():
            for a in (1, 2):
                finish(3, a)
                launch(4, a)

        at = pl.multiple_of(i * tile, tile)
        q = q_s[pl.ds(at, tile), :]
        s = mm(q, k_s[pl.ds(at, tile), :], NT)
        allowed = diagonal_mask(tile, flags, i * (tile // PIECE), False)
        s = jnp.where(allowed, s, masked_score)
        m = jnp.max(s, axis=1, keepdims=True) * scale
        p = jnp.exp2(s * scale - m)
        m_s[...] = jnp.broadcast_to(m, m_s.shape)
        acc_s[...] = mm(p.astype(BF16), v_s[pl.ds(at, tile), :])

        @pl.loop(0, i)
        def _(j):
            begin = pl.multiple_of(j * tile, tile)
            s = mm(q_s[pl.ds(at, tile), :], k_s[pl.ds(begin, tile), :], NT)
            old = m_s[...]
            new = jnp.maximum(old, jnp.max(s, axis=1, keepdims=True) * scale)
            p = jnp.exp2(s * scale - new[:, :1])
            m_s[...] = new
            acc_s[...] = acc_s[...] * jnp.exp2(old - new) + mm(
                p.astype(BF16), v_s[pl.ds(begin, tile), :]
            )

        acc = acc_s[...]
        total = jnp.broadcast_to(acc[:, :1], acc.shape)
        o = acc / total
        o_ref[pl.ds(at, tile), :] = o
        lse = m_s[...] + jnp.log2(total)
        lse_ref[:, pl.ds(at, tile)] = jnp.transpose(lse)[:8]
        for t in range(2):
            b = 2 * i + t
            top = o[t * rows : t * rows + half]
            low = o[t * rows + half : (t + 1) * rows]
            o2_s[b] = jnp.where(left_half, swap_halves(top), low).astype(BF16)
            index = xor8(b, me)

            @pl.when(b == me)
            def _():
                pltpu.make_async_copy(o2_s.at[b], mix.at[me], o_recv.at[0]).start()

            @pl.when(b != me)
            def _():
                remote(
                    o2_s.at[b],
                    mix.at[me],
                    o_send.at[index],
                    o_recv.at[index],
                    device(x, core, i, t),
                ).start()

    for a in (1, 2):
        finish(4, a)
    for index in range(8):
        block_wait(o_recv, index, mix.at[0])
        if index:
            block_wait(x_send, index, packed.at[0])
            block_wait(o_send, index, o2_s.at[0])


def forward(flags, tokens, small, qkv_flat, out_flat, up_flat, down_flat, cid):
    rows, width = tokens.shape
    length = rows * HEADS
    hidden = up_flat.shape[0] * 128 // 16
    down_rows = down_flat.shape[0] * 128 // width
    lanes = 2 * HALF
    every = (2, 2, 4, 2)
    vmem = pltpu.VMEM
    dma = pltpu.SemaphoreType.DMA
    return pl.pallas_call(
        forward_kernel,
        out_shape=[
            jax.ShapeDtypeStruct((rows, width), BF16),
            jax.ShapeDtypeStruct((HEADS, rows + rows // 2, lanes), BF16),
            jax.ShapeDtypeStruct((HEADS, rows // 2, lanes), BF16),
            jax.ShapeDtypeStruct((length, lanes), F32),
            jax.ShapeDtypeStruct((8, length), F32),
            jax.ShapeDtypeStruct((8, 4096 + 4 * width), F32),
            jax.ShapeDtypeStruct(every + (16, 3 * width + 128), BF16),
            jax.ShapeDtypeStruct(every + (16, width + hidden), BF16),
            jax.ShapeDtypeStruct(every + (down_rows, width), BF16),
        ],
        in_specs=[SMEM_SPEC] + [VMEM_SPEC] * 6,
        out_specs=[VMEM_SPEC] * 7 + [ANY_SPEC] * 2,
        scratch_shapes=[
            vmem((256, 128), F32),
            vmem((16, 3 * width + 128), BF16),
            vmem((16, width + hidden), BF16),
            vmem((down_rows, width), BF16),
            vmem((rows, width), F32),
            vmem((HEADS, rows + rows // 2, lanes), BF16),
            vmem((length, lanes), BF16),
            vmem((length, lanes), BF16),
            vmem((length, lanes), BF16),
            vmem((2 * rows, lanes), F32),
            vmem((2 * rows, lanes), F32),
            vmem((HEADS, rows // 2, lanes), BF16),
            dma((3,)),
            dma((33,)),
            dma((33,)),
            dma((8,)),
            dma((8,)),
            dma((8,)),
            dma((8,)),
        ],
        compiler_params=params(cid),
    )(flags, tokens, small, qkv_flat, out_flat, up_flat, down_flat)


def middle_kernel(
    tokens,
    cot,
    mix,
    vec,
    ou_all,
    down_all,
    out_ref,
    dx_ref,
    do2_ref,
    acc_ou,
    acc_down,
    sums_ref,
    o_s,
    x1_s,
    n2_s,
    a2_s,
    gl_s,
    du_s,
    dh_s,
    da_s,
    r_s,
    send2,
    core_ou,
    core_down,
    got_ou,
    got_down,
    x_send,
    x_recv,
    c_send,
    c_recv,
):
    x, core, z, y = place()
    oc, oy = 1 - core, 1 - y
    me = z * 2 + y
    rows, width = tokens.shape
    half = rows // 2
    hidden = ou_all.shape[-1] - width
    left_half = left_lanes(half)
    to_core = device(x, oc, z, y)
    every = (2, 2, 4, 2)
    greet(
        [device(x, core, (z + a) % 4, (y + b) % 2) for a in range(4) for b in range(2)][1:]
        + [to_core]
    )
    bias_o = vec[0:1, 2 * width : 3 * width]
    bias_down = vec[0:1, 3 * width + hidden : 4 * width + hidden]
    base = 4 * width + hidden
    gain = vec[0:1, base + 2 * width : base + 3 * width]
    shift = vec[0:1, base + 3 * width : base + 4 * width]

    for j in range(HEADS // 2):
        even, odd = mix[2 * j], mix[2 * j + 1]
        at = 128 * j
        o_s[:half, at : at + 128] = jnp.where(left_half, even, swap_halves(odd))
        o_s[half:, at : at + 128] = jnp.where(left_half, swap_halves(even), odd)
    w_out = ou_all[:, :, :, :, :, :width].reshape(width, width)
    x1 = tokens[...].astype(F32) + mm(o_s[...], w_out) + bias_o
    x1_s[...] = x1
    center = jnp.mean(x1, axis=1, keepdims=True)
    offset = x1 - center
    spread = jnp.mean(offset * offset, axis=1, keepdims=True)
    inverse = lax.rsqrt(spread + eps_norm)
    r_s[...] = jnp.broadcast_to(inverse, r_s.shape)
    n2 = offset * inverse
    n2_s[...] = n2
    a2_s[...] = (n2 * gain + shift).astype(BF16)
    sums_ref[...] = jnp.zeros_like(sums_ref)

    @pl.loop(0, hidden // width)
    def _(j):
        at = pl.multiple_of(j * width, width)
        w_up = ou_all[:, :, :, :, :, pl.ds(pl.multiple_of(width + at, width), width)].reshape(
            width, width
        )
        b_up = vec[0:1, pl.ds(pl.multiple_of(3 * width + at, width), width)]
        w_down = down_all[j // 2, j % 2].reshape(width, width)
        u = mm(a2_s[...], w_up) + b_up
        phi = 0.5 * (1.0 + lax.erf(u * (0.5**0.5)))
        slope = phi + u * jnp.exp(-0.5 * u * u) * (1.0 / math.sqrt(2.0 * math.pi))
        gl_s[:, pl.ds(at, width)] = (u * phi).astype(BF16)
        grad = mm(cot[...], w_down, NT)
        du = (grad * slope).astype(BF16)
        du_s[:, pl.ds(at, width)] = du
        sums_ref[0:1, pl.ds(pl.multiple_of(3 * width + at, width), width)] = jnp.sum(
            du.astype(F32), axis=0, keepdims=True
        )
        part = mm(du, w_up, NT)

        @pl.when(j == 0)
        def _():
            dh_s[...] = part

        @pl.when(j > 0)
        def _():
            dh_s[...] += part

    dh2 = dh_s[...]
    n2 = n2_s[...]
    sums_ref[0:1, base + 2 * width : base + 3 * width] = jnp.sum(dh2 * n2, axis=0, keepdims=True)
    sums_ref[0:1, base + 3 * width : base + 4 * width] = jnp.sum(dh2, axis=0, keepdims=True)
    e = dh2 * gain
    mean_e = jnp.mean(e, axis=1, keepdims=True)
    mean_en = jnp.mean(e * n2, axis=1, keepdims=True)
    dx = cot[...].astype(F32) + r_s[:, :1] * (e - mean_e - n2 * mean_en)
    dx_ref[...] = dx
    da = dx.astype(BF16)
    da_s[...] = da
    w_out = ou_all[:, :, :, :, :, :width].reshape(width, width)
    grad_o = mm(da, w_out, NT).astype(BF16)
    for j in range(HEADS // 2):
        group = grad_o[:, 128 * j : 128 * (j + 1)]
        top, low = group[:half], group[half:]
        send2[2 * j] = jnp.where(left_half, top, swap_halves(low))
        send2[2 * j + 1] = jnp.where(left_half, swap_halves(top), low)
    hz = z // 2
    order = ((1 - hz) * 2 + z % 2, (1 - hz) * 2 + 1 - z % 2, hz * 2 + 1 - z % 2, z)
    for tz, mark in zip(order, (4, 6, 2, 0)):
        for step in range(2):
            ty = (y + step) % 2
            index = mark + step
            src = send2.at[2 * tz + ty]
            if index == 0:
                pltpu.make_async_copy(src, do2_ref.at[me], x_recv.at[0]).start()
            else:
                remote(
                    src,
                    do2_ref.at[me],
                    x_send.at[index],
                    x_recv.at[index],
                    device(x, core, tz, ty),
                ).start()

    def grads(c, n):
        dp = 2 * n + c
        at = pl.multiple_of(dp * 128, 128)
        down_at = pl.multiple_of(dp * width, width)
        d_down = mm(gl_s[:, pl.ds(down_at, width)], cot[...], TN)
        d_up = mm(a2_s[:, pl.ds(at, 128)], du_s[...], TN)
        d_out = mm(o_s[:, pl.ds(at, 128)], da_s[...], TN)
        return (
            d_down.reshape(4, 2, width // 8, width),
            d_up.reshape(4, 2, 16, hidden),
            d_out.reshape(4, 2, 16, width),
        )

    for n in range(2):
        d_down, d_up, d_out = grads(oc, n)
        core_down[n] = d_down.astype(BF16)
        core_ou[n, :, :, :, width:] = d_up.astype(BF16)
        core_ou[n, :, :, :, :width] = d_out.astype(BF16)
    to_ou = remote(core_ou, got_ou, c_send.at[0], c_recv.at[0], to_core)
    to_down = remote(core_down, got_down, c_send.at[1], c_recv.at[1], to_core)
    to_ou.start()
    to_down.start()
    sums_ref[0:1, 2 * width : 3 * width] = jnp.sum(da_s[...].astype(F32), axis=0, keepdims=True)
    sums_ref[0:1, 3 * width + hidden : 4 * width + hidden] = jnp.sum(
        cot[...].astype(F32), axis=0, keepdims=True
    )
    result = x1_s[...] + mm(gl_s[...], down_all[...].reshape(hidden, width)) + bias_down
    out_ref[...] = result.astype(BF16)
    for n in range(2):
        d_down, d_up, d_out = grads(core, n)
        acc_down[n] = d_down
        acc_ou[n, :, :, :, width:] = d_up
        acc_ou[n, :, :, :, :width] = d_out
    to_ou.wait()
    to_down.wait()
    acc_ou[...] += got_ou[...].astype(F32)
    acc_down[...] += got_down[...].astype(F32)
    for index in range(8):
        pltpu.make_async_copy(do2_ref.at[0], do2_ref.at[0], x_recv.at[index]).wait()
        if index:
            pltpu.make_async_copy(send2.at[0], send2.at[0], x_send.at[index]).wait()


def middle(tokens, cot, mix, vec, ou_all, down_all, cid):
    rows, width = tokens.shape
    hidden = ou_all.shape[-1] - width
    lanes = 2 * HALF
    vmem = pltpu.VMEM
    dma = pltpu.SemaphoreType.DMA
    ou = (2, 4, 2, 16, width + hidden)
    down = (2, 4, 2, hidden // 32, width)
    return pl.pallas_call(
        middle_kernel,
        out_shape=[
            jax.ShapeDtypeStruct((rows, width), BF16),
            jax.ShapeDtypeStruct((rows, width), F32),
            jax.ShapeDtypeStruct((HEADS, rows // 2, lanes), BF16),
            jax.ShapeDtypeStruct(ou, F32),
            jax.ShapeDtypeStruct(down, F32),
            jax.ShapeDtypeStruct(vec.shape, F32),
        ],
        in_specs=[VMEM_SPEC] * 6,
        out_specs=[VMEM_SPEC] * 6,
        scratch_shapes=[
            vmem((rows, width), BF16),
            vmem((rows, width), F32),
            vmem((rows, width), F32),
            vmem((rows, width), BF16),
            vmem((rows, hidden), BF16),
            vmem((rows, hidden), BF16),
            vmem((rows, width), F32),
            vmem((rows, width), BF16),
            vmem((rows, lanes), F32),
            vmem((HEADS, rows // 2, lanes), BF16),
            vmem(ou, BF16),
            vmem(down, BF16),
            vmem(ou, BF16),
            vmem(down, BF16),
            dma((8,)),
            dma((8,)),
            dma((2,)),
            dma((2,)),
        ],
        compiler_params=params(cid),
    )(tokens, cot, mix, vec, ou_all, down_all)


def reduce_buffers(rows, width, wire):
    vmem = pltpu.VMEM
    return [
        vmem((2, 2, rows, width), wire),
        vmem((2, 2, rows, width), wire),
        vmem((2, 2, rows, width), wire),
        vmem((2, 2, rows, width), wire),
        vmem((2, 2, rows, width), wire),
        vmem((2, 2, rows, width), wire),
        vmem((4, rows, width), wire),
        vmem((3, rows, width), wire),
        vmem((4, rows, width), F32),
    ]


REDUCE_BUFFERS = 9
REDUCE_COPIES = 7


def reducer(acc, bufs, send, recv, first):
    to_wire_x, from_x, to_wire_y, from_y, to_two, from_two, to_three, from_three, total = bufs
    wire = to_wire_x.dtype
    x, core, z, y = place()
    ox, oy = 1 - x, 1 - y
    to_x = device(ox, core, z, y)
    to_y = device(x, core, z, oy)
    others = [(z + j) % 4 for j in range(1, 4)]

    def copies(stage):
        def make(n, src, dst, peer):
            return remote(src, dst, send.at[first + n], recv.at[first + n], peer)

        if stage == 1:
            return [make(0, to_wire_x, from_x, to_x), make(1, to_wire_y, from_y, to_y)]
        if stage == 2:
            return [
                make(2, to_two.at[0], from_two.at[0], to_y),
                make(3, to_two.at[1], from_two.at[1], to_x),
            ]
        return [
            make(4 + j, to_three.at[other], from_three.at[j], device(x, core, other, y))
            for j, other in enumerate(others)
        ]

    def launch(stage):
        if stage == 1:
            to_wire_x[...] = acc[ox, pl.ds(0, 2)].astype(wire)
            for n in range(2):
                to_wire_y[n] = acc[n, pl.ds(2, 2), oy].astype(wire)
        elif stage == 2:
            to_two[0] = (acc[x, pl.ds(0, 2), oy] + from_x[:, oy].astype(F32)).astype(wire)
            to_two[1] = (acc[ox, pl.ds(2, 2), y] + from_y[ox].astype(F32)).astype(wire)
        else:
            low = acc[x, pl.ds(0, 2), y] + from_x[:, y].astype(F32) + from_two[0].astype(F32)
            high = acc[x, pl.ds(2, 2), y] + from_y[x].astype(F32) + from_two[1].astype(F32)
            total[pl.ds(0, 2)] = low
            total[pl.ds(2, 2)] = high
            to_three[pl.ds(0, 2)] = low.astype(wire)
            to_three[pl.ds(2, 2)] = high.astype(wire)
        for copy in copies(stage):
            copy.start()

    def finish(stage):
        for copy in copies(stage):
            copy.wait()

    def result():
        value = total[z]
        for j in range(3):
            value = value + from_three[j].astype(F32)
        return value

    return launch, finish, result


def reduce_peers():
    x, core, z, y = place()
    return [device(x, core, (z + j) % 4, y) for j in range(1, 4)] + [
        device(1 - x, core, z, y),
        device(x, core, z, 1 - y),
    ]


def backward_kernel(*refs):
    flags, got, do2_ref, o_ref, lse_ref, acc_ou, acc_down = refs[:7]
    grads, sum_ou, sum_down = refs[7:10]
    packed, qd_s, k_s, v_s, delta_s, dq_s, dkv_s = refs[10:17]
    bufs_ou = refs[17 : 17 + REDUCE_BUFFERS]
    bufs_down = refs[17 + REDUCE_BUFFERS : 17 + 2 * REDUCE_BUFFERS]
    r_send, r_recv, x_send, x_recv = refs[17 + 2 * REDUCE_BUFFERS :]
    x, core, z, y = place()
    me = z * 2 + y
    blocks = got.shape[0]
    rows = got.shape[1] // 3 * 2
    half = rows // 2
    scale = math.log2(math.e) * HALF**-0.5
    left = left_lanes(rows)
    left_half = left_lanes(half)
    greet(
        [device(x, core, (z + a) % 4, (y + b) % 2) for a in range(4) for b in range(2)][1:]
        + [device(1 - x, core, z, y)]
    )
    sums = (
        reducer(acc_ou, bufs_ou, r_send, r_recv, 0),
        reducer(acc_down, bufs_down, r_send, r_recv, REDUCE_COPIES),
    )
    for launch, _, _ in sums:
        launch(1)

    @pl.loop(0, blocks)
    def _(b):
        at = pl.multiple_of(b * rows, rows)
        pair = got[b, :rows]
        k_s[pl.ds(at, rows), :] = jnp.where(left, pair, 0).astype(BF16)
        v_s[pl.ds(at, rows), :] = jnp.where(left, 0, pair).astype(BF16)
        both = got[b, rows:]
        grad = do2_ref[b]
        top = jnp.where(left_half, both, swap_halves(grad))
        low = jnp.where(left_half, swap_halves(both), grad)
        qd_s[pl.ds(at, half), :] = top
        qd_s[pl.ds(at + half, half), :] = low
        for part, begin in ((top, 0), (low, half)):
            product = jnp.where(
                left_half, 0.0, part.astype(F32) * o_ref[pl.ds(at + begin, half), :]
            )
            delta = jnp.sum(jnp.transpose(product), axis=0, keepdims=True)
            delta_s[:, pl.ds(at + begin, half)] = jnp.broadcast_to(delta, (8, half))
        dq_s[pl.ds(at, rows), :] = jnp.zeros((rows, 2 * HALF), F32)
        dkv_s[pl.ds(at, rows), :] = jnp.zeros((rows, 2 * HALF), F32)

    def tile(kj, qi, diagonal):
        k0 = pl.multiple_of(kj * rows, rows)
        q0 = pl.multiple_of(qi * rows, rows)
        k = k_s[pl.ds(k0, rows), :]
        v = v_s[pl.ds(k0, rows), :]
        qd = qd_s[pl.ds(q0, rows), :]
        scores = mm(k, qd, NT)
        dprobs = mm(v, qd, NT)
        p = jnp.exp2(scores * scale - lse_ref[:1, pl.ds(q0, rows)])
        if diagonal:
            allowed = diagonal_mask(rows, flags, kj * (rows // PIECE), True)
            p = jnp.where(allowed, p, 0.0)
        ds = (p * (dprobs - delta_s[:1, pl.ds(q0, rows)])).astype(BF16)
        dkv_s[pl.ds(k0, rows), :] += jnp.where(left, mm(ds, qd), mm(p.astype(BF16), qd))
        dq_s[pl.ds(q0, rows), :] += mm(ds, k, TN)

    down = 1 - me // (blocks // 2)

    @pl.loop(0, blocks)
    def _(t):
        a = down * (blocks - 1 - t) + (1 - down) * t
        for stage, step in ((1, 2), (2, 4)):

            @pl.when(t == step)
            def _():
                for _, finish, _ in sums:
                    finish(stage)
                for launch, _, _ in sums:
                    launch(stage + 1)

        tile(a, a, True)

        @pl.loop(0, blocks - 1 - t)
        def _(u):
            b = down * u + (1 - down) * (a + 1 + u)
            tile(down * b + (1 - down) * a, down * a + (1 - down) * b, False)

        factor = HALF**-0.5
        at = pl.multiple_of(a * rows, rows)
        block = dkv_s[pl.ds(at, rows), :]
        packed[a, :rows] = jnp.where(left, block * factor, block).astype(BF16)
        top = dq_s[pl.ds(at, half), :]
        low = dq_s[pl.ds(at + half, half), :]
        packed[a, rows:] = (jnp.where(left_half, top, swap_halves(low)) * factor).astype(BF16)
        index = xor8(a, me)

        @pl.when(a == me)
        def _():
            pltpu.make_async_copy(packed.at[a], grads.at[me], x_recv.at[0]).start()

        @pl.when(a != me)
        def _():
            remote(
                packed.at[a],
                grads.at[me],
                x_send.at[index],
                x_recv.at[index],
                device(x, core, a // 2, a % 2),
            ).start()

    for _, finish, _ in sums:
        finish(3)
    sum_ou[...] = sums[0][2]()
    sum_down[...] = sums[1][2]()
    for index in range(blocks):
        pltpu.make_async_copy(grads.at[0], grads.at[0], x_recv.at[index]).wait()
        if index:
            pltpu.make_async_copy(packed.at[0], packed.at[0], x_send.at[index]).wait()


def backward(flags, got, do2, o, lse, acc_ou, acc_down, cid):
    blocks = got.shape[0]
    rows = got.shape[1] // 3 * 2
    length = blocks * rows
    lanes = 2 * HALF
    vmem = pltpu.VMEM
    dma = pltpu.SemaphoreType.DMA
    ou, low = acc_ou.shape[3:], acc_down.shape[3:]
    return pl.pallas_call(
        backward_kernel,
        out_shape=[
            jax.ShapeDtypeStruct(got.shape, BF16),
            jax.ShapeDtypeStruct(ou, F32),
            jax.ShapeDtypeStruct(low, F32),
        ],
        in_specs=[SMEM_SPEC] + [VMEM_SPEC] * 6,
        out_specs=[VMEM_SPEC] * 3,
        scratch_shapes=[
            vmem(got.shape, BF16),
            vmem((length, lanes), BF16),
            vmem((length, lanes), BF16),
            vmem((length, lanes), BF16),
            vmem((8, length), F32),
            vmem((length, lanes), F32),
            vmem((length, lanes), F32),
        ]
        + reduce_buffers(*ou, BF16)
        + reduce_buffers(*low, BF16)
        + [dma((2 * REDUCE_COPIES,)), dma((2 * REDUCE_COPIES,)), dma((blocks,)), dma((blocks,))],
        compiler_params=params(cid),
    )(flags, got, do2, o, lse, acc_ou, acc_down)


def last_kernel(*refs):
    grads, a1, tokens, dx, qkv_all, vec, sums_in = refs[:7]
    out_ref, sum_qkv, sum_small = refs[7:10]
    dqkv_s, sums, core_q, got_q, acc_q, core_small, got_small, acc_small = refs[10:18]
    bufs_q = refs[18 : 18 + REDUCE_BUFFERS]
    bufs_small = refs[18 + REDUCE_BUFFERS : 18 + 2 * REDUCE_BUFFERS]
    r_send, r_recv, c_send, c_recv = refs[18 + 2 * REDUCE_BUFFERS :]
    x, core, z, y = place()
    oc = 1 - core
    to_core = device(x, oc, z, y)
    rows, width = tokens.shape
    half = rows // 2
    left_half = left_lanes(half)
    left1 = left_lanes(1)
    base = vec.shape[1] - 4 * width
    greet(reduce_peers() + [to_core])
    for j in range(HEADS // 2):
        even, odd = grads[2 * j, rows:], grads[2 * j + 1, rows:]
        at = 128 * j
        dqkv_s[:half, at : at + 128] = jnp.where(left_half, even, swap_halves(odd))
        dqkv_s[half:, at : at + 128] = jnp.where(left_half, swap_halves(even), odd)
    for h in range(HEADS):
        at = width + 128 * h
        dqkv_s[:, at : at + 128] = grads[h, :rows]

    def weight_grad(c, n):
        at = pl.multiple_of((2 * n + c) * 128, 128)
        return mm(a1[:, pl.ds(at, 128)], dqkv_s[...], TN).reshape(4, 2, 16, 3 * width)

    for n in range(2):
        core_q[n] = weight_grad(oc, n).astype(BF16)
    over_q = remote(core_q, got_q, c_send.at[0], c_recv.at[0], to_core)
    over_q.start()

    sums[...] = sums_in[...]
    dqkv = dqkv_s[...].astype(F32)
    columns = jnp.sum(dqkv, axis=0, keepdims=True)
    sums[0:1, :width] = columns[:, :width]
    for j in range(HEADS // 2):
        at = width + 256 * j
        pair = jnp.where(
            left1, swap_halves(columns[:, at : at + 128]), columns[:, at + 128 : at + 256]
        )
        sums[0:1, width + 128 * j : width + 128 * (j + 1)] = pair

    w_qkv = qkv_all[:, :, :, :, :, : 3 * width].reshape(width, 3 * width)
    dh = mm(dqkv_s[...], w_qkv, NT)
    gain = vec[0:1, base : base + width]
    value = tokens[...].astype(F32)
    center = jnp.mean(value, axis=1, keepdims=True)
    offset = value - center
    spread = jnp.mean(offset * offset, axis=1, keepdims=True)
    inverse = lax.rsqrt(spread + eps_norm)
    norm = offset * inverse
    sums[0:1, base : base + width] = jnp.sum(dh * norm, axis=0, keepdims=True)
    sums[0:1, base + width : base + 2 * width] = jnp.sum(dh, axis=0, keepdims=True)

    def small_block(a, b, c, d):
        n = (a * 2 + b) * 8 + c * 2 + d
        group = sums[0:1, pl.ds(pl.multiple_of(128 * n, 128), 128)]
        pair = sums[0:1, pl.ds(pl.multiple_of(base + 128 * (n // 2), 128), 128)]
        own = pair if d == 0 else swap_halves(pair)
        return jnp.concatenate([group, own, jnp.zeros((6, 128), F32)], axis=0)

    for a in range(2):
        for c in range(4):
            for d in range(2):
                core_small[a, c, d] = small_block(a, oc, c, d)
                acc_small[a, c, d] = small_block(a, core, c, d)
    over_small = remote(core_small, got_small, c_send.at[1], c_recv.at[1], to_core)
    over_small.start()
    for n in range(2):
        acc_q[n] = weight_grad(core, n)
    over_q.wait()
    acc_q[...] += got_q[...].astype(F32)
    over_small.wait()
    acc_small[...] += got_small[...]
    parts = (
        reducer(acc_q, bufs_q, r_send, r_recv, 0),
        reducer(acc_small, bufs_small, r_send, r_recv, REDUCE_COPIES),
    )
    for launch, _, _ in parts:
        launch(1)
    e = dh * gain
    mean_e = jnp.mean(e, axis=1, keepdims=True)
    mean_en = jnp.mean(e * norm, axis=1, keepdims=True)
    out_ref[...] = dx[...] + inverse * (e - mean_e - norm * mean_en)
    for stage in (1, 2):
        for _, finish, _ in parts:
            finish(stage)
        for launch, _, _ in parts:
            launch(stage + 1)
    for _, finish, _ in parts:
        finish(3)
    sum_qkv[...] = parts[0][2]()
    sum_small[...] = parts[1][2]()


def last(grads, a1, tokens, dx, qkv_all, vec, sums, cid):
    rows, width = tokens.shape
    vmem = pltpu.VMEM
    dma = pltpu.SemaphoreType.DMA
    part = (2, 4, 2, 16, 3 * width)
    small = (2, 4, 2, 8, 128)
    return pl.pallas_call(
        last_kernel,
        out_shape=[
            jax.ShapeDtypeStruct((rows, width), F32),
            jax.ShapeDtypeStruct((16, 3 * width), F32),
            jax.ShapeDtypeStruct((8, 128), F32),
        ],
        in_specs=[VMEM_SPEC] * 7,
        out_specs=[VMEM_SPEC] * 3,
        scratch_shapes=[
            vmem((rows, 3 * width), BF16),
            vmem(sums.shape, F32),
            vmem(part, BF16),
            vmem(part, BF16),
            vmem(part, F32),
            vmem(small, F32),
            vmem(small, F32),
            vmem(small, F32),
        ]
        + reduce_buffers(16, 3 * width, BF16)
        + reduce_buffers(8, 128, F32)
        + [dma((2 * REDUCE_COPIES,)), dma((2 * REDUCE_COPIES,)), dma((2,)), dma((2,))],
        compiler_params=params(cid),
    )(grads, a1, tokens, dx, qkv_all, vec, sums)


def flatten_kernel(sum_qkv, sum_ou, sum_down, sum_small, qkv_o, out_o, up_o, down_o, bias_o, norm_o):
    groups = sum_down.shape[1] // 128
    left = left_lanes(16)

    def group(ref, j):
        return ref[:, 128 * j : 128 * (j + 1)]

    for j in range(groups):
        qkv_o[pl.ds(j, 16, stride=3 * groups), :] = group(sum_qkv, j)
        even, odd = group(sum_qkv, groups + 2 * j), group(sum_qkv, groups + 2 * j + 1)
        qkv_o[pl.ds(groups + j, 16, stride=3 * groups), :] = jnp.where(
            left, even, swap_halves(odd)
        )
        qkv_o[pl.ds(2 * groups + j, 16, stride=3 * groups), :] = jnp.where(
            left, swap_halves(even), odd
        )
        out_o[pl.ds(j, 16, stride=groups), :] = group(sum_ou, j)
        down_o[pl.ds(j, sum_down.shape[0], stride=groups), :] = group(sum_down, j)
    ups = sum_ou.shape[1] // 128 - groups
    for j in range(ups):
        up_o[pl.ds(j, 16, stride=ups), :] = group(sum_ou, groups + j)
    bias_o[...] = sum_small[0:1]
    norm_o[...] = sum_small[1:2, : norm_o.shape[1]]


def flatten(sum_qkv, sum_ou, sum_down, sum_small, norm_len):
    width = sum_down.shape[1]
    sizes = (
        sum_qkv.size // 128,
        width * 16 // 128,
        (sum_ou.shape[1] - width) * 16 // 128,
        sum_down.size // 128,
    )
    return pl.pallas_call(
        flatten_kernel,
        out_shape=[jax.ShapeDtypeStruct((n, 128), F32) for n in sizes]
        + [jax.ShapeDtypeStruct((1, 128), F32), jax.ShapeDtypeStruct((1, norm_len), F32)],
        in_specs=[VMEM_SPEC] * 4,
        out_specs=[VMEM_SPEC] * 6,
        compiler_params=params(),
    )(sum_qkv, sum_ou, sum_down, sum_small)


def fast_device(
    tokens, piece_starts, qkv_weight, out_weight, up_weight, down_weight, biases, norms, cotangent
):
    seq_rows = tokens.shape[1]
    length = seq_rows * HEADS
    openings = jnp.arange(length // PIECE, dtype=jnp.int32) * PIECE
    flags = jnp.any(openings[:, None] == piece_starts[0][None, :], axis=1).astype(jnp.int32)
    bias_len = biases.shape[0]
    norm_len = norms.shape[0]
    small = jnp.concatenate([biases, norms, jnp.zeros((16 * 128 - bias_len - norm_len,), BF16)])
    first_in, got, mix, o_heads, lse, vec, qkv_all, ou_all, down_all = forward(
        flags,
        tokens[0],
        small.reshape(16, 128),
        qkv_weight.reshape(-1, 128),
        out_weight.reshape(-1, 128),
        up_weight.reshape(-1, 128),
        down_weight.reshape(-1, 128),
        1,
    )
    output, grad_after, do2, acc_ou, acc_down, sums = middle(
        tokens[0], cotangent[0], mix, vec, ou_all, down_all, 2
    )
    grads, sum_ou, sum_down = backward(flags, got, do2, o_heads, lse, acc_ou, acc_down, 3)
    grad_tokens, sum_qkv, sum_small = last(
        grads, first_in, tokens[0], grad_after, qkv_all, vec, sums, 4
    )
    flats = flatten(sum_qkv, sum_ou, sum_down, sum_small, norm_len)
    return (output[None], grad_tokens[None]) + tuple(f.reshape(-1) for f in flats)


def solution(mesh):
    flat = P(("dp", "ctx"))
    rows = P("dp", "ctx", None)
    fast = mesh.shape["dp"] == 4 and mesh.shape["ctx"] == HEADS
    return jax.shard_map(
        fast_device if fast else general_device,
        mesh=mesh,
        in_specs=(rows, P("dp", None), flat, flat, flat, flat, flat, flat, rows),
        out_specs=(rows, rows, flat, flat, flat, flat, flat, flat),
        check_vma=False,
    )
```

```python
import math
import types

import jax
import jax.numpy as jnp
from jax import lax
from jax.experimental import pallas as pl
from jax.experimental.pallas import tpu as pltpu
from jax.sharding import PartitionSpec as P

HEADS = 8
PIECE = 256


eps_norm = 1e-05
masked_score = -1e30


def layer_norm(values, gain, shift):
    center = jnp.mean(values, axis=-1, keepdims=True)
    offsets = values - center
    spread = jnp.mean(offsets * offsets, axis=-1, keepdims=True)
    return offsets * lax.rsqrt(spread + eps_norm) * gain + shift


def gelu_exact(values):
    return jax.nn.gelu(values, approximate=False)


def piece_flags(positions, starts_row):
    opening = positions // PIECE * PIECE
    return jnp.any(opening[:, None] == starts_row[None, :], axis=1)


def visible(query_pos, query_flag, key_pos):
    causal = key_pos[None, :] <= query_pos[:, None]
    same_piece = key_pos[None, :] // PIECE == query_pos[:, None] // PIECE
    return jnp.logical_or(causal, jnp.logical_and(same_piece, query_flag[:, None]))


def to_blocks(arrays, shard_rows):
    block_len = 256
    block_count = shard_rows // block_len
    shaped = tuple((member.reshape(block_count, block_len, HEADS, -1) for member in arrays))
    return (block_len, block_count, shaped)


def keep_state(state):
    return state


def unpack(flats, model_width):
    qkv_flat, out_flat, up_flat, down_flat, bias_flat, norm_flat = flats
    hidden = up_flat.shape[0] // model_width
    return (
        qkv_flat.reshape(model_width, 3 * model_width),
        out_flat.reshape(model_width, model_width),
        up_flat.reshape(model_width, hidden),
        down_flat.reshape(hidden, model_width),
        bias_flat.astype(jnp.float32),
        norm_flat.astype(jnp.float32),
    )


def norm_back(values, gain, shift, upstream):
    _, pullback = jax.vjp(layer_norm, values, gain, shift)
    return pullback(upstream)


def column_sum(matrix):
    return jnp.sum(matrix.astype(jnp.float32), axis=0)


def query_terms(
    query_heads,
    grad_heads,
    own_lse,
    own_delta,
    query_pos,
    query_flag,
    key_block,
    value_block,
    key_pos,
    factor,
):
    scores = (
        jnp.einsum("qhd,khd->hqk", query_heads, key_block, preferred_element_type=jnp.float32)
        * factor
    )
    allowed = visible(query_pos, query_flag, key_pos)[None]
    softmax_p = jnp.where(allowed, jnp.exp(scores - own_lse[:, :, None]), 0.0)
    dprobs = jnp.einsum("qhd,khd->hqk", grad_heads, value_block, preferred_element_type=jnp.float32)
    dscores = (softmax_p * (dprobs - own_delta[:, :, None])).astype(jnp.bfloat16)
    return (
        jnp.einsum("hqk,khd->hqd", dscores, key_block, preferred_element_type=jnp.float32) * factor
    )


def key_terms(
    query_block,
    grad_block,
    lse_block,
    delta_block,
    remote_pos,
    remote_flag,
    key_heads,
    value_heads,
    key_pos,
    factor,
):
    scores = (
        jnp.einsum("qhd,khd->hqk", query_block, key_heads, preferred_element_type=jnp.float32)
        * factor
    )
    allowed = visible(remote_pos, remote_flag, key_pos)[None]
    softmax_p = jnp.where(allowed, jnp.exp(scores - lse_block[:, :, None]), 0.0)
    dprobs = jnp.einsum("qhd,khd->hqk", grad_block, value_heads, preferred_element_type=jnp.float32)
    dscores = (softmax_p * (dprobs - delta_block[:, :, None])).astype(jnp.bfloat16)
    grad_keys = (
        jnp.einsum("hqk,qhd->hkd", dscores, query_block, preferred_element_type=jnp.float32)
        * factor
    )
    grad_values = jnp.einsum(
        "hqk,qhd->hkd",
        softmax_p.astype(jnp.bfloat16),
        grad_block,
        preferred_element_type=jnp.float32,
    )
    return (grad_keys, grad_values)


def general_device(
    tokens, piece_starts, qkv_weight, out_weight, up_weight, down_weight, biases, norms, cotangent
):
    model_width = tokens.shape[2]
    seq_rows = tokens.shape[1]
    params = unpack(
        (
            lax.all_gather(qkv_weight, ("dp", "ctx"), axis=0, tiled=True),
            lax.all_gather(out_weight, ("dp", "ctx"), axis=0, tiled=True),
            lax.all_gather(up_weight, ("dp", "ctx"), axis=0, tiled=True),
            lax.all_gather(down_weight, ("dp", "ctx"), axis=0, tiled=True),
            lax.all_gather(biases, ("dp", "ctx"), axis=0, tiled=True),
            lax.all_gather(norms, ("dp", "ctx"), axis=0, tiled=True),
        ),
        model_width,
    )
    qkv_mat, out_mat, up_mat, down_mat, bias_all, norm_all = params
    hidden = up_mat.shape[1]
    head_dim = model_width // HEADS
    factor = head_dim ** (-0.5)
    first_row = lax.axis_index("ctx") * seq_rows
    last_row = first_row + seq_rows - 1
    query_pos = first_row + jnp.arange(seq_rows, dtype=jnp.int32)
    starts_row = piece_starts[0]
    query_flag = piece_flags(query_pos, starts_row)
    bias_q = bias_all[:model_width]
    bias_v = bias_all[model_width : 2 * model_width]
    bias_o = bias_all[2 * model_width : 3 * model_width]
    bias_up = bias_all[3 * model_width : 3 * model_width + hidden]
    bias_down = bias_all[3 * model_width + hidden :]
    gain_one = norm_all[:model_width]
    shift_one = norm_all[model_width : 2 * model_width]
    gain_two = norm_all[2 * model_width : 3 * model_width]
    shift_two = norm_all[3 * model_width :]
    inputs = tokens[0].astype(jnp.float32)
    first_in = layer_norm(inputs, gain_one, shift_one).astype(jnp.bfloat16)
    projected = jnp.dot(first_in, qkv_mat, preferred_element_type=jnp.float32)
    queries = (projected[:, :model_width] + bias_q).astype(jnp.bfloat16)
    key_rows = projected[:, model_width : 2 * model_width].astype(jnp.bfloat16)
    value_rows = (projected[:, 2 * model_width :] + bias_v).astype(jnp.bfloat16)
    query_heads = queries.reshape(seq_rows, HEADS, head_dim)
    key_heads = key_rows.reshape(seq_rows, HEADS, head_dim)
    value_heads = value_rows.reshape(seq_rows, HEADS, head_dim)
    start_state = (
        jnp.full((HEADS, seq_rows), masked_score, jnp.float32),
        jnp.zeros((HEADS, seq_rows), jnp.float32),
        jnp.zeros((HEADS, seq_rows, head_dim), jnp.float32),
    )
    shard = (
        lax.all_gather(key_rows, "ctx", axis=0, tiled=True),
        lax.all_gather(value_rows, "ctx", axis=0, tiled=True),
    )
    shard_rows = shard[0].shape[0]
    block_len, block_count, (key_blocks, value_blocks) = to_blocks(shard, shard_rows)

    def forward_one_block(state, block_in):
        running_max, running_sum, running_acc = state
        key_block, value_block, position = block_in
        key_pos = position * block_len + jnp.arange(block_len, dtype=jnp.int32)
        scores = (
            jnp.einsum("qhd,khd->hqk", query_heads, key_block, preferred_element_type=jnp.float32)
            * factor
        )
        allowed = visible(query_pos, query_flag, key_pos)[None]
        scores = jnp.where(allowed, scores, masked_score)
        new_max = jnp.maximum(running_max, jnp.max(scores, axis=-1))
        correction = jnp.exp(running_max - new_max)
        exp_scores = jnp.where(allowed, jnp.exp(scores - new_max[:, :, None]), 0.0)
        running_sum = running_sum * correction + jnp.sum(exp_scores, axis=-1)
        running_acc = running_acc * correction[:, :, None] + jnp.einsum(
            "hqk,khd->hqd",
            exp_scores.astype(jnp.bfloat16),
            value_block,
            preferred_element_type=jnp.float32,
        )
        return ((new_max, running_sum, running_acc), None)

    def forward_compute(state):
        return lax.scan(
            forward_one_block,
            state,
            (key_blocks, value_blocks, jnp.arange(block_count, dtype=jnp.int32)),
        )[0]

    run_max, run_sum, run_acc = lax.cond(
        jnp.int32(0) <= last_row, forward_compute, keep_state, start_state
    )
    mixed_heads = run_acc / run_sum[:, :, None]
    mixed_f = jnp.transpose(mixed_heads, (1, 0, 2)).reshape(seq_rows, model_width)
    mixed_b = mixed_f.astype(jnp.bfloat16)
    log_sum = run_max + jnp.log(run_sum)
    after_attn = inputs + jnp.dot(mixed_b, out_mat, preferred_element_type=jnp.float32) + bias_o
    second_in = layer_norm(after_attn, gain_two, shift_two).astype(jnp.bfloat16)
    pre_act = jnp.dot(second_in, up_mat, preferred_element_type=jnp.float32) + bias_up
    activated = gelu_exact(pre_act).astype(jnp.bfloat16)
    result = (
        after_attn + jnp.dot(activated, down_mat, preferred_element_type=jnp.float32) + bias_down
    )
    output = result.astype(jnp.bfloat16)[None]
    back = unpack(
        (
            lax.all_gather(qkv_weight, ("dp", "ctx"), axis=0, tiled=True),
            lax.all_gather(out_weight, ("dp", "ctx"), axis=0, tiled=True),
            lax.all_gather(up_weight, ("dp", "ctx"), axis=0, tiled=True),
            lax.all_gather(down_weight, ("dp", "ctx"), axis=0, tiled=True),
            lax.all_gather(biases, ("dp", "ctx"), axis=0, tiled=True),
            lax.all_gather(norms, ("dp", "ctx"), axis=0, tiled=True),
        ),
        model_width,
    )
    qkv_back, out_back, up_back, down_back, bias_back, norm_vec = back
    gain_one_b = norm_vec[:model_width]
    shift_one_b = norm_vec[model_width : 2 * model_width]
    gain_two_b = norm_vec[2 * model_width : 3 * model_width]
    shift_two_b = norm_vec[3 * model_width :]
    upstream = cotangent[0].astype(jnp.float32)
    grad_mlp = upstream.astype(jnp.bfloat16)
    grad_down_loc = jnp.einsum("ta,tb->ab", activated, grad_mlp, preferred_element_type=jnp.float32)
    grad_act = jnp.einsum("tb,ab->ta", grad_mlp, down_back, preferred_element_type=jnp.float32)
    _, gelu_pull = jax.vjp(gelu_exact, pre_act)
    grad_pre = gelu_pull(grad_act)[0].astype(jnp.bfloat16)
    grad_up_loc = jnp.einsum("ta,tb->ab", second_in, grad_pre, preferred_element_type=jnp.float32)
    grad_second = jnp.einsum("tb,ab->ta", grad_pre, up_back, preferred_element_type=jnp.float32)
    grad_after_part, grad_gain_two, grad_shift_two = norm_back(
        after_attn, gain_two_b, shift_two_b, grad_second
    )
    grad_after = upstream + grad_after_part
    grad_attn = grad_after.astype(jnp.bfloat16)
    grad_out_loc = jnp.einsum("ta,tb->ab", mixed_b, grad_attn, preferred_element_type=jnp.float32)
    grad_mixed = jnp.einsum(
        "tb,ab->ta", grad_attn, out_back, preferred_element_type=jnp.float32
    ).astype(jnp.bfloat16)
    grad_heads = grad_mixed.reshape(seq_rows, HEADS, head_dim)
    delta_rows = jnp.sum(
        grad_heads.astype(jnp.float32) * mixed_f.reshape(seq_rows, HEADS, head_dim), axis=-1
    )
    delta_heads = delta_rows.T
    stats = jnp.concatenate([log_sum.T, delta_rows], axis=1)
    all_stats = lax.all_gather(stats, "ctx", axis=0, tiled=True)
    zero_heads = jnp.zeros((HEADS, seq_rows, head_dim), jnp.float32)
    shard = (
        lax.all_gather(key_rows, "ctx", axis=0, tiled=True),
        lax.all_gather(value_rows, "ctx", axis=0, tiled=True),
    )
    shard_rows = shard[0].shape[0]
    query_block_len, query_block_count, (query_key_blocks, query_value_blocks) = to_blocks(
        shard, shard_rows
    )

    def query_one_block(total, block_in):
        key_block, value_block, position = block_in
        key_pos = position * query_block_len + jnp.arange(query_block_len, dtype=jnp.int32)
        term = query_terms(
            query_heads,
            grad_heads,
            log_sum,
            delta_heads,
            query_pos,
            query_flag,
            key_block,
            value_block,
            key_pos,
            factor,
        )
        return (total + term, None)

    def query_compute(total):
        return lax.scan(
            query_one_block,
            total,
            (query_key_blocks, query_value_blocks, jnp.arange(query_block_count, dtype=jnp.int32)),
        )[0]

    grad_q = lax.cond(jnp.int32(0) <= last_row, query_compute, keep_state, zero_heads)
    shard = (
        lax.all_gather(queries, "ctx", axis=0, tiled=True),
        lax.all_gather(grad_mixed, "ctx", axis=0, tiled=True),
    )
    shard_rows = shard[0].shape[0]
    key_block_len, key_block_count, (query_blocks, grad_blocks) = to_blocks(shard, shard_rows)

    def key_one_block(totals, block_in):
        query_block, grad_block, position = block_in
        begin = position * key_block_len
        remote_pos = begin + jnp.arange(key_block_len, dtype=jnp.int32)
        remote_flag = piece_flags(remote_pos, starts_row)
        stats_block = lax.dynamic_slice_in_dim(all_stats, begin, key_block_len, 0)
        lse_block = stats_block[:, :HEADS].T
        delta_block = stats_block[:, HEADS:].T
        grad_keys, grad_values = key_terms(
            query_block,
            grad_block,
            lse_block,
            delta_block,
            remote_pos,
            remote_flag,
            key_heads,
            value_heads,
            query_pos,
            factor,
        )
        return ((totals[0] + grad_keys, totals[1] + grad_values), None)

    def key_compute(totals):
        return lax.scan(
            key_one_block,
            totals,
            (query_blocks, grad_blocks, jnp.arange(key_block_count, dtype=jnp.int32)),
        )[0]

    grad_k, grad_v = lax.cond(
        jnp.int32(0) + shard_rows - 1 >= first_row,
        key_compute,
        keep_state,
        (zero_heads, zero_heads),
    )

    def merge_heads(grad_part):
        return (
            jnp.transpose(grad_part, (1, 0, 2)).reshape(seq_rows, model_width).astype(jnp.bfloat16)
        )

    grad_qkv_rows = jnp.concatenate(
        [merge_heads(grad_q), merge_heads(grad_k), merge_heads(grad_v)], axis=1
    )
    grad_qkv_loc = jnp.einsum(
        "ta,tb->ab", first_in, grad_qkv_rows, preferred_element_type=jnp.float32
    )
    grad_first = jnp.einsum(
        "tb,ab->ta", grad_qkv_rows, qkv_back, preferred_element_type=jnp.float32
    )
    grad_in_part, grad_gain_one, grad_shift_one = norm_back(
        inputs, gain_one_b, shift_one_b, grad_first
    )
    grad_tokens = (grad_after + grad_in_part)[None]
    grad_bias_loc = jnp.concatenate(
        [
            column_sum(grad_qkv_rows[:, :model_width]),
            column_sum(grad_qkv_rows[:, 2 * model_width :]),
            column_sum(grad_attn),
            column_sum(grad_pre),
            column_sum(grad_mlp),
        ]
    )
    grad_norm_loc = jnp.concatenate([grad_gain_one, grad_shift_one, grad_gain_two, grad_shift_two])
    summed = (
        lax.psum_scatter(grad_qkv_loc.reshape(-1), ("dp", "ctx"), scatter_dimension=0, tiled=True),
        lax.psum_scatter(grad_out_loc.reshape(-1), ("dp", "ctx"), scatter_dimension=0, tiled=True),
        lax.psum_scatter(grad_up_loc.reshape(-1), ("dp", "ctx"), scatter_dimension=0, tiled=True),
        lax.psum_scatter(grad_down_loc.reshape(-1), ("dp", "ctx"), scatter_dimension=0, tiled=True),
        lax.psum_scatter(grad_bias_loc, ("dp", "ctx"), scatter_dimension=0, tiled=True),
        lax.psum_scatter(grad_norm_loc, ("dp", "ctx"), scatter_dimension=0, tiled=True),
    )
    return (output, grad_tokens, summed[0], summed[1], summed[2], summed[3], summed[4], summed[5])


MESH = pl.DeviceIdType.MESH
BF16 = jnp.bfloat16
F32 = jnp.float32
VMEM_SPEC = pl.BlockSpec(memory_space=pltpu.VMEM)
SMEM_SPEC = pl.BlockSpec(memory_space=pltpu.SMEM)
ANY_SPEC = pl.BlockSpec(memory_space=pl.ANY)
HALF = 64
NT = (((1,), (1,)), ((), ()))
TN = (((0,), (0,)), ((), ()))
VMEM_LIMIT = 60 << 20


def params(cid=None):
    if cid is None:
        return pltpu.CompilerParams(vmem_limit_bytes=VMEM_LIMIT)
    return pltpu.CompilerParams(
        collective_id=cid, has_side_effects=True, vmem_limit_bytes=VMEM_LIMIT
    )


def place():
    dp = lax.axis_index("dp")
    ctx = lax.axis_index("ctx")
    return dp // 2, dp % 2, ctx // 2, ctx % 2


def device(x, core, z, y):
    return (x * 2 + core, z * 2 + y)


def greet(peers):
    barrier = pltpu.get_barrier_semaphore()
    for peer in peers:
        pl.semaphore_signal(barrier, inc=1, device_id=peer, device_id_type=MESH)
    pl.semaphore_wait(barrier, len(peers))


def remote(src, dst, send, recv, peer):
    return pltpu.make_async_remote_copy(
        src_ref=src,
        dst_ref=dst,
        send_sem=send,
        recv_sem=recv,
        device_id=peer,
        device_id_type=MESH,
    )


def mm(a, b, dims=None):
    if dims is None:
        return jnp.dot(a, b, preferred_element_type=F32)
    return lax.dot_general(a, b, dims, preferred_element_type=F32)


def swap_halves(v):
    return jnp.concatenate([v[:, HALF:], v[:, :HALF]], axis=1)


def left_lanes(rows):
    return lax.broadcasted_iota(jnp.int32, (rows, 2 * HALF), 1) < HALF


def diagonal_mask(size, flags, first, transposed):
    row = lax.broadcasted_iota(jnp.int32, (size, size), 0)
    col = lax.broadcasted_iota(jnp.int32, (size, size), 1)
    key, query = (row, col) if transposed else (col, row)
    allowed = key <= query
    same = (key // PIECE) == (query // PIECE)
    for t in range(size // PIECE):
        inside = jnp.logical_and(same, (query // PIECE) == t)
        allowed = jnp.logical_or(allowed, jnp.logical_and(inside, flags[first + t] > 0))
    return allowed


def xor8(a, b):
    return (
        (a // 4 + b // 4) % 2 * 4 + (a // 2 % 2 + b // 2 % 2) % 2 * 2 + (a % 2 + b % 2) % 2
    )


def unflatten(flat_ref, stage, rows, groups):
    count = rows * groups
    stage[pl.ds(0, count), :] = flat_ref[...].astype(F32)
    return [stage[pl.ds(j, rows, stride=groups), :] for j in range(groups)]


def reduce_buffers(rows, width, wire):
    vmem = pltpu.VMEM
    return [
        vmem((2, 2, rows, width), wire),
        vmem((2, 2, rows, width), wire),
        vmem((2, 2, rows, width), wire),
        vmem((2, 2, rows, width), wire),
        vmem((2, 2, rows, width), wire),
        vmem((2, 2, rows, width), wire),
        vmem((4, rows, width), wire),
        vmem((3, rows, width), wire),
        vmem((4, rows, width), F32),
    ]


REDUCE_BUFFERS = 9
REDUCE_COPIES = 7


def reducer(acc, bufs, send, recv, first):
    to_wire_x, from_x, to_wire_y, from_y, to_two, from_two, to_three, from_three, total = bufs
    wire = to_wire_x.dtype
    x, core, z, y = place()
    ox, oy = 1 - x, 1 - y
    to_x = device(ox, core, z, y)
    to_y = device(x, core, z, oy)
    others = [(z + j) % 4 for j in range(1, 4)]

    def copies(stage):
        def make(n, src, dst, peer):
            return remote(src, dst, send.at[first + n], recv.at[first + n], peer)

        if stage == 1:
            return [make(0, to_wire_x, from_x, to_x), make(1, to_wire_y, from_y, to_y)]
        if stage == 2:
            return [
                make(2, to_two.at[0], from_two.at[0], to_y),
                make(3, to_two.at[1], from_two.at[1], to_x),
            ]
        return [
            make(4 + j, to_three.at[other], from_three.at[j], device(x, core, other, y))
            for j, other in enumerate(others)
        ]

    def launch(stage):
        if stage == 1:
            to_wire_x[...] = acc[ox, pl.ds(0, 2)].astype(wire)
            for n in range(2):
                to_wire_y[n] = acc[n, pl.ds(2, 2), oy].astype(wire)
        elif stage == 2:
            to_two[0] = (acc[x, pl.ds(0, 2), oy] + from_x[:, oy].astype(F32)).astype(wire)
            to_two[1] = (acc[ox, pl.ds(2, 2), y] + from_y[ox].astype(F32)).astype(wire)
        else:
            low = acc[x, pl.ds(0, 2), y] + from_x[:, y].astype(F32) + from_two[0].astype(F32)
            high = acc[x, pl.ds(2, 2), y] + from_y[x].astype(F32) + from_two[1].astype(F32)
            total[pl.ds(0, 2)] = low
            total[pl.ds(2, 2)] = high
            to_three[pl.ds(0, 2)] = low.astype(wire)
            to_three[pl.ds(2, 2)] = high.astype(wire)
        for copy in copies(stage):
            copy.start()

    def finish(stage):
        for copy in copies(stage):
            copy.wait()

    def result():
        value = total[z]
        for j in range(3):
            value = value + from_three[j].astype(F32)
        return value

    return launch, finish, result


def digits(values):
    return sum(v * 4**n for n, v in enumerate(values))


TILES = (
    (
        digits((0, 1, 1, 2, 2, 2, 3, 3, 3, 3)),
        digits((0, 1, 0, 0, 1, 2, 0, 1, 2, 3)),
        digits((1, 0, 1, 0, 0, 1, 0, 0, 0, 1)),
    ),
    (
        digits((2, 3, 3, 2, 3, 0, 2, 3, 1, 1)),
        digits((2, 3, 2, 0, 0, 0, 1, 1, 0, 1)),
        digits((0, 0, 0, 0, 0, 1, 1, 1, 0, 1)),
    ),
)


def forward_phase(r):
    flags = r.flags
    tokens = r.tokens
    small = r.small
    qkv_flat = r.qkv_flat
    out_flat = r.out_flat
    up_flat = r.up_flat
    down_flat = r.down_flat
    a1_ref = r.a1
    got = r.got
    mix = r.mix
    o_ref = r.o_heads
    lse_ref = r.lse
    vec_ref = r.vec
    qkv_all = r.qkv_all
    ou_all = r.ou_all
    down_all = r.down_all
    stage = r.stage
    qkv_own = r.qkv_own
    ou_own = r.ou_own
    down_own = r.down_own
    norm_s = r.n2_s
    packed = r.packed
    q_s = r.q_s
    k_s = r.k_s
    v_s = r.v_s
    m_s = r.m_s
    acc_s = r.acc_s
    o2_s = r.o2_s
    g_own = r.g_own
    g_send = r.g_send
    g_recv = r.g_recv
    f_send = r.f_send
    f_recv = r.f_recv
    x_send = r.x_send
    x_recv = r.x_recv
    o_send = r.o_send
    o_recv = r.o_recv
    x, core, z, y = place()
    ox, oc, oy = 1 - x, 1 - core, 1 - y
    me = z * 2 + y
    width = tokens.shape[1]
    rows = tokens.shape[0]
    half = rows // 2
    tile = 2 * rows
    groups = width // 128
    group = 3 * width // 2
    scale = math.log2(math.e) * HALF**-0.5
    left = left_lanes(rows)
    left_half = left_lanes(half)
    to_x = device(ox, core, z, y)
    to_y = device(x, core, z, oy)
    to_core = device(x, oc, z, y)
    others = [(z + j) % 4 for j in range(1, 4)]

    qkv = unflatten(qkv_flat, stage, 16, 3 * groups)
    left16 = left_lanes(16)
    for j in range(groups):
        k_pair, v_pair = qkv[groups + j], qkv[2 * groups + j]
        at = (j // 2) * group + (j % 2) * 128
        qkv_own[:, at : at + 128] = qkv[j].astype(BF16)
        at = (j // 2) * group + 256 + (j % 2) * 256
        qkv_own[:, at : at + 128] = jnp.where(left16, k_pair, swap_halves(v_pair)).astype(BF16)
        at += 128
        qkv_own[:, at : at + 128] = jnp.where(left16, swap_halves(k_pair), v_pair).astype(BF16)
    qkv_own[:, 3 * width :] = small[...]
    greet(
        [device(x, core, (z + c) % 4, (y + d) % 2) for c in range(4) for d in range(2)][1:]
        + [to_x, to_core]
    )
    arrays = ((qkv_own, qkv_all), (ou_own, ou_all), (down_own, down_all))

    def moves(phase, a):
        own, full = arrays[a]
        if phase == 1:
            mine = full.at[x, core, z, y]
            return [(own, mine, device(x, core, o, y), j) for j, o in enumerate(others)]
        if phase == 2:
            part = full.at[x, core, :, y]
            return [(part, part, to_x, 3), (part, part, to_y, 4), (part, part, to_core, 5)]
        if phase == 3:
            low = full.at[x, core, pl.ds(0, 2), oy]
            high = full.at[ox, core, pl.ds(2, 2), y]
            from_x = full.at[ox, core, :, y]
            from_y = full.at[x, core, :, oy]
            return [
                (low, low, to_x, 6),
                (high, high, to_y, 7),
                (from_x, from_x, to_core, 8),
                (from_y, from_y, to_core, 9),
            ]
        part = full.at[ox, core, :, oy]
        return [(part, part, to_core, 10)]

    def phase_copies(phase, a):
        copies = [
            remote(src, dst, g_send.at[a * 11 + n], g_recv.at[a * 11 + n], peer)
            for src, dst, peer, n in moves(phase, a)
        ]
        if phase == 1:
            own, full = arrays[a]
            copies.append(pltpu.make_async_copy(own, full.at[x, core, z, y], g_own.at[a]))
        return copies

    def launch(phase, a):
        for copy in phase_copies(phase, a):
            copy.start()

    def finish(phase, a):
        for copy in phase_copies(phase, a):
            copy.wait()

    first = arrays[0][1]

    def hop(src, dst, peer, n):
        return remote(src, dst, f_send.at[n], f_recv.at[n], peer)

    def to_xy(c):
        part = first.at[x, core, c, y]
        return hop(part, part, to_x, 4 + c), hop(part, part, to_y, 8 + c)

    def corner(c, over_x):
        if over_x:
            part = first.at[x, core, c, oy]
            return hop(part, part, to_x, 12 + c)
        part = first.at[ox, core, c, y]
        return hop(part, part, to_y, 12 + c)

    def to_sibling(n):
        part = (
            first.at[x, core, :, y],
            first.at[ox, core, :, y],
            first.at[x, core, :, oy],
            first.at[ox, core, :, oy],
        )[n]
        return hop(part, part, to_core, 16 + n)

    own_first = pltpu.make_async_copy(qkv_own, first.at[x, core, z, y], g_own.at[0])
    own_first.start()
    along = [
        hop(qkv_own, first.at[x, core, z, y], device(x, core, other, y), n)
        for n, other in enumerate(others)
    ]
    own_xy = [
        hop(qkv_own, first.at[x, core, z, y], to_x, 4 + z),
        hop(qkv_own, first.at[x, core, z, y], to_y, 8 + z),
    ]
    for copy in along + own_xy:
        copy.start()
    out_parts = unflatten(out_flat, stage, 16, groups)
    for j in range(groups):
        ou_own[:, 128 * j : 128 * (j + 1)] = out_parts[j].astype(BF16)
    up_groups = up_flat.shape[0] // 16
    up_parts = unflatten(up_flat, stage, 16, up_groups)
    for j in range(up_groups):
        at = width + 128 * j
        ou_own[:, at : at + 128] = up_parts[j].astype(BF16)
    down_rows = down_flat.shape[0] // groups
    down_parts = unflatten(down_flat, stage, down_rows, groups)
    for j in range(groups):
        down_own[:, 128 * j : 128 * (j + 1)] = down_parts[j].astype(BF16)
    launch(1, 1)
    launch(1, 2)
    own_first.wait()
    for n in range(3):
        along[n].wait_recv()
        for copy in to_xy((z + 3 - n) % 4):
            copy.start()
    to_sibling(0).start()
    value = tokens[...].astype(F32)
    center = jnp.mean(value, axis=1, keepdims=True)
    offset = value - center
    spread = jnp.mean(offset * offset, axis=1, keepdims=True)
    norm_s[...] = offset * lax.rsqrt(spread + eps_norm)
    for c in [z] + others:
        over_x, over_y = to_xy(c)
        over_x.wait_recv()
        over_y.wait_recv()

        @pl.when(c < 2)
        def _():
            corner(c, True).start()

        @pl.when(c >= 2)
        def _():
            corner(c, False).start()

    to_sibling(1).start()
    to_sibling(2).start()
    for c in range(4):
        corner(c, c < 2).wait()
    to_sibling(3).start()
    for n in range(4):
        to_sibling(n).wait()
    for copy in along:
        copy.wait_send()
    for c in range(4):
        for copy in to_xy(c):
            copy.wait_send()

    vec_ref[...] = jnp.zeros_like(vec_ref)
    devices = [(a, b, c, d) for a in range(2) for b in range(2) for c in range(4) for d in range(2)]
    base = 128 * len(devices)

    def bias_rows(begin, end):
        for n in range(begin, end):
            piece = first[devices[n] + (slice(None), pl.ds(3 * width, 128))].astype(F32)
            vec_ref[0:1, 128 * n : 128 * (n + 1)] = piece[0:1]

    def norm_rows(begin, end):
        for n in range(begin, end):
            pair = [
                first[devices[2 * n + d] + (slice(None), pl.ds(3 * width, 128))].astype(F32)
                for d in range(2)
            ]
            joined = jnp.concatenate([pair[0][1:2, :HALF], pair[1][1:2, :HALF]], axis=1)
            vec_ref[0:1, base + 128 * n : base + 128 * (n + 1)] = joined

    bias_rows(0, 2 * groups)
    norm_rows(0, 2 * groups)
    gain = vec_ref[0:1, base : base + width]
    shift = vec_ref[0:1, base + width : base + 2 * width]
    a1_ref[...] = (norm_s[...] * gain + shift).astype(BF16)

    def part_of(is_query):
        return pl.ds(rows, half) if is_query else pl.ds(0, rows)

    def send_part(tz, mark, is_query):
        for step in range(2):
            ty = (y + step) % 2
            index = mark + step
            src = packed.at[2 * tz + ty, part_of(is_query)]
            dst = got.at[me, part_of(is_query)]
            n = index + 8 * is_query
            if index == 0:
                pltpu.make_async_copy(src, dst, x_recv.at[n]).start()
            else:
                remote(src, dst, x_send.at[n], x_recv.at[n], device(x, core, tz, ty)).start()

    hz = z // 2
    order = (hz * 2 + 1 - z % 2, z, (1 - hz) * 2 + z % 2, (1 - hz) * 2 + 1 - z % 2)
    marks = (2, 0, 4, 6)
    left1 = left_lanes(1)
    for tz, mark in zip(order, marks):
        a1 = a1_ref[...]
        at = pl.multiple_of(tz // 2 * group + tz % 2 * 128, 128)
        w_q = qkv_all[:, :, :, :, :, pl.ds(at, 128)].reshape(width, 128)
        q = (mm(a1, w_q) + vec_ref[0:1, pl.ds(pl.multiple_of(128 * tz, 128), 128)]).astype(BF16)
        at_kv = pl.multiple_of(tz // 2 * group + 256 + tz % 2 * 256, 128)
        w_kv = qkv_all[:, :, :, :, :, pl.ds(at_kv, 256)].reshape(width, 256)
        bias = vec_ref[0:1, pl.ds(pl.multiple_of(width + 128 * tz, 128), 128)]
        kv = mm(a1, w_kv)
        even = kv[:, :128] + jnp.where(left1, 0.0, swap_halves(bias))
        odd = kv[:, 128:] + jnp.where(left1, 0.0, bias)
        packed[2 * tz, :rows] = even.astype(BF16)
        packed[2 * tz + 1, :rows] = odd.astype(BF16)
        top, low = q[:half], q[half:]
        packed[2 * tz, rows:] = jnp.where(left_half, top, swap_halves(low))
        packed[2 * tz + 1, rows:] = jnp.where(left_half, swap_halves(top), low)
        if mark < 4:
            send_part(tz, mark, False)
            send_part(tz, mark, True)

    def send_cross():
        def send_all(is_query):
            for tz, mark in zip(order[2:], marks[2:]):
                send_part(tz, mark, is_query)

        pl.when(hz == 1)(lambda: send_all(True))
        send_all(False)
        pl.when(hz == 0)(lambda: send_all(True))

    pl.when(z % 2 == 0)(send_cross)
    finish(1, 1)
    finish(1, 2)
    launch(2, 1)
    launch(2, 2)
    bias_rows(2 * groups, len(devices))
    norm_rows(2 * groups, len(devices) // 2)

    def block_wait(sems, index, view):
        pltpu.make_async_copy(view, view, sems.at[index]).wait()

    def arrive(part, is_query):
        for t in range(2):
            b = 2 * part + t
            block_wait(x_recv, xor8(b, me) + 8 * is_query, got.at[b, part_of(is_query)])
            at = pl.multiple_of(b * rows, rows)
            if is_query:
                both = got[b, rows:]
                q_s[pl.ds(at, half), :] = jnp.where(left_half, both, 0).astype(BF16)
                q_s[pl.ds(at + half, half), :] = jnp.where(
                    left_half, swap_halves(both), 0
                ).astype(BF16)
            else:
                pair = got[b, :rows]
                k_s[pl.ds(at, rows), :] = jnp.where(left, pair, 0).astype(BF16)
                v_s[pl.ds(at, rows), :] = jnp.where(left, 1, pair).astype(BF16)

    low = 1 - hz
    queries = low * TILES[0][0] + hz * TILES[1][0]
    keys = low * TILES[0][1] + hz * TILES[1][1]
    ends = low * TILES[0][2] + hz * TILES[1][2]
    m_s[...] = jnp.full(m_s.shape, masked_score, F32)
    acc_s[...] = jnp.zeros(acc_s.shape, F32)
    for n in range(2):
        arrive(2 * hz + n, False)
        arrive(2 * hz + n, True)

    def step(n, carry):
        q_left, k_left, e_left = carry
        i, j, done = q_left % 4, k_left % 4, e_left % 4

        @pl.when(n == 3)
        def _():
            pl.when(z % 2 == 1)(send_cross)
            for a in (1, 2):
                finish(2, a)
                launch(3, a)

        @pl.when(n == 6)
        def _():
            for a in (1, 2):
                finish(3, a)
                launch(4, a)

        for when, part, is_query in ((3, 2, 1), (5, 2, 0), (6, 3, 1), (9, 3, 0)):
            pl.when(n == when + 16 * hz)(lambda: arrive(part, is_query))
        for when, part, is_query in ((3, 0, 0), (5, 0, 1), (6, 1, 0), (8, 1, 1)):
            pl.when(n == when + 16 * low)(lambda: arrive(part, is_query))

        at = pl.multiple_of(i * tile, tile)
        begin = pl.multiple_of(j * tile, tile)

        def update(diagonal):
            s = mm(q_s[pl.ds(at, tile), :], k_s[pl.ds(begin, tile), :], NT)
            if diagonal:
                allowed = diagonal_mask(tile, flags, i * (tile // PIECE), False)
                s = jnp.where(allowed, s, masked_score)
            old = m_s[pl.ds(at, tile), :]
            new = jnp.maximum(old, jnp.max(s, axis=1, keepdims=True) * scale)
            p = jnp.exp2(s * scale - new[:, :1])
            m_s[pl.ds(at, tile), :] = new
            acc_s[pl.ds(at, tile), :] = acc_s[pl.ds(at, tile), :] * jnp.exp2(old - new) + mm(
                p.astype(BF16), v_s[pl.ds(begin, tile), :]
            )

        pl.when(i == j)(lambda: update(True))
        pl.when(i != j)(lambda: update(False))

        @pl.when(done == 1)
        def _():
            acc = acc_s[pl.ds(at, tile), :]
            total = jnp.broadcast_to(acc[:, :1], acc.shape)
            o = acc / total
            o_ref[pl.ds(at, tile), :] = o
            lse = m_s[pl.ds(at, tile), :] + jnp.log2(total)
            lse_ref[:, pl.ds(at, tile)] = jnp.transpose(lse)[:8]
            for t in range(2):
                b = 2 * i + t
                top = o[t * rows : t * rows + half]
                bottom = o[t * rows + half : (t + 1) * rows]
                o2_s[b] = jnp.where(left_half, swap_halves(top), bottom).astype(BF16)
                index = xor8(b, me)

                @pl.when(b == me)
                def _():
                    pltpu.make_async_copy(o2_s.at[b], mix.at[me], o_recv.at[0]).start()

                @pl.when(b != me)
                def _():
                    remote(
                        o2_s.at[b],
                        mix.at[me],
                        o_send.at[index],
                        o_recv.at[index],
                        device(x, core, i, t),
                    ).start()

        return q_left // 4, k_left // 4, e_left // 4

    lax.fori_loop(0, 10, step, (queries, keys, ends))
    for a in (1, 2):
        finish(4, a)
    for index in range(8):
        block_wait(o_recv, index, mix.at[0])
        if index:
            block_wait(x_send, index, packed.at[0, part_of(False)])
            block_wait(x_send, index + 8, packed.at[0, part_of(True)])
            block_wait(o_send, index, o2_s.at[0])


def middle_phase(r):
    tokens = r.tokens
    cot = r.cot
    mix = r.mix
    vec = r.vec
    ou_all = r.ou_all
    down_all = r.down_all
    out_ref = r.out_ref
    dx_ref = r.n2_s
    do2_ref = r.do2
    acc_ou = r.acc_ou
    acc_down = r.acc_down
    sums_ref = r.sums
    o_s = r.o_s
    x1_s = r.x1_s
    n2_s = r.n2_s
    a2_s = r.a2_s
    gl_s = r.gl_s
    du_s = r.du_s
    dh_s = r.dh_s
    da_s = r.da_s
    r_s = r.r_s
    send2 = r.o2_s
    core_ou = r.core_ou
    core_down = r.core_down
    got_ou = r.got_ou
    got_down = r.got_down
    x_send = r.d_send
    x_recv = r.d_recv
    c_send = r.c_send
    c_recv = r.c_recv
    x, core, z, y = place()
    oc, oy = 1 - core, 1 - y
    me = z * 2 + y
    rows, width = tokens.shape
    half = rows // 2
    hidden = ou_all.shape[-1] - width
    left_half = left_lanes(half)
    to_core = device(x, oc, z, y)
    bias_o = vec[0:1, 2 * width : 3 * width]
    bias_down = vec[0:1, 3 * width + hidden : 4 * width + hidden]
    base = 4 * width + hidden
    gain = vec[0:1, base + 2 * width : base + 3 * width]
    shift = vec[0:1, base + 3 * width : base + 4 * width]

    for j in range(HEADS // 2):
        even, odd = mix[2 * j], mix[2 * j + 1]
        at = 128 * j
        o_s[:half, at : at + 128] = jnp.where(left_half, even, swap_halves(odd))
        o_s[half:, at : at + 128] = jnp.where(left_half, swap_halves(even), odd)
    w_out = ou_all[:, :, :, :, :, :width].reshape(width, width)
    x1 = tokens[...].astype(F32) + mm(o_s[...], w_out) + bias_o
    x1_s[...] = x1
    center = jnp.mean(x1, axis=1, keepdims=True)
    offset = x1 - center
    spread = jnp.mean(offset * offset, axis=1, keepdims=True)
    inverse = lax.rsqrt(spread + eps_norm)
    r_s[...] = jnp.broadcast_to(inverse, r_s.shape)
    n2 = offset * inverse
    n2_s[...] = n2
    a2_s[...] = (n2 * gain + shift).astype(BF16)
    sums_ref[...] = jnp.zeros_like(sums_ref)

    @pl.loop(0, hidden // width)
    def _(j):
        at = pl.multiple_of(j * width, width)
        w_up = ou_all[:, :, :, :, :, pl.ds(pl.multiple_of(width + at, width), width)].reshape(
            width, width
        )
        b_up = vec[0:1, pl.ds(pl.multiple_of(3 * width + at, width), width)]
        w_down = down_all[j // 2, j % 2].reshape(width, width)
        u = mm(a2_s[...], w_up) + b_up
        phi = 0.5 * (1.0 + lax.erf(u * (0.5**0.5)))
        slope = phi + u * jnp.exp(-0.5 * u * u) * (1.0 / math.sqrt(2.0 * math.pi))
        gl_s[:, pl.ds(at, width)] = (u * phi).astype(BF16)
        grad = mm(cot[...], w_down, NT)
        du = (grad * slope).astype(BF16)
        du_s[:, pl.ds(at, width)] = du
        sums_ref[0:1, pl.ds(pl.multiple_of(3 * width + at, width), width)] = jnp.sum(
            du.astype(F32), axis=0, keepdims=True
        )
        part = mm(du, w_up, NT)

        @pl.when(j == 0)
        def _():
            dh_s[...] = part

        @pl.when(j > 0)
        def _():
            dh_s[...] += part

    dh2 = dh_s[...]
    n2 = n2_s[...]
    sums_ref[0:1, base + 2 * width : base + 3 * width] = jnp.sum(dh2 * n2, axis=0, keepdims=True)
    sums_ref[0:1, base + 3 * width : base + 4 * width] = jnp.sum(dh2, axis=0, keepdims=True)
    e = dh2 * gain
    mean_e = jnp.mean(e, axis=1, keepdims=True)
    mean_en = jnp.mean(e * n2, axis=1, keepdims=True)
    dx = cot[...].astype(F32) + r_s[:, :1] * (e - mean_e - n2 * mean_en)
    dx_ref[...] = dx
    da = dx.astype(BF16)
    da_s[...] = da
    w_out = ou_all[:, :, :, :, :, :width].reshape(width, width)
    grad_o = mm(da, w_out, NT).astype(BF16)
    for j in range(HEADS // 2):
        group = grad_o[:, 128 * j : 128 * (j + 1)]
        top, low = group[:half], group[half:]
        send2[2 * j] = jnp.where(left_half, top, swap_halves(low))
        send2[2 * j + 1] = jnp.where(left_half, swap_halves(top), low)
    hz = z // 2
    order = ((1 - hz) * 2 + z % 2, (1 - hz) * 2 + 1 - z % 2, hz * 2 + 1 - z % 2, z)
    for tz, mark in zip(order, (4, 6, 2, 0)):
        for step in range(2):
            ty = (y + step) % 2
            index = mark + step
            src = send2.at[2 * tz + ty]
            if index == 0:
                pltpu.make_async_copy(src, do2_ref.at[me], x_recv.at[0]).start()
            else:
                remote(
                    src,
                    do2_ref.at[me],
                    x_send.at[index],
                    x_recv.at[index],
                    device(x, core, tz, ty),
                ).start()

    def grads(c, n):
        dp = 2 * n + c
        at = pl.multiple_of(dp * 128, 128)
        down_at = pl.multiple_of(dp * width, width)
        d_down = mm(gl_s[:, pl.ds(down_at, width)], cot[...], TN)
        d_up = mm(a2_s[:, pl.ds(at, 128)], du_s[...], TN)
        d_out = mm(o_s[:, pl.ds(at, 128)], da_s[...], TN)
        return (
            d_down.reshape(4, 2, width // 8, width),
            d_up.reshape(4, 2, 16, hidden),
            d_out.reshape(4, 2, 16, width),
        )

    for n in range(2):
        d_down, d_up, d_out = grads(oc, n)
        core_down[n] = d_down.astype(BF16)
        core_ou[n, :, :, :, width:] = d_up.astype(BF16)
        core_ou[n, :, :, :, :width] = d_out.astype(BF16)
    to_ou = remote(core_ou, got_ou, c_send.at[0], c_recv.at[0], to_core)
    to_down = remote(core_down, got_down, c_send.at[1], c_recv.at[1], to_core)
    to_ou.start()
    to_down.start()
    sums_ref[0:1, 2 * width : 3 * width] = jnp.sum(da_s[...].astype(F32), axis=0, keepdims=True)
    sums_ref[0:1, 3 * width + hidden : 4 * width + hidden] = jnp.sum(
        cot[...].astype(F32), axis=0, keepdims=True
    )
    result = x1_s[...] + mm(gl_s[...], down_all[...].reshape(hidden, width)) + bias_down
    out_ref[...] = result.astype(BF16)
    for n in range(2):
        d_down, d_up, d_out = grads(core, n)
        acc_down[n] = d_down
        acc_ou[n, :, :, :, width:] = d_up
        acc_ou[n, :, :, :, :width] = d_out
    to_ou.wait()
    to_down.wait()
    acc_ou[...] += got_ou[...].astype(F32)
    acc_down[...] += got_down[...].astype(F32)


def lanes_of(ref, r, g):
    group = r.tokens.shape[1] * 3 // 2
    return ref.at[:, :, :, :, pl.ds(pl.multiple_of(g * group, 128), group)]


def reducer_of(r, name, first, at=None):
    bufs = [getattr(r, f"{name}{n}") for n in range(REDUCE_BUFFERS)]
    if at is not None:
        return reducer(lanes_of(r.acc_ou, r, at), [b.at[at] for b in bufs], r.r_send, r.r_recv, first)
    acc = getattr(r, f"acc_{name}")
    return reducer(acc, bufs, r.r_send, r.r_recv, first)


def backward_phase(r):
    got, do2, o_heads, lse, grads, packed = r.got, r.do2, r.o_heads, r.lse, r.grads, r.packed
    qd_s, k_s, v_s, delta_s, dq_s, dkv_s = r.q_s, r.k_s, r.v_s, r.delta_s, r.acc_s, r.m_s
    flags = r.flags
    x, core, z, y = place()
    me = z * 2 + y
    hz = z // 2
    low = 1 - hz
    blocks = got.shape[0]
    rows = got.shape[1] // 3 * 2
    half = rows // 2
    quarter = blocks // 2
    scale = math.log2(math.e) * HALF**-0.5
    factor = HALF**-0.5
    left = left_lanes(rows)
    left_half = left_lanes(half)
    sums = (reducer_of(r, "ou", 0), reducer_of(r, "down", REDUCE_COPIES))
    for launch, _, _ in sums:
        launch(1)

    def enter(b):
        at = pl.multiple_of(b * rows, rows)
        pltpu.make_async_copy(do2.at[b], do2.at[b], r.d_recv.at[xor8(b, me)]).wait()
        v_s[pl.ds(at, rows), :] = jnp.where(left, 0, v_s[pl.ds(at, rows), :]).astype(BF16)
        grad = do2[b]
        for part, begin in ((swap_halves(grad), 0), (grad, half)):
            rows_at = pl.ds(at + begin, half)
            qd_s[rows_at, :] = jnp.where(left_half, qd_s[rows_at, :], part)
            product = jnp.where(left_half, 0.0, part.astype(F32) * o_heads[rows_at, :])
            delta = jnp.sum(jnp.transpose(product), axis=0, keepdims=True)
            delta_s[:, rows_at] = jnp.broadcast_to(delta, (8, half))
        dq_s[pl.ds(at, rows), :] = jnp.zeros((rows, 2 * HALF), F32)
        dkv_s[pl.ds(at, rows), :] = jnp.zeros((rows, 2 * HALF), F32)

    def tile(kj, qi, diagonal):
        k0 = pl.multiple_of(kj * rows, rows)
        q0 = pl.multiple_of(qi * rows, rows)
        k = k_s[pl.ds(k0, rows), :]
        v = v_s[pl.ds(k0, rows), :]
        qd = qd_s[pl.ds(q0, rows), :]
        scores = mm(k, qd, NT)
        dprobs = mm(v, qd, NT)
        p = jnp.exp2(scores * scale - lse[:1, pl.ds(q0, rows)])
        if diagonal:
            allowed = diagonal_mask(rows, flags, kj * (rows // PIECE), True)
            p = jnp.where(allowed, p, 0.0)
        ds = (p * (dprobs - delta_s[:1, pl.ds(q0, rows)])).astype(BF16)
        dkv_s[pl.ds(k0, rows), :] += jnp.where(left, mm(ds, qd), mm(p.astype(BF16), qd))
        dq_s[pl.ds(q0, rows), :] += mm(ds, k, TN)

    def part_of(is_query):
        return pl.ds(rows, half) if is_query else pl.ds(0, rows)

    def leave(a, is_query):
        at = pl.multiple_of(a * rows, rows)
        if is_query:
            top = dq_s[pl.ds(at, half), :]
            bottom = dq_s[pl.ds(at + half, half), :]
            packed[a, rows:] = (
                jnp.where(left_half, top, swap_halves(bottom)) * factor
            ).astype(BF16)
        else:
            block = dkv_s[pl.ds(at, rows), :]
            packed[a, :rows] = jnp.where(left, block * factor, block).astype(BF16)
        index = xor8(a, me) + 8 * is_query
        src = packed.at[a, part_of(is_query)]
        dst = grads.at[me, part_of(is_query)]

        @pl.when(a == me)
        def _():
            pltpu.make_async_copy(src, dst, r.b_recv.at[index]).start()

        @pl.when(a != me)
        def _():
            remote(
                src, dst, r.b_send.at[index], r.b_recv.at[index], device(x, core, a // 2, a % 2)
            ).start()

    for n in range(quarter):
        enter(hz * quarter + n)

    @pl.loop(0, 12)
    def _(row):
        seg = (row + 3) // 4
        last = seg // 3
        first = (3 - seg) // 3
        square = seg // 2 - last
        cross = seg % 2 - last
        own = first + last
        i = (row + 3) % 4 + last - 3 * first

        @pl.when(row == 1)
        def _():
            for n in range(quarter):
                enter(low * quarter + n)

        for stage, step in ((1, 4), (2, 6)):

            @pl.when(row == step)
            def _():
                for _, finish, _ in sums:
                    finish(stage)
                for launch, _, _ in sums:
                    launch(stage + 1)

        a_low = own * (3 - i) + (1 - own) * (7 - i)
        a_high = own * (4 + i) + (1 - own) * i
        a = low * a_low + hz * a_high
        count = own * (3 - i) + cross * i + square * 4

        @pl.when(square == 0)
        def _():
            tile(a, a, True)

        @pl.loop(0, count)
        def _(u):
            k_low = (own + square) * u + cross * a_low
            q_low = (own + square) * a_low + cross * (7 - u)
            k_high = (own + square) * a_high + cross * u
            q_high = own * (5 + i + u) + cross * a_high + square * (4 + u)
            tile(low * k_low + hz * k_high, low * q_low + hz * q_high, False)

        @pl.when(cross * hz + square * low + last > 0)
        def _():
            leave(a, 1)

        @pl.when(cross * low + square * hz + last > 0)
        def _():
            leave(a, 0)

        @pl.when(row == 8)
        def _():
            begin = low * 3 + hz * 4
            leave(begin, 1)
            leave(begin, 0)


def last_phase(r):
    grads, a1, tokens, dx, qkv_all, vec, sums = (
        r.grads,
        r.a1,
        r.tokens,
        r.n2_s,
        r.qkv_all,
        r.vec,
        r.sums,
    )
    dqkv_s, got_q = r.gl_s, r.got_q
    core_small, got_small, acc_small = r.core_small, r.got_small, r.acc_small
    x, core, z, y = place()
    me = z * 2 + y
    hz = z // 2
    oc = 1 - core
    to_core = device(x, oc, z, y)
    rows, width = tokens.shape
    half = rows // 2
    group = 3 * width // 2
    left_half = left_lanes(half)
    left1 = left_lanes(1)
    base = vec.shape[1] - 4 * width

    def columns_of(g):
        return pl.ds(pl.multiple_of(g * group, 128), group)

    def enter(g):
        for n in range(HEADS // 2):
            h = g * (HEADS // 2) + n
            for is_query in range(2):
                view = grads.at[h, pl.ds(rows, half) if is_query else pl.ds(0, rows)]
                pltpu.make_async_copy(view, view, r.b_recv.at[xor8(h, me) + 8 * is_query]).wait()
        begin = g * group
        for j in range(HEADS // 4):
            h = g * (HEADS // 2) + 2 * j
            even, odd = grads[h, rows:], grads[h + 1, rows:]
            at = pl.ds(pl.multiple_of(begin + 128 * j, 128), 128)
            dqkv_s[:half, at] = jnp.where(left_half, even, swap_halves(odd))
            dqkv_s[half:, at] = jnp.where(left_half, swap_halves(even), odd)
        for n in range(HEADS // 2):
            at = pl.ds(pl.multiple_of(begin + 256 + 128 * n, 128), 128)
            dqkv_s[:, at] = grads[g * (HEADS // 2) + n, :rows]

    def weight_grad(c, n, g):
        at = pl.multiple_of((2 * n + c) * 128, 128)
        return mm(a1[:, pl.ds(at, 128)], dqkv_s[:, columns_of(g)], TN).reshape(4, 2, 16, group)

    def over(g):
        return remote(lanes_of(r.core_ou, r, g), got_q.at[g], r.e_send.at[g], r.e_recv.at[g], to_core)

    parts = []
    for position, g in enumerate((1 - hz, hz)):
        enter(g)
        for n in range(2):
            lanes_of(r.core_ou, r, g)[n] = weight_grad(oc, n, g).astype(BF16)
        over(g).start()
        w = qkv_all[:, :, :, :, :, columns_of(g)].reshape(width, group)
        part = mm(dqkv_s[:, columns_of(g)], w, NT)
        if position:
            r.dh_s[...] += part
        else:
            r.dh_s[...] = part
        for n in range(2):
            lanes_of(r.acc_ou, r, g)[n] = weight_grad(core, n, g)
        over(g).wait()
        acc_q = lanes_of(r.acc_ou, r, g)
        acc_q[...] = acc_q[...] + got_q[g].astype(F32)
        parts.append(reducer_of(r, "q", (2 + g) * REDUCE_COPIES, g))
        parts[-1][0](1)

    columns = jnp.sum(dqkv_s[:, : 3 * width].astype(F32), axis=0, keepdims=True)
    for j in range(HEADS // 2):
        at = (j // 2) * group + (j % 2) * 128
        sums[0:1, 128 * j : 128 * (j + 1)] = columns[:, at : at + 128]
        at = (j // 2) * group + 256 + (j % 2) * 256
        pair = jnp.where(
            left1, swap_halves(columns[:, at : at + 128]), columns[:, at + 128 : at + 256]
        )
        sums[0:1, width + 128 * j : width + 128 * (j + 1)] = pair
    dh = r.dh_s[...]
    gain = vec[0:1, base : base + width]
    value = tokens[...].astype(F32)
    center = jnp.mean(value, axis=1, keepdims=True)
    offset = value - center
    spread = jnp.mean(offset * offset, axis=1, keepdims=True)
    inverse = lax.rsqrt(spread + eps_norm)
    norm = offset * inverse
    sums[0:1, base : base + width] = jnp.sum(dh * norm, axis=0, keepdims=True)
    sums[0:1, base + width : base + 2 * width] = jnp.sum(dh, axis=0, keepdims=True)

    def small_block(a, b, c, d):
        n = (a * 2 + b) * 8 + c * 2 + d
        piece = sums[0:1, pl.ds(pl.multiple_of(128 * n, 128), 128)]
        pair = sums[0:1, pl.ds(pl.multiple_of(base + 128 * (n // 2), 128), 128)]
        own = pair if d == 0 else swap_halves(pair)
        return jnp.concatenate([piece, own, jnp.zeros((6, 128), F32)], axis=0)

    for a in range(2):
        for c in range(4):
            for d in range(2):
                core_small[a, c, d] = small_block(a, oc, c, d)
                acc_small[a, c, d] = small_block(a, core, c, d)
    over_small = remote(core_small, got_small, r.e_send.at[2], r.e_recv.at[2], to_core)
    over_small.start()
    parts[0][1](1)
    parts[0][0](2)
    over_small.wait()
    acc_small[...] += got_small[...]
    parts.append(reducer_of(r, "small", 4 * REDUCE_COPIES))
    parts[2][0](1)
    e = dh * gain
    mean_e = jnp.mean(e, axis=1, keepdims=True)
    mean_en = jnp.mean(e * norm, axis=1, keepdims=True)
    r.grad_tokens[...] = dx[...] + inverse * (e - mean_e - norm * mean_en)
    parts[1][1](1)
    parts[1][0](2)
    parts[0][1](2)
    parts[0][0](3)
    parts[2][1](1)
    parts[2][0](2)
    parts[1][1](2)
    parts[1][0](3)
    parts[2][1](2)
    parts[2][0](3)
    for part in (reducer_of(r, "ou", 0), reducer_of(r, "down", REDUCE_COPIES)):
        part[1](3)
    r.sum_ou[...] = reducer_of(r, "ou", 0)[2]()
    r.sum_down[...] = reducer_of(r, "down", REDUCE_COPIES)[2]()
    for _, finish, _ in parts:
        finish(3)
    for g, part in zip((1 - hz, hz), parts):
        r.sum_qkv[g] = part[2]()
    r.sum_small[...] = parts[2][2]()
    for index in range(HEADS):
        if index:
            for is_query, count in ((0, rows), (1, half)):
                view = r.packed.at[0, pl.ds(rows * is_query, count)]
                pltpu.make_async_copy(view, view, r.b_send.at[index + 8 * is_query]).wait()
            view = r.o2_s.at[0]
            pltpu.make_async_copy(view, view, r.d_send.at[index]).wait()


def layer_kernel(names, *refs):
    r = types.SimpleNamespace(**dict(zip(names, refs)))
    forward_phase(r)
    middle_phase(r)
    backward_phase(r)
    last_phase(r)


def layer(inputs, cid):
    rows, width = inputs["tokens"].shape
    length = rows * HEADS
    lanes = 2 * HALF
    hidden = inputs["up_flat"].shape[0] * 128 // 16
    down_rows = inputs["down_flat"].shape[0] * 128 // width
    group = 3 * width // 2
    every = (2, 2, 4, 2)
    mine = (2, 4, 2)
    row = (8, 4096 + 4 * width)
    vmem = pltpu.VMEM
    dma = pltpu.SemaphoreType.DMA
    outputs = {
        "out_ref": jax.ShapeDtypeStruct((rows, width), BF16),
        "grad_tokens": jax.ShapeDtypeStruct((rows, width), F32),
        "sum_qkv": jax.ShapeDtypeStruct((2, 16, group), F32),
        "sum_ou": jax.ShapeDtypeStruct((16, width + hidden), F32),
        "sum_down": jax.ShapeDtypeStruct((down_rows, width), F32),
        "sum_small": jax.ShapeDtypeStruct((8, 128), F32),
    }
    scratch = {
        "a1": vmem((rows, width), BF16),
        "got": vmem((HEADS, rows + rows // 2, lanes), BF16),
        "mix": vmem((HEADS, rows // 2, lanes), BF16),
        "o_heads": vmem((length, lanes), F32),
        "lse": vmem((8, length), F32),
        "vec": vmem(row, F32),
        "qkv_all": vmem(every + (16, 3 * width + 128), BF16),
        "ou_all": vmem(every + (16, width + hidden), BF16),
        "down_all": vmem(every + (down_rows, width), BF16),
        "stage": vmem((256, 128), F32),
        "qkv_own": vmem((16, 3 * width + 128), BF16),
        "ou_own": vmem((16, width + hidden), BF16),
        "down_own": vmem((down_rows, width), BF16),
        "packed": vmem((HEADS, rows + rows // 2, lanes), BF16),
        "q_s": vmem((length, lanes), BF16),
        "k_s": vmem((length, lanes), BF16),
        "v_s": vmem((length, lanes), BF16),
        "m_s": vmem((length, lanes), F32),
        "acc_s": vmem((length, lanes), F32),
        "o2_s": vmem((HEADS, rows // 2, lanes), BF16),
        "do2": vmem((HEADS, rows // 2, lanes), BF16),
        "acc_ou": vmem(mine + (16, width + hidden), F32),
        "acc_down": vmem(mine + (down_rows, width), F32),
        "sums": vmem(row, F32),
        "o_s": vmem((rows, width), BF16),
        "x1_s": vmem((rows, width), F32),
        "n2_s": vmem((rows, width), F32),
        "a2_s": vmem((rows, width), BF16),
        "gl_s": vmem((rows, hidden), BF16),
        "du_s": vmem((rows, hidden), BF16),
        "dh_s": vmem((rows, width), F32),
        "da_s": vmem((rows, width), BF16),
        "r_s": vmem((rows, lanes), F32),
        "core_ou": vmem(mine + (16, width + hidden), BF16),
        "core_down": vmem(mine + (down_rows, width), BF16),
        "got_ou": vmem(mine + (16, width + hidden), BF16),
        "got_down": vmem(mine + (down_rows, width), BF16),
        "delta_s": vmem((8, length), F32),
        "grads": vmem((HEADS, rows + rows // 2, lanes), BF16),
        "got_q": vmem((2,) + mine + (16, group), BF16),
        "core_small": vmem(mine + (8, 128), F32),
        "got_small": vmem(mine + (8, 128), F32),
        "acc_small": vmem(mine + (8, 128), F32),
    }
    for name, lead, r, w, wire in (
        ("ou", (), 16, width + hidden, BF16),
        ("down", (), down_rows, width, BF16),
        ("q", (2,), 16, group, BF16),
        ("small", (), 8, 128, F32),
    ):
        for n, buf in enumerate(reduce_buffers(r, w, wire)):
            scratch[f"{name}{n}"] = vmem(lead + buf.shape, buf.dtype)
    for name, count in (
        ("g_own", 3),
        ("g_send", 33),
        ("g_recv", 33),
        ("f_send", 20),
        ("f_recv", 20),
        ("x_send", 16),
        ("x_recv", 16),
        ("o_send", 8),
        ("o_recv", 8),
        ("d_send", 8),
        ("d_recv", 8),
        ("c_send", 2),
        ("c_recv", 2),
        ("r_send", 5 * REDUCE_COPIES),
        ("r_recv", 5 * REDUCE_COPIES),
        ("b_send", 16),
        ("b_recv", 16),
        ("e_send", 3),
        ("e_recv", 3),
    ):
        scratch[name] = dma((count,))
    names = tuple(inputs) + tuple(outputs) + tuple(scratch)

    def kernel(*refs):
        layer_kernel(names, *refs)

    return pl.pallas_call(
        kernel,
        out_shape=list(outputs.values()),
        in_specs=[SMEM_SPEC if n == "flags" else VMEM_SPEC for n in inputs],
        out_specs=[VMEM_SPEC] * len(outputs),
        scratch_shapes=list(scratch.values()),
        compiler_params=params(cid),
    )(*inputs.values())


def flatten_kernel(sum_qkv, sum_ou, sum_down, sum_small, qkv_o, out_o, up_o, down_o, bias_o, norm_o):
    groups = sum_down.shape[1] // 128
    left = left_lanes(16)

    def group(ref, j):
        return ref[:, 128 * j : 128 * (j + 1)]

    for j in range(groups):
        part = sum_qkv.at[j // 2]
        pair = j % 2
        qkv_o[pl.ds(j, 16, stride=3 * groups), :] = group(part, pair)
        even, odd = group(part, 2 + 2 * pair), group(part, 3 + 2 * pair)
        qkv_o[pl.ds(groups + j, 16, stride=3 * groups), :] = jnp.where(
            left, even, swap_halves(odd)
        )
        qkv_o[pl.ds(2 * groups + j, 16, stride=3 * groups), :] = jnp.where(
            left, swap_halves(even), odd
        )
        out_o[pl.ds(j, 16, stride=groups), :] = group(sum_ou, j)
        down_o[pl.ds(j, sum_down.shape[0], stride=groups), :] = group(sum_down, j)
    ups = sum_ou.shape[1] // 128 - groups
    for j in range(ups):
        up_o[pl.ds(j, 16, stride=ups), :] = group(sum_ou, groups + j)
    bias_o[...] = sum_small[0:1]
    norm_o[...] = sum_small[1:2, : norm_o.shape[1]]


def flatten(sum_qkv, sum_ou, sum_down, sum_small, norm_len):
    width = sum_down.shape[1]
    sizes = (
        sum_qkv.size // 128,
        width * 16 // 128,
        (sum_ou.shape[1] - width) * 16 // 128,
        sum_down.size // 128,
    )
    return pl.pallas_call(
        flatten_kernel,
        out_shape=[jax.ShapeDtypeStruct((n, 128), F32) for n in sizes]
        + [jax.ShapeDtypeStruct((1, 128), F32), jax.ShapeDtypeStruct((1, norm_len), F32)],
        in_specs=[VMEM_SPEC] * 4,
        out_specs=[VMEM_SPEC] * 6,
        compiler_params=params(),
    )(sum_qkv, sum_ou, sum_down, sum_small)


def fast_device(
    tokens, piece_starts, qkv_weight, out_weight, up_weight, down_weight, biases, norms, cotangent
):
    length = tokens.shape[1] * HEADS
    openings = jnp.arange(length // PIECE, dtype=jnp.int32) * PIECE
    flags = jnp.any(openings[:, None] == piece_starts[0][None, :], axis=1).astype(jnp.int32)
    bias_len = biases.shape[0]
    norm_len = norms.shape[0]
    small = jnp.concatenate([biases, norms, jnp.zeros((16 * 128 - bias_len - norm_len,), BF16)])
    output, grad_tokens, sum_qkv, sum_ou, sum_down, sum_small = layer(
        {
            "flags": flags,
            "tokens": tokens[0],
            "cot": cotangent[0],
            "small": small.reshape(16, 128),
            "qkv_flat": qkv_weight.reshape(-1, 128),
            "out_flat": out_weight.reshape(-1, 128),
            "up_flat": up_weight.reshape(-1, 128),
            "down_flat": down_weight.reshape(-1, 128),
        },
        1,
    )
    flats = flatten(sum_qkv, sum_ou, sum_down, sum_small, norm_len)
    return (output[None], grad_tokens[None]) + tuple(f.reshape(-1) for f in flats)


def solution(mesh):
    flat = P(("dp", "ctx"))
    rows = P("dp", "ctx", None)
    fast = mesh.shape["dp"] == 4 and mesh.shape["ctx"] == HEADS
    return jax.shard_map(
        fast_device if fast else general_device,
        mesh=mesh,
        in_specs=(rows, P("dp", None), flat, flat, flat, flat, flat, flat, rows),
        out_specs=(rows, rows, flat, flat, flat, flat, flat, flat),
        check_vma=False,
    )
```

```python
import math
import types

import jax
import jax.numpy as jnp
from jax import lax
from jax.experimental import pallas as pl
from jax.experimental.pallas import tpu as pltpu
from jax.sharding import PartitionSpec as P

HEADS = 8
PIECE = 256


eps_norm = 1e-05
masked_score = -1e30


def layer_norm(values, gain, shift):
    center = jnp.mean(values, axis=-1, keepdims=True)
    offsets = values - center
    spread = jnp.mean(offsets * offsets, axis=-1, keepdims=True)
    return offsets * lax.rsqrt(spread + eps_norm) * gain + shift


def gelu_exact(values):
    return jax.nn.gelu(values, approximate=False)


def piece_flags(positions, starts_row):
    opening = positions // PIECE * PIECE
    return jnp.any(opening[:, None] == starts_row[None, :], axis=1)


def visible(query_pos, query_flag, key_pos):
    causal = key_pos[None, :] <= query_pos[:, None]
    same_piece = key_pos[None, :] // PIECE == query_pos[:, None] // PIECE
    return jnp.logical_or(causal, jnp.logical_and(same_piece, query_flag[:, None]))


def to_blocks(arrays, shard_rows):
    block_len = 256
    block_count = shard_rows // block_len
    shaped = tuple((member.reshape(block_count, block_len, HEADS, -1) for member in arrays))
    return (block_len, block_count, shaped)


def keep_state(state):
    return state


def unpack(flats, model_width):
    qkv_flat, out_flat, up_flat, down_flat, bias_flat, norm_flat = flats
    hidden = up_flat.shape[0] // model_width
    return (
        qkv_flat.reshape(model_width, 3 * model_width),
        out_flat.reshape(model_width, model_width),
        up_flat.reshape(model_width, hidden),
        down_flat.reshape(hidden, model_width),
        bias_flat.astype(jnp.float32),
        norm_flat.astype(jnp.float32),
    )


def norm_back(values, gain, shift, upstream):
    _, pullback = jax.vjp(layer_norm, values, gain, shift)
    return pullback(upstream)


def column_sum(matrix):
    return jnp.sum(matrix.astype(jnp.float32), axis=0)


def query_terms(
    query_heads,
    grad_heads,
    own_lse,
    own_delta,
    query_pos,
    query_flag,
    key_block,
    value_block,
    key_pos,
    factor,
):
    scores = (
        jnp.einsum("qhd,khd->hqk", query_heads, key_block, preferred_element_type=jnp.float32)
        * factor
    )
    allowed = visible(query_pos, query_flag, key_pos)[None]
    softmax_p = jnp.where(allowed, jnp.exp(scores - own_lse[:, :, None]), 0.0)
    dprobs = jnp.einsum("qhd,khd->hqk", grad_heads, value_block, preferred_element_type=jnp.float32)
    dscores = (softmax_p * (dprobs - own_delta[:, :, None])).astype(jnp.bfloat16)
    return (
        jnp.einsum("hqk,khd->hqd", dscores, key_block, preferred_element_type=jnp.float32) * factor
    )


def key_terms(
    query_block,
    grad_block,
    lse_block,
    delta_block,
    remote_pos,
    remote_flag,
    key_heads,
    value_heads,
    key_pos,
    factor,
):
    scores = (
        jnp.einsum("qhd,khd->hqk", query_block, key_heads, preferred_element_type=jnp.float32)
        * factor
    )
    allowed = visible(remote_pos, remote_flag, key_pos)[None]
    softmax_p = jnp.where(allowed, jnp.exp(scores - lse_block[:, :, None]), 0.0)
    dprobs = jnp.einsum("qhd,khd->hqk", grad_block, value_heads, preferred_element_type=jnp.float32)
    dscores = (softmax_p * (dprobs - delta_block[:, :, None])).astype(jnp.bfloat16)
    grad_keys = (
        jnp.einsum("hqk,qhd->hkd", dscores, query_block, preferred_element_type=jnp.float32)
        * factor
    )
    grad_values = jnp.einsum(
        "hqk,qhd->hkd",
        softmax_p.astype(jnp.bfloat16),
        grad_block,
        preferred_element_type=jnp.float32,
    )
    return (grad_keys, grad_values)


def general_device(
    tokens, piece_starts, qkv_weight, out_weight, up_weight, down_weight, biases, norms, cotangent
):
    model_width = tokens.shape[2]
    seq_rows = tokens.shape[1]
    params = unpack(
        (
            lax.all_gather(qkv_weight, ("dp", "ctx"), axis=0, tiled=True),
            lax.all_gather(out_weight, ("dp", "ctx"), axis=0, tiled=True),
            lax.all_gather(up_weight, ("dp", "ctx"), axis=0, tiled=True),
            lax.all_gather(down_weight, ("dp", "ctx"), axis=0, tiled=True),
            lax.all_gather(biases, ("dp", "ctx"), axis=0, tiled=True),
            lax.all_gather(norms, ("dp", "ctx"), axis=0, tiled=True),
        ),
        model_width,
    )
    qkv_mat, out_mat, up_mat, down_mat, bias_all, norm_all = params
    hidden = up_mat.shape[1]
    head_dim = model_width // HEADS
    factor = head_dim ** (-0.5)
    first_row = lax.axis_index("ctx") * seq_rows
    last_row = first_row + seq_rows - 1
    query_pos = first_row + jnp.arange(seq_rows, dtype=jnp.int32)
    starts_row = piece_starts[0]
    query_flag = piece_flags(query_pos, starts_row)
    bias_q = bias_all[:model_width]
    bias_v = bias_all[model_width : 2 * model_width]
    bias_o = bias_all[2 * model_width : 3 * model_width]
    bias_up = bias_all[3 * model_width : 3 * model_width + hidden]
    bias_down = bias_all[3 * model_width + hidden :]
    gain_one = norm_all[:model_width]
    shift_one = norm_all[model_width : 2 * model_width]
    gain_two = norm_all[2 * model_width : 3 * model_width]
    shift_two = norm_all[3 * model_width :]
    inputs = tokens[0].astype(jnp.float32)
    first_in = layer_norm(inputs, gain_one, shift_one).astype(jnp.bfloat16)
    projected = jnp.dot(first_in, qkv_mat, preferred_element_type=jnp.float32)
    queries = (projected[:, :model_width] + bias_q).astype(jnp.bfloat16)
    key_rows = projected[:, model_width : 2 * model_width].astype(jnp.bfloat16)
    value_rows = (projected[:, 2 * model_width :] + bias_v).astype(jnp.bfloat16)
    query_heads = queries.reshape(seq_rows, HEADS, head_dim)
    key_heads = key_rows.reshape(seq_rows, HEADS, head_dim)
    value_heads = value_rows.reshape(seq_rows, HEADS, head_dim)
    start_state = (
        jnp.full((HEADS, seq_rows), masked_score, jnp.float32),
        jnp.zeros((HEADS, seq_rows), jnp.float32),
        jnp.zeros((HEADS, seq_rows, head_dim), jnp.float32),
    )
    shard = (
        lax.all_gather(key_rows, "ctx", axis=0, tiled=True),
        lax.all_gather(value_rows, "ctx", axis=0, tiled=True),
    )
    shard_rows = shard[0].shape[0]
    block_len, block_count, (key_blocks, value_blocks) = to_blocks(shard, shard_rows)

    def forward_one_block(state, block_in):
        running_max, running_sum, running_acc = state
        key_block, value_block, position = block_in
        key_pos = position * block_len + jnp.arange(block_len, dtype=jnp.int32)
        scores = (
            jnp.einsum("qhd,khd->hqk", query_heads, key_block, preferred_element_type=jnp.float32)
            * factor
        )
        allowed = visible(query_pos, query_flag, key_pos)[None]
        scores = jnp.where(allowed, scores, masked_score)
        new_max = jnp.maximum(running_max, jnp.max(scores, axis=-1))
        correction = jnp.exp(running_max - new_max)
        exp_scores = jnp.where(allowed, jnp.exp(scores - new_max[:, :, None]), 0.0)
        running_sum = running_sum * correction + jnp.sum(exp_scores, axis=-1)
        running_acc = running_acc * correction[:, :, None] + jnp.einsum(
            "hqk,khd->hqd",
            exp_scores.astype(jnp.bfloat16),
            value_block,
            preferred_element_type=jnp.float32,
        )
        return ((new_max, running_sum, running_acc), None)

    def forward_compute(state):
        return lax.scan(
            forward_one_block,
            state,
            (key_blocks, value_blocks, jnp.arange(block_count, dtype=jnp.int32)),
        )[0]

    run_max, run_sum, run_acc = lax.cond(
        jnp.int32(0) <= last_row, forward_compute, keep_state, start_state
    )
    mixed_heads = run_acc / run_sum[:, :, None]
    mixed_f = jnp.transpose(mixed_heads, (1, 0, 2)).reshape(seq_rows, model_width)
    mixed_b = mixed_f.astype(jnp.bfloat16)
    log_sum = run_max + jnp.log(run_sum)
    after_attn = inputs + jnp.dot(mixed_b, out_mat, preferred_element_type=jnp.float32) + bias_o
    second_in = layer_norm(after_attn, gain_two, shift_two).astype(jnp.bfloat16)
    pre_act = jnp.dot(second_in, up_mat, preferred_element_type=jnp.float32) + bias_up
    activated = gelu_exact(pre_act).astype(jnp.bfloat16)
    result = (
        after_attn + jnp.dot(activated, down_mat, preferred_element_type=jnp.float32) + bias_down
    )
    output = result.astype(jnp.bfloat16)[None]
    back = unpack(
        (
            lax.all_gather(qkv_weight, ("dp", "ctx"), axis=0, tiled=True),
            lax.all_gather(out_weight, ("dp", "ctx"), axis=0, tiled=True),
            lax.all_gather(up_weight, ("dp", "ctx"), axis=0, tiled=True),
            lax.all_gather(down_weight, ("dp", "ctx"), axis=0, tiled=True),
            lax.all_gather(biases, ("dp", "ctx"), axis=0, tiled=True),
            lax.all_gather(norms, ("dp", "ctx"), axis=0, tiled=True),
        ),
        model_width,
    )
    qkv_back, out_back, up_back, down_back, bias_back, norm_vec = back
    gain_one_b = norm_vec[:model_width]
    shift_one_b = norm_vec[model_width : 2 * model_width]
    gain_two_b = norm_vec[2 * model_width : 3 * model_width]
    shift_two_b = norm_vec[3 * model_width :]
    upstream = cotangent[0].astype(jnp.float32)
    grad_mlp = upstream.astype(jnp.bfloat16)
    grad_down_loc = jnp.einsum("ta,tb->ab", activated, grad_mlp, preferred_element_type=jnp.float32)
    grad_act = jnp.einsum("tb,ab->ta", grad_mlp, down_back, preferred_element_type=jnp.float32)
    _, gelu_pull = jax.vjp(gelu_exact, pre_act)
    grad_pre = gelu_pull(grad_act)[0].astype(jnp.bfloat16)
    grad_up_loc = jnp.einsum("ta,tb->ab", second_in, grad_pre, preferred_element_type=jnp.float32)
    grad_second = jnp.einsum("tb,ab->ta", grad_pre, up_back, preferred_element_type=jnp.float32)
    grad_after_part, grad_gain_two, grad_shift_two = norm_back(
        after_attn, gain_two_b, shift_two_b, grad_second
    )
    grad_after = upstream + grad_after_part
    grad_attn = grad_after.astype(jnp.bfloat16)
    grad_out_loc = jnp.einsum("ta,tb->ab", mixed_b, grad_attn, preferred_element_type=jnp.float32)
    grad_mixed = jnp.einsum(
        "tb,ab->ta", grad_attn, out_back, preferred_element_type=jnp.float32
    ).astype(jnp.bfloat16)
    grad_heads = grad_mixed.reshape(seq_rows, HEADS, head_dim)
    delta_rows = jnp.sum(
        grad_heads.astype(jnp.float32) * mixed_f.reshape(seq_rows, HEADS, head_dim), axis=-1
    )
    delta_heads = delta_rows.T
    stats = jnp.concatenate([log_sum.T, delta_rows], axis=1)
    all_stats = lax.all_gather(stats, "ctx", axis=0, tiled=True)
    zero_heads = jnp.zeros((HEADS, seq_rows, head_dim), jnp.float32)
    shard = (
        lax.all_gather(key_rows, "ctx", axis=0, tiled=True),
        lax.all_gather(value_rows, "ctx", axis=0, tiled=True),
    )
    shard_rows = shard[0].shape[0]
    query_block_len, query_block_count, (query_key_blocks, query_value_blocks) = to_blocks(
        shard, shard_rows
    )

    def query_one_block(total, block_in):
        key_block, value_block, position = block_in
        key_pos = position * query_block_len + jnp.arange(query_block_len, dtype=jnp.int32)
        term = query_terms(
            query_heads,
            grad_heads,
            log_sum,
            delta_heads,
            query_pos,
            query_flag,
            key_block,
            value_block,
            key_pos,
            factor,
        )
        return (total + term, None)

    def query_compute(total):
        return lax.scan(
            query_one_block,
            total,
            (query_key_blocks, query_value_blocks, jnp.arange(query_block_count, dtype=jnp.int32)),
        )[0]

    grad_q = lax.cond(jnp.int32(0) <= last_row, query_compute, keep_state, zero_heads)
    shard = (
        lax.all_gather(queries, "ctx", axis=0, tiled=True),
        lax.all_gather(grad_mixed, "ctx", axis=0, tiled=True),
    )
    shard_rows = shard[0].shape[0]
    key_block_len, key_block_count, (query_blocks, grad_blocks) = to_blocks(shard, shard_rows)

    def key_one_block(totals, block_in):
        query_block, grad_block, position = block_in
        begin = position * key_block_len
        remote_pos = begin + jnp.arange(key_block_len, dtype=jnp.int32)
        remote_flag = piece_flags(remote_pos, starts_row)
        stats_block = lax.dynamic_slice_in_dim(all_stats, begin, key_block_len, 0)
        lse_block = stats_block[:, :HEADS].T
        delta_block = stats_block[:, HEADS:].T
        grad_keys, grad_values = key_terms(
            query_block,
            grad_block,
            lse_block,
            delta_block,
            remote_pos,
            remote_flag,
            key_heads,
            value_heads,
            query_pos,
            factor,
        )
        return ((totals[0] + grad_keys, totals[1] + grad_values), None)

    def key_compute(totals):
        return lax.scan(
            key_one_block,
            totals,
            (query_blocks, grad_blocks, jnp.arange(key_block_count, dtype=jnp.int32)),
        )[0]

    grad_k, grad_v = lax.cond(
        jnp.int32(0) + shard_rows - 1 >= first_row,
        key_compute,
        keep_state,
        (zero_heads, zero_heads),
    )

    def merge_heads(grad_part):
        return (
            jnp.transpose(grad_part, (1, 0, 2)).reshape(seq_rows, model_width).astype(jnp.bfloat16)
        )

    grad_qkv_rows = jnp.concatenate(
        [merge_heads(grad_q), merge_heads(grad_k), merge_heads(grad_v)], axis=1
    )
    grad_qkv_loc = jnp.einsum(
        "ta,tb->ab", first_in, grad_qkv_rows, preferred_element_type=jnp.float32
    )
    grad_first = jnp.einsum(
        "tb,ab->ta", grad_qkv_rows, qkv_back, preferred_element_type=jnp.float32
    )
    grad_in_part, grad_gain_one, grad_shift_one = norm_back(
        inputs, gain_one_b, shift_one_b, grad_first
    )
    grad_tokens = (grad_after + grad_in_part)[None]
    grad_bias_loc = jnp.concatenate(
        [
            column_sum(grad_qkv_rows[:, :model_width]),
            column_sum(grad_qkv_rows[:, 2 * model_width :]),
            column_sum(grad_attn),
            column_sum(grad_pre),
            column_sum(grad_mlp),
        ]
    )
    grad_norm_loc = jnp.concatenate([grad_gain_one, grad_shift_one, grad_gain_two, grad_shift_two])
    summed = (
        lax.psum_scatter(grad_qkv_loc.reshape(-1), ("dp", "ctx"), scatter_dimension=0, tiled=True),
        lax.psum_scatter(grad_out_loc.reshape(-1), ("dp", "ctx"), scatter_dimension=0, tiled=True),
        lax.psum_scatter(grad_up_loc.reshape(-1), ("dp", "ctx"), scatter_dimension=0, tiled=True),
        lax.psum_scatter(grad_down_loc.reshape(-1), ("dp", "ctx"), scatter_dimension=0, tiled=True),
        lax.psum_scatter(grad_bias_loc, ("dp", "ctx"), scatter_dimension=0, tiled=True),
        lax.psum_scatter(grad_norm_loc, ("dp", "ctx"), scatter_dimension=0, tiled=True),
    )
    return (output, grad_tokens, summed[0], summed[1], summed[2], summed[3], summed[4], summed[5])


MESH = pl.DeviceIdType.MESH
BF16 = jnp.bfloat16
F32 = jnp.float32
VMEM_SPEC = pl.BlockSpec(memory_space=pltpu.VMEM)
SMEM_SPEC = pl.BlockSpec(memory_space=pltpu.SMEM)
ANY_SPEC = pl.BlockSpec(memory_space=pl.ANY)
HALF = 64
NT = (((1,), (1,)), ((), ()))
TN = (((0,), (0,)), ((), ()))
VMEM_LIMIT = 60 << 20


def params(cid=None):
    if cid is None:
        return pltpu.CompilerParams(vmem_limit_bytes=VMEM_LIMIT)
    return pltpu.CompilerParams(
        collective_id=cid, has_side_effects=True, vmem_limit_bytes=VMEM_LIMIT
    )


def place():
    dp = lax.axis_index("dp")
    ctx = lax.axis_index("ctx")
    return dp // 2, dp % 2, ctx // 2, ctx % 2


def device(x, core, z, y):
    return (x * 2 + core, z * 2 + y)


def greet(peers):
    barrier = pltpu.get_barrier_semaphore()
    for peer in peers:
        pl.semaphore_signal(barrier, inc=1, device_id=peer, device_id_type=MESH)
    pl.semaphore_wait(barrier, len(peers))


def remote(src, dst, send, recv, peer):
    return pltpu.make_async_remote_copy(
        src_ref=src,
        dst_ref=dst,
        send_sem=send,
        recv_sem=recv,
        device_id=peer,
        device_id_type=MESH,
    )


def mm(a, b, dims=None):
    if dims is None:
        return jnp.dot(a, b, preferred_element_type=F32)
    return lax.dot_general(a, b, dims, preferred_element_type=F32)


def swap_halves(v):
    return jnp.concatenate([v[:, HALF:], v[:, :HALF]], axis=1)


def left_lanes(rows):
    return lax.broadcasted_iota(jnp.int32, (rows, 2 * HALF), 1) < HALF


def diagonal_mask(size, flags, first, transposed):
    row = lax.broadcasted_iota(jnp.int32, (size, size), 0)
    col = lax.broadcasted_iota(jnp.int32, (size, size), 1)
    key, query = (row, col) if transposed else (col, row)
    allowed = key <= query
    same = (key // PIECE) == (query // PIECE)
    for t in range(size // PIECE):
        inside = jnp.logical_and(same, (query // PIECE) == t)
        allowed = jnp.logical_or(allowed, jnp.logical_and(inside, flags[first + t] > 0))
    return allowed


def xor8(a, b):
    return (
        (a // 4 + b // 4) % 2 * 4 + (a // 2 % 2 + b // 2 % 2) % 2 * 2 + (a % 2 + b % 2) % 2
    )


def unflatten(flat_ref, stage, rows, groups):
    count = rows * groups
    stage[pl.ds(0, count), :] = flat_ref[...].astype(F32)
    return [stage[pl.ds(j, rows, stride=groups), :] for j in range(groups)]


def reduce_buffers(rows, width, wire):
    vmem = pltpu.VMEM
    return [
        vmem((2, 2, rows, width), wire),
        vmem((2, 2, rows, width), wire),
        vmem((2, 2, rows, width), wire),
        vmem((2, 2, rows, width), wire),
        vmem((2, 2, rows, width), wire),
        vmem((2, 2, rows, width), wire),
        vmem((4, rows, width), wire),
        vmem((3, rows, width), wire),
        vmem((4, rows, width), F32),
    ]


REDUCE_BUFFERS = 9
REDUCE_COPIES = 7


def reducer(acc, bufs, send, recv, first):
    to_wire_x, from_x, to_wire_y, from_y, to_two, from_two, to_three, from_three, total = bufs
    wire = to_wire_x.dtype
    x, core, z, y = place()
    ox, oy = 1 - x, 1 - y
    to_x = device(ox, core, z, y)
    to_y = device(x, core, z, oy)
    others = [(z + j) % 4 for j in range(1, 4)]

    def copies(stage):
        def make(n, src, dst, peer):
            return remote(src, dst, send.at[first + n], recv.at[first + n], peer)

        if stage == 1:
            return [make(0, to_wire_x, from_x, to_x), make(1, to_wire_y, from_y, to_y)]
        if stage == 2:
            return [
                make(2, to_two.at[0], from_two.at[0], to_y),
                make(3, to_two.at[1], from_two.at[1], to_x),
            ]
        return [
            make(4 + j, to_three.at[other], from_three.at[j], device(x, core, other, y))
            for j, other in enumerate(others)
        ]

    def launch(stage):
        if stage == 1:
            to_wire_x[...] = acc[ox, pl.ds(0, 2)].astype(wire)
            for n in range(2):
                to_wire_y[n] = acc[n, pl.ds(2, 2), oy].astype(wire)
        elif stage == 2:
            to_two[0] = (acc[x, pl.ds(0, 2), oy] + from_x[:, oy].astype(F32)).astype(wire)
            to_two[1] = (acc[ox, pl.ds(2, 2), y] + from_y[ox].astype(F32)).astype(wire)
        else:
            low = acc[x, pl.ds(0, 2), y] + from_x[:, y].astype(F32) + from_two[0].astype(F32)
            high = acc[x, pl.ds(2, 2), y] + from_y[x].astype(F32) + from_two[1].astype(F32)
            total[pl.ds(0, 2)] = low
            total[pl.ds(2, 2)] = high
            to_three[pl.ds(0, 2)] = low.astype(wire)
            to_three[pl.ds(2, 2)] = high.astype(wire)
        for copy in copies(stage):
            copy.start()

    def finish(stage):
        for copy in copies(stage):
            copy.wait()

    def result():
        value = total[z]
        for j in range(3):
            value = value + from_three[j].astype(F32)
        return value

    return launch, finish, result


def digits(values):
    return sum(v * 4**n for n, v in enumerate(values))


TILES = (
    (
        digits((0, 1, 1, 2, 2, 2, 3, 3, 3, 3)),
        digits((0, 1, 0, 0, 1, 2, 0, 1, 2, 3)),
        digits((1, 0, 1, 0, 0, 1, 0, 0, 0, 1)),
    ),
    (
        digits((2, 3, 3, 2, 3, 0, 2, 3, 1, 1)),
        digits((2, 3, 2, 0, 0, 0, 1, 1, 0, 1)),
        digits((0, 0, 0, 0, 0, 1, 1, 1, 0, 1)),
    ),
)


def forward_phase(r):
    flags = r.flags
    tokens = r.tokens
    small = r.small
    qkv_flat = r.qkv_flat
    out_flat = r.out_flat
    up_flat = r.up_flat
    down_flat = r.down_flat
    a1_ref = r.a1
    got = r.got
    mix = r.mix
    o_ref = r.o_heads
    lse_ref = r.lse
    vec_ref = r.vec
    qkv_all = r.qkv_all
    ou_all = r.ou_all
    down_all = r.down_all
    stage = r.stage
    qkv_own = r.qkv_own
    ou_own = r.ou_own
    down_own = r.down_own
    norm_s = r.n2_s
    packed = r.packed
    q_s = r.q_s
    k_s = r.k_s
    v_s = r.v_s
    m_s = r.m_s
    acc_s = r.acc_s
    o2_s = r.o2_s
    g_own = r.g_own
    g_send = r.g_send
    g_recv = r.g_recv
    f_send = r.f_send
    f_recv = r.f_recv
    x_send = r.x_send
    x_recv = r.x_recv
    o_send = r.o_send
    o_recv = r.o_recv
    x, core, z, y = place()
    ox, oc, oy = 1 - x, 1 - core, 1 - y
    me = z * 2 + y
    width = tokens.shape[1]
    rows = tokens.shape[0]
    half = rows // 2
    tile = 2 * rows
    groups = width // 128
    group = 3 * width // 2
    scale = math.log2(math.e) * HALF**-0.5
    left = left_lanes(rows)
    left_half = left_lanes(half)
    to_x = device(ox, core, z, y)
    to_y = device(x, core, z, oy)
    to_core = device(x, oc, z, y)
    others = [(z + j) % 4 for j in range(1, 4)]

    qkv = unflatten(qkv_flat, stage, 16, 3 * groups)
    left16 = left_lanes(16)
    for j in range(groups):
        k_pair, v_pair = qkv[groups + j], qkv[2 * groups + j]
        own = qkv_own.at[j // 2]
        at = (j % 2) * 128
        own[:, at : at + 128] = qkv[j].astype(BF16)
        at = 256 + (j % 2) * 256
        own[:, at : at + 128] = jnp.where(left16, k_pair, swap_halves(v_pair)).astype(BF16)
        at += 128
        own[:, at : at + 128] = jnp.where(left16, swap_halves(k_pair), v_pair).astype(BF16)
    for g in range(2):
        qkv_own[g, :, group:] = small[...]
    greet(
        [device(x, core, (z + c) % 4, (y + d) % 2) for c in range(4) for d in range(2)][1:]
        + [to_x, to_core]
    )
    arrays = ((qkv_own, qkv_all), (ou_own, ou_all), (down_own, down_all))

    def moves(phase, a):
        own, full = arrays[a]
        if phase == 1:
            mine = full.at[x, core, z, y]
            return [(own, mine, device(x, core, o, y), j) for j, o in enumerate(others)]
        if phase == 2:
            part = full.at[x, core, :, y]
            return [(part, part, to_x, 3), (part, part, to_y, 4), (part, part, to_core, 5)]
        if phase == 3:
            low = full.at[x, core, pl.ds(0, 2), oy]
            high = full.at[ox, core, pl.ds(2, 2), y]
            from_x = full.at[ox, core, :, y]
            from_y = full.at[x, core, :, oy]
            return [
                (low, low, to_x, 6),
                (high, high, to_y, 7),
                (from_x, from_x, to_core, 8),
                (from_y, from_y, to_core, 9),
            ]
        part = full.at[ox, core, :, oy]
        return [(part, part, to_core, 10)]

    def phase_copies(phase, a):
        copies = [
            remote(src, dst, g_send.at[a * 11 + n], g_recv.at[a * 11 + n], peer)
            for src, dst, peer, n in moves(phase, a)
        ]
        if phase == 1:
            own, full = arrays[a]
            copies.append(pltpu.make_async_copy(own, full.at[x, core, z, y], g_own.at[a]))
        return copies

    def launch(phase, a):
        for copy in phase_copies(phase, a):
            copy.start()

    def finish(phase, a):
        for copy in phase_copies(phase, a):
            copy.wait()

    hz = z // 2

    def picked(position, half_z):
        return half_z * (1 - position) + (1 - half_z) * position

    def hop(src, dst, peer, g, n):
        return remote(src, dst, f_send.at[20 * g + n], f_recv.at[20 * g + n], peer)

    def to_xy(g, c):
        part = qkv_all.at[g, x, core, c, y]
        return hop(part, part, to_x, g, 4 + c), hop(part, part, to_y, g, 8 + c)

    def corner(g, c, over_x):
        if over_x:
            part = qkv_all.at[g, x, core, c, oy]
            return hop(part, part, to_x, g, 12 + c)
        part = qkv_all.at[g, ox, core, c, y]
        return hop(part, part, to_y, g, 12 + c)

    def to_sibling(g, n):
        part = (
            qkv_all.at[g, x, core, :, y],
            qkv_all.at[g, ox, core, :, y],
            qkv_all.at[g, x, core, :, oy],
            qkv_all.at[g, ox, core, :, oy],
        )[n]
        return hop(part, part, to_core, g, 16 + n)

    def along(g, n):
        return hop(
            qkv_own.at[g], qkv_all.at[g, x, core, z, y], device(x, core, others[n], y), g, n
        )

    own_first = pltpu.make_async_copy(qkv_own, qkv_all.at[:, x, core, z, y], g_own.at[0])
    own_first.start()
    for position in range(2):
        for n, other in enumerate(others):
            along(picked(position, other // 2), n).start()
        g = picked(position, hz)
        own = qkv_all.at[g, x, core, z, y]
        hop(qkv_own.at[g], own, to_x, g, 4 + z).start()
        hop(qkv_own.at[g], own, to_y, g, 8 + z).start()
    out_parts = unflatten(out_flat, stage, 16, groups)
    for j in range(groups):
        ou_own[:, 128 * j : 128 * (j + 1)] = out_parts[j].astype(BF16)
    up_groups = up_flat.shape[0] // 16
    up_parts = unflatten(up_flat, stage, 16, up_groups)
    for j in range(up_groups):
        at = width + 128 * j
        ou_own[:, at : at + 128] = up_parts[j].astype(BF16)
    down_rows = down_flat.shape[0] // groups
    down_parts = unflatten(down_flat, stage, down_rows, groups)
    for j in range(groups):
        down_own[:, 128 * j : 128 * (j + 1)] = down_parts[j].astype(BF16)
    launch(1, 1)
    launch(1, 2)
    own_first.wait()
    one, two = picked(0, hz), picked(1, hz)
    for g in (one, two):
        for n in range(3):
            along(g, n).wait_recv()
            for copy in to_xy(g, (z + 3 - n) % 4):
                copy.start()
        to_sibling(g, 0).start()
    value = tokens[...].astype(F32)
    center = jnp.mean(value, axis=1, keepdims=True)
    offset = value - center
    spread = jnp.mean(offset * offset, axis=1, keepdims=True)
    norm_s[...] = offset * lax.rsqrt(spread + eps_norm)

    def meet(g):
        for c in [z] + others:
            over_x, over_y = to_xy(g, c)
            over_x.wait_recv()
            over_y.wait_recv()

            @pl.when(c < 2)
            def _():
                corner(g, c, True).start()

            @pl.when(c >= 2)
            def _():
                corner(g, c, False).start()

        to_sibling(g, 1).start()
        to_sibling(g, 2).start()

    def turn(g):
        for c in range(4):
            corner(g, c, c < 2).wait()
        to_sibling(g, 3).start()

    def close(g):
        for n in range(4):
            to_sibling(g, n).wait()

    meet(one)
    meet(two)
    turn(one)
    turn(two)
    close(one)

    vec_ref[...] = jnp.zeros_like(vec_ref)
    devices = [(a, b, c, d) for a in range(2) for b in range(2) for c in range(4) for d in range(2)]
    base = 128 * len(devices)

    def bias_rows(begin, end):
        for n in range(begin, end):
            piece = qkv_all[(one,) + devices[n] + (slice(None), pl.ds(group, 128))].astype(F32)
            vec_ref[0:1, 128 * n : 128 * (n + 1)] = piece[0:1]

    def norm_rows(begin, end):
        for n in range(begin, end):
            pair = [
                qkv_all[(one,) + devices[2 * n + d] + (slice(None), pl.ds(group, 128))].astype(F32)
                for d in range(2)
            ]
            joined = jnp.concatenate([pair[0][1:2, :HALF], pair[1][1:2, :HALF]], axis=1)
            vec_ref[0:1, base + 128 * n : base + 128 * (n + 1)] = joined

    bias_rows(0, 2 * groups)
    norm_rows(0, 2 * groups)
    gain = vec_ref[0:1, base : base + width]
    shift = vec_ref[0:1, base + width : base + 2 * width]
    a1_ref[...] = (norm_s[...] * gain + shift).astype(BF16)

    def part_of(is_query):
        return pl.ds(rows, half) if is_query else pl.ds(0, rows)

    def send_part(tz, mark, is_query):
        for step in range(2):
            ty = (y + step) % 2
            index = mark + step
            src = packed.at[2 * tz + ty, part_of(is_query)]
            dst = got.at[me, part_of(is_query)]
            n = index + 8 * is_query
            if index == 0:
                pltpu.make_async_copy(src, dst, x_recv.at[n]).start()
            else:
                remote(src, dst, x_send.at[n], x_recv.at[n], device(x, core, tz, ty)).start()

    order = (
        hz * 2 + 1 - z % 2,
        z,
        (1 - hz) * 2 + z % 2,
        (1 - hz) * 2 + 1 - z % 2,
    )
    marks = (2, 0, 4, 6)
    left1 = left_lanes(1)
    for place_of, (tz, mark) in enumerate(zip(order, marks)):
        if place_of == 2:
            close(two)
        g = one if place_of < 2 else two
        a1 = a1_ref[...]
        at = pl.multiple_of(tz % 2 * 128, 128)
        w_q = qkv_all[g, :, :, :, :, :, pl.ds(at, 128)].reshape(width, 128)
        q = (mm(a1, w_q) + vec_ref[0:1, pl.ds(pl.multiple_of(128 * tz, 128), 128)]).astype(BF16)
        at_kv = pl.multiple_of(256 + tz % 2 * 256, 128)
        w_kv = qkv_all[g, :, :, :, :, :, pl.ds(at_kv, 256)].reshape(width, 256)
        bias = vec_ref[0:1, pl.ds(pl.multiple_of(width + 128 * tz, 128), 128)]
        kv = mm(a1, w_kv)
        even = kv[:, :128] + jnp.where(left1, 0.0, swap_halves(bias))
        odd = kv[:, 128:] + jnp.where(left1, 0.0, bias)
        packed[2 * tz, :rows] = even.astype(BF16)
        packed[2 * tz + 1, :rows] = odd.astype(BF16)
        top, low = q[:half], q[half:]
        packed[2 * tz, rows:] = jnp.where(left_half, top, swap_halves(low))
        packed[2 * tz + 1, rows:] = jnp.where(left_half, swap_halves(top), low)
        if mark < 4:
            send_part(tz, mark, False)
            send_part(tz, mark, True)

    def send_cross():
        def send_all(is_query):
            for tz, mark in zip(order[2:], marks[2:]):
                send_part(tz, mark, is_query)

        pl.when(hz == 1)(lambda: send_all(True))
        send_all(False)
        pl.when(hz == 0)(lambda: send_all(True))

    send_cross()
    finish(1, 1)
    finish(1, 2)
    launch(2, 1)
    launch(2, 2)
    bias_rows(2 * groups, len(devices))
    norm_rows(2 * groups, len(devices) // 2)

    def block_wait(sems, index, view):
        pltpu.make_async_copy(view, view, sems.at[index]).wait()

    def arrive(part, is_query):
        for t in range(2):
            b = 2 * part + t
            block_wait(x_recv, xor8(b, me) + 8 * is_query, got.at[b, part_of(is_query)])
            at = pl.multiple_of(b * rows, rows)
            if is_query:
                both = got[b, rows:]
                q_s[pl.ds(at, half), :] = jnp.where(left_half, both, 0).astype(BF16)
                q_s[pl.ds(at + half, half), :] = jnp.where(
                    left_half, swap_halves(both), 0
                ).astype(BF16)
            else:
                pair = got[b, :rows]
                k_s[pl.ds(at, rows), :] = jnp.where(left, pair, 0).astype(BF16)
                v_s[pl.ds(at, rows), :] = jnp.where(left, 1, pair).astype(BF16)

    low = 1 - hz
    queries = low * TILES[0][0] + hz * TILES[1][0]
    keys = low * TILES[0][1] + hz * TILES[1][1]
    ends = low * TILES[0][2] + hz * TILES[1][2]
    m_s[...] = jnp.full(m_s.shape, masked_score, F32)
    acc_s[...] = jnp.zeros(acc_s.shape, F32)
    for n in range(2):
        arrive(2 * hz + n, False)
        arrive(2 * hz + n, True)

    def step(n, carry):
        q_left, k_left, e_left = carry
        i, j, done = q_left % 4, k_left % 4, e_left % 4

        @pl.when(n == 3)
        def _():
            for a in (1, 2):
                finish(2, a)
                launch(3, a)

        @pl.when(n == 6)
        def _():
            for a in (1, 2):
                finish(3, a)
                launch(4, a)

        for when, part, is_query in ((3, 2, 1), (5, 2, 0), (6, 3, 1), (9, 3, 0)):
            pl.when(n == when + 16 * hz)(lambda: arrive(part, is_query))
        for when, part, is_query in ((3, 0, 0), (5, 0, 1), (6, 1, 0), (8, 1, 1)):
            pl.when(n == when + 16 * low)(lambda: arrive(part, is_query))

        at = pl.multiple_of(i * tile, tile)
        begin = pl.multiple_of(j * tile, tile)

        def update(diagonal):
            s = mm(q_s[pl.ds(at, tile), :], k_s[pl.ds(begin, tile), :], NT)
            if diagonal:
                allowed = diagonal_mask(tile, flags, i * (tile // PIECE), False)
                s = jnp.where(allowed, s, masked_score)
            old = m_s[pl.ds(at, tile), :]
            new = jnp.maximum(old, jnp.max(s, axis=1, keepdims=True) * scale)
            p = jnp.exp2(s * scale - new[:, :1])
            m_s[pl.ds(at, tile), :] = new
            acc_s[pl.ds(at, tile), :] = acc_s[pl.ds(at, tile), :] * jnp.exp2(old - new) + mm(
                p.astype(BF16), v_s[pl.ds(begin, tile), :]
            )

        pl.when(i == j)(lambda: update(True))
        pl.when(i != j)(lambda: update(False))

        @pl.when(done == 1)
        def _():
            acc = acc_s[pl.ds(at, tile), :]
            total = jnp.broadcast_to(acc[:, :1], acc.shape)
            o = acc / total
            o_ref[pl.ds(at, tile), :] = o
            lse = m_s[pl.ds(at, tile), :] + jnp.log2(total)
            lse_ref[:, pl.ds(at, tile)] = jnp.transpose(lse)[:8]
            for t in range(2):
                b = 2 * i + t
                top = o[t * rows : t * rows + half]
                bottom = o[t * rows + half : (t + 1) * rows]
                o2_s[b] = jnp.where(left_half, swap_halves(top), bottom).astype(BF16)
                index = xor8(b, me)

                @pl.when(b == me)
                def _():
                    pltpu.make_async_copy(o2_s.at[b], mix.at[me], o_recv.at[0]).start()

                @pl.when(b != me)
                def _():
                    remote(
                        o2_s.at[b],
                        mix.at[me],
                        o_send.at[index],
                        o_recv.at[index],
                        device(x, core, i, t),
                    ).start()

        return q_left // 4, k_left // 4, e_left // 4

    lax.fori_loop(0, 10, step, (queries, keys, ends))
    for a in (1, 2):
        finish(4, a)
    for g in range(2):
        for n in range(3):
            along(g, n).wait_send()
        for c in range(4):
            for copy in to_xy(g, c):
                copy.wait_send()
    for index in range(8):
        block_wait(o_recv, index, mix.at[0])
        if index:
            block_wait(x_send, index, packed.at[0, part_of(False)])
            block_wait(x_send, index + 8, packed.at[0, part_of(True)])
            block_wait(o_send, index, o2_s.at[0])


def middle_phase(r):
    tokens = r.tokens
    cot = r.cot
    mix = r.mix
    vec = r.vec
    ou_all = r.ou_all
    down_all = r.down_all
    out_ref = r.out_ref
    dx_ref = r.n2_s
    do2_ref = r.do2
    acc_ou = r.acc_ou
    acc_down = r.acc_down
    sums_ref = r.sums
    o_s = r.o_s
    x1_s = r.x1_s
    n2_s = r.n2_s
    a2_s = r.a2_s
    gl_s = r.gl_s
    du_s = r.du_s
    dh_s = r.dh_s
    da_s = r.da_s
    r_s = r.r_s
    send2 = r.o2_s
    core_ou = r.core_ou
    core_down = r.core_down
    got_ou = r.got_ou
    got_down = r.got_down
    x_send = r.d_send
    x_recv = r.d_recv
    c_send = r.c_send
    c_recv = r.c_recv
    x, core, z, y = place()
    oc, oy = 1 - core, 1 - y
    me = z * 2 + y
    rows, width = tokens.shape
    half = rows // 2
    hidden = ou_all.shape[-1] - width
    left_half = left_lanes(half)
    to_core = device(x, oc, z, y)
    bias_o = vec[0:1, 2 * width : 3 * width]
    bias_down = vec[0:1, 3 * width + hidden : 4 * width + hidden]
    base = 4 * width + hidden
    gain = vec[0:1, base + 2 * width : base + 3 * width]
    shift = vec[0:1, base + 3 * width : base + 4 * width]

    for j in range(HEADS // 2):
        even, odd = mix[2 * j], mix[2 * j + 1]
        at = 128 * j
        o_s[:half, at : at + 128] = jnp.where(left_half, even, swap_halves(odd))
        o_s[half:, at : at + 128] = jnp.where(left_half, swap_halves(even), odd)
    w_out = ou_all[:, :, :, :, :, :width].reshape(width, width)
    x1 = tokens[...].astype(F32) + mm(o_s[...], w_out) + bias_o
    x1_s[...] = x1
    center = jnp.mean(x1, axis=1, keepdims=True)
    offset = x1 - center
    spread = jnp.mean(offset * offset, axis=1, keepdims=True)
    inverse = lax.rsqrt(spread + eps_norm)
    r_s[...] = jnp.broadcast_to(inverse, r_s.shape)
    n2 = offset * inverse
    n2_s[...] = n2
    a2_s[...] = (n2 * gain + shift).astype(BF16)
    sums_ref[...] = jnp.zeros_like(sums_ref)

    @pl.loop(0, hidden // width)
    def _(j):
        at = pl.multiple_of(j * width, width)
        w_up = ou_all[:, :, :, :, :, pl.ds(pl.multiple_of(width + at, width), width)].reshape(
            width, width
        )
        b_up = vec[0:1, pl.ds(pl.multiple_of(3 * width + at, width), width)]
        w_down = down_all[j // 2, j % 2].reshape(width, width)
        u = mm(a2_s[...], w_up) + b_up
        phi = 0.5 * (1.0 + lax.erf(u * (0.5**0.5)))
        slope = phi + u * jnp.exp(-0.5 * u * u) * (1.0 / math.sqrt(2.0 * math.pi))
        gl_s[:, pl.ds(at, width)] = (u * phi).astype(BF16)
        grad = mm(cot[...], w_down, NT)
        du = (grad * slope).astype(BF16)
        du_s[:, pl.ds(at, width)] = du
        sums_ref[0:1, pl.ds(pl.multiple_of(3 * width + at, width), width)] = jnp.sum(
            du.astype(F32), axis=0, keepdims=True
        )
        part = mm(du, w_up, NT)

        @pl.when(j == 0)
        def _():
            dh_s[...] = part

        @pl.when(j > 0)
        def _():
            dh_s[...] += part

    dh2 = dh_s[...]
    n2 = n2_s[...]
    sums_ref[0:1, base + 2 * width : base + 3 * width] = jnp.sum(dh2 * n2, axis=0, keepdims=True)
    sums_ref[0:1, base + 3 * width : base + 4 * width] = jnp.sum(dh2, axis=0, keepdims=True)
    e = dh2 * gain
    mean_e = jnp.mean(e, axis=1, keepdims=True)
    mean_en = jnp.mean(e * n2, axis=1, keepdims=True)
    dx = cot[...].astype(F32) + r_s[:, :1] * (e - mean_e - n2 * mean_en)
    dx_ref[...] = dx
    da = dx.astype(BF16)
    da_s[...] = da
    w_out = ou_all[:, :, :, :, :, :width].reshape(width, width)
    grad_o = mm(da, w_out, NT).astype(BF16)
    for j in range(HEADS // 2):
        group = grad_o[:, 128 * j : 128 * (j + 1)]
        top, low = group[:half], group[half:]
        send2[2 * j] = jnp.where(left_half, top, swap_halves(low))
        send2[2 * j + 1] = jnp.where(left_half, swap_halves(top), low)
    hz = z // 2
    order = ((1 - hz) * 2 + z % 2, (1 - hz) * 2 + 1 - z % 2, hz * 2 + 1 - z % 2, z)
    for tz, mark in zip(order, (4, 6, 2, 0)):
        for step in range(2):
            ty = (y + step) % 2
            index = mark + step
            src = send2.at[2 * tz + ty]
            if index == 0:
                pltpu.make_async_copy(src, do2_ref.at[me], x_recv.at[0]).start()
            else:
                remote(
                    src,
                    do2_ref.at[me],
                    x_send.at[index],
                    x_recv.at[index],
                    device(x, core, tz, ty),
                ).start()

    def grads(c, n):
        dp = 2 * n + c
        at = pl.multiple_of(dp * 128, 128)
        down_at = pl.multiple_of(dp * width, width)
        d_down = mm(gl_s[:, pl.ds(down_at, width)], cot[...], TN)
        d_up = mm(a2_s[:, pl.ds(at, 128)], du_s[...], TN)
        d_out = mm(o_s[:, pl.ds(at, 128)], da_s[...], TN)
        return (
            d_down.reshape(4, 2, width // 8, width),
            d_up.reshape(4, 2, 16, hidden),
            d_out.reshape(4, 2, 16, width),
        )

    for n in range(2):
        d_down, d_up, d_out = grads(oc, n)
        core_down[n] = d_down.astype(BF16)
        core_ou[n, :, :, :, width:] = d_up.astype(BF16)
        core_ou[n, :, :, :, :width] = d_out.astype(BF16)
    to_ou = remote(core_ou, got_ou, c_send.at[0], c_recv.at[0], to_core)
    to_down = remote(core_down, got_down, c_send.at[1], c_recv.at[1], to_core)
    to_ou.start()
    to_down.start()
    sums_ref[0:1, 2 * width : 3 * width] = jnp.sum(da_s[...].astype(F32), axis=0, keepdims=True)
    sums_ref[0:1, 3 * width + hidden : 4 * width + hidden] = jnp.sum(
        cot[...].astype(F32), axis=0, keepdims=True
    )
    result = x1_s[...] + mm(gl_s[...], down_all[...].reshape(hidden, width)) + bias_down
    out_ref[...] = result.astype(BF16)
    for n in range(2):
        d_down, d_up, d_out = grads(core, n)
        acc_down[n] = d_down
        acc_ou[n, :, :, :, width:] = d_up
        acc_ou[n, :, :, :, :width] = d_out
    to_ou.wait()
    to_down.wait()
    acc_ou[...] += got_ou[...].astype(F32)
    acc_down[...] += got_down[...].astype(F32)


def lanes_of(ref, r, g):
    group = r.tokens.shape[1] * 3 // 2
    return ref.at[:, :, :, :, pl.ds(pl.multiple_of(g * group, 128), group)]


def reducer_of(r, name, first, at=None):
    bufs = [getattr(r, f"{name}{n}") for n in range(REDUCE_BUFFERS)]
    if at is not None:
        return reducer(lanes_of(r.acc_ou, r, at), [b.at[at] for b in bufs], r.r_send, r.r_recv, first)
    acc = getattr(r, f"acc_{name}")
    return reducer(acc, bufs, r.r_send, r.r_recv, first)


def backward_phase(r):
    got, do2, o_heads, lse, grads, packed = r.got, r.do2, r.o_heads, r.lse, r.grads, r.packed
    qd_s, k_s, v_s, delta_s, dq_s, dkv_s = r.q_s, r.k_s, r.v_s, r.delta_s, r.acc_s, r.m_s
    flags = r.flags
    x, core, z, y = place()
    me = z * 2 + y
    hz = z // 2
    low = 1 - hz
    blocks = got.shape[0]
    rows = got.shape[1] // 3 * 2
    half = rows // 2
    quarter = blocks // 2
    scale = math.log2(math.e) * HALF**-0.5
    factor = HALF**-0.5
    left = left_lanes(rows)
    left_half = left_lanes(half)
    sums = (reducer_of(r, "ou", 0), reducer_of(r, "down", REDUCE_COPIES))
    for launch, _, _ in sums:
        launch(1)

    def enter(b):
        at = pl.multiple_of(b * rows, rows)
        pltpu.make_async_copy(do2.at[b], do2.at[b], r.d_recv.at[xor8(b, me)]).wait()
        v_s[pl.ds(at, rows), :] = jnp.where(left, 0, v_s[pl.ds(at, rows), :]).astype(BF16)
        grad = do2[b]
        for part, begin in ((swap_halves(grad), 0), (grad, half)):
            rows_at = pl.ds(at + begin, half)
            qd_s[rows_at, :] = jnp.where(left_half, qd_s[rows_at, :], part)
            product = jnp.where(left_half, 0.0, part.astype(F32) * o_heads[rows_at, :])
            delta = jnp.sum(jnp.transpose(product), axis=0, keepdims=True)
            delta_s[:, rows_at] = jnp.broadcast_to(delta, (8, half))
        dq_s[pl.ds(at, rows), :] = jnp.zeros((rows, 2 * HALF), F32)
        dkv_s[pl.ds(at, rows), :] = jnp.zeros((rows, 2 * HALF), F32)

    def tile(kj, qi, diagonal):
        k0 = pl.multiple_of(kj * rows, rows)
        q0 = pl.multiple_of(qi * rows, rows)
        k = k_s[pl.ds(k0, rows), :]
        v = v_s[pl.ds(k0, rows), :]
        qd = qd_s[pl.ds(q0, rows), :]
        scores = mm(k, qd, NT)
        dprobs = mm(v, qd, NT)
        p = jnp.exp2(scores * scale - lse[:1, pl.ds(q0, rows)])
        if diagonal:
            allowed = diagonal_mask(rows, flags, kj * (rows // PIECE), True)
            p = jnp.where(allowed, p, 0.0)
        ds = (p * (dprobs - delta_s[:1, pl.ds(q0, rows)])).astype(BF16)
        dkv_s[pl.ds(k0, rows), :] += jnp.where(left, mm(ds, qd), mm(p.astype(BF16), qd))
        dq_s[pl.ds(q0, rows), :] += mm(ds, k, TN)

    def part_of(is_query):
        return pl.ds(rows, half) if is_query else pl.ds(0, rows)

    def leave(a, is_query):
        at = pl.multiple_of(a * rows, rows)
        if is_query:
            top = dq_s[pl.ds(at, half), :]
            bottom = dq_s[pl.ds(at + half, half), :]
            packed[a, rows:] = (
                jnp.where(left_half, top, swap_halves(bottom)) * factor
            ).astype(BF16)
        else:
            block = dkv_s[pl.ds(at, rows), :]
            packed[a, :rows] = jnp.where(left, block * factor, block).astype(BF16)
        index = xor8(a, me) + 8 * is_query
        src = packed.at[a, part_of(is_query)]
        dst = grads.at[me, part_of(is_query)]

        @pl.when(a == me)
        def _():
            pltpu.make_async_copy(src, dst, r.b_recv.at[index]).start()

        @pl.when(a != me)
        def _():
            remote(
                src, dst, r.b_send.at[index], r.b_recv.at[index], device(x, core, a // 2, a % 2)
            ).start()

    for n in range(quarter):
        enter(hz * quarter + n)

    @pl.loop(0, 12)
    def _(row):
        seg = (row + 3) // 4
        last = seg // 3
        first = (3 - seg) // 3
        square = seg // 2 - last
        cross = seg % 2 - last
        own = first + last
        i = (row + 3) % 4 + last - 3 * first

        @pl.when(row == 1)
        def _():
            for n in range(quarter):
                enter(low * quarter + n)

        @pl.when(row == 4)
        def _():
            for _, finish, _ in sums:
                finish(1)
            for launch, _, _ in sums:
                launch(2)

        a_low = own * (3 - i) + (1 - own) * (7 - i)
        a_high = own * (4 + i) + (1 - own) * i
        a = low * a_low + hz * a_high
        count = own * (3 - i) + cross * i + square * 4

        @pl.when(square == 0)
        def _():
            tile(a, a, True)

        @pl.loop(0, count)
        def _(u):
            k_low = (own + square) * u + cross * a_low
            q_low = (own + square) * a_low + cross * (7 - u)
            k_high = (own + square) * a_high + cross * u
            q_high = own * (5 + i + u) + cross * a_high + square * (4 + u)
            tile(low * k_low + hz * k_high, low * q_low + hz * q_high, False)

        @pl.when(cross * hz + square * low + last > 0)
        def _():
            leave(a, 1)

        @pl.when(cross * low + square * hz + last > 0)
        def _():
            leave(a, 0)

        @pl.when(row == 8)
        def _():
            begin = low * 3 + hz * 4
            leave(begin, 1)
            leave(begin, 0)


def last_phase(r):
    grads, a1, tokens, dx, qkv_all, vec, sums = (
        r.grads,
        r.a1,
        r.tokens,
        r.n2_s,
        r.qkv_all,
        r.vec,
        r.sums,
    )
    dqkv_s, got_q = r.gl_s, r.got_q
    core_small, got_small, acc_small = r.core_small, r.got_small, r.acc_small
    x, core, z, y = place()
    me = z * 2 + y
    hz = z // 2
    oc = 1 - core
    to_core = device(x, oc, z, y)
    rows, width = tokens.shape
    half = rows // 2
    group = 3 * width // 2
    left_half = left_lanes(half)
    left1 = left_lanes(1)
    base = vec.shape[1] - 4 * width

    def columns_of(g):
        return pl.ds(pl.multiple_of(g * group, 128), group)

    def enter(g):
        for n in range(HEADS // 2):
            h = g * (HEADS // 2) + n
            for is_query in range(2):
                view = grads.at[h, pl.ds(rows, half) if is_query else pl.ds(0, rows)]
                pltpu.make_async_copy(view, view, r.b_recv.at[xor8(h, me) + 8 * is_query]).wait()
        begin = g * group
        for j in range(HEADS // 4):
            h = g * (HEADS // 2) + 2 * j
            even, odd = grads[h, rows:], grads[h + 1, rows:]
            at = pl.ds(pl.multiple_of(begin + 128 * j, 128), 128)
            dqkv_s[:half, at] = jnp.where(left_half, even, swap_halves(odd))
            dqkv_s[half:, at] = jnp.where(left_half, swap_halves(even), odd)
        for n in range(HEADS // 2):
            at = pl.ds(pl.multiple_of(begin + 256 + 128 * n, 128), 128)
            dqkv_s[:, at] = grads[g * (HEADS // 2) + n, :rows]

    def weight_grad(c, n, g):
        at = pl.multiple_of((2 * n + c) * 128, 128)
        return mm(a1[:, pl.ds(at, 128)], dqkv_s[:, columns_of(g)], TN).reshape(4, 2, 16, group)

    def over(g):
        return remote(lanes_of(r.core_ou, r, g), got_q.at[g], r.e_send.at[g], r.e_recv.at[g], to_core)

    parts = []
    for position, g in enumerate((1 - hz, hz)):
        enter(g)
        if position == 0:
            for early in (reducer_of(r, "ou", 0), reducer_of(r, "down", REDUCE_COPIES)):
                early[1](2)
                early[0](3)
        for n in range(2):
            lanes_of(r.core_ou, r, g)[n] = weight_grad(oc, n, g).astype(BF16)
        over(g).start()
        w = qkv_all[g, :, :, :, :, :, :group].reshape(width, group)
        part = mm(dqkv_s[:, columns_of(g)], w, NT)
        if position:
            r.dh_s[...] += part
        else:
            r.dh_s[...] = part
        for n in range(2):
            lanes_of(r.acc_ou, r, g)[n] = weight_grad(core, n, g)
        over(g).wait()
        acc_q = lanes_of(r.acc_ou, r, g)
        acc_q[...] = acc_q[...] + got_q[g].astype(F32)
        parts.append(reducer_of(r, "q", (2 + g) * REDUCE_COPIES, g))
        parts[-1][0](1)

    columns = jnp.sum(dqkv_s[:, : 3 * width].astype(F32), axis=0, keepdims=True)
    for j in range(HEADS // 2):
        at = (j // 2) * group + (j % 2) * 128
        sums[0:1, 128 * j : 128 * (j + 1)] = columns[:, at : at + 128]
        at = (j // 2) * group + 256 + (j % 2) * 256
        pair = jnp.where(
            left1, swap_halves(columns[:, at : at + 128]), columns[:, at + 128 : at + 256]
        )
        sums[0:1, width + 128 * j : width + 128 * (j + 1)] = pair
    dh = r.dh_s[...]
    gain = vec[0:1, base : base + width]
    value = tokens[...].astype(F32)
    center = jnp.mean(value, axis=1, keepdims=True)
    offset = value - center
    spread = jnp.mean(offset * offset, axis=1, keepdims=True)
    inverse = lax.rsqrt(spread + eps_norm)
    norm = offset * inverse
    sums[0:1, base : base + width] = jnp.sum(dh * norm, axis=0, keepdims=True)
    sums[0:1, base + width : base + 2 * width] = jnp.sum(dh, axis=0, keepdims=True)

    def small_block(a, b, c, d):
        n = (a * 2 + b) * 8 + c * 2 + d
        piece = sums[0:1, pl.ds(pl.multiple_of(128 * n, 128), 128)]
        pair = sums[0:1, pl.ds(pl.multiple_of(base + 128 * (n // 2), 128), 128)]
        own = pair if d == 0 else swap_halves(pair)
        return jnp.concatenate([piece, own, jnp.zeros((6, 128), F32)], axis=0)

    for a in range(2):
        for c in range(4):
            for d in range(2):
                core_small[a, c, d] = small_block(a, oc, c, d)
                acc_small[a, c, d] = small_block(a, core, c, d)
    over_small = remote(core_small, got_small, r.e_send.at[2], r.e_recv.at[2], to_core)
    over_small.start()
    parts[0][1](1)
    parts[0][0](2)
    over_small.wait()
    acc_small[...] += got_small[...]
    parts.append(reducer_of(r, "small", 4 * REDUCE_COPIES))
    parts[2][0](1)
    e = dh * gain
    mean_e = jnp.mean(e, axis=1, keepdims=True)
    mean_en = jnp.mean(e * norm, axis=1, keepdims=True)
    r.grad_tokens[...] = dx[...] + inverse * (e - mean_e - norm * mean_en)
    parts[1][1](1)
    parts[1][0](2)
    parts[0][1](2)
    parts[0][0](3)
    parts[2][1](1)
    parts[2][0](2)
    parts[1][1](2)
    parts[1][0](3)
    parts[2][1](2)
    parts[2][0](3)
    for part in (reducer_of(r, "ou", 0), reducer_of(r, "down", REDUCE_COPIES)):
        part[1](3)
    r.sum_ou[...] = reducer_of(r, "ou", 0)[2]()
    r.sum_down[...] = reducer_of(r, "down", REDUCE_COPIES)[2]()
    for _, finish, _ in parts:
        finish(3)
    for g, part in zip((1 - hz, hz), parts):
        r.sum_qkv[g] = part[2]()
    r.sum_small[...] = parts[2][2]()
    for index in range(HEADS):
        if index:
            for is_query, count in ((0, rows), (1, half)):
                view = r.packed.at[0, pl.ds(rows * is_query, count)]
                pltpu.make_async_copy(view, view, r.b_send.at[index + 8 * is_query]).wait()
            view = r.o2_s.at[0]
            pltpu.make_async_copy(view, view, r.d_send.at[index]).wait()


def layer_kernel(names, *refs):
    r = types.SimpleNamespace(**dict(zip(names, refs)))
    forward_phase(r)
    middle_phase(r)
    backward_phase(r)
    last_phase(r)


def layer(inputs, cid):
    rows, width = inputs["tokens"].shape
    length = rows * HEADS
    lanes = 2 * HALF
    hidden = inputs["up_flat"].shape[0] * 128 // 16
    down_rows = inputs["down_flat"].shape[0] * 128 // width
    group = 3 * width // 2
    every = (2, 2, 4, 2)
    mine = (2, 4, 2)
    row = (8, 4096 + 4 * width)
    vmem = pltpu.VMEM
    dma = pltpu.SemaphoreType.DMA
    outputs = {
        "out_ref": jax.ShapeDtypeStruct((rows, width), BF16),
        "grad_tokens": jax.ShapeDtypeStruct((rows, width), F32),
        "sum_qkv": jax.ShapeDtypeStruct((2, 16, group), F32),
        "sum_ou": jax.ShapeDtypeStruct((16, width + hidden), F32),
        "sum_down": jax.ShapeDtypeStruct((down_rows, width), F32),
        "sum_small": jax.ShapeDtypeStruct((8, 128), F32),
    }
    scratch = {
        "a1": vmem((rows, width), BF16),
        "got": vmem((HEADS, rows + rows // 2, lanes), BF16),
        "mix": vmem((HEADS, rows // 2, lanes), BF16),
        "o_heads": vmem((length, lanes), F32),
        "lse": vmem((8, length), F32),
        "vec": vmem(row, F32),
        "qkv_all": vmem((2,) + every + (16, group + 128), BF16),
        "ou_all": vmem(every + (16, width + hidden), BF16),
        "down_all": vmem(every + (down_rows, width), BF16),
        "stage": vmem((256, 128), F32),
        "qkv_own": vmem((2, 16, group + 128), BF16),
        "ou_own": vmem((16, width + hidden), BF16),
        "down_own": vmem((down_rows, width), BF16),
        "packed": vmem((HEADS, rows + rows // 2, lanes), BF16),
        "q_s": vmem((length, lanes), BF16),
        "k_s": vmem((length, lanes), BF16),
        "v_s": vmem((length, lanes), BF16),
        "m_s": vmem((length, lanes), F32),
        "acc_s": vmem((length, lanes), F32),
        "o2_s": vmem((HEADS, rows // 2, lanes), BF16),
        "do2": vmem((HEADS, rows // 2, lanes), BF16),
        "acc_ou": vmem(mine + (16, width + hidden), F32),
        "acc_down": vmem(mine + (down_rows, width), F32),
        "sums": vmem(row, F32),
        "o_s": vmem((rows, width), BF16),
        "x1_s": vmem((rows, width), F32),
        "n2_s": vmem((rows, width), F32),
        "a2_s": vmem((rows, width), BF16),
        "gl_s": vmem((rows, hidden), BF16),
        "du_s": vmem((rows, hidden), BF16),
        "dh_s": vmem((rows, width), F32),
        "da_s": vmem((rows, width), BF16),
        "r_s": vmem((rows, lanes), F32),
        "core_ou": vmem(mine + (16, width + hidden), BF16),
        "core_down": vmem(mine + (down_rows, width), BF16),
        "got_ou": vmem(mine + (16, width + hidden), BF16),
        "got_down": vmem(mine + (down_rows, width), BF16),
        "delta_s": vmem((8, length), F32),
        "grads": vmem((HEADS, rows + rows // 2, lanes), BF16),
        "got_q": vmem((2,) + mine + (16, group), BF16),
        "core_small": vmem(mine + (8, 128), F32),
        "got_small": vmem(mine + (8, 128), F32),
        "acc_small": vmem(mine + (8, 128), F32),
    }
    for name, lead, r, w, wire in (
        ("ou", (), 16, width + hidden, BF16),
        ("down", (), down_rows, width, BF16),
        ("q", (2,), 16, group, BF16),
        ("small", (), 8, 128, F32),
    ):
        for n, buf in enumerate(reduce_buffers(r, w, wire)):
            scratch[f"{name}{n}"] = vmem(lead + buf.shape, buf.dtype)
    for name, count in (
        ("g_own", 3),
        ("g_send", 33),
        ("g_recv", 33),
        ("f_send", 40),
        ("f_recv", 40),
        ("x_send", 16),
        ("x_recv", 16),
        ("o_send", 8),
        ("o_recv", 8),
        ("d_send", 8),
        ("d_recv", 8),
        ("c_send", 2),
        ("c_recv", 2),
        ("r_send", 5 * REDUCE_COPIES),
        ("r_recv", 5 * REDUCE_COPIES),
        ("b_send", 16),
        ("b_recv", 16),
        ("e_send", 3),
        ("e_recv", 3),
    ):
        scratch[name] = dma((count,))
    names = tuple(inputs) + tuple(outputs) + tuple(scratch)

    def kernel(*refs):
        layer_kernel(names, *refs)

    return pl.pallas_call(
        kernel,
        out_shape=list(outputs.values()),
        in_specs=[SMEM_SPEC if n == "flags" else VMEM_SPEC for n in inputs],
        out_specs=[VMEM_SPEC] * len(outputs),
        scratch_shapes=list(scratch.values()),
        compiler_params=params(cid),
    )(*inputs.values())


def flatten_kernel(sum_qkv, sum_ou, sum_down, sum_small, qkv_o, out_o, up_o, down_o, bias_o, norm_o):
    groups = sum_down.shape[1] // 128
    left = left_lanes(16)

    def group(ref, j):
        return ref[:, 128 * j : 128 * (j + 1)]

    for j in range(groups):
        part = sum_qkv.at[j // 2]
        pair = j % 2
        qkv_o[pl.ds(j, 16, stride=3 * groups), :] = group(part, pair)
        even, odd = group(part, 2 + 2 * pair), group(part, 3 + 2 * pair)
        qkv_o[pl.ds(groups + j, 16, stride=3 * groups), :] = jnp.where(
            left, even, swap_halves(odd)
        )
        qkv_o[pl.ds(2 * groups + j, 16, stride=3 * groups), :] = jnp.where(
            left, swap_halves(even), odd
        )
        out_o[pl.ds(j, 16, stride=groups), :] = group(sum_ou, j)
        down_o[pl.ds(j, sum_down.shape[0], stride=groups), :] = group(sum_down, j)
    ups = sum_ou.shape[1] // 128 - groups
    for j in range(ups):
        up_o[pl.ds(j, 16, stride=ups), :] = group(sum_ou, groups + j)
    bias_o[...] = sum_small[0:1]
    norm_o[...] = sum_small[1:2, : norm_o.shape[1]]


def flatten(sum_qkv, sum_ou, sum_down, sum_small, norm_len):
    width = sum_down.shape[1]
    sizes = (
        sum_qkv.size // 128,
        width * 16 // 128,
        (sum_ou.shape[1] - width) * 16 // 128,
        sum_down.size // 128,
    )
    return pl.pallas_call(
        flatten_kernel,
        out_shape=[jax.ShapeDtypeStruct((n, 128), F32) for n in sizes]
        + [jax.ShapeDtypeStruct((1, 128), F32), jax.ShapeDtypeStruct((1, norm_len), F32)],
        in_specs=[VMEM_SPEC] * 4,
        out_specs=[VMEM_SPEC] * 6,
        compiler_params=params(),
    )(sum_qkv, sum_ou, sum_down, sum_small)


def fast_device(
    tokens, piece_starts, qkv_weight, out_weight, up_weight, down_weight, biases, norms, cotangent
):
    length = tokens.shape[1] * HEADS
    openings = jnp.arange(length // PIECE, dtype=jnp.int32) * PIECE
    flags = jnp.any(openings[:, None] == piece_starts[0][None, :], axis=1).astype(jnp.int32)
    bias_len = biases.shape[0]
    norm_len = norms.shape[0]
    small = jnp.concatenate([biases, norms, jnp.zeros((16 * 128 - bias_len - norm_len,), BF16)])
    output, grad_tokens, sum_qkv, sum_ou, sum_down, sum_small = layer(
        {
            "flags": flags,
            "tokens": tokens[0],
            "cot": cotangent[0],
            "small": small.reshape(16, 128),
            "qkv_flat": qkv_weight.reshape(-1, 128),
            "out_flat": out_weight.reshape(-1, 128),
            "up_flat": up_weight.reshape(-1, 128),
            "down_flat": down_weight.reshape(-1, 128),
        },
        1,
    )
    flats = flatten(sum_qkv, sum_ou, sum_down, sum_small, norm_len)
    return (output[None], grad_tokens[None]) + tuple(f.reshape(-1) for f in flats)


def solution(mesh):
    flat = P(("dp", "ctx"))
    rows = P("dp", "ctx", None)
    fast = mesh.shape["dp"] == 4 and mesh.shape["ctx"] == HEADS
    return jax.shard_map(
        fast_device if fast else general_device,
        mesh=mesh,
        in_specs=(rows, P("dp", None), flat, flat, flat, flat, flat, flat, rows),
        out_specs=(rows, rows, flat, flat, flat, flat, flat, flat),
        check_vma=False,
    )
```

```python
import math
import types

import jax
import jax.numpy as jnp
from jax import lax
from jax.experimental import pallas as pl
from jax.experimental.pallas import tpu as pltpu
from jax.sharding import PartitionSpec as P

HEADS = 8
PIECE = 256


eps_norm = 1e-05
masked_score = -1e30


def layer_norm(values, gain, shift):
    center = jnp.mean(values, axis=-1, keepdims=True)
    offsets = values - center
    spread = jnp.mean(offsets * offsets, axis=-1, keepdims=True)
    return offsets * lax.rsqrt(spread + eps_norm) * gain + shift


def gelu_exact(values):
    return jax.nn.gelu(values, approximate=False)


def piece_flags(positions, starts_row):
    opening = positions // PIECE * PIECE
    return jnp.any(opening[:, None] == starts_row[None, :], axis=1)


def visible(query_pos, query_flag, key_pos):
    causal = key_pos[None, :] <= query_pos[:, None]
    same_piece = key_pos[None, :] // PIECE == query_pos[:, None] // PIECE
    return jnp.logical_or(causal, jnp.logical_and(same_piece, query_flag[:, None]))


def to_blocks(arrays, shard_rows):
    block_len = 256
    block_count = shard_rows // block_len
    shaped = tuple((member.reshape(block_count, block_len, HEADS, -1) for member in arrays))
    return (block_len, block_count, shaped)


def keep_state(state):
    return state


def unpack(flats, model_width):
    qkv_flat, out_flat, up_flat, down_flat, bias_flat, norm_flat = flats
    hidden = up_flat.shape[0] // model_width
    return (
        qkv_flat.reshape(model_width, 3 * model_width),
        out_flat.reshape(model_width, model_width),
        up_flat.reshape(model_width, hidden),
        down_flat.reshape(hidden, model_width),
        bias_flat.astype(jnp.float32),
        norm_flat.astype(jnp.float32),
    )


def norm_back(values, gain, shift, upstream):
    _, pullback = jax.vjp(layer_norm, values, gain, shift)
    return pullback(upstream)


def column_sum(matrix):
    return jnp.sum(matrix.astype(jnp.float32), axis=0)


def query_terms(
    query_heads,
    grad_heads,
    own_lse,
    own_delta,
    query_pos,
    query_flag,
    key_block,
    value_block,
    key_pos,
    factor,
):
    scores = (
        jnp.einsum("qhd,khd->hqk", query_heads, key_block, preferred_element_type=jnp.float32)
        * factor
    )
    allowed = visible(query_pos, query_flag, key_pos)[None]
    softmax_p = jnp.where(allowed, jnp.exp(scores - own_lse[:, :, None]), 0.0)
    dprobs = jnp.einsum("qhd,khd->hqk", grad_heads, value_block, preferred_element_type=jnp.float32)
    dscores = (softmax_p * (dprobs - own_delta[:, :, None])).astype(jnp.bfloat16)
    return (
        jnp.einsum("hqk,khd->hqd", dscores, key_block, preferred_element_type=jnp.float32) * factor
    )


def key_terms(
    query_block,
    grad_block,
    lse_block,
    delta_block,
    remote_pos,
    remote_flag,
    key_heads,
    value_heads,
    key_pos,
    factor,
):
    scores = (
        jnp.einsum("qhd,khd->hqk", query_block, key_heads, preferred_element_type=jnp.float32)
        * factor
    )
    allowed = visible(remote_pos, remote_flag, key_pos)[None]
    softmax_p = jnp.where(allowed, jnp.exp(scores - lse_block[:, :, None]), 0.0)
    dprobs = jnp.einsum("qhd,khd->hqk", grad_block, value_heads, preferred_element_type=jnp.float32)
    dscores = (softmax_p * (dprobs - delta_block[:, :, None])).astype(jnp.bfloat16)
    grad_keys = (
        jnp.einsum("hqk,qhd->hkd", dscores, query_block, preferred_element_type=jnp.float32)
        * factor
    )
    grad_values = jnp.einsum(
        "hqk,qhd->hkd",
        softmax_p.astype(jnp.bfloat16),
        grad_block,
        preferred_element_type=jnp.float32,
    )
    return (grad_keys, grad_values)


def general_device(
    tokens, piece_starts, qkv_weight, out_weight, up_weight, down_weight, biases, norms, cotangent
):
    model_width = tokens.shape[2]
    seq_rows = tokens.shape[1]
    params = unpack(
        (
            lax.all_gather(qkv_weight, ("dp", "ctx"), axis=0, tiled=True),
            lax.all_gather(out_weight, ("dp", "ctx"), axis=0, tiled=True),
            lax.all_gather(up_weight, ("dp", "ctx"), axis=0, tiled=True),
            lax.all_gather(down_weight, ("dp", "ctx"), axis=0, tiled=True),
            lax.all_gather(biases, ("dp", "ctx"), axis=0, tiled=True),
            lax.all_gather(norms, ("dp", "ctx"), axis=0, tiled=True),
        ),
        model_width,
    )
    qkv_mat, out_mat, up_mat, down_mat, bias_all, norm_all = params
    hidden = up_mat.shape[1]
    head_dim = model_width // HEADS
    factor = head_dim ** (-0.5)
    first_row = lax.axis_index("ctx") * seq_rows
    last_row = first_row + seq_rows - 1
    query_pos = first_row + jnp.arange(seq_rows, dtype=jnp.int32)
    starts_row = piece_starts[0]
    query_flag = piece_flags(query_pos, starts_row)
    bias_q = bias_all[:model_width]
    bias_v = bias_all[model_width : 2 * model_width]
    bias_o = bias_all[2 * model_width : 3 * model_width]
    bias_up = bias_all[3 * model_width : 3 * model_width + hidden]
    bias_down = bias_all[3 * model_width + hidden :]
    gain_one = norm_all[:model_width]
    shift_one = norm_all[model_width : 2 * model_width]
    gain_two = norm_all[2 * model_width : 3 * model_width]
    shift_two = norm_all[3 * model_width :]
    inputs = tokens[0].astype(jnp.float32)
    first_in = layer_norm(inputs, gain_one, shift_one).astype(jnp.bfloat16)
    projected = jnp.dot(first_in, qkv_mat, preferred_element_type=jnp.float32)
    queries = (projected[:, :model_width] + bias_q).astype(jnp.bfloat16)
    key_rows = projected[:, model_width : 2 * model_width].astype(jnp.bfloat16)
    value_rows = (projected[:, 2 * model_width :] + bias_v).astype(jnp.bfloat16)
    query_heads = queries.reshape(seq_rows, HEADS, head_dim)
    key_heads = key_rows.reshape(seq_rows, HEADS, head_dim)
    value_heads = value_rows.reshape(seq_rows, HEADS, head_dim)
    start_state = (
        jnp.full((HEADS, seq_rows), masked_score, jnp.float32),
        jnp.zeros((HEADS, seq_rows), jnp.float32),
        jnp.zeros((HEADS, seq_rows, head_dim), jnp.float32),
    )
    shard = (
        lax.all_gather(key_rows, "ctx", axis=0, tiled=True),
        lax.all_gather(value_rows, "ctx", axis=0, tiled=True),
    )
    shard_rows = shard[0].shape[0]
    block_len, block_count, (key_blocks, value_blocks) = to_blocks(shard, shard_rows)

    def forward_one_block(state, block_in):
        running_max, running_sum, running_acc = state
        key_block, value_block, position = block_in
        key_pos = position * block_len + jnp.arange(block_len, dtype=jnp.int32)
        scores = (
            jnp.einsum("qhd,khd->hqk", query_heads, key_block, preferred_element_type=jnp.float32)
            * factor
        )
        allowed = visible(query_pos, query_flag, key_pos)[None]
        scores = jnp.where(allowed, scores, masked_score)
        new_max = jnp.maximum(running_max, jnp.max(scores, axis=-1))
        correction = jnp.exp(running_max - new_max)
        exp_scores = jnp.where(allowed, jnp.exp(scores - new_max[:, :, None]), 0.0)
        running_sum = running_sum * correction + jnp.sum(exp_scores, axis=-1)
        running_acc = running_acc * correction[:, :, None] + jnp.einsum(
            "hqk,khd->hqd",
            exp_scores.astype(jnp.bfloat16),
            value_block,
            preferred_element_type=jnp.float32,
        )
        return ((new_max, running_sum, running_acc), None)

    def forward_compute(state):
        return lax.scan(
            forward_one_block,
            state,
            (key_blocks, value_blocks, jnp.arange(block_count, dtype=jnp.int32)),
        )[0]

    run_max, run_sum, run_acc = lax.cond(
        jnp.int32(0) <= last_row, forward_compute, keep_state, start_state
    )
    mixed_heads = run_acc / run_sum[:, :, None]
    mixed_f = jnp.transpose(mixed_heads, (1, 0, 2)).reshape(seq_rows, model_width)
    mixed_b = mixed_f.astype(jnp.bfloat16)
    log_sum = run_max + jnp.log(run_sum)
    after_attn = inputs + jnp.dot(mixed_b, out_mat, preferred_element_type=jnp.float32) + bias_o
    second_in = layer_norm(after_attn, gain_two, shift_two).astype(jnp.bfloat16)
    pre_act = jnp.dot(second_in, up_mat, preferred_element_type=jnp.float32) + bias_up
    activated = gelu_exact(pre_act).astype(jnp.bfloat16)
    result = (
        after_attn + jnp.dot(activated, down_mat, preferred_element_type=jnp.float32) + bias_down
    )
    output = result.astype(jnp.bfloat16)[None]
    back = unpack(
        (
            lax.all_gather(qkv_weight, ("dp", "ctx"), axis=0, tiled=True),
            lax.all_gather(out_weight, ("dp", "ctx"), axis=0, tiled=True),
            lax.all_gather(up_weight, ("dp", "ctx"), axis=0, tiled=True),
            lax.all_gather(down_weight, ("dp", "ctx"), axis=0, tiled=True),
            lax.all_gather(biases, ("dp", "ctx"), axis=0, tiled=True),
            lax.all_gather(norms, ("dp", "ctx"), axis=0, tiled=True),
        ),
        model_width,
    )
    qkv_back, out_back, up_back, down_back, bias_back, norm_vec = back
    gain_one_b = norm_vec[:model_width]
    shift_one_b = norm_vec[model_width : 2 * model_width]
    gain_two_b = norm_vec[2 * model_width : 3 * model_width]
    shift_two_b = norm_vec[3 * model_width :]
    upstream = cotangent[0].astype(jnp.float32)
    grad_mlp = upstream.astype(jnp.bfloat16)
    grad_down_loc = jnp.einsum("ta,tb->ab", activated, grad_mlp, preferred_element_type=jnp.float32)
    grad_act = jnp.einsum("tb,ab->ta", grad_mlp, down_back, preferred_element_type=jnp.float32)
    _, gelu_pull = jax.vjp(gelu_exact, pre_act)
    grad_pre = gelu_pull(grad_act)[0].astype(jnp.bfloat16)
    grad_up_loc = jnp.einsum("ta,tb->ab", second_in, grad_pre, preferred_element_type=jnp.float32)
    grad_second = jnp.einsum("tb,ab->ta", grad_pre, up_back, preferred_element_type=jnp.float32)
    grad_after_part, grad_gain_two, grad_shift_two = norm_back(
        after_attn, gain_two_b, shift_two_b, grad_second
    )
    grad_after = upstream + grad_after_part
    grad_attn = grad_after.astype(jnp.bfloat16)
    grad_out_loc = jnp.einsum("ta,tb->ab", mixed_b, grad_attn, preferred_element_type=jnp.float32)
    grad_mixed = jnp.einsum(
        "tb,ab->ta", grad_attn, out_back, preferred_element_type=jnp.float32
    ).astype(jnp.bfloat16)
    grad_heads = grad_mixed.reshape(seq_rows, HEADS, head_dim)
    delta_rows = jnp.sum(
        grad_heads.astype(jnp.float32) * mixed_f.reshape(seq_rows, HEADS, head_dim), axis=-1
    )
    delta_heads = delta_rows.T
    stats = jnp.concatenate([log_sum.T, delta_rows], axis=1)
    all_stats = lax.all_gather(stats, "ctx", axis=0, tiled=True)
    zero_heads = jnp.zeros((HEADS, seq_rows, head_dim), jnp.float32)
    shard = (
        lax.all_gather(key_rows, "ctx", axis=0, tiled=True),
        lax.all_gather(value_rows, "ctx", axis=0, tiled=True),
    )
    shard_rows = shard[0].shape[0]
    query_block_len, query_block_count, (query_key_blocks, query_value_blocks) = to_blocks(
        shard, shard_rows
    )

    def query_one_block(total, block_in):
        key_block, value_block, position = block_in
        key_pos = position * query_block_len + jnp.arange(query_block_len, dtype=jnp.int32)
        term = query_terms(
            query_heads,
            grad_heads,
            log_sum,
            delta_heads,
            query_pos,
            query_flag,
            key_block,
            value_block,
            key_pos,
            factor,
        )
        return (total + term, None)

    def query_compute(total):
        return lax.scan(
            query_one_block,
            total,
            (query_key_blocks, query_value_blocks, jnp.arange(query_block_count, dtype=jnp.int32)),
        )[0]

    grad_q = lax.cond(jnp.int32(0) <= last_row, query_compute, keep_state, zero_heads)
    shard = (
        lax.all_gather(queries, "ctx", axis=0, tiled=True),
        lax.all_gather(grad_mixed, "ctx", axis=0, tiled=True),
    )
    shard_rows = shard[0].shape[0]
    key_block_len, key_block_count, (query_blocks, grad_blocks) = to_blocks(shard, shard_rows)

    def key_one_block(totals, block_in):
        query_block, grad_block, position = block_in
        begin = position * key_block_len
        remote_pos = begin + jnp.arange(key_block_len, dtype=jnp.int32)
        remote_flag = piece_flags(remote_pos, starts_row)
        stats_block = lax.dynamic_slice_in_dim(all_stats, begin, key_block_len, 0)
        lse_block = stats_block[:, :HEADS].T
        delta_block = stats_block[:, HEADS:].T
        grad_keys, grad_values = key_terms(
            query_block,
            grad_block,
            lse_block,
            delta_block,
            remote_pos,
            remote_flag,
            key_heads,
            value_heads,
            query_pos,
            factor,
        )
        return ((totals[0] + grad_keys, totals[1] + grad_values), None)

    def key_compute(totals):
        return lax.scan(
            key_one_block,
            totals,
            (query_blocks, grad_blocks, jnp.arange(key_block_count, dtype=jnp.int32)),
        )[0]

    grad_k, grad_v = lax.cond(
        jnp.int32(0) + shard_rows - 1 >= first_row,
        key_compute,
        keep_state,
        (zero_heads, zero_heads),
    )

    def merge_heads(grad_part):
        return (
            jnp.transpose(grad_part, (1, 0, 2)).reshape(seq_rows, model_width).astype(jnp.bfloat16)
        )

    grad_qkv_rows = jnp.concatenate(
        [merge_heads(grad_q), merge_heads(grad_k), merge_heads(grad_v)], axis=1
    )
    grad_qkv_loc = jnp.einsum(
        "ta,tb->ab", first_in, grad_qkv_rows, preferred_element_type=jnp.float32
    )
    grad_first = jnp.einsum(
        "tb,ab->ta", grad_qkv_rows, qkv_back, preferred_element_type=jnp.float32
    )
    grad_in_part, grad_gain_one, grad_shift_one = norm_back(
        inputs, gain_one_b, shift_one_b, grad_first
    )
    grad_tokens = (grad_after + grad_in_part)[None]
    grad_bias_loc = jnp.concatenate(
        [
            column_sum(grad_qkv_rows[:, :model_width]),
            column_sum(grad_qkv_rows[:, 2 * model_width :]),
            column_sum(grad_attn),
            column_sum(grad_pre),
            column_sum(grad_mlp),
        ]
    )
    grad_norm_loc = jnp.concatenate([grad_gain_one, grad_shift_one, grad_gain_two, grad_shift_two])
    summed = (
        lax.psum_scatter(grad_qkv_loc.reshape(-1), ("dp", "ctx"), scatter_dimension=0, tiled=True),
        lax.psum_scatter(grad_out_loc.reshape(-1), ("dp", "ctx"), scatter_dimension=0, tiled=True),
        lax.psum_scatter(grad_up_loc.reshape(-1), ("dp", "ctx"), scatter_dimension=0, tiled=True),
        lax.psum_scatter(grad_down_loc.reshape(-1), ("dp", "ctx"), scatter_dimension=0, tiled=True),
        lax.psum_scatter(grad_bias_loc, ("dp", "ctx"), scatter_dimension=0, tiled=True),
        lax.psum_scatter(grad_norm_loc, ("dp", "ctx"), scatter_dimension=0, tiled=True),
    )
    return (output, grad_tokens, summed[0], summed[1], summed[2], summed[3], summed[4], summed[5])


MESH = pl.DeviceIdType.MESH
BF16 = jnp.bfloat16
F32 = jnp.float32
VMEM_SPEC = pl.BlockSpec(memory_space=pltpu.VMEM)
SMEM_SPEC = pl.BlockSpec(memory_space=pltpu.SMEM)
ANY_SPEC = pl.BlockSpec(memory_space=pl.ANY)
HALF = 64
NT = (((1,), (1,)), ((), ()))
TN = (((0,), (0,)), ((), ()))
VMEM_LIMIT = 60 << 20


def params(cid=None):
    if cid is None:
        return pltpu.CompilerParams(vmem_limit_bytes=VMEM_LIMIT)
    return pltpu.CompilerParams(
        collective_id=cid, has_side_effects=True, vmem_limit_bytes=VMEM_LIMIT
    )


def place():
    dp = lax.axis_index("dp")
    ctx = lax.axis_index("ctx")
    return dp // 2, dp % 2, ctx // 2, ctx % 2


def device(x, core, z, y):
    return (x * 2 + core, z * 2 + y)


def greet(peers):
    barrier = pltpu.get_barrier_semaphore()
    for peer in peers:
        pl.semaphore_signal(barrier, inc=1, device_id=peer, device_id_type=MESH)
    pl.semaphore_wait(barrier, len(peers))


def remote(src, dst, send, recv, peer):
    return pltpu.make_async_remote_copy(
        src_ref=src,
        dst_ref=dst,
        send_sem=send,
        recv_sem=recv,
        device_id=peer,
        device_id_type=MESH,
    )


def mm(a, b, dims=None):
    if dims is None:
        return jnp.dot(a, b, preferred_element_type=F32)
    return lax.dot_general(a, b, dims, preferred_element_type=F32)


def swap_halves(v):
    return jnp.concatenate([v[:, HALF:], v[:, :HALF]], axis=1)


def left_lanes(rows):
    return lax.broadcasted_iota(jnp.int32, (rows, 2 * HALF), 1) < HALF


def diagonal_mask(size, flags, first, transposed):
    row = lax.broadcasted_iota(jnp.int32, (size, size), 0)
    col = lax.broadcasted_iota(jnp.int32, (size, size), 1)
    key, query = (row, col) if transposed else (col, row)
    allowed = key <= query
    same = (key // PIECE) == (query // PIECE)
    for t in range(size // PIECE):
        inside = jnp.logical_and(same, (query // PIECE) == t)
        allowed = jnp.logical_or(allowed, jnp.logical_and(inside, flags[first + t] > 0))
    return allowed


def xor8(a, b):
    return (
        (a // 4 + b // 4) % 2 * 4 + (a // 2 % 2 + b // 2 % 2) % 2 * 2 + (a % 2 + b % 2) % 2
    )


def unflatten(flat_ref, stage, rows, groups):
    count = rows * groups
    stage[pl.ds(0, count), :] = flat_ref[...].astype(F32)
    return [stage[pl.ds(j, rows, stride=groups), :] for j in range(groups)]


def reduce_buffers(rows, width, wire):
    vmem = pltpu.VMEM
    return [
        vmem((2, 2, rows, width), wire),
        vmem((2, 2, rows, width), wire),
        vmem((2, 2, rows, width), wire),
        vmem((2, 2, rows, width), wire),
        vmem((2, 2, rows, width), wire),
        vmem((2, 2, rows, width), wire),
        vmem((4, rows, width), wire),
        vmem((3, rows, width), wire),
        vmem((4, rows, width), F32),
    ]


REDUCE_BUFFERS = 9
REDUCE_COPIES = 7


def reducer(acc, bufs, send, recv, first):
    to_wire_x, from_x, to_wire_y, from_y, to_two, from_two, to_three, from_three, total = bufs
    wire = to_wire_x.dtype
    x, core, z, y = place()
    ox, oy = 1 - x, 1 - y
    to_x = device(ox, core, z, y)
    to_y = device(x, core, z, oy)
    others = [(z + j) % 4 for j in range(1, 4)]

    def copies(stage):
        def make(n, src, dst, peer):
            return remote(src, dst, send.at[first + n], recv.at[first + n], peer)

        if stage == 1:
            return [make(0, to_wire_x, from_x, to_x), make(1, to_wire_y, from_y, to_y)]
        if stage == 2:
            return [
                make(2, to_two.at[0], from_two.at[0], to_y),
                make(3, to_two.at[1], from_two.at[1], to_x),
            ]
        return [
            make(4 + j, to_three.at[other], from_three.at[j], device(x, core, other, y))
            for j, other in enumerate(others)
        ]

    def launch(stage):
        if stage == 1:
            to_wire_x[...] = acc[ox, pl.ds(0, 2)].astype(wire)
            for n in range(2):
                to_wire_y[n] = acc[n, pl.ds(2, 2), oy].astype(wire)
        elif stage == 2:
            to_two[0] = (acc[x, pl.ds(0, 2), oy] + from_x[:, oy].astype(F32)).astype(wire)
            to_two[1] = (acc[ox, pl.ds(2, 2), y] + from_y[ox].astype(F32)).astype(wire)
        else:
            low = acc[x, pl.ds(0, 2), y] + from_x[:, y].astype(F32) + from_two[0].astype(F32)
            high = acc[x, pl.ds(2, 2), y] + from_y[x].astype(F32) + from_two[1].astype(F32)
            total[pl.ds(0, 2)] = low
            total[pl.ds(2, 2)] = high
            to_three[pl.ds(0, 2)] = low.astype(wire)
            to_three[pl.ds(2, 2)] = high.astype(wire)
        for copy in copies(stage):
            copy.start()

    def finish(stage):
        for copy in copies(stage):
            copy.wait()

    def result():
        value = total[z]
        for j in range(3):
            value = value + from_three[j].astype(F32)
        return value

    return launch, finish, result


def digits(values):
    return sum(v * 4**n for n, v in enumerate(values))


TILES = (
    (
        digits((0, 1, 1, 2, 2, 2, 3, 3, 3, 3)),
        digits((0, 1, 0, 0, 1, 2, 0, 1, 2, 3)),
        digits((1, 0, 1, 0, 0, 1, 0, 0, 0, 1)),
    ),
    (
        digits((2, 3, 3, 2, 3, 0, 2, 3, 1, 1)),
        digits((2, 3, 2, 0, 0, 0, 1, 1, 0, 1)),
        digits((0, 0, 0, 0, 0, 1, 1, 1, 0, 1)),
    ),
)


def forward_phase(r):
    flags = r.flags
    tokens = r.tokens
    qkv_flat = r.qkv_flat
    out_flat = r.out_flat
    up_flat = r.up_flat
    down_flat = r.down_flat
    a1_ref = r.a1
    got = r.got
    mix = r.mix
    o_ref = r.o_heads
    lse_ref = r.lse
    vec_ref = r.vec
    qkv_all = r.qkv_all
    ou_all = r.ou_all
    down_all = r.down_all
    stage = r.stage
    qkv_own = r.qkv_own
    ou_own = r.ou_own
    down_own = r.down_own
    norm_s = r.n2_s
    packed = r.packed
    q_s = r.q_s
    k_s = r.k_s
    v_s = r.v_s
    m_s = r.m_s
    acc_s = r.acc_s
    o2_s = r.o2_s
    g_own = r.g_own
    g_send = r.g_send
    g_recv = r.g_recv
    f_send = r.f_send
    f_recv = r.f_recv
    x_send = r.x_send
    x_recv = r.x_recv
    o_send = r.o_send
    o_recv = r.o_recv
    x, core, z, y = place()
    ox, oc, oy = 1 - x, 1 - core, 1 - y
    me = z * 2 + y
    width = tokens.shape[1]
    rows = tokens.shape[0]
    half = rows // 2
    tile = 2 * rows
    groups = width // 128
    group = 3 * width // 2
    scale = math.log2(math.e) * HALF**-0.5
    left = left_lanes(rows)
    left_half = left_lanes(half)
    to_x = device(ox, core, z, y)
    to_y = device(x, core, z, oy)
    to_core = device(x, oc, z, y)
    others = [(z + j) % 4 for j in range(1, 4)]

    qkv = unflatten(qkv_flat, stage, 16, 3 * groups)
    left16 = left_lanes(16)
    for j in range(groups):
        k_pair, v_pair = qkv[groups + j], qkv[2 * groups + j]
        own = qkv_own.at[j // 2]
        at = (j % 2) * 128
        own[:, at : at + 128] = qkv[j].astype(BF16)
        at = 256 + (j % 2) * 256
        own[:, at : at + 128] = jnp.where(left16, k_pair, swap_halves(v_pair)).astype(BF16)
        at += 128
        own[:, at : at + 128] = jnp.where(left16, swap_halves(k_pair), v_pair).astype(BF16)
    norm_row = jnp.concatenate(
        [r.norms[...].astype(F32), jnp.zeros((1, 128 - r.norms.shape[1]), F32)], axis=1
    )
    block = jnp.concatenate(
        [r.biases[...].astype(F32), norm_row, jnp.zeros((14, 128), F32)], axis=0
    )
    for g in range(2):
        qkv_own[g, :, group:] = block.astype(BF16)
    for t in range(flags.shape[0]):
        found = jnp.int32(0)
        for j in range(r.starts.shape[1]):
            found = found + (r.starts[0, j] == t * PIECE).astype(jnp.int32)
        flags[t] = found
    greet(
        [device(x, core, (z + c) % 4, (y + d) % 2) for c in range(4) for d in range(2)][1:]
        + [to_x, to_core]
    )
    arrays = ((qkv_own, qkv_all), (ou_own, ou_all), (down_own, down_all))

    def moves(phase, a):
        own, full = arrays[a]
        if phase == 1:
            mine = full.at[x, core, z, y]
            return [(own, mine, device(x, core, o, y), j) for j, o in enumerate(others)]
        if phase == 2:
            part = full.at[x, core, :, y]
            return [(part, part, to_x, 3), (part, part, to_y, 4), (part, part, to_core, 5)]
        if phase == 3:
            low = full.at[x, core, pl.ds(0, 2), oy]
            high = full.at[ox, core, pl.ds(2, 2), y]
            from_x = full.at[ox, core, :, y]
            from_y = full.at[x, core, :, oy]
            return [
                (low, low, to_x, 6),
                (high, high, to_y, 7),
                (from_x, from_x, to_core, 8),
                (from_y, from_y, to_core, 9),
            ]
        part = full.at[ox, core, :, oy]
        return [(part, part, to_core, 10)]

    def phase_copies(phase, a):
        copies = [
            remote(src, dst, g_send.at[a * 11 + n], g_recv.at[a * 11 + n], peer)
            for src, dst, peer, n in moves(phase, a)
        ]
        if phase == 1:
            own, full = arrays[a]
            copies.append(pltpu.make_async_copy(own, full.at[x, core, z, y], g_own.at[a]))
        return copies

    def launch(phase, a):
        for copy in phase_copies(phase, a):
            copy.start()

    def finish(phase, a):
        for copy in phase_copies(phase, a):
            copy.wait()

    hz = z // 2

    def picked(position, half_z):
        return half_z * (1 - position) + (1 - half_z) * position

    def hop(src, dst, peer, g, n):
        return remote(src, dst, f_send.at[20 * g + n], f_recv.at[20 * g + n], peer)

    def to_xy(g, c):
        part = qkv_all.at[g, x, core, c, y]
        return hop(part, part, to_x, g, 4 + c), hop(part, part, to_y, g, 8 + c)

    def corner(g, c, over_x):
        if over_x:
            part = qkv_all.at[g, x, core, c, oy]
            return hop(part, part, to_x, g, 12 + c)
        part = qkv_all.at[g, ox, core, c, y]
        return hop(part, part, to_y, g, 12 + c)

    def to_sibling(g, n):
        part = (
            qkv_all.at[g, x, core, :, y],
            qkv_all.at[g, ox, core, :, y],
            qkv_all.at[g, x, core, :, oy],
            qkv_all.at[g, ox, core, :, oy],
        )[n]
        return hop(part, part, to_core, g, 16 + n)

    def along(g, n):
        return hop(
            qkv_own.at[g], qkv_all.at[g, x, core, z, y], device(x, core, others[n], y), g, n
        )

    own_first = pltpu.make_async_copy(qkv_own, qkv_all.at[:, x, core, z, y], g_own.at[0])
    own_first.start()
    for position in range(2):
        for n, other in enumerate(others):
            along(picked(position, other // 2), n).start()
        g = picked(position, hz)
        own = qkv_all.at[g, x, core, z, y]
        hop(qkv_own.at[g], own, to_x, g, 4 + z).start()
        hop(qkv_own.at[g], own, to_y, g, 8 + z).start()
    out_parts = unflatten(out_flat, stage, 16, groups)
    for j in range(groups):
        ou_own[:, 128 * j : 128 * (j + 1)] = out_parts[j].astype(BF16)
    up_groups = up_flat.shape[0] // 16
    up_parts = unflatten(up_flat, stage, 16, up_groups)
    for j in range(up_groups):
        at = width + 128 * j
        ou_own[:, at : at + 128] = up_parts[j].astype(BF16)
    down_rows = down_flat.shape[0] // groups
    down_parts = unflatten(down_flat, stage, down_rows, groups)
    for j in range(groups):
        down_own[:, 128 * j : 128 * (j + 1)] = down_parts[j].astype(BF16)
    launch(1, 1)
    launch(1, 2)
    own_first.wait()
    one, two = picked(0, hz), picked(1, hz)
    for g in (one, two):
        for n in range(3):
            along(g, n).wait_recv()
            for copy in to_xy(g, (z + 3 - n) % 4):
                copy.start()
        to_sibling(g, 0).start()
    value = tokens[...].astype(F32)
    center = jnp.mean(value, axis=1, keepdims=True)
    offset = value - center
    spread = jnp.mean(offset * offset, axis=1, keepdims=True)
    norm_s[...] = offset * lax.rsqrt(spread + eps_norm)

    def meet(g):
        for c in [z] + others:
            over_x, over_y = to_xy(g, c)
            over_x.wait_recv()
            over_y.wait_recv()

            @pl.when(c < 2)
            def _():
                corner(g, c, True).start()

            @pl.when(c >= 2)
            def _():
                corner(g, c, False).start()

        to_sibling(g, 1).start()
        to_sibling(g, 2).start()

    def turn(g):
        for c in range(4):
            corner(g, c, c < 2).wait()
        to_sibling(g, 3).start()

    def close(g):
        for n in range(4):
            to_sibling(g, n).wait()

    meet(one)
    meet(two)
    turn(one)
    turn(two)
    close(one)

    vec_ref[...] = jnp.zeros_like(vec_ref)
    devices = [(a, b, c, d) for a in range(2) for b in range(2) for c in range(4) for d in range(2)]
    base = 128 * len(devices)

    def bias_rows(begin, end):
        for n in range(begin, end):
            piece = qkv_all[(one,) + devices[n] + (slice(None), pl.ds(group, 128))].astype(F32)
            vec_ref[0:1, 128 * n : 128 * (n + 1)] = piece[0:1]

    def norm_rows(begin, end):
        for n in range(begin, end):
            pair = [
                qkv_all[(one,) + devices[2 * n + d] + (slice(None), pl.ds(group, 128))].astype(F32)
                for d in range(2)
            ]
            joined = jnp.concatenate([pair[0][1:2, :HALF], pair[1][1:2, :HALF]], axis=1)
            vec_ref[0:1, base + 128 * n : base + 128 * (n + 1)] = joined

    bias_rows(0, 2 * groups)
    norm_rows(0, 2 * groups)
    gain = vec_ref[0:1, base : base + width]
    shift = vec_ref[0:1, base + width : base + 2 * width]
    a1_ref[...] = (norm_s[...] * gain + shift).astype(BF16)

    def part_of(is_query):
        return pl.ds(rows, half) if is_query else pl.ds(0, rows)

    def send_part(tz, mark, is_query):
        for step in range(2):
            ty = (y + step) % 2
            index = mark + step
            src = packed.at[2 * tz + ty, part_of(is_query)]
            dst = got.at[me, part_of(is_query)]
            n = index + 8 * is_query
            if index == 0:
                pltpu.make_async_copy(src, dst, x_recv.at[n]).start()
            else:
                remote(src, dst, x_send.at[n], x_recv.at[n], device(x, core, tz, ty)).start()

    order = (
        hz * 2 + 1 - z % 2,
        z,
        (1 - hz) * 2 + z % 2,
        (1 - hz) * 2 + 1 - z % 2,
    )
    marks = (2, 0, 4, 6)
    left1 = left_lanes(1)
    for place_of, (tz, mark) in enumerate(zip(order, marks)):
        if place_of == 2:
            close(two)
        g = one if place_of < 2 else two
        a1 = a1_ref[...]
        at = pl.multiple_of(tz % 2 * 128, 128)
        w_q = qkv_all[g, :, :, :, :, :, pl.ds(at, 128)].reshape(width, 128)
        q = (mm(a1, w_q) + vec_ref[0:1, pl.ds(pl.multiple_of(128 * tz, 128), 128)]).astype(BF16)
        at_kv = pl.multiple_of(256 + tz % 2 * 256, 128)
        w_kv = qkv_all[g, :, :, :, :, :, pl.ds(at_kv, 256)].reshape(width, 256)
        bias = vec_ref[0:1, pl.ds(pl.multiple_of(width + 128 * tz, 128), 128)]
        kv = mm(a1, w_kv)
        even = kv[:, :128] + jnp.where(left1, 0.0, swap_halves(bias))
        odd = kv[:, 128:] + jnp.where(left1, 0.0, bias)
        packed[2 * tz, :rows] = even.astype(BF16)
        packed[2 * tz + 1, :rows] = odd.astype(BF16)
        top, low = q[:half], q[half:]
        packed[2 * tz, rows:] = jnp.where(left_half, top, swap_halves(low))
        packed[2 * tz + 1, rows:] = jnp.where(left_half, swap_halves(top), low)
        if mark < 4:
            send_part(tz, mark, False)
            send_part(tz, mark, True)

    def send_cross():
        def send_all(is_query):
            for tz, mark in zip(order[2:], marks[2:]):
                send_part(tz, mark, is_query)

        pl.when(hz == 1)(lambda: send_all(True))
        send_all(False)
        pl.when(hz == 0)(lambda: send_all(True))

    send_cross()
    finish(1, 1)
    finish(1, 2)
    launch(2, 1)
    launch(2, 2)
    bias_rows(2 * groups, len(devices))
    norm_rows(2 * groups, len(devices) // 2)

    def block_wait(sems, index, view):
        pltpu.make_async_copy(view, view, sems.at[index]).wait()

    def arrive(part, is_query):
        for t in range(2):
            b = 2 * part + t
            block_wait(x_recv, xor8(b, me) + 8 * is_query, got.at[b, part_of(is_query)])
            at = pl.multiple_of(b * rows, rows)
            if is_query:
                both = got[b, rows:]
                q_s[pl.ds(at, half), :] = jnp.where(left_half, both, 0).astype(BF16)
                q_s[pl.ds(at + half, half), :] = jnp.where(
                    left_half, swap_halves(both), 0
                ).astype(BF16)
            else:
                pair = got[b, :rows]
                k_s[pl.ds(at, rows), :] = jnp.where(left, pair, 0).astype(BF16)
                v_s[pl.ds(at, rows), :] = jnp.where(left, 1, pair).astype(BF16)

    low = 1 - hz
    queries = low * TILES[0][0] + hz * TILES[1][0]
    keys = low * TILES[0][1] + hz * TILES[1][1]
    ends = low * TILES[0][2] + hz * TILES[1][2]
    m_s[...] = jnp.full(m_s.shape, masked_score, F32)
    acc_s[...] = jnp.zeros(acc_s.shape, F32)
    for n in range(2):
        arrive(2 * hz + n, False)
        arrive(2 * hz + n, True)

    def step(n, carry):
        q_left, k_left, e_left = carry
        i, j, done = q_left % 4, k_left % 4, e_left % 4

        @pl.when(n == 3)
        def _():
            for a in (1, 2):
                finish(2, a)
                launch(3, a)

        @pl.when(n == 6)
        def _():
            for a in (1, 2):
                finish(3, a)
                launch(4, a)

        for when, part, is_query in ((3, 2, 1), (5, 2, 0), (6, 3, 1), (9, 3, 0)):
            pl.when(n == when + 16 * hz)(lambda: arrive(part, is_query))
        for when, part, is_query in ((3, 0, 0), (5, 0, 1), (6, 1, 0), (8, 1, 1)):
            pl.when(n == when + 16 * low)(lambda: arrive(part, is_query))

        at = pl.multiple_of(i * tile, tile)
        begin = pl.multiple_of(j * tile, tile)

        def update(diagonal):
            s = mm(q_s[pl.ds(at, tile), :], k_s[pl.ds(begin, tile), :], NT)
            if diagonal:
                allowed = diagonal_mask(tile, flags, i * (tile // PIECE), False)
                s = jnp.where(allowed, s, masked_score)
            old = m_s[pl.ds(at, tile), :]
            new = jnp.maximum(old, jnp.max(s, axis=1, keepdims=True) * scale)
            p = jnp.exp2(s * scale - new[:, :1])
            m_s[pl.ds(at, tile), :] = new
            acc_s[pl.ds(at, tile), :] = acc_s[pl.ds(at, tile), :] * jnp.exp2(old - new) + mm(
                p.astype(BF16), v_s[pl.ds(begin, tile), :]
            )

        pl.when(i == j)(lambda: update(True))
        pl.when(i != j)(lambda: update(False))

        @pl.when(done == 1)
        def _():
            acc = acc_s[pl.ds(at, tile), :]
            total = jnp.broadcast_to(acc[:, :1], acc.shape)
            o = acc / total
            o_ref[pl.ds(at, tile), :] = o
            lse = m_s[pl.ds(at, tile), :] + jnp.log2(total)
            lse_ref[:, pl.ds(at, tile)] = jnp.transpose(lse)[:8]
            for t in range(2):
                b = 2 * i + t
                top = o[t * rows : t * rows + half]
                bottom = o[t * rows + half : (t + 1) * rows]
                o2_s[b] = jnp.where(left_half, swap_halves(top), bottom).astype(BF16)
                index = xor8(b, me)

                @pl.when(b == me)
                def _():
                    pltpu.make_async_copy(o2_s.at[b], mix.at[me], o_recv.at[0]).start()

                @pl.when(b != me)
                def _():
                    remote(
                        o2_s.at[b],
                        mix.at[me],
                        o_send.at[index],
                        o_recv.at[index],
                        device(x, core, i, t),
                    ).start()

        return q_left // 4, k_left // 4, e_left // 4

    lax.fori_loop(0, 10, step, (queries, keys, ends))
    for a in (1, 2):
        finish(4, a)
    for g in range(2):
        for n in range(3):
            along(g, n).wait_send()
        for c in range(4):
            for copy in to_xy(g, c):
                copy.wait_send()
    for index in range(8):
        block_wait(o_recv, index, mix.at[0])
        if index:
            block_wait(x_send, index, packed.at[0, part_of(False)])
            block_wait(x_send, index + 8, packed.at[0, part_of(True)])
            block_wait(o_send, index, o2_s.at[0])


def middle_phase(r):
    tokens = r.tokens
    cot = r.cot
    mix = r.mix
    vec = r.vec
    ou_all = r.ou_all
    down_all = r.down_all
    out_ref = r.out_ref
    dx_ref = r.n2_s
    do2_ref = r.do2
    acc_ou = r.acc_ou
    acc_down = r.acc_down
    sums_ref = r.sums
    o_s = r.o_s
    x1_s = r.x1_s
    n2_s = r.n2_s
    a2_s = r.a2_s
    gl_s = r.gl_s
    du_s = r.du_s
    dh_s = r.dh_s
    da_s = r.da_s
    r_s = r.r_s
    send2 = r.o2_s
    core_ou = r.core_ou
    core_down = r.core_down
    got_ou = r.got_ou
    got_down = r.got_down
    x_send = r.d_send
    x_recv = r.d_recv
    c_send = r.c_send
    c_recv = r.c_recv
    x, core, z, y = place()
    oc, oy = 1 - core, 1 - y
    me = z * 2 + y
    rows, width = tokens.shape
    half = rows // 2
    hidden = ou_all.shape[-1] - width
    left_half = left_lanes(half)
    to_core = device(x, oc, z, y)
    bias_o = vec[0:1, 2 * width : 3 * width]
    bias_down = vec[0:1, 3 * width + hidden : 4 * width + hidden]
    base = 4 * width + hidden
    gain = vec[0:1, base + 2 * width : base + 3 * width]
    shift = vec[0:1, base + 3 * width : base + 4 * width]

    for j in range(HEADS // 2):
        even, odd = mix[2 * j], mix[2 * j + 1]
        at = 128 * j
        o_s[:half, at : at + 128] = jnp.where(left_half, even, swap_halves(odd))
        o_s[half:, at : at + 128] = jnp.where(left_half, swap_halves(even), odd)
    w_out = ou_all[:, :, :, :, :, :width].reshape(width, width)
    x1 = tokens[...].astype(F32) + mm(o_s[...], w_out) + bias_o
    x1_s[...] = x1
    center = jnp.mean(x1, axis=1, keepdims=True)
    offset = x1 - center
    spread = jnp.mean(offset * offset, axis=1, keepdims=True)
    inverse = lax.rsqrt(spread + eps_norm)
    r_s[...] = jnp.broadcast_to(inverse, r_s.shape)
    n2 = offset * inverse
    n2_s[...] = n2
    a2_s[...] = (n2 * gain + shift).astype(BF16)
    sums_ref[...] = jnp.zeros_like(sums_ref)

    @pl.loop(0, hidden // width)
    def _(j):
        at = pl.multiple_of(j * width, width)
        w_up = ou_all[:, :, :, :, :, pl.ds(pl.multiple_of(width + at, width), width)].reshape(
            width, width
        )
        b_up = vec[0:1, pl.ds(pl.multiple_of(3 * width + at, width), width)]
        w_down = down_all[j // 2, j % 2].reshape(width, width)
        u = mm(a2_s[...], w_up) + b_up
        phi = 0.5 * (1.0 + lax.erf(u * (0.5**0.5)))
        slope = phi + u * jnp.exp(-0.5 * u * u) * (1.0 / math.sqrt(2.0 * math.pi))
        gl_s[:, pl.ds(at, width)] = (u * phi).astype(BF16)
        grad = mm(cot[...], w_down, NT)
        du = (grad * slope).astype(BF16)
        du_s[:, pl.ds(at, width)] = du
        sums_ref[0:1, pl.ds(pl.multiple_of(3 * width + at, width), width)] = jnp.sum(
            du.astype(F32), axis=0, keepdims=True
        )
        part = mm(du, w_up, NT)

        @pl.when(j == 0)
        def _():
            dh_s[...] = part

        @pl.when(j > 0)
        def _():
            dh_s[...] += part

    dh2 = dh_s[...]
    n2 = n2_s[...]
    sums_ref[0:1, base + 2 * width : base + 3 * width] = jnp.sum(dh2 * n2, axis=0, keepdims=True)
    sums_ref[0:1, base + 3 * width : base + 4 * width] = jnp.sum(dh2, axis=0, keepdims=True)
    e = dh2 * gain
    mean_e = jnp.mean(e, axis=1, keepdims=True)
    mean_en = jnp.mean(e * n2, axis=1, keepdims=True)
    dx = cot[...].astype(F32) + r_s[:, :1] * (e - mean_e - n2 * mean_en)
    dx_ref[...] = dx
    da = dx.astype(BF16)
    da_s[...] = da
    w_out = ou_all[:, :, :, :, :, :width].reshape(width, width)
    grad_o = mm(da, w_out, NT).astype(BF16)
    for j in range(HEADS // 2):
        group = grad_o[:, 128 * j : 128 * (j + 1)]
        top, low = group[:half], group[half:]
        send2[2 * j] = jnp.where(left_half, top, swap_halves(low))
        send2[2 * j + 1] = jnp.where(left_half, swap_halves(top), low)
    hz = z // 2
    order = ((1 - hz) * 2 + z % 2, (1 - hz) * 2 + 1 - z % 2, hz * 2 + 1 - z % 2, z)
    for tz, mark in zip(order, (4, 6, 2, 0)):
        for step in range(2):
            ty = (y + step) % 2
            index = mark + step
            src = send2.at[2 * tz + ty]
            if index == 0:
                pltpu.make_async_copy(src, do2_ref.at[me], x_recv.at[0]).start()
            else:
                remote(
                    src,
                    do2_ref.at[me],
                    x_send.at[index],
                    x_recv.at[index],
                    device(x, core, tz, ty),
                ).start()

    def grads(c, n):
        dp = 2 * n + c
        at = pl.multiple_of(dp * 128, 128)
        down_at = pl.multiple_of(dp * width, width)
        d_down = mm(gl_s[:, pl.ds(down_at, width)], cot[...], TN)
        d_up = mm(a2_s[:, pl.ds(at, 128)], du_s[...], TN)
        d_out = mm(o_s[:, pl.ds(at, 128)], da_s[...], TN)
        return (
            d_down.reshape(4, 2, width // 8, width),
            d_up.reshape(4, 2, 16, hidden),
            d_out.reshape(4, 2, 16, width),
        )

    for n in range(2):
        d_down, d_up, d_out = grads(oc, n)
        core_down[n] = d_down.astype(BF16)
        core_ou[n, :, :, :, width:] = d_up.astype(BF16)
        core_ou[n, :, :, :, :width] = d_out.astype(BF16)
    to_ou = remote(core_ou, got_ou, c_send.at[0], c_recv.at[0], to_core)
    to_down = remote(core_down, got_down, c_send.at[1], c_recv.at[1], to_core)
    to_ou.start()
    to_down.start()
    sums_ref[0:1, 2 * width : 3 * width] = jnp.sum(da_s[...].astype(F32), axis=0, keepdims=True)
    sums_ref[0:1, 3 * width + hidden : 4 * width + hidden] = jnp.sum(
        cot[...].astype(F32), axis=0, keepdims=True
    )
    result = x1_s[...] + mm(gl_s[...], down_all[...].reshape(hidden, width)) + bias_down
    out_ref[...] = result.astype(BF16)
    for n in range(2):
        d_down, d_up, d_out = grads(core, n)
        acc_down[n] = d_down
        acc_ou[n, :, :, :, width:] = d_up
        acc_ou[n, :, :, :, :width] = d_out
    to_ou.wait()
    to_down.wait()
    acc_ou[...] += got_ou[...].astype(F32)
    acc_down[...] += got_down[...].astype(F32)


def lanes_of(ref, r, g):
    group = r.tokens.shape[1] * 3 // 2
    return ref.at[:, :, :, :, pl.ds(pl.multiple_of(g * group, 128), group)]


def reducer_of(r, name, first, at=None):
    bufs = [getattr(r, f"{name}{n}") for n in range(REDUCE_BUFFERS)]
    if at is not None:
        return reducer(lanes_of(r.acc_ou, r, at), [b.at[at] for b in bufs], r.r_send, r.r_recv, first)
    acc = getattr(r, f"acc_{name}")
    return reducer(acc, bufs, r.r_send, r.r_recv, first)


def backward_phase(r):
    got, do2, o_heads, lse, grads, packed = r.got, r.do2, r.o_heads, r.lse, r.grads, r.packed
    qd_s, k_s, v_s, delta_s, dq_s, dkv_s = r.q_s, r.k_s, r.v_s, r.delta_s, r.acc_s, r.m_s
    flags = r.flags
    x, core, z, y = place()
    me = z * 2 + y
    hz = z // 2
    low = 1 - hz
    blocks = got.shape[0]
    rows = got.shape[1] // 3 * 2
    half = rows // 2
    quarter = blocks // 2
    scale = math.log2(math.e) * HALF**-0.5
    factor = HALF**-0.5
    left = left_lanes(rows)
    left_half = left_lanes(half)
    sums = (reducer_of(r, "ou", 0), reducer_of(r, "down", REDUCE_COPIES))
    for launch, _, _ in sums:
        launch(1)

    def enter(b):
        at = pl.multiple_of(b * rows, rows)
        pltpu.make_async_copy(do2.at[b], do2.at[b], r.d_recv.at[xor8(b, me)]).wait()
        v_s[pl.ds(at, rows), :] = jnp.where(left, 0, v_s[pl.ds(at, rows), :]).astype(BF16)
        grad = do2[b]
        for part, begin in ((swap_halves(grad), 0), (grad, half)):
            rows_at = pl.ds(at + begin, half)
            qd_s[rows_at, :] = jnp.where(left_half, qd_s[rows_at, :], part)
            product = jnp.where(left_half, 0.0, part.astype(F32) * o_heads[rows_at, :])
            delta = jnp.sum(jnp.transpose(product), axis=0, keepdims=True)
            delta_s[:, rows_at] = jnp.broadcast_to(delta, (8, half))
        dq_s[pl.ds(at, rows), :] = jnp.zeros((rows, 2 * HALF), F32)
        dkv_s[pl.ds(at, rows), :] = jnp.zeros((rows, 2 * HALF), F32)

    def tile(kj, qi, diagonal):
        k0 = pl.multiple_of(kj * rows, rows)
        q0 = pl.multiple_of(qi * rows, rows)
        k = k_s[pl.ds(k0, rows), :]
        v = v_s[pl.ds(k0, rows), :]
        qd = qd_s[pl.ds(q0, rows), :]
        scores = mm(k, qd, NT)
        dprobs = mm(v, qd, NT)
        p = jnp.exp2(scores * scale - lse[:1, pl.ds(q0, rows)])
        if diagonal:
            allowed = diagonal_mask(rows, flags, kj * (rows // PIECE), True)
            p = jnp.where(allowed, p, 0.0)
        ds = (p * (dprobs - delta_s[:1, pl.ds(q0, rows)])).astype(BF16)
        dkv_s[pl.ds(k0, rows), :] += jnp.where(left, mm(ds, qd), mm(p.astype(BF16), qd))
        dq_s[pl.ds(q0, rows), :] += mm(ds, k, TN)

    def part_of(is_query):
        return pl.ds(rows, half) if is_query else pl.ds(0, rows)

    def leave(a, is_query):
        at = pl.multiple_of(a * rows, rows)
        if is_query:
            top = dq_s[pl.ds(at, half), :]
            bottom = dq_s[pl.ds(at + half, half), :]
            packed[a, rows:] = (
                jnp.where(left_half, top, swap_halves(bottom)) * factor
            ).astype(BF16)
        else:
            block = dkv_s[pl.ds(at, rows), :]
            packed[a, :rows] = jnp.where(left, block * factor, block).astype(BF16)
        index = xor8(a, me) + 8 * is_query
        src = packed.at[a, part_of(is_query)]
        dst = grads.at[me, part_of(is_query)]

        @pl.when(a == me)
        def _():
            pltpu.make_async_copy(src, dst, r.b_recv.at[index]).start()

        @pl.when(a != me)
        def _():
            remote(
                src, dst, r.b_send.at[index], r.b_recv.at[index], device(x, core, a // 2, a % 2)
            ).start()

    for n in range(quarter):
        enter(hz * quarter + n)

    @pl.loop(0, 12)
    def _(row):
        seg = (row + 3) // 4
        last = seg // 3
        first = (3 - seg) // 3
        square = seg // 2 - last
        cross = seg % 2 - last
        own = first + last
        i = (row + 3) % 4 + last - 3 * first

        @pl.when(row == 1)
        def _():
            for n in range(quarter):
                enter(low * quarter + n)

        @pl.when(row == 4)
        def _():
            for _, finish, _ in sums:
                finish(1)
            for launch, _, _ in sums:
                launch(2)

        a_low = own * (3 - i) + (1 - own) * (7 - i)
        a_high = own * (4 + i) + (1 - own) * i
        a = low * a_low + hz * a_high
        count = own * (3 - i) + cross * i + square * 4

        @pl.when(square == 0)
        def _():
            tile(a, a, True)

        @pl.loop(0, count)
        def _(u):
            k_low = (own + square) * u + cross * a_low
            q_low = (own + square) * a_low + cross * (7 - u)
            k_high = (own + square) * a_high + cross * u
            q_high = own * (5 + i + u) + cross * a_high + square * (4 + u)
            tile(low * k_low + hz * k_high, low * q_low + hz * q_high, False)

        @pl.when(cross * hz + square * low + last > 0)
        def _():
            leave(a, 1)

        @pl.when(cross * low + square * hz + last > 0)
        def _():
            leave(a, 0)

        @pl.when(row == 8)
        def _():
            begin = low * 3 + hz * 4
            leave(begin, 1)
            leave(begin, 0)


def last_phase(r):
    grads, a1, tokens, dx, qkv_all, vec, sums = (
        r.grads,
        r.a1,
        r.tokens,
        r.n2_s,
        r.qkv_all,
        r.vec,
        r.sums,
    )
    dqkv_s, got_q = r.gl_s, r.got_q
    core_small, got_small, acc_small = r.core_small, r.got_small, r.acc_small
    x, core, z, y = place()
    me = z * 2 + y
    hz = z // 2
    oc = 1 - core
    to_core = device(x, oc, z, y)
    rows, width = tokens.shape
    half = rows // 2
    group = 3 * width // 2
    left_half = left_lanes(half)
    left1 = left_lanes(1)
    base = vec.shape[1] - 4 * width

    def columns_of(g):
        return pl.ds(pl.multiple_of(g * group, 128), group)

    def enter(g):
        for n in range(HEADS // 2):
            h = g * (HEADS // 2) + n
            for is_query in range(2):
                view = grads.at[h, pl.ds(rows, half) if is_query else pl.ds(0, rows)]
                pltpu.make_async_copy(view, view, r.b_recv.at[xor8(h, me) + 8 * is_query]).wait()
        begin = g * group
        for j in range(HEADS // 4):
            h = g * (HEADS // 2) + 2 * j
            even, odd = grads[h, rows:], grads[h + 1, rows:]
            at = pl.ds(pl.multiple_of(begin + 128 * j, 128), 128)
            dqkv_s[:half, at] = jnp.where(left_half, even, swap_halves(odd))
            dqkv_s[half:, at] = jnp.where(left_half, swap_halves(even), odd)
        for n in range(HEADS // 2):
            at = pl.ds(pl.multiple_of(begin + 256 + 128 * n, 128), 128)
            dqkv_s[:, at] = grads[g * (HEADS // 2) + n, :rows]

    def weight_grad(c, n, g):
        at = pl.multiple_of((2 * n + c) * 128, 128)
        return mm(a1[:, pl.ds(at, 128)], dqkv_s[:, columns_of(g)], TN).reshape(4, 2, 16, group)

    def over(g):
        return remote(lanes_of(r.core_ou, r, g), got_q.at[g], r.e_send.at[g], r.e_recv.at[g], to_core)

    parts = []
    for position, g in enumerate((1 - hz, hz)):
        enter(g)
        if position == 0:
            for early in (reducer_of(r, "ou", 0), reducer_of(r, "down", REDUCE_COPIES)):
                early[1](2)
                early[0](3)
        for n in range(2):
            lanes_of(r.core_ou, r, g)[n] = weight_grad(oc, n, g).astype(BF16)
        over(g).start()
        w = qkv_all[g, :, :, :, :, :, :group].reshape(width, group)
        part = mm(dqkv_s[:, columns_of(g)], w, NT)
        if position:
            r.dh_s[...] += part
        else:
            r.dh_s[...] = part
        for n in range(2):
            lanes_of(r.acc_ou, r, g)[n] = weight_grad(core, n, g)
        over(g).wait()
        acc_q = lanes_of(r.acc_ou, r, g)
        acc_q[...] = acc_q[...] + got_q[g].astype(F32)
        parts.append(reducer_of(r, "q", (2 + g) * REDUCE_COPIES, g))
        parts[-1][0](1)

    columns = jnp.sum(dqkv_s[:, : 3 * width].astype(F32), axis=0, keepdims=True)
    for j in range(HEADS // 2):
        at = (j // 2) * group + (j % 2) * 128
        sums[0:1, 128 * j : 128 * (j + 1)] = columns[:, at : at + 128]
        at = (j // 2) * group + 256 + (j % 2) * 256
        pair = jnp.where(
            left1, swap_halves(columns[:, at : at + 128]), columns[:, at + 128 : at + 256]
        )
        sums[0:1, width + 128 * j : width + 128 * (j + 1)] = pair
    dh = r.dh_s[...]
    gain = vec[0:1, base : base + width]
    value = tokens[...].astype(F32)
    center = jnp.mean(value, axis=1, keepdims=True)
    offset = value - center
    spread = jnp.mean(offset * offset, axis=1, keepdims=True)
    inverse = lax.rsqrt(spread + eps_norm)
    norm = offset * inverse
    sums[0:1, base : base + width] = jnp.sum(dh * norm, axis=0, keepdims=True)
    sums[0:1, base + width : base + 2 * width] = jnp.sum(dh, axis=0, keepdims=True)

    def small_block(a, b, c, d):
        n = (a * 2 + b) * 8 + c * 2 + d
        piece = sums[0:1, pl.ds(pl.multiple_of(128 * n, 128), 128)]
        pair = sums[0:1, pl.ds(pl.multiple_of(base + 128 * (n // 2), 128), 128)]
        own = pair if d == 0 else swap_halves(pair)
        return jnp.concatenate([piece, own, jnp.zeros((6, 128), F32)], axis=0)

    for a in range(2):
        for c in range(4):
            for d in range(2):
                core_small[a, c, d] = small_block(a, oc, c, d)
                acc_small[a, c, d] = small_block(a, core, c, d)
    over_small = remote(core_small, got_small, r.e_send.at[2], r.e_recv.at[2], to_core)
    over_small.start()
    parts[0][1](1)
    parts[0][0](2)
    over_small.wait()
    acc_small[...] += got_small[...]
    parts.append(reducer_of(r, "small", 4 * REDUCE_COPIES))
    parts[2][0](1)
    e = dh * gain
    mean_e = jnp.mean(e, axis=1, keepdims=True)
    mean_en = jnp.mean(e * norm, axis=1, keepdims=True)
    r.grad_tokens[...] = dx[...] + inverse * (e - mean_e - norm * mean_en)
    parts[1][1](1)
    parts[1][0](2)
    parts[0][1](2)
    parts[0][0](3)
    parts[2][1](1)
    parts[2][0](2)
    parts[1][1](2)
    parts[1][0](3)
    parts[2][1](2)
    parts[2][0](3)
    for part in (reducer_of(r, "ou", 0), reducer_of(r, "down", REDUCE_COPIES)):
        part[1](3)
    r.sum_ou[...] = reducer_of(r, "ou", 0)[2]()
    r.sum_down[...] = reducer_of(r, "down", REDUCE_COPIES)[2]()
    for _, finish, _ in parts:
        finish(3)
    for g, part in zip((1 - hz, hz), parts):
        r.sum_qkv[g] = part[2]()
    r.sum_small[...] = parts[2][2]()
    for index in range(HEADS):
        if index:
            for is_query, count in ((0, rows), (1, half)):
                view = r.packed.at[0, pl.ds(rows * is_query, count)]
                pltpu.make_async_copy(view, view, r.b_send.at[index + 8 * is_query]).wait()
            view = r.o2_s.at[0]
            pltpu.make_async_copy(view, view, r.d_send.at[index]).wait()


def layer_kernel(names, *refs):
    r = types.SimpleNamespace(**dict(zip(names, refs)))
    forward_phase(r)
    middle_phase(r)
    backward_phase(r)
    last_phase(r)


def layer(inputs, cid):
    rows, width = inputs["tokens"].shape
    length = rows * HEADS
    lanes = 2 * HALF
    hidden = inputs["up_flat"].shape[0] * 128 // 16
    down_rows = inputs["down_flat"].shape[0] * 128 // width
    group = 3 * width // 2
    every = (2, 2, 4, 2)
    mine = (2, 4, 2)
    row = (8, 4096 + 4 * width)
    vmem = pltpu.VMEM
    dma = pltpu.SemaphoreType.DMA
    outputs = {
        "out_ref": jax.ShapeDtypeStruct((rows, width), BF16),
        "grad_tokens": jax.ShapeDtypeStruct((rows, width), F32),
        "sum_qkv": jax.ShapeDtypeStruct((2, 16, group), F32),
        "sum_ou": jax.ShapeDtypeStruct((16, width + hidden), F32),
        "sum_down": jax.ShapeDtypeStruct((down_rows, width), F32),
        "sum_small": jax.ShapeDtypeStruct((8, 128), F32),
    }
    scratch = {
        "flags": pltpu.SMEM((length // PIECE,), jnp.int32),
        "a1": vmem((rows, width), BF16),
        "got": vmem((HEADS, rows + rows // 2, lanes), BF16),
        "mix": vmem((HEADS, rows // 2, lanes), BF16),
        "o_heads": vmem((length, lanes), F32),
        "lse": vmem((8, length), F32),
        "vec": vmem(row, F32),
        "qkv_all": vmem((2,) + every + (16, group + 128), BF16),
        "ou_all": vmem(every + (16, width + hidden), BF16),
        "down_all": vmem(every + (down_rows, width), BF16),
        "stage": vmem((256, 128), F32),
        "qkv_own": vmem((2, 16, group + 128), BF16),
        "ou_own": vmem((16, width + hidden), BF16),
        "down_own": vmem((down_rows, width), BF16),
        "packed": vmem((HEADS, rows + rows // 2, lanes), BF16),
        "q_s": vmem((length, lanes), BF16),
        "k_s": vmem((length, lanes), BF16),
        "v_s": vmem((length, lanes), BF16),
        "m_s": vmem((length, lanes), F32),
        "acc_s": vmem((length, lanes), F32),
        "o2_s": vmem((HEADS, rows // 2, lanes), BF16),
        "do2": vmem((HEADS, rows // 2, lanes), BF16),
        "acc_ou": vmem(mine + (16, width + hidden), F32),
        "acc_down": vmem(mine + (down_rows, width), F32),
        "sums": vmem(row, F32),
        "o_s": vmem((rows, width), BF16),
        "x1_s": vmem((rows, width), F32),
        "n2_s": vmem((rows, width), F32),
        "a2_s": vmem((rows, width), BF16),
        "gl_s": vmem((rows, hidden), BF16),
        "du_s": vmem((rows, hidden), BF16),
        "dh_s": vmem((rows, width), F32),
        "da_s": vmem((rows, width), BF16),
        "r_s": vmem((rows, lanes), F32),
        "core_ou": vmem(mine + (16, width + hidden), BF16),
        "core_down": vmem(mine + (down_rows, width), BF16),
        "got_ou": vmem(mine + (16, width + hidden), BF16),
        "got_down": vmem(mine + (down_rows, width), BF16),
        "delta_s": vmem((8, length), F32),
        "grads": vmem((HEADS, rows + rows // 2, lanes), BF16),
        "got_q": vmem((2,) + mine + (16, group), BF16),
        "core_small": vmem(mine + (8, 128), F32),
        "got_small": vmem(mine + (8, 128), F32),
        "acc_small": vmem(mine + (8, 128), F32),
    }
    for name, lead, r, w, wire in (
        ("ou", (), 16, width + hidden, BF16),
        ("down", (), down_rows, width, BF16),
        ("q", (2,), 16, group, BF16),
        ("small", (), 8, 128, F32),
    ):
        for n, buf in enumerate(reduce_buffers(r, w, wire)):
            scratch[f"{name}{n}"] = vmem(lead + buf.shape, buf.dtype)
    for name, count in (
        ("g_own", 3),
        ("g_send", 33),
        ("g_recv", 33),
        ("f_send", 40),
        ("f_recv", 40),
        ("x_send", 16),
        ("x_recv", 16),
        ("o_send", 8),
        ("o_recv", 8),
        ("d_send", 8),
        ("d_recv", 8),
        ("c_send", 2),
        ("c_recv", 2),
        ("r_send", 5 * REDUCE_COPIES),
        ("r_recv", 5 * REDUCE_COPIES),
        ("b_send", 16),
        ("b_recv", 16),
        ("e_send", 3),
        ("e_recv", 3),
    ):
        scratch[name] = dma((count,))
    names = tuple(inputs) + tuple(outputs) + tuple(scratch)

    def kernel(*refs):
        layer_kernel(names, *refs)

    return pl.pallas_call(
        kernel,
        out_shape=list(outputs.values()),
        in_specs=[SMEM_SPEC if n == "starts" else VMEM_SPEC for n in inputs],
        out_specs=[VMEM_SPEC] * len(outputs),
        scratch_shapes=list(scratch.values()),
        compiler_params=params(cid),
    )(*inputs.values())


def flatten_kernel(
    output,
    grad_tokens,
    sum_qkv,
    sum_ou,
    sum_down,
    sum_small,
    output_o,
    tokens_o,
    qkv_o,
    out_o,
    up_o,
    down_o,
    bias_o,
    norm_o,
):
    output_o[...] = output[...]
    tokens_o[...] = grad_tokens[...]
    groups = sum_down.shape[1] // 128
    left = left_lanes(16)

    def group(ref, j):
        return ref[:, 128 * j : 128 * (j + 1)]

    for j in range(groups):
        part = sum_qkv.at[j // 2]
        pair = j % 2
        qkv_o[pl.ds(j, 16, stride=3 * groups), :] = group(part, pair)
        even, odd = group(part, 2 + 2 * pair), group(part, 3 + 2 * pair)
        qkv_o[pl.ds(groups + j, 16, stride=3 * groups), :] = jnp.where(
            left, even, swap_halves(odd)
        )
        qkv_o[pl.ds(2 * groups + j, 16, stride=3 * groups), :] = jnp.where(
            left, swap_halves(even), odd
        )
        out_o[pl.ds(j, 16, stride=groups), :] = group(sum_ou, j)
        down_o[pl.ds(j, sum_down.shape[0], stride=groups), :] = group(sum_down, j)
    ups = sum_ou.shape[1] // 128 - groups
    for j in range(ups):
        up_o[pl.ds(j, 16, stride=ups), :] = group(sum_ou, groups + j)
    bias_o[...] = sum_small[0:1]
    norm_o[...] = sum_small[1:2, : norm_o.shape[1]]


def flatten(output, grad_tokens, sum_qkv, sum_ou, sum_down, sum_small, norm_len):
    width = sum_down.shape[1]
    sizes = (
        sum_qkv.size // 128,
        width * 16 // 128,
        (sum_ou.shape[1] - width) * 16 // 128,
        sum_down.size // 128,
    )
    return pl.pallas_call(
        flatten_kernel,
        out_shape=[
            jax.ShapeDtypeStruct(output.shape, output.dtype),
            jax.ShapeDtypeStruct(grad_tokens.shape, grad_tokens.dtype),
        ]
        + [jax.ShapeDtypeStruct((n, 128), F32) for n in sizes]
        + [jax.ShapeDtypeStruct((1, 128), F32), jax.ShapeDtypeStruct((1, norm_len), F32)],
        in_specs=[VMEM_SPEC] * 6,
        out_specs=[VMEM_SPEC] * 8,
        compiler_params=params(),
    )(output, grad_tokens, sum_qkv, sum_ou, sum_down, sum_small)


def fast_device(
    tokens, piece_starts, qkv_weight, out_weight, up_weight, down_weight, biases, norms, cotangent
):
    output, grad_tokens, sum_qkv, sum_ou, sum_down, sum_small = layer(
        {
            "starts": piece_starts,
            "tokens": tokens[0],
            "cot": cotangent[0],
            "biases": biases.reshape(1, -1),
            "norms": norms.reshape(1, -1),
            "qkv_flat": qkv_weight.reshape(-1, 128),
            "out_flat": out_weight.reshape(-1, 128),
            "up_flat": up_weight.reshape(-1, 128),
            "down_flat": down_weight.reshape(-1, 128),
        },
        1,
    )
    output, grad_tokens, *flats = flatten(
        output, grad_tokens, sum_qkv, sum_ou, sum_down, sum_small, norms.shape[0]
    )
    return (output[None], grad_tokens[None]) + tuple(f.reshape(-1) for f in flats)


def solution(mesh):
    flat = P(("dp", "ctx"))
    rows = P("dp", "ctx", None)
    fast = mesh.shape["dp"] == 4 and mesh.shape["ctx"] == HEADS
    return jax.shard_map(
        fast_device if fast else general_device,
        mesh=mesh,
        in_specs=(rows, P("dp", None), flat, flat, flat, flat, flat, flat, rows),
        out_specs=(rows, rows, flat, flat, flat, flat, flat, flat),
        check_vma=False,
    )
```

```python
import math
import types

import jax
import jax.numpy as jnp
from jax import lax
from jax.experimental import pallas as pl
from jax.experimental.pallas import tpu as pltpu
from jax.sharding import PartitionSpec as P

HEADS = 8
PIECE = 256


eps_norm = 1e-05
masked_score = -1e30


def layer_norm(values, gain, shift):
    center = jnp.mean(values, axis=-1, keepdims=True)
    offsets = values - center
    spread = jnp.mean(offsets * offsets, axis=-1, keepdims=True)
    return offsets * lax.rsqrt(spread + eps_norm) * gain + shift


def gelu_exact(values):
    return jax.nn.gelu(values, approximate=False)


def piece_flags(positions, starts_row):
    opening = positions // PIECE * PIECE
    return jnp.any(opening[:, None] == starts_row[None, :], axis=1)


def visible(query_pos, query_flag, key_pos):
    causal = key_pos[None, :] <= query_pos[:, None]
    same_piece = key_pos[None, :] // PIECE == query_pos[:, None] // PIECE
    return jnp.logical_or(causal, jnp.logical_and(same_piece, query_flag[:, None]))


def to_blocks(arrays, shard_rows):
    block_len = 256
    block_count = shard_rows // block_len
    shaped = tuple((member.reshape(block_count, block_len, HEADS, -1) for member in arrays))
    return (block_len, block_count, shaped)


def keep_state(state):
    return state


def unpack(flats, model_width):
    qkv_flat, out_flat, up_flat, down_flat, bias_flat, norm_flat = flats
    hidden = up_flat.shape[0] // model_width
    return (
        qkv_flat.reshape(model_width, 3 * model_width),
        out_flat.reshape(model_width, model_width),
        up_flat.reshape(model_width, hidden),
        down_flat.reshape(hidden, model_width),
        bias_flat.astype(jnp.float32),
        norm_flat.astype(jnp.float32),
    )


def norm_back(values, gain, shift, upstream):
    _, pullback = jax.vjp(layer_norm, values, gain, shift)
    return pullback(upstream)


def column_sum(matrix):
    return jnp.sum(matrix.astype(jnp.float32), axis=0)


def query_terms(
    query_heads,
    grad_heads,
    own_lse,
    own_delta,
    query_pos,
    query_flag,
    key_block,
    value_block,
    key_pos,
    factor,
):
    scores = (
        jnp.einsum("qhd,khd->hqk", query_heads, key_block, preferred_element_type=jnp.float32)
        * factor
    )
    allowed = visible(query_pos, query_flag, key_pos)[None]
    softmax_p = jnp.where(allowed, jnp.exp(scores - own_lse[:, :, None]), 0.0)
    dprobs = jnp.einsum("qhd,khd->hqk", grad_heads, value_block, preferred_element_type=jnp.float32)
    dscores = (softmax_p * (dprobs - own_delta[:, :, None])).astype(jnp.bfloat16)
    return (
        jnp.einsum("hqk,khd->hqd", dscores, key_block, preferred_element_type=jnp.float32) * factor
    )


def key_terms(
    query_block,
    grad_block,
    lse_block,
    delta_block,
    remote_pos,
    remote_flag,
    key_heads,
    value_heads,
    key_pos,
    factor,
):
    scores = (
        jnp.einsum("qhd,khd->hqk", query_block, key_heads, preferred_element_type=jnp.float32)
        * factor
    )
    allowed = visible(remote_pos, remote_flag, key_pos)[None]
    softmax_p = jnp.where(allowed, jnp.exp(scores - lse_block[:, :, None]), 0.0)
    dprobs = jnp.einsum("qhd,khd->hqk", grad_block, value_heads, preferred_element_type=jnp.float32)
    dscores = (softmax_p * (dprobs - delta_block[:, :, None])).astype(jnp.bfloat16)
    grad_keys = (
        jnp.einsum("hqk,qhd->hkd", dscores, query_block, preferred_element_type=jnp.float32)
        * factor
    )
    grad_values = jnp.einsum(
        "hqk,qhd->hkd",
        softmax_p.astype(jnp.bfloat16),
        grad_block,
        preferred_element_type=jnp.float32,
    )
    return (grad_keys, grad_values)


def general_device(
    tokens, piece_starts, qkv_weight, out_weight, up_weight, down_weight, biases, norms, cotangent
):
    model_width = tokens.shape[2]
    seq_rows = tokens.shape[1]
    params = unpack(
        (
            lax.all_gather(qkv_weight, ("dp", "ctx"), axis=0, tiled=True),
            lax.all_gather(out_weight, ("dp", "ctx"), axis=0, tiled=True),
            lax.all_gather(up_weight, ("dp", "ctx"), axis=0, tiled=True),
            lax.all_gather(down_weight, ("dp", "ctx"), axis=0, tiled=True),
            lax.all_gather(biases, ("dp", "ctx"), axis=0, tiled=True),
            lax.all_gather(norms, ("dp", "ctx"), axis=0, tiled=True),
        ),
        model_width,
    )
    qkv_mat, out_mat, up_mat, down_mat, bias_all, norm_all = params
    hidden = up_mat.shape[1]
    head_dim = model_width // HEADS
    factor = head_dim ** (-0.5)
    first_row = lax.axis_index("ctx") * seq_rows
    last_row = first_row + seq_rows - 1
    query_pos = first_row + jnp.arange(seq_rows, dtype=jnp.int32)
    starts_row = piece_starts[0]
    query_flag = piece_flags(query_pos, starts_row)
    bias_q = bias_all[:model_width]
    bias_v = bias_all[model_width : 2 * model_width]
    bias_o = bias_all[2 * model_width : 3 * model_width]
    bias_up = bias_all[3 * model_width : 3 * model_width + hidden]
    bias_down = bias_all[3 * model_width + hidden :]
    gain_one = norm_all[:model_width]
    shift_one = norm_all[model_width : 2 * model_width]
    gain_two = norm_all[2 * model_width : 3 * model_width]
    shift_two = norm_all[3 * model_width :]
    inputs = tokens[0].astype(jnp.float32)
    first_in = layer_norm(inputs, gain_one, shift_one).astype(jnp.bfloat16)
    projected = jnp.dot(first_in, qkv_mat, preferred_element_type=jnp.float32)
    queries = (projected[:, :model_width] + bias_q).astype(jnp.bfloat16)
    key_rows = projected[:, model_width : 2 * model_width].astype(jnp.bfloat16)
    value_rows = (projected[:, 2 * model_width :] + bias_v).astype(jnp.bfloat16)
    query_heads = queries.reshape(seq_rows, HEADS, head_dim)
    key_heads = key_rows.reshape(seq_rows, HEADS, head_dim)
    value_heads = value_rows.reshape(seq_rows, HEADS, head_dim)
    start_state = (
        jnp.full((HEADS, seq_rows), masked_score, jnp.float32),
        jnp.zeros((HEADS, seq_rows), jnp.float32),
        jnp.zeros((HEADS, seq_rows, head_dim), jnp.float32),
    )
    shard = (
        lax.all_gather(key_rows, "ctx", axis=0, tiled=True),
        lax.all_gather(value_rows, "ctx", axis=0, tiled=True),
    )
    shard_rows = shard[0].shape[0]
    block_len, block_count, (key_blocks, value_blocks) = to_blocks(shard, shard_rows)

    def forward_one_block(state, block_in):
        running_max, running_sum, running_acc = state
        key_block, value_block, position = block_in
        key_pos = position * block_len + jnp.arange(block_len, dtype=jnp.int32)
        scores = (
            jnp.einsum("qhd,khd->hqk", query_heads, key_block, preferred_element_type=jnp.float32)
            * factor
        )
        allowed = visible(query_pos, query_flag, key_pos)[None]
        scores = jnp.where(allowed, scores, masked_score)
        new_max = jnp.maximum(running_max, jnp.max(scores, axis=-1))
        correction = jnp.exp(running_max - new_max)
        exp_scores = jnp.where(allowed, jnp.exp(scores - new_max[:, :, None]), 0.0)
        running_sum = running_sum * correction + jnp.sum(exp_scores, axis=-1)
        running_acc = running_acc * correction[:, :, None] + jnp.einsum(
            "hqk,khd->hqd",
            exp_scores.astype(jnp.bfloat16),
            value_block,
            preferred_element_type=jnp.float32,
        )
        return ((new_max, running_sum, running_acc), None)

    def forward_compute(state):
        return lax.scan(
            forward_one_block,
            state,
            (key_blocks, value_blocks, jnp.arange(block_count, dtype=jnp.int32)),
        )[0]

    run_max, run_sum, run_acc = lax.cond(
        jnp.int32(0) <= last_row, forward_compute, keep_state, start_state
    )
    mixed_heads = run_acc / run_sum[:, :, None]
    mixed_f = jnp.transpose(mixed_heads, (1, 0, 2)).reshape(seq_rows, model_width)
    mixed_b = mixed_f.astype(jnp.bfloat16)
    log_sum = run_max + jnp.log(run_sum)
    after_attn = inputs + jnp.dot(mixed_b, out_mat, preferred_element_type=jnp.float32) + bias_o
    second_in = layer_norm(after_attn, gain_two, shift_two).astype(jnp.bfloat16)
    pre_act = jnp.dot(second_in, up_mat, preferred_element_type=jnp.float32) + bias_up
    activated = gelu_exact(pre_act).astype(jnp.bfloat16)
    result = (
        after_attn + jnp.dot(activated, down_mat, preferred_element_type=jnp.float32) + bias_down
    )
    output = result.astype(jnp.bfloat16)[None]
    back = unpack(
        (
            lax.all_gather(qkv_weight, ("dp", "ctx"), axis=0, tiled=True),
            lax.all_gather(out_weight, ("dp", "ctx"), axis=0, tiled=True),
            lax.all_gather(up_weight, ("dp", "ctx"), axis=0, tiled=True),
            lax.all_gather(down_weight, ("dp", "ctx"), axis=0, tiled=True),
            lax.all_gather(biases, ("dp", "ctx"), axis=0, tiled=True),
            lax.all_gather(norms, ("dp", "ctx"), axis=0, tiled=True),
        ),
        model_width,
    )
    qkv_back, out_back, up_back, down_back, bias_back, norm_vec = back
    gain_one_b = norm_vec[:model_width]
    shift_one_b = norm_vec[model_width : 2 * model_width]
    gain_two_b = norm_vec[2 * model_width : 3 * model_width]
    shift_two_b = norm_vec[3 * model_width :]
    upstream = cotangent[0].astype(jnp.float32)
    grad_mlp = upstream.astype(jnp.bfloat16)
    grad_down_loc = jnp.einsum("ta,tb->ab", activated, grad_mlp, preferred_element_type=jnp.float32)
    grad_act = jnp.einsum("tb,ab->ta", grad_mlp, down_back, preferred_element_type=jnp.float32)
    _, gelu_pull = jax.vjp(gelu_exact, pre_act)
    grad_pre = gelu_pull(grad_act)[0].astype(jnp.bfloat16)
    grad_up_loc = jnp.einsum("ta,tb->ab", second_in, grad_pre, preferred_element_type=jnp.float32)
    grad_second = jnp.einsum("tb,ab->ta", grad_pre, up_back, preferred_element_type=jnp.float32)
    grad_after_part, grad_gain_two, grad_shift_two = norm_back(
        after_attn, gain_two_b, shift_two_b, grad_second
    )
    grad_after = upstream + grad_after_part
    grad_attn = grad_after.astype(jnp.bfloat16)
    grad_out_loc = jnp.einsum("ta,tb->ab", mixed_b, grad_attn, preferred_element_type=jnp.float32)
    grad_mixed = jnp.einsum(
        "tb,ab->ta", grad_attn, out_back, preferred_element_type=jnp.float32
    ).astype(jnp.bfloat16)
    grad_heads = grad_mixed.reshape(seq_rows, HEADS, head_dim)
    delta_rows = jnp.sum(
        grad_heads.astype(jnp.float32) * mixed_f.reshape(seq_rows, HEADS, head_dim), axis=-1
    )
    delta_heads = delta_rows.T
    stats = jnp.concatenate([log_sum.T, delta_rows], axis=1)
    all_stats = lax.all_gather(stats, "ctx", axis=0, tiled=True)
    zero_heads = jnp.zeros((HEADS, seq_rows, head_dim), jnp.float32)
    shard = (
        lax.all_gather(key_rows, "ctx", axis=0, tiled=True),
        lax.all_gather(value_rows, "ctx", axis=0, tiled=True),
    )
    shard_rows = shard[0].shape[0]
    query_block_len, query_block_count, (query_key_blocks, query_value_blocks) = to_blocks(
        shard, shard_rows
    )

    def query_one_block(total, block_in):
        key_block, value_block, position = block_in
        key_pos = position * query_block_len + jnp.arange(query_block_len, dtype=jnp.int32)
        term = query_terms(
            query_heads,
            grad_heads,
            log_sum,
            delta_heads,
            query_pos,
            query_flag,
            key_block,
            value_block,
            key_pos,
            factor,
        )
        return (total + term, None)

    def query_compute(total):
        return lax.scan(
            query_one_block,
            total,
            (query_key_blocks, query_value_blocks, jnp.arange(query_block_count, dtype=jnp.int32)),
        )[0]

    grad_q = lax.cond(jnp.int32(0) <= last_row, query_compute, keep_state, zero_heads)
    shard = (
        lax.all_gather(queries, "ctx", axis=0, tiled=True),
        lax.all_gather(grad_mixed, "ctx", axis=0, tiled=True),
    )
    shard_rows = shard[0].shape[0]
    key_block_len, key_block_count, (query_blocks, grad_blocks) = to_blocks(shard, shard_rows)

    def key_one_block(totals, block_in):
        query_block, grad_block, position = block_in
        begin = position * key_block_len
        remote_pos = begin + jnp.arange(key_block_len, dtype=jnp.int32)
        remote_flag = piece_flags(remote_pos, starts_row)
        stats_block = lax.dynamic_slice_in_dim(all_stats, begin, key_block_len, 0)
        lse_block = stats_block[:, :HEADS].T
        delta_block = stats_block[:, HEADS:].T
        grad_keys, grad_values = key_terms(
            query_block,
            grad_block,
            lse_block,
            delta_block,
            remote_pos,
            remote_flag,
            key_heads,
            value_heads,
            query_pos,
            factor,
        )
        return ((totals[0] + grad_keys, totals[1] + grad_values), None)

    def key_compute(totals):
        return lax.scan(
            key_one_block,
            totals,
            (query_blocks, grad_blocks, jnp.arange(key_block_count, dtype=jnp.int32)),
        )[0]

    grad_k, grad_v = lax.cond(
        jnp.int32(0) + shard_rows - 1 >= first_row,
        key_compute,
        keep_state,
        (zero_heads, zero_heads),
    )

    def merge_heads(grad_part):
        return (
            jnp.transpose(grad_part, (1, 0, 2)).reshape(seq_rows, model_width).astype(jnp.bfloat16)
        )

    grad_qkv_rows = jnp.concatenate(
        [merge_heads(grad_q), merge_heads(grad_k), merge_heads(grad_v)], axis=1
    )
    grad_qkv_loc = jnp.einsum(
        "ta,tb->ab", first_in, grad_qkv_rows, preferred_element_type=jnp.float32
    )
    grad_first = jnp.einsum(
        "tb,ab->ta", grad_qkv_rows, qkv_back, preferred_element_type=jnp.float32
    )
    grad_in_part, grad_gain_one, grad_shift_one = norm_back(
        inputs, gain_one_b, shift_one_b, grad_first
    )
    grad_tokens = (grad_after + grad_in_part)[None]
    grad_bias_loc = jnp.concatenate(
        [
            column_sum(grad_qkv_rows[:, :model_width]),
            column_sum(grad_qkv_rows[:, 2 * model_width :]),
            column_sum(grad_attn),
            column_sum(grad_pre),
            column_sum(grad_mlp),
        ]
    )
    grad_norm_loc = jnp.concatenate([grad_gain_one, grad_shift_one, grad_gain_two, grad_shift_two])
    summed = (
        lax.psum_scatter(grad_qkv_loc.reshape(-1), ("dp", "ctx"), scatter_dimension=0, tiled=True),
        lax.psum_scatter(grad_out_loc.reshape(-1), ("dp", "ctx"), scatter_dimension=0, tiled=True),
        lax.psum_scatter(grad_up_loc.reshape(-1), ("dp", "ctx"), scatter_dimension=0, tiled=True),
        lax.psum_scatter(grad_down_loc.reshape(-1), ("dp", "ctx"), scatter_dimension=0, tiled=True),
        lax.psum_scatter(grad_bias_loc, ("dp", "ctx"), scatter_dimension=0, tiled=True),
        lax.psum_scatter(grad_norm_loc, ("dp", "ctx"), scatter_dimension=0, tiled=True),
    )
    return (output, grad_tokens, summed[0], summed[1], summed[2], summed[3], summed[4], summed[5])


MESH = pl.DeviceIdType.MESH
BF16 = jnp.bfloat16
F32 = jnp.float32
VMEM_SPEC = pl.BlockSpec(memory_space=pltpu.VMEM)
SMEM_SPEC = pl.BlockSpec(memory_space=pltpu.SMEM)
ANY_SPEC = pl.BlockSpec(memory_space=pl.ANY)
HALF = 64
NT = (((1,), (1,)), ((), ()))
TN = (((0,), (0,)), ((), ()))
VMEM_LIMIT = 60 << 20


def params(cid=None):
    if cid is None:
        return pltpu.CompilerParams(vmem_limit_bytes=VMEM_LIMIT)
    return pltpu.CompilerParams(
        collective_id=cid, has_side_effects=True, vmem_limit_bytes=VMEM_LIMIT
    )


def place():
    dp = lax.axis_index("dp")
    ctx = lax.axis_index("ctx")
    return dp // 2, dp % 2, ctx // 2, ctx % 2


def device(x, core, z, y):
    return (x * 2 + core, z * 2 + y)


def greet(peers):
    barrier = pltpu.get_barrier_semaphore()
    for peer in peers:
        pl.semaphore_signal(barrier, inc=1, device_id=peer, device_id_type=MESH)
    pl.semaphore_wait(barrier, len(peers))


def remote(src, dst, send, recv, peer):
    return pltpu.make_async_remote_copy(
        src_ref=src,
        dst_ref=dst,
        send_sem=send,
        recv_sem=recv,
        device_id=peer,
        device_id_type=MESH,
    )


def mm(a, b, dims=None):
    if dims is None:
        return jnp.dot(a, b, preferred_element_type=F32)
    return lax.dot_general(a, b, dims, preferred_element_type=F32)


def swap_halves(v):
    return jnp.concatenate([v[:, HALF:], v[:, :HALF]], axis=1)


def left_lanes(rows):
    return lax.broadcasted_iota(jnp.int32, (rows, 2 * HALF), 1) < HALF


def diagonal_mask(size, flags, first, transposed):
    row = lax.broadcasted_iota(jnp.int32, (size, size), 0)
    col = lax.broadcasted_iota(jnp.int32, (size, size), 1)
    key, query = (row, col) if transposed else (col, row)
    allowed = key <= query
    same = (key // PIECE) == (query // PIECE)
    for t in range(size // PIECE):
        inside = jnp.logical_and(same, (query // PIECE) == t)
        allowed = jnp.logical_or(allowed, jnp.logical_and(inside, flags[first + t] > 0))
    return allowed


def xor8(a, b):
    return (
        (a // 4 + b // 4) % 2 * 4 + (a // 2 % 2 + b // 2 % 2) % 2 * 2 + (a % 2 + b % 2) % 2
    )


def unflatten(flat_ref, stage, rows, groups):
    count = rows * groups
    stage[pl.ds(0, count), :] = flat_ref[...].astype(F32)
    return [stage[pl.ds(j, rows, stride=groups), :] for j in range(groups)]


def reduce_buffers(rows, width, wire):
    vmem = pltpu.VMEM
    return [
        vmem((2, 2, rows, width), wire),
        vmem((2, 2, rows, width), wire),
        vmem((2, 2, rows, width), wire),
        vmem((2, 2, rows, width), wire),
        vmem((2, 2, rows, width), wire),
        vmem((2, 2, rows, width), wire),
        vmem((4, rows, width), wire),
        vmem((3, rows, width), wire),
        vmem((4, rows, width), F32),
    ]


REDUCE_BUFFERS = 9
REDUCE_COPIES = 7


def reducer(acc, bufs, send, recv, first):
    to_wire_x, from_x, to_wire_y, from_y, to_two, from_two, to_three, from_three, total = bufs
    wire = to_wire_x.dtype
    x, core, z, y = place()
    ox, oy = 1 - x, 1 - y
    to_x = device(ox, core, z, y)
    to_y = device(x, core, z, oy)
    others = [(z + j) % 4 for j in range(1, 4)]

    def copies(stage):
        def make(n, src, dst, peer):
            return remote(src, dst, send.at[first + n], recv.at[first + n], peer)

        if stage == 1:
            return [make(0, to_wire_x, from_x, to_x), make(1, to_wire_y, from_y, to_y)]
        if stage == 2:
            return [
                make(2, to_two.at[0], from_two.at[0], to_y),
                make(3, to_two.at[1], from_two.at[1], to_x),
            ]
        return [
            make(4 + j, to_three.at[other], from_three.at[j], device(x, core, other, y))
            for j, other in enumerate(others)
        ]

    def launch(stage):
        if stage == 1:
            to_wire_x[...] = acc[ox, pl.ds(0, 2)].astype(wire)
            for n in range(2):
                to_wire_y[n] = acc[n, pl.ds(2, 2), oy].astype(wire)
        elif stage == 2:
            to_two[0] = (acc[x, pl.ds(0, 2), oy] + from_x[:, oy].astype(F32)).astype(wire)
            to_two[1] = (acc[ox, pl.ds(2, 2), y] + from_y[ox].astype(F32)).astype(wire)
        else:
            low = acc[x, pl.ds(0, 2), y] + from_x[:, y].astype(F32) + from_two[0].astype(F32)
            high = acc[x, pl.ds(2, 2), y] + from_y[x].astype(F32) + from_two[1].astype(F32)
            total[pl.ds(0, 2)] = low
            total[pl.ds(2, 2)] = high
            to_three[pl.ds(0, 2)] = low.astype(wire)
            to_three[pl.ds(2, 2)] = high.astype(wire)
        for copy in copies(stage):
            copy.start()

    def finish(stage):
        for copy in copies(stage):
            copy.wait()

    def result():
        value = total[z]
        for j in range(3):
            value = value + from_three[j].astype(F32)
        return value

    return launch, finish, result


def digits(values):
    return sum(v * 4**n for n, v in enumerate(values))


TILES = (
    (
        digits((0, 1, 1, 2, 2, 2, 3, 3, 3, 3)),
        digits((0, 1, 0, 0, 1, 2, 0, 1, 2, 3)),
        digits((1, 0, 1, 0, 0, 1, 0, 0, 0, 1)),
    ),
    (
        digits((2, 3, 3, 2, 3, 0, 2, 3, 1, 1)),
        digits((2, 3, 2, 0, 0, 0, 1, 1, 0, 1)),
        digits((0, 0, 0, 0, 0, 1, 1, 1, 0, 1)),
    ),
)


def forward_phase(r):
    flags = r.flags
    tokens = r.tokens
    qkv_flat = r.qkv_flat
    out_flat = r.out_flat
    up_flat = r.up_flat
    down_flat = r.down_flat
    a1_ref = r.a1
    got = r.got
    mix = r.mix
    o_ref = r.o_heads
    lse_ref = r.lse
    vec_ref = r.vec
    qkv_all = r.qkv_all
    ou_all = r.ou_all
    down_all = r.down_all
    stage = r.stage
    qkv_own = r.qkv_own
    ou_own = r.ou_own
    down_own = r.down_own
    norm_s = r.n2_s
    packed = r.packed
    q_s = r.q_s
    k_s = r.k_s
    v_s = r.v_s
    m_s = r.m_s
    acc_s = r.acc_s
    o2_s = r.o2_s
    g_own = r.g_own
    g_send = r.g_send
    g_recv = r.g_recv
    f_send = r.f_send
    f_recv = r.f_recv
    x_send = r.x_send
    x_recv = r.x_recv
    o_send = r.o_send
    o_recv = r.o_recv
    x, core, z, y = place()
    ox, oc, oy = 1 - x, 1 - core, 1 - y
    me = z * 2 + y
    width = tokens.shape[1]
    rows = tokens.shape[0]
    half = rows // 2
    tile = 2 * rows
    groups = width // 128
    group = 3 * width // 2
    scale = math.log2(math.e) * HALF**-0.5
    left = left_lanes(rows)
    left_half = left_lanes(half)
    to_x = device(ox, core, z, y)
    to_y = device(x, core, z, oy)
    to_core = device(x, oc, z, y)
    others = [(z + j) % 4 for j in range(1, 4)]

    qkv = unflatten(qkv_flat, stage, 16, 3 * groups)
    left16 = left_lanes(16)
    for j in range(groups):
        k_pair, v_pair = qkv[groups + j], qkv[2 * groups + j]
        own = qkv_own.at[j // 2]
        at = (j % 2) * 128
        own[:, at : at + 128] = qkv[j].astype(BF16)
        at = 256 + (j % 2) * 256
        own[:, at : at + 128] = jnp.where(left16, k_pair, swap_halves(v_pair)).astype(BF16)
        at += 128
        own[:, at : at + 128] = jnp.where(left16, swap_halves(k_pair), v_pair).astype(BF16)
    norm_row = jnp.concatenate(
        [r.norms[...].astype(F32), jnp.zeros((1, 128 - r.norms.shape[1]), F32)], axis=1
    )
    block = jnp.concatenate(
        [r.biases[...].astype(F32), norm_row, jnp.zeros((14, 128), F32)], axis=0
    )
    for g in range(2):
        qkv_own[g, :, group:] = block.astype(BF16)
    for t in range(flags.shape[0]):
        found = jnp.int32(0)
        for j in range(r.starts.shape[1]):
            found = found + (r.starts[0, j] == t * PIECE).astype(jnp.int32)
        flags[t] = found
    greet(
        [device(x, core, (z + c) % 4, (y + d) % 2) for c in range(4) for d in range(2)][1:]
        + [to_x, to_core]
    )
    arrays = ((qkv_own, qkv_all), (ou_own, ou_all), (down_own, down_all))

    def moves(phase, a):
        own, full = arrays[a]
        if phase == 1:
            mine = full.at[x, core, z, y]
            return [(own, mine, device(x, core, o, y), j) for j, o in enumerate(others)]
        if phase == 2:
            part = full.at[x, core, :, y]
            return [(part, part, to_x, 3), (part, part, to_y, 4), (part, part, to_core, 5)]
        if phase == 3:
            low = full.at[x, core, pl.ds(0, 2), oy]
            high = full.at[ox, core, pl.ds(2, 2), y]
            from_x = full.at[ox, core, :, y]
            from_y = full.at[x, core, :, oy]
            return [
                (low, low, to_x, 6),
                (high, high, to_y, 7),
                (from_x, from_x, to_core, 8),
                (from_y, from_y, to_core, 9),
            ]
        part = full.at[ox, core, :, oy]
        return [(part, part, to_core, 10)]

    def phase_copies(phase, a):
        copies = [
            remote(src, dst, g_send.at[a * 11 + n], g_recv.at[a * 11 + n], peer)
            for src, dst, peer, n in moves(phase, a)
        ]
        if phase == 1:
            own, full = arrays[a]
            copies.append(pltpu.make_async_copy(own, full.at[x, core, z, y], g_own.at[a]))
        return copies

    def launch(phase, a):
        for copy in phase_copies(phase, a):
            copy.start()

    def finish(phase, a):
        for copy in phase_copies(phase, a):
            copy.wait()

    hz = z // 2

    def picked(position, half_z):
        return half_z * (1 - position) + (1 - half_z) * position

    def hop(src, dst, peer, g, n):
        return remote(src, dst, f_send.at[20 * g + n], f_recv.at[20 * g + n], peer)

    def to_xy(g, c):
        part = qkv_all.at[g, x, core, c, y]
        return hop(part, part, to_x, g, 4 + c), hop(part, part, to_y, g, 8 + c)

    def corner(g, c, over_x):
        if over_x:
            part = qkv_all.at[g, x, core, c, oy]
            return hop(part, part, to_x, g, 12 + c)
        part = qkv_all.at[g, ox, core, c, y]
        return hop(part, part, to_y, g, 12 + c)

    def to_sibling(g, n):
        part = (
            qkv_all.at[g, x, core, :, y],
            qkv_all.at[g, ox, core, :, y],
            qkv_all.at[g, x, core, :, oy],
            qkv_all.at[g, ox, core, :, oy],
        )[n]
        return hop(part, part, to_core, g, 16 + n)

    def along(g, n):
        return hop(
            qkv_own.at[g], qkv_all.at[g, x, core, z, y], device(x, core, others[n], y), g, n
        )

    own_first = pltpu.make_async_copy(qkv_own, qkv_all.at[:, x, core, z, y], g_own.at[0])
    own_first.start()
    for position in range(2):
        for n, other in enumerate(others):
            along(picked(position, other // 2), n).start()
        g = picked(position, hz)
        own = qkv_all.at[g, x, core, z, y]
        hop(qkv_own.at[g], own, to_x, g, 4 + z).start()
        hop(qkv_own.at[g], own, to_y, g, 8 + z).start()
    out_parts = unflatten(out_flat, stage, 16, groups)
    for j in range(groups):
        ou_own[:, 128 * j : 128 * (j + 1)] = out_parts[j].astype(BF16)
    up_groups = up_flat.shape[0] // 16
    up_parts = unflatten(up_flat, stage, 16, up_groups)
    for j in range(up_groups):
        at = width + 128 * j
        ou_own[:, at : at + 128] = up_parts[j].astype(BF16)
    down_rows = down_flat.shape[0] // groups
    down_parts = unflatten(down_flat, stage, down_rows, groups)
    for j in range(groups):
        down_own[:, 128 * j : 128 * (j + 1)] = down_parts[j].astype(BF16)
    launch(1, 1)
    launch(1, 2)
    own_first.wait()
    one, two = picked(0, hz), picked(1, hz)
    for g in (one, two):
        for n in range(3):
            along(g, n).wait_recv()
            for copy in to_xy(g, (z + 3 - n) % 4):
                copy.start()
        to_sibling(g, 0).start()
    value = tokens[...].astype(F32)
    center = jnp.mean(value, axis=1, keepdims=True)
    offset = value - center
    spread = jnp.mean(offset * offset, axis=1, keepdims=True)
    norm_s[...] = offset * lax.rsqrt(spread + eps_norm)

    def meet(g):
        for c in [z] + others:
            over_x, over_y = to_xy(g, c)
            over_x.wait_recv()
            over_y.wait_recv()

            @pl.when(c < 2)
            def _():
                corner(g, c, True).start()

            @pl.when(c >= 2)
            def _():
                corner(g, c, False).start()

        to_sibling(g, 1).start()
        to_sibling(g, 2).start()

    def turn(g):
        for c in range(4):
            corner(g, c, c < 2).wait()
        to_sibling(g, 3).start()

    def close(g):
        for n in range(4):
            to_sibling(g, n).wait()

    meet(one)
    meet(two)
    turn(one)
    turn(two)
    close(one)

    vec_ref[...] = jnp.zeros_like(vec_ref)
    devices = [(a, b, c, d) for a in range(2) for b in range(2) for c in range(4) for d in range(2)]
    base = 128 * len(devices)

    def bias_rows(begin, end):
        for n in range(begin, end):
            piece = qkv_all[(one,) + devices[n] + (slice(None), pl.ds(group, 128))].astype(F32)
            vec_ref[0:1, 128 * n : 128 * (n + 1)] = piece[0:1]

    def norm_rows(begin, end):
        for n in range(begin, end):
            pair = [
                qkv_all[(one,) + devices[2 * n + d] + (slice(None), pl.ds(group, 128))].astype(F32)
                for d in range(2)
            ]
            joined = jnp.concatenate([pair[0][1:2, :HALF], pair[1][1:2, :HALF]], axis=1)
            vec_ref[0:1, base + 128 * n : base + 128 * (n + 1)] = joined

    bias_rows(0, 2 * groups)
    norm_rows(0, 2 * groups)
    gain = vec_ref[0:1, base : base + width]
    shift = vec_ref[0:1, base + width : base + 2 * width]
    a1_ref[...] = (norm_s[...] * gain + shift).astype(BF16)

    def part_of(is_query):
        return pl.ds(rows, half) if is_query else pl.ds(0, rows)

    def send_part(tz, mark, is_query):
        for step in range(2):
            ty = (y + step) % 2
            index = mark + step
            src = packed.at[2 * tz + ty, part_of(is_query)]
            dst = got.at[me, part_of(is_query)]
            n = index + 8 * is_query
            if index == 0:
                pltpu.make_async_copy(src, dst, x_recv.at[n]).start()
            else:
                remote(src, dst, x_send.at[n], x_recv.at[n], device(x, core, tz, ty)).start()

    order = (
        hz * 2 + 1 - z % 2,
        z,
        (1 - hz) * 2 + z % 2,
        (1 - hz) * 2 + 1 - z % 2,
    )
    marks = (2, 0, 4, 6)
    left1 = left_lanes(1)
    for place_of, (tz, mark) in enumerate(zip(order, marks)):
        if place_of == 2:
            close(two)
        g = one if place_of < 2 else two
        a1 = a1_ref[...]
        at = pl.multiple_of(tz % 2 * 128, 128)
        w_q = qkv_all[g, :, :, :, :, :, pl.ds(at, 128)].reshape(width, 128)
        q = (mm(a1, w_q) + vec_ref[0:1, pl.ds(pl.multiple_of(128 * tz, 128), 128)]).astype(BF16)
        at_kv = pl.multiple_of(256 + tz % 2 * 256, 128)
        w_kv = qkv_all[g, :, :, :, :, :, pl.ds(at_kv, 256)].reshape(width, 256)
        bias = vec_ref[0:1, pl.ds(pl.multiple_of(width + 128 * tz, 128), 128)]
        kv = mm(a1, w_kv)
        even = kv[:, :128] + jnp.where(left1, 0.0, swap_halves(bias))
        odd = kv[:, 128:] + jnp.where(left1, 0.0, bias)
        packed[2 * tz, :rows] = even.astype(BF16)
        packed[2 * tz + 1, :rows] = odd.astype(BF16)
        top, low = q[:half], q[half:]
        packed[2 * tz, rows:] = jnp.where(left_half, top, swap_halves(low))
        packed[2 * tz + 1, rows:] = jnp.where(left_half, swap_halves(top), low)
        if mark < 4:
            send_part(tz, mark, False)
            send_part(tz, mark, True)

    def send_cross():
        def send_all(is_query):
            for tz, mark in zip(order[2:], marks[2:]):
                send_part(tz, mark, is_query)

        pl.when(hz == 1)(lambda: send_all(True))
        send_all(False)
        pl.when(hz == 0)(lambda: send_all(True))

    send_cross()
    finish(1, 1)
    finish(1, 2)
    launch(2, 1)
    launch(2, 2)
    bias_rows(2 * groups, len(devices))
    norm_rows(2 * groups, len(devices) // 2)

    def block_wait(sems, index, view):
        pltpu.make_async_copy(view, view, sems.at[index]).wait()

    def arrive(part, is_query):
        for t in range(2):
            b = 2 * part + t
            block_wait(x_recv, xor8(b, me) + 8 * is_query, got.at[b, part_of(is_query)])
            at = pl.multiple_of(b * rows, rows)
            if is_query:
                both = got[b, rows:]
                q_s[pl.ds(at, half), :] = jnp.where(left_half, both, 0).astype(BF16)
                q_s[pl.ds(at + half, half), :] = jnp.where(
                    left_half, swap_halves(both), 0
                ).astype(BF16)
            else:
                pair = got[b, :rows]
                k_s[pl.ds(at, rows), :] = jnp.where(left, pair, 0).astype(BF16)
                v_s[pl.ds(at, rows), :] = jnp.where(left, 1, pair).astype(BF16)

    low = 1 - hz
    queries = low * TILES[0][0] + hz * TILES[1][0]
    keys = low * TILES[0][1] + hz * TILES[1][1]
    ends = low * TILES[0][2] + hz * TILES[1][2]
    m_s[...] = jnp.full(m_s.shape, masked_score, F32)
    acc_s[...] = jnp.zeros(acc_s.shape, F32)
    for n in range(2):
        arrive(2 * hz + n, False)
        arrive(2 * hz + n, True)

    def step(n, carry):
        q_left, k_left, e_left = carry
        i, j, done = q_left % 4, k_left % 4, e_left % 4

        @pl.when(n == 3)
        def _():
            for a in (1, 2):
                finish(2, a)
                launch(3, a)

        @pl.when(n == 6)
        def _():
            for a in (1, 2):
                finish(3, a)
                launch(4, a)

        for when, part, is_query in ((3, 2, 1), (5, 2, 0), (6, 3, 1), (9, 3, 0)):
            pl.when(n == when + 16 * hz)(lambda: arrive(part, is_query))
        for when, part, is_query in ((3, 0, 0), (5, 0, 1), (6, 1, 0), (8, 1, 1)):
            pl.when(n == when + 16 * low)(lambda: arrive(part, is_query))

        at = pl.multiple_of(i * tile, tile)
        begin = pl.multiple_of(j * tile, tile)

        def update(diagonal):
            s = mm(q_s[pl.ds(at, tile), :], k_s[pl.ds(begin, tile), :], NT)
            if diagonal:
                allowed = diagonal_mask(tile, flags, i * (tile // PIECE), False)
                s = jnp.where(allowed, s, masked_score)
            old = m_s[pl.ds(at, tile), :]
            new = jnp.maximum(old, jnp.max(s, axis=1, keepdims=True) * scale)
            p = jnp.exp2(s * scale - new[:, :1])
            m_s[pl.ds(at, tile), :] = new
            acc_s[pl.ds(at, tile), :] = acc_s[pl.ds(at, tile), :] * jnp.exp2(old - new) + mm(
                p.astype(BF16), v_s[pl.ds(begin, tile), :]
            )

        pl.when(i == j)(lambda: update(True))
        pl.when(i != j)(lambda: update(False))

        @pl.when(done == 1)
        def _():
            acc = acc_s[pl.ds(at, tile), :]
            total = jnp.broadcast_to(acc[:, :1], acc.shape)
            o = acc / total
            o_ref[pl.ds(at, tile), :] = o
            lse = m_s[pl.ds(at, tile), :] + jnp.log2(total)
            lse_ref[:, pl.ds(at, tile)] = jnp.transpose(lse)[:8]
            for t in range(2):
                b = 2 * i + t
                top = o[t * rows : t * rows + half]
                bottom = o[t * rows + half : (t + 1) * rows]
                o2_s[b] = jnp.where(left_half, swap_halves(top), bottom).astype(BF16)
                index = xor8(b, me)

                @pl.when(b == me)
                def _():
                    pltpu.make_async_copy(o2_s.at[b], mix.at[me], o_recv.at[0]).start()

                @pl.when(b != me)
                def _():
                    remote(
                        o2_s.at[b],
                        mix.at[me],
                        o_send.at[index],
                        o_recv.at[index],
                        device(x, core, i, t),
                    ).start()

        return q_left // 4, k_left // 4, e_left // 4

    lax.fori_loop(0, 10, step, (queries, keys, ends))
    for a in (1, 2):
        finish(4, a)
    for g in range(2):
        for n in range(3):
            along(g, n).wait_send()
        for c in range(4):
            for copy in to_xy(g, c):
                copy.wait_send()
    for index in range(8):
        block_wait(o_recv, index, mix.at[0])
        if index:
            block_wait(x_send, index, packed.at[0, part_of(False)])
            block_wait(x_send, index + 8, packed.at[0, part_of(True)])
            block_wait(o_send, index, o2_s.at[0])


def middle_phase(r):
    tokens = r.tokens
    cot = r.cot
    mix = r.mix
    vec = r.vec
    ou_all = r.ou_all
    down_all = r.down_all
    out_ref = r.out_ref
    dx_ref = r.n2_s
    do2_ref = r.do2
    acc_ou = r.acc_ou
    acc_down = r.acc_down
    sums_ref = r.sums
    o_s = r.o_s
    x1_s = r.x1_s
    n2_s = r.n2_s
    a2_s = r.a2_s
    gl_s = r.gl_s
    du_s = r.du_s
    dh_s = r.dh_s
    da_s = r.da_s
    r_s = r.r_s
    send2 = r.o2_s
    core_ou = r.core_ou
    core_down = r.core_down
    got_ou = r.got_ou
    got_down = r.got_down
    x_send = r.d_send
    x_recv = r.d_recv
    c_send = r.c_send
    c_recv = r.c_recv
    x, core, z, y = place()
    oc, oy = 1 - core, 1 - y
    me = z * 2 + y
    rows, width = tokens.shape
    half = rows // 2
    hidden = ou_all.shape[-1] - width
    left_half = left_lanes(half)
    to_core = device(x, oc, z, y)
    bias_o = vec[0:1, 2 * width : 3 * width]
    bias_down = vec[0:1, 3 * width + hidden : 4 * width + hidden]
    base = 4 * width + hidden
    gain = vec[0:1, base + 2 * width : base + 3 * width]
    shift = vec[0:1, base + 3 * width : base + 4 * width]

    for j in range(HEADS // 2):
        even, odd = mix[2 * j], mix[2 * j + 1]
        at = 128 * j
        o_s[:half, at : at + 128] = jnp.where(left_half, even, swap_halves(odd))
        o_s[half:, at : at + 128] = jnp.where(left_half, swap_halves(even), odd)
    w_out = ou_all[:, :, :, :, :, :width].reshape(width, width)
    x1 = tokens[...].astype(F32) + mm(o_s[...], w_out) + bias_o
    x1_s[...] = x1
    center = jnp.mean(x1, axis=1, keepdims=True)
    offset = x1 - center
    spread = jnp.mean(offset * offset, axis=1, keepdims=True)
    inverse = lax.rsqrt(spread + eps_norm)
    r_s[...] = jnp.broadcast_to(inverse, r_s.shape)
    n2 = offset * inverse
    n2_s[...] = n2
    a2_s[...] = (n2 * gain + shift).astype(BF16)
    sums_ref[...] = jnp.zeros_like(sums_ref)

    @pl.loop(0, hidden // width, unroll=True)
    def _(j):
        at = pl.multiple_of(j * width, width)
        w_up = ou_all[:, :, :, :, :, pl.ds(pl.multiple_of(width + at, width), width)].reshape(
            width, width
        )
        b_up = vec[0:1, pl.ds(pl.multiple_of(3 * width + at, width), width)]
        w_down = down_all[j // 2, j % 2].reshape(width, width)
        u = mm(a2_s[...], w_up) + b_up
        phi = 0.5 * (1.0 + lax.erf(u * (0.5**0.5)))
        slope = phi + u * jnp.exp(-0.5 * u * u) * (1.0 / math.sqrt(2.0 * math.pi))
        gl_s[:, pl.ds(at, width)] = (u * phi).astype(BF16)
        grad = mm(cot[...], w_down, NT)
        du = (grad * slope).astype(BF16)
        du_s[:, pl.ds(at, width)] = du
        sums_ref[0:1, pl.ds(pl.multiple_of(3 * width + at, width), width)] = jnp.sum(
            du.astype(F32), axis=0, keepdims=True
        )
        part = mm(du, w_up, NT)

        @pl.when(j == 0)
        def _():
            dh_s[...] = part

        @pl.when(j > 0)
        def _():
            dh_s[...] += part

    dh2 = dh_s[...]
    n2 = n2_s[...]
    sums_ref[0:1, base + 2 * width : base + 3 * width] = jnp.sum(dh2 * n2, axis=0, keepdims=True)
    sums_ref[0:1, base + 3 * width : base + 4 * width] = jnp.sum(dh2, axis=0, keepdims=True)
    e = dh2 * gain
    mean_e = jnp.mean(e, axis=1, keepdims=True)
    mean_en = jnp.mean(e * n2, axis=1, keepdims=True)
    dx = cot[...].astype(F32) + r_s[:, :1] * (e - mean_e - n2 * mean_en)
    dx_ref[...] = dx
    da = dx.astype(BF16)
    da_s[...] = da
    w_out = ou_all[:, :, :, :, :, :width].reshape(width, width)
    grad_o = mm(da, w_out, NT).astype(BF16)
    for j in range(HEADS // 2):
        group = grad_o[:, 128 * j : 128 * (j + 1)]
        top, low = group[:half], group[half:]
        send2[2 * j] = jnp.where(left_half, top, swap_halves(low))
        send2[2 * j + 1] = jnp.where(left_half, swap_halves(top), low)
    hz = z // 2
    order = (hz * 2 + 1 - z % 2, z, (1 - hz) * 2 + z % 2, (1 - hz) * 2 + 1 - z % 2)
    for tz, mark in zip(order, (2, 0, 4, 6)):
        for step in range(2):
            ty = (y + step) % 2
            index = mark + step
            src = send2.at[2 * tz + ty]
            if index == 0:
                pltpu.make_async_copy(src, do2_ref.at[me], x_recv.at[0]).start()
            else:
                remote(
                    src,
                    do2_ref.at[me],
                    x_send.at[index],
                    x_recv.at[index],
                    device(x, core, tz, ty),
                ).start()

    def grads(c, n):
        dp = 2 * n + c
        at = pl.multiple_of(dp * 128, 128)
        down_at = pl.multiple_of(dp * width, width)
        d_down = mm(gl_s[:, pl.ds(down_at, width)], cot[...], TN)
        d_up = mm(a2_s[:, pl.ds(at, 128)], du_s[...], TN)
        d_out = mm(o_s[:, pl.ds(at, 128)], da_s[...], TN)
        return (
            d_down.reshape(4, 2, width // 8, width),
            d_up.reshape(4, 2, 16, hidden),
            d_out.reshape(4, 2, 16, width),
        )

    for n in range(2):
        d_down, d_up, d_out = grads(oc, n)
        core_down[n] = d_down.astype(BF16)
        core_ou[n, :, :, :, width:] = d_up.astype(BF16)
        core_ou[n, :, :, :, :width] = d_out.astype(BF16)
    to_ou = remote(core_ou, got_ou, c_send.at[0], c_recv.at[0], to_core)
    to_down = remote(core_down, got_down, c_send.at[1], c_recv.at[1], to_core)
    to_ou.start()
    to_down.start()
    sums_ref[0:1, 2 * width : 3 * width] = jnp.sum(da_s[...].astype(F32), axis=0, keepdims=True)
    sums_ref[0:1, 3 * width + hidden : 4 * width + hidden] = jnp.sum(
        cot[...].astype(F32), axis=0, keepdims=True
    )
    result = x1_s[...] + mm(gl_s[...], down_all[...].reshape(hidden, width)) + bias_down
    out_ref[...] = result.astype(BF16)
    for n in range(2):
        d_down, d_up, d_out = grads(core, n)
        acc_down[n] = d_down
        acc_ou[n, :, :, :, width:] = d_up
        acc_ou[n, :, :, :, :width] = d_out
    to_ou.wait()
    to_down.wait()
    acc_ou[...] += got_ou[...].astype(F32)
    acc_down[...] += got_down[...].astype(F32)


def lanes_of(ref, r, g):
    group = r.tokens.shape[1] * 3 // 2
    return ref.at[:, :, :, :, pl.ds(pl.multiple_of(g * group, 128), group)]


def reducer_of(r, name, first, at=None):
    bufs = [getattr(r, f"{name}{n}") for n in range(REDUCE_BUFFERS)]
    if at is not None:
        return reducer(lanes_of(r.acc_ou, r, at), [b.at[at] for b in bufs], r.r_send, r.r_recv, first)
    acc = getattr(r, f"acc_{name}")
    return reducer(acc, bufs, r.r_send, r.r_recv, first)


def backward_phase(r):
    got, do2, o_heads, lse, grads, packed = r.got, r.do2, r.o_heads, r.lse, r.grads, r.packed
    qd_s, k_s, v_s, delta_s, dq_s, dkv_s = r.q_s, r.k_s, r.v_s, r.delta_s, r.acc_s, r.m_s
    flags = r.flags
    x, core, z, y = place()
    me = z * 2 + y
    hz = z // 2
    low = 1 - hz
    blocks = got.shape[0]
    rows = got.shape[1] // 3 * 2
    half = rows // 2
    quarter = blocks // 2
    scale = math.log2(math.e) * HALF**-0.5
    factor = HALF**-0.5
    left = left_lanes(rows)
    left_half = left_lanes(half)
    sums = (reducer_of(r, "ou", 0), reducer_of(r, "down", REDUCE_COPIES))
    for launch, _, _ in sums:
        launch(1)

    def enter(b):
        at = pl.multiple_of(b * rows, rows)
        pltpu.make_async_copy(do2.at[b], do2.at[b], r.d_recv.at[xor8(b, me)]).wait()
        v_s[pl.ds(at, rows), :] = jnp.where(left, 0, v_s[pl.ds(at, rows), :]).astype(BF16)
        grad = do2[b]
        for part, begin in ((swap_halves(grad), 0), (grad, half)):
            rows_at = pl.ds(at + begin, half)
            qd_s[rows_at, :] = jnp.where(left_half, qd_s[rows_at, :], part)
            product = jnp.where(left_half, 0.0, part.astype(F32) * o_heads[rows_at, :])
            delta = jnp.sum(jnp.transpose(product), axis=0, keepdims=True)
            delta_s[:, rows_at] = jnp.broadcast_to(delta, (8, half))
        dq_s[pl.ds(at, rows), :] = jnp.zeros((rows, 2 * HALF), F32)
        dkv_s[pl.ds(at, rows), :] = jnp.zeros((rows, 2 * HALF), F32)

    def tile(kj, qi, diagonal):
        k0 = pl.multiple_of(kj * rows, rows)
        q0 = pl.multiple_of(qi * rows, rows)
        k = k_s[pl.ds(k0, rows), :]
        v = v_s[pl.ds(k0, rows), :]
        qd = qd_s[pl.ds(q0, rows), :]
        scores = mm(k, qd, NT)
        dprobs = mm(v, qd, NT)
        p = jnp.exp2(scores * scale - lse[:1, pl.ds(q0, rows)])
        if diagonal:
            allowed = diagonal_mask(rows, flags, kj * (rows // PIECE), True)
            p = jnp.where(allowed, p, 0.0)
        ds = (p * (dprobs - delta_s[:1, pl.ds(q0, rows)])).astype(BF16)
        dkv_s[pl.ds(k0, rows), :] += jnp.where(left, mm(ds, qd), mm(p.astype(BF16), qd))
        dq_s[pl.ds(q0, rows), :] += mm(ds, k, TN)

    def part_of(is_query):
        return pl.ds(rows, half) if is_query else pl.ds(0, rows)

    def leave(a, is_query):
        at = pl.multiple_of(a * rows, rows)
        if is_query:
            top = dq_s[pl.ds(at, half), :]
            bottom = dq_s[pl.ds(at + half, half), :]
            packed[a, rows:] = (
                jnp.where(left_half, top, swap_halves(bottom)) * factor
            ).astype(BF16)
        else:
            block = dkv_s[pl.ds(at, rows), :]
            packed[a, :rows] = jnp.where(left, block * factor, block).astype(BF16)
        index = xor8(a, me) + 8 * is_query
        src = packed.at[a, part_of(is_query)]
        dst = grads.at[me, part_of(is_query)]

        @pl.when(a == me)
        def _():
            pltpu.make_async_copy(src, dst, r.b_recv.at[index]).start()

        @pl.when(a != me)
        def _():
            remote(
                src, dst, r.b_send.at[index], r.b_recv.at[index], device(x, core, a // 2, a % 2)
            ).start()

    for n in range(quarter):
        enter(hz * quarter + n)

    @pl.loop(0, 12)
    def _(row):
        seg = (row + 3) // 4
        last = seg // 3
        first = (3 - seg) // 3
        square = seg // 2 - last
        cross = seg % 2 - last
        own = first + last
        i = (row + 3) % 4 + last - 3 * first

        @pl.when(row == 6)
        def _():
            for _, finish, _ in sums:
                finish(1)
            for launch, _, _ in sums:
                launch(2)

        a_low = own * (3 - i) + (1 - own) * (7 - i)
        a_high = own * (4 + i) + (1 - own) * i
        a = low * a_low + hz * a_high
        count = own * (3 - i) + cross * i + square * 4

        @pl.when(cross == 1)
        def _():
            enter(a)


        @pl.when(square == 0)
        def _():
            tile(a, a, True)

        @pl.loop(0, count)
        def _(u):
            k_low = (own + square) * u + cross * a_low
            q_low = (own + square) * a_low + cross * (7 - u)
            k_high = (own + square) * a_high + cross * u
            q_high = own * (5 + i + u) + cross * a_high + square * (4 + u)
            tile(low * k_low + hz * k_high, low * q_low + hz * q_high, False)

        @pl.when(cross * hz + square * low + last > 0)
        def _():
            leave(a, 1)

        @pl.when(cross * low + square * hz + last > 0)
        def _():
            leave(a, 0)

        @pl.when(row == 8)
        def _():
            begin = low * 3 + hz * 4
            leave(begin, 1)
            leave(begin, 0)


def last_phase(r):
    grads, a1, tokens, dx, qkv_all, vec, sums = (
        r.grads,
        r.a1,
        r.tokens,
        r.n2_s,
        r.qkv_all,
        r.vec,
        r.sums,
    )
    dqkv_s, got_q = r.gl_s, r.got_q
    core_small, got_small, acc_small = r.core_small, r.got_small, r.acc_small
    x, core, z, y = place()
    me = z * 2 + y
    hz = z // 2
    oc = 1 - core
    to_core = device(x, oc, z, y)
    rows, width = tokens.shape
    half = rows // 2
    group = 3 * width // 2
    left_half = left_lanes(half)
    left1 = left_lanes(1)
    base = vec.shape[1] - 4 * width

    def columns_of(g):
        return pl.ds(pl.multiple_of(g * group, 128), group)

    def enter(g):
        for n in range(HEADS // 2):
            h = g * (HEADS // 2) + n
            for is_query in range(2):
                view = grads.at[h, pl.ds(rows, half) if is_query else pl.ds(0, rows)]
                pltpu.make_async_copy(view, view, r.b_recv.at[xor8(h, me) + 8 * is_query]).wait()
        begin = g * group
        for j in range(HEADS // 4):
            h = g * (HEADS // 2) + 2 * j
            even, odd = grads[h, rows:], grads[h + 1, rows:]
            at = pl.ds(pl.multiple_of(begin + 128 * j, 128), 128)
            dqkv_s[:half, at] = jnp.where(left_half, even, swap_halves(odd))
            dqkv_s[half:, at] = jnp.where(left_half, swap_halves(even), odd)
        for n in range(HEADS // 2):
            at = pl.ds(pl.multiple_of(begin + 256 + 128 * n, 128), 128)
            dqkv_s[:, at] = grads[g * (HEADS // 2) + n, :rows]

    def weight_grad(c, n, g):
        at = pl.multiple_of((2 * n + c) * 128, 128)
        return mm(a1[:, pl.ds(at, 128)], dqkv_s[:, columns_of(g)], TN).reshape(4, 2, 16, group)

    def over(g):
        return remote(lanes_of(r.core_ou, r, g), got_q.at[g], r.e_send.at[g], r.e_recv.at[g], to_core)

    parts = []
    for position, g in enumerate((1 - hz, hz)):
        enter(g)
        if position == 0:
            for early in (reducer_of(r, "ou", 0), reducer_of(r, "down", REDUCE_COPIES)):
                early[1](2)
                early[0](3)
        for n in range(2):
            lanes_of(r.core_ou, r, g)[n] = weight_grad(oc, n, g).astype(BF16)
        over(g).start()
        w = qkv_all[g, :, :, :, :, :, :group].reshape(width, group)
        part = mm(dqkv_s[:, columns_of(g)], w, NT)
        if position:
            r.dh_s[...] += part
        else:
            r.dh_s[...] = part
        for n in range(2):
            lanes_of(r.acc_ou, r, g)[n] = weight_grad(core, n, g)
        over(g).wait()
        acc_q = lanes_of(r.acc_ou, r, g)
        acc_q[...] = acc_q[...] + got_q[g].astype(F32)
        parts.append(reducer_of(r, "q", (2 + g) * REDUCE_COPIES, g))
        parts[-1][0](1)

    columns = jnp.sum(dqkv_s[:, : 3 * width].astype(F32), axis=0, keepdims=True)
    for j in range(HEADS // 2):
        at = (j // 2) * group + (j % 2) * 128
        sums[0:1, 128 * j : 128 * (j + 1)] = columns[:, at : at + 128]
        at = (j // 2) * group + 256 + (j % 2) * 256
        pair = jnp.where(
            left1, swap_halves(columns[:, at : at + 128]), columns[:, at + 128 : at + 256]
        )
        sums[0:1, width + 128 * j : width + 128 * (j + 1)] = pair
    dh = r.dh_s[...]
    gain = vec[0:1, base : base + width]
    value = tokens[...].astype(F32)
    center = jnp.mean(value, axis=1, keepdims=True)
    offset = value - center
    spread = jnp.mean(offset * offset, axis=1, keepdims=True)
    inverse = lax.rsqrt(spread + eps_norm)
    norm = offset * inverse
    sums[0:1, base : base + width] = jnp.sum(dh * norm, axis=0, keepdims=True)
    sums[0:1, base + width : base + 2 * width] = jnp.sum(dh, axis=0, keepdims=True)

    def small_block(a, b, c, d):
        n = (a * 2 + b) * 8 + c * 2 + d
        piece = sums[0:1, pl.ds(pl.multiple_of(128 * n, 128), 128)]
        pair = sums[0:1, pl.ds(pl.multiple_of(base + 128 * (n // 2), 128), 128)]
        own = pair if d == 0 else swap_halves(pair)
        return jnp.concatenate([piece, own, jnp.zeros((6, 128), F32)], axis=0)

    for a in range(2):
        for c in range(4):
            for d in range(2):
                core_small[a, c, d] = small_block(a, oc, c, d)
                acc_small[a, c, d] = small_block(a, core, c, d)
    over_small = remote(core_small, got_small, r.e_send.at[2], r.e_recv.at[2], to_core)
    over_small.start()
    parts[0][1](1)
    parts[0][0](2)
    over_small.wait()
    acc_small[...] += got_small[...]
    parts.append(reducer_of(r, "small", 4 * REDUCE_COPIES))
    parts[2][0](1)
    e = dh * gain
    mean_e = jnp.mean(e, axis=1, keepdims=True)
    mean_en = jnp.mean(e * norm, axis=1, keepdims=True)
    r.grad_tokens[...] = dx[...] + inverse * (e - mean_e - norm * mean_en)
    parts[1][1](1)
    parts[1][0](2)
    parts[0][1](2)
    parts[0][0](3)
    parts[2][1](1)
    parts[2][0](2)
    parts[1][1](2)
    parts[1][0](3)
    parts[2][1](2)
    parts[2][0](3)
    for part in (reducer_of(r, "ou", 0), reducer_of(r, "down", REDUCE_COPIES)):
        part[1](3)
    r.sum_ou[...] = reducer_of(r, "ou", 0)[2]()
    r.sum_down[...] = reducer_of(r, "down", REDUCE_COPIES)[2]()
    for _, finish, _ in parts:
        finish(3)
    for g, part in zip((1 - hz, hz), parts):
        r.sum_qkv[g] = part[2]()
    r.sum_small[...] = parts[2][2]()
    for index in range(HEADS):
        if index:
            for is_query, count in ((0, rows), (1, half)):
                view = r.packed.at[0, pl.ds(rows * is_query, count)]
                pltpu.make_async_copy(view, view, r.b_send.at[index + 8 * is_query]).wait()
            view = r.o2_s.at[0]
            pltpu.make_async_copy(view, view, r.d_send.at[index]).wait()


def layer_kernel(names, *refs):
    r = types.SimpleNamespace(**dict(zip(names, refs)))
    forward_phase(r)
    middle_phase(r)
    backward_phase(r)
    last_phase(r)


def layer(inputs, cid):
    rows, width = inputs["tokens"].shape
    length = rows * HEADS
    lanes = 2 * HALF
    hidden = inputs["up_flat"].shape[0] * 128 // 16
    down_rows = inputs["down_flat"].shape[0] * 128 // width
    group = 3 * width // 2
    every = (2, 2, 4, 2)
    mine = (2, 4, 2)
    row = (8, 4096 + 4 * width)
    vmem = pltpu.VMEM
    dma = pltpu.SemaphoreType.DMA
    outputs = {
        "out_ref": jax.ShapeDtypeStruct((rows, width), BF16),
        "grad_tokens": jax.ShapeDtypeStruct((rows, width), F32),
        "sum_qkv": jax.ShapeDtypeStruct((2, 16, group), F32),
        "sum_ou": jax.ShapeDtypeStruct((16, width + hidden), F32),
        "sum_down": jax.ShapeDtypeStruct((down_rows, width), F32),
        "sum_small": jax.ShapeDtypeStruct((8, 128), F32),
    }
    scratch = {
        "flags": pltpu.SMEM((length // PIECE,), jnp.int32),
        "a1": vmem((rows, width), BF16),
        "got": vmem((HEADS, rows + rows // 2, lanes), BF16),
        "mix": vmem((HEADS, rows // 2, lanes), BF16),
        "o_heads": vmem((length, lanes), F32),
        "lse": vmem((8, length), F32),
        "vec": vmem(row, F32),
        "qkv_all": vmem((2,) + every + (16, group + 128), BF16),
        "ou_all": vmem(every + (16, width + hidden), BF16),
        "down_all": vmem(every + (down_rows, width), BF16),
        "stage": vmem((256, 128), F32),
        "qkv_own": vmem((2, 16, group + 128), BF16),
        "ou_own": vmem((16, width + hidden), BF16),
        "down_own": vmem((down_rows, width), BF16),
        "packed": vmem((HEADS, rows + rows // 2, lanes), BF16),
        "q_s": vmem((length, lanes), BF16),
        "k_s": vmem((length, lanes), BF16),
        "v_s": vmem((length, lanes), BF16),
        "m_s": vmem((length, lanes), F32),
        "acc_s": vmem((length, lanes), F32),
        "o2_s": vmem((HEADS, rows // 2, lanes), BF16),
        "do2": vmem((HEADS, rows // 2, lanes), BF16),
        "acc_ou": vmem(mine + (16, width + hidden), F32),
        "acc_down": vmem(mine + (down_rows, width), F32),
        "sums": vmem(row, F32),
        "o_s": vmem((rows, width), BF16),
        "x1_s": vmem((rows, width), F32),
        "n2_s": vmem((rows, width), F32),
        "a2_s": vmem((rows, width), BF16),
        "gl_s": vmem((rows, hidden), BF16),
        "du_s": vmem((rows, hidden), BF16),
        "dh_s": vmem((rows, width), F32),
        "da_s": vmem((rows, width), BF16),
        "r_s": vmem((rows, lanes), F32),
        "core_ou": vmem(mine + (16, width + hidden), BF16),
        "core_down": vmem(mine + (down_rows, width), BF16),
        "got_ou": vmem(mine + (16, width + hidden), BF16),
        "got_down": vmem(mine + (down_rows, width), BF16),
        "delta_s": vmem((8, length), F32),
        "grads": vmem((HEADS, rows + rows // 2, lanes), BF16),
        "got_q": vmem((2,) + mine + (16, group), BF16),
        "core_small": vmem(mine + (8, 128), F32),
        "got_small": vmem(mine + (8, 128), F32),
        "acc_small": vmem(mine + (8, 128), F32),
    }
    for name, lead, r, w, wire in (
        ("ou", (), 16, width + hidden, BF16),
        ("down", (), down_rows, width, BF16),
        ("q", (2,), 16, group, BF16),
        ("small", (), 8, 128, F32),
    ):
        for n, buf in enumerate(reduce_buffers(r, w, wire)):
            scratch[f"{name}{n}"] = vmem(lead + buf.shape, buf.dtype)
    for name, count in (
        ("g_own", 3),
        ("g_send", 33),
        ("g_recv", 33),
        ("f_send", 40),
        ("f_recv", 40),
        ("x_send", 16),
        ("x_recv", 16),
        ("o_send", 8),
        ("o_recv", 8),
        ("d_send", 8),
        ("d_recv", 8),
        ("c_send", 2),
        ("c_recv", 2),
        ("r_send", 5 * REDUCE_COPIES),
        ("r_recv", 5 * REDUCE_COPIES),
        ("b_send", 16),
        ("b_recv", 16),
        ("e_send", 3),
        ("e_recv", 3),
    ):
        scratch[name] = dma((count,))
    names = tuple(inputs) + tuple(outputs) + tuple(scratch)

    def kernel(*refs):
        layer_kernel(names, *refs)

    return pl.pallas_call(
        kernel,
        out_shape=list(outputs.values()),
        in_specs=[SMEM_SPEC if n == "starts" else VMEM_SPEC for n in inputs],
        out_specs=[VMEM_SPEC] * len(outputs),
        scratch_shapes=list(scratch.values()),
        compiler_params=params(cid),
    )(*inputs.values())


def flatten_kernel(
    output,
    grad_tokens,
    sum_qkv,
    sum_ou,
    sum_down,
    sum_small,
    output_o,
    tokens_o,
    qkv_o,
    out_o,
    up_o,
    down_o,
    bias_o,
    norm_o,
):
    output_o[...] = output[...]
    tokens_o[...] = grad_tokens[...]
    groups = sum_down.shape[1] // 128
    left = left_lanes(16)

    def group(ref, j):
        return ref[:, 128 * j : 128 * (j + 1)]

    for j in range(groups):
        part = sum_qkv.at[j // 2]
        pair = j % 2
        qkv_o[pl.ds(j, 16, stride=3 * groups), :] = group(part, pair)
        even, odd = group(part, 2 + 2 * pair), group(part, 3 + 2 * pair)
        qkv_o[pl.ds(groups + j, 16, stride=3 * groups), :] = jnp.where(
            left, even, swap_halves(odd)
        )
        qkv_o[pl.ds(2 * groups + j, 16, stride=3 * groups), :] = jnp.where(
            left, swap_halves(even), odd
        )
        out_o[pl.ds(j, 16, stride=groups), :] = group(sum_ou, j)
        down_o[pl.ds(j, sum_down.shape[0], stride=groups), :] = group(sum_down, j)
    ups = sum_ou.shape[1] // 128 - groups
    for j in range(ups):
        up_o[pl.ds(j, 16, stride=ups), :] = group(sum_ou, groups + j)
    bias_o[...] = sum_small[0:1]
    norm_o[...] = sum_small[1:2, : norm_o.shape[1]]


def flatten(output, grad_tokens, sum_qkv, sum_ou, sum_down, sum_small, norm_len):
    width = sum_down.shape[1]
    sizes = (
        sum_qkv.size // 128,
        width * 16 // 128,
        (sum_ou.shape[1] - width) * 16 // 128,
        sum_down.size // 128,
    )
    return pl.pallas_call(
        flatten_kernel,
        out_shape=[
            jax.ShapeDtypeStruct(output.shape, output.dtype),
            jax.ShapeDtypeStruct(grad_tokens.shape, grad_tokens.dtype),
        ]
        + [jax.ShapeDtypeStruct((n, 128), F32) for n in sizes]
        + [jax.ShapeDtypeStruct((1, 128), F32), jax.ShapeDtypeStruct((1, norm_len), F32)],
        in_specs=[VMEM_SPEC] * 6,
        out_specs=[VMEM_SPEC] * 8,
        compiler_params=params(),
    )(output, grad_tokens, sum_qkv, sum_ou, sum_down, sum_small)


def fast_device(
    tokens, piece_starts, qkv_weight, out_weight, up_weight, down_weight, biases, norms, cotangent
):
    output, grad_tokens, sum_qkv, sum_ou, sum_down, sum_small = layer(
        {
            "starts": piece_starts,
            "tokens": tokens[0],
            "cot": cotangent[0],
            "biases": biases.reshape(1, -1),
            "norms": norms.reshape(1, -1),
            "qkv_flat": qkv_weight.reshape(-1, 128),
            "out_flat": out_weight.reshape(-1, 128),
            "up_flat": up_weight.reshape(-1, 128),
            "down_flat": down_weight.reshape(-1, 128),
        },
        1,
    )
    output, grad_tokens, *flats = flatten(
        output, grad_tokens, sum_qkv, sum_ou, sum_down, sum_small, norms.shape[0]
    )
    return (output[None], grad_tokens[None]) + tuple(f.reshape(-1) for f in flats)


def solution(mesh):
    flat = P(("dp", "ctx"))
    rows = P("dp", "ctx", None)
    fast = mesh.shape["dp"] == 4 and mesh.shape["ctx"] == HEADS
    return jax.shard_map(
        fast_device if fast else general_device,
        mesh=mesh,
        in_specs=(rows, P("dp", None), flat, flat, flat, flat, flat, flat, rows),
        out_specs=(rows, rows, flat, flat, flat, flat, flat, flat),
        check_vma=False,
    )
```

```python
import math
import types

import jax
import jax.numpy as jnp
from jax import lax
from jax.experimental import pallas as pl
from jax.experimental.pallas import tpu as pltpu
from jax.sharding import PartitionSpec as P

HEADS = 8
PIECE = 256


eps_norm = 1e-05
masked_score = -1e30


def layer_norm(values, gain, shift):
    center = jnp.mean(values, axis=-1, keepdims=True)
    offsets = values - center
    spread = jnp.mean(offsets * offsets, axis=-1, keepdims=True)
    return offsets * lax.rsqrt(spread + eps_norm) * gain + shift


def gelu_exact(values):
    return jax.nn.gelu(values, approximate=False)


def piece_flags(positions, starts_row):
    opening = positions // PIECE * PIECE
    return jnp.any(opening[:, None] == starts_row[None, :], axis=1)


def visible(query_pos, query_flag, key_pos):
    causal = key_pos[None, :] <= query_pos[:, None]
    same_piece = key_pos[None, :] // PIECE == query_pos[:, None] // PIECE
    return jnp.logical_or(causal, jnp.logical_and(same_piece, query_flag[:, None]))


def to_blocks(arrays, shard_rows):
    block_len = 256
    block_count = shard_rows // block_len
    shaped = tuple((member.reshape(block_count, block_len, HEADS, -1) for member in arrays))
    return (block_len, block_count, shaped)


def keep_state(state):
    return state


def unpack(flats, model_width):
    qkv_flat, out_flat, up_flat, down_flat, bias_flat, norm_flat = flats
    hidden = up_flat.shape[0] // model_width
    return (
        qkv_flat.reshape(model_width, 3 * model_width),
        out_flat.reshape(model_width, model_width),
        up_flat.reshape(model_width, hidden),
        down_flat.reshape(hidden, model_width),
        bias_flat.astype(jnp.float32),
        norm_flat.astype(jnp.float32),
    )


def norm_back(values, gain, shift, upstream):
    _, pullback = jax.vjp(layer_norm, values, gain, shift)
    return pullback(upstream)


def column_sum(matrix):
    return jnp.sum(matrix.astype(jnp.float32), axis=0)


def query_terms(
    query_heads,
    grad_heads,
    own_lse,
    own_delta,
    query_pos,
    query_flag,
    key_block,
    value_block,
    key_pos,
    factor,
):
    scores = (
        jnp.einsum("qhd,khd->hqk", query_heads, key_block, preferred_element_type=jnp.float32)
        * factor
    )
    allowed = visible(query_pos, query_flag, key_pos)[None]
    softmax_p = jnp.where(allowed, jnp.exp(scores - own_lse[:, :, None]), 0.0)
    dprobs = jnp.einsum("qhd,khd->hqk", grad_heads, value_block, preferred_element_type=jnp.float32)
    dscores = (softmax_p * (dprobs - own_delta[:, :, None])).astype(jnp.bfloat16)
    return (
        jnp.einsum("hqk,khd->hqd", dscores, key_block, preferred_element_type=jnp.float32) * factor
    )


def key_terms(
    query_block,
    grad_block,
    lse_block,
    delta_block,
    remote_pos,
    remote_flag,
    key_heads,
    value_heads,
    key_pos,
    factor,
):
    scores = (
        jnp.einsum("qhd,khd->hqk", query_block, key_heads, preferred_element_type=jnp.float32)
        * factor
    )
    allowed = visible(remote_pos, remote_flag, key_pos)[None]
    softmax_p = jnp.where(allowed, jnp.exp(scores - lse_block[:, :, None]), 0.0)
    dprobs = jnp.einsum("qhd,khd->hqk", grad_block, value_heads, preferred_element_type=jnp.float32)
    dscores = (softmax_p * (dprobs - delta_block[:, :, None])).astype(jnp.bfloat16)
    grad_keys = (
        jnp.einsum("hqk,qhd->hkd", dscores, query_block, preferred_element_type=jnp.float32)
        * factor
    )
    grad_values = jnp.einsum(
        "hqk,qhd->hkd",
        softmax_p.astype(jnp.bfloat16),
        grad_block,
        preferred_element_type=jnp.float32,
    )
    return (grad_keys, grad_values)


def general_device(
    tokens, piece_starts, qkv_weight, out_weight, up_weight, down_weight, biases, norms, cotangent
):
    model_width = tokens.shape[2]
    seq_rows = tokens.shape[1]
    params = unpack(
        (
            lax.all_gather(qkv_weight, ("dp", "ctx"), axis=0, tiled=True),
            lax.all_gather(out_weight, ("dp", "ctx"), axis=0, tiled=True),
            lax.all_gather(up_weight, ("dp", "ctx"), axis=0, tiled=True),
            lax.all_gather(down_weight, ("dp", "ctx"), axis=0, tiled=True),
            lax.all_gather(biases, ("dp", "ctx"), axis=0, tiled=True),
            lax.all_gather(norms, ("dp", "ctx"), axis=0, tiled=True),
        ),
        model_width,
    )
    qkv_mat, out_mat, up_mat, down_mat, bias_all, norm_all = params
    hidden = up_mat.shape[1]
    head_dim = model_width // HEADS
    factor = head_dim ** (-0.5)
    first_row = lax.axis_index("ctx") * seq_rows
    last_row = first_row + seq_rows - 1
    query_pos = first_row + jnp.arange(seq_rows, dtype=jnp.int32)
    starts_row = piece_starts[0]
    query_flag = piece_flags(query_pos, starts_row)
    bias_q = bias_all[:model_width]
    bias_v = bias_all[model_width : 2 * model_width]
    bias_o = bias_all[2 * model_width : 3 * model_width]
    bias_up = bias_all[3 * model_width : 3 * model_width + hidden]
    bias_down = bias_all[3 * model_width + hidden :]
    gain_one = norm_all[:model_width]
    shift_one = norm_all[model_width : 2 * model_width]
    gain_two = norm_all[2 * model_width : 3 * model_width]
    shift_two = norm_all[3 * model_width :]
    inputs = tokens[0].astype(jnp.float32)
    first_in = layer_norm(inputs, gain_one, shift_one).astype(jnp.bfloat16)
    projected = jnp.dot(first_in, qkv_mat, preferred_element_type=jnp.float32)
    queries = (projected[:, :model_width] + bias_q).astype(jnp.bfloat16)
    key_rows = projected[:, model_width : 2 * model_width].astype(jnp.bfloat16)
    value_rows = (projected[:, 2 * model_width :] + bias_v).astype(jnp.bfloat16)
    query_heads = queries.reshape(seq_rows, HEADS, head_dim)
    key_heads = key_rows.reshape(seq_rows, HEADS, head_dim)
    value_heads = value_rows.reshape(seq_rows, HEADS, head_dim)
    start_state = (
        jnp.full((HEADS, seq_rows), masked_score, jnp.float32),
        jnp.zeros((HEADS, seq_rows), jnp.float32),
        jnp.zeros((HEADS, seq_rows, head_dim), jnp.float32),
    )
    shard = (
        lax.all_gather(key_rows, "ctx", axis=0, tiled=True),
        lax.all_gather(value_rows, "ctx", axis=0, tiled=True),
    )
    shard_rows = shard[0].shape[0]
    block_len, block_count, (key_blocks, value_blocks) = to_blocks(shard, shard_rows)

    def forward_one_block(state, block_in):
        running_max, running_sum, running_acc = state
        key_block, value_block, position = block_in
        key_pos = position * block_len + jnp.arange(block_len, dtype=jnp.int32)
        scores = (
            jnp.einsum("qhd,khd->hqk", query_heads, key_block, preferred_element_type=jnp.float32)
            * factor
        )
        allowed = visible(query_pos, query_flag, key_pos)[None]
        scores = jnp.where(allowed, scores, masked_score)
        new_max = jnp.maximum(running_max, jnp.max(scores, axis=-1))
        correction = jnp.exp(running_max - new_max)
        exp_scores = jnp.where(allowed, jnp.exp(scores - new_max[:, :, None]), 0.0)
        running_sum = running_sum * correction + jnp.sum(exp_scores, axis=-1)
        running_acc = running_acc * correction[:, :, None] + jnp.einsum(
            "hqk,khd->hqd",
            exp_scores.astype(jnp.bfloat16),
            value_block,
            preferred_element_type=jnp.float32,
        )
        return ((new_max, running_sum, running_acc), None)

    def forward_compute(state):
        return lax.scan(
            forward_one_block,
            state,
            (key_blocks, value_blocks, jnp.arange(block_count, dtype=jnp.int32)),
        )[0]

    run_max, run_sum, run_acc = lax.cond(
        jnp.int32(0) <= last_row, forward_compute, keep_state, start_state
    )
    mixed_heads = run_acc / run_sum[:, :, None]
    mixed_f = jnp.transpose(mixed_heads, (1, 0, 2)).reshape(seq_rows, model_width)
    mixed_b = mixed_f.astype(jnp.bfloat16)
    log_sum = run_max + jnp.log(run_sum)
    after_attn = inputs + jnp.dot(mixed_b, out_mat, preferred_element_type=jnp.float32) + bias_o
    second_in = layer_norm(after_attn, gain_two, shift_two).astype(jnp.bfloat16)
    pre_act = jnp.dot(second_in, up_mat, preferred_element_type=jnp.float32) + bias_up
    activated = gelu_exact(pre_act).astype(jnp.bfloat16)
    result = (
        after_attn + jnp.dot(activated, down_mat, preferred_element_type=jnp.float32) + bias_down
    )
    output = result.astype(jnp.bfloat16)[None]
    back = unpack(
        (
            lax.all_gather(qkv_weight, ("dp", "ctx"), axis=0, tiled=True),
            lax.all_gather(out_weight, ("dp", "ctx"), axis=0, tiled=True),
            lax.all_gather(up_weight, ("dp", "ctx"), axis=0, tiled=True),
            lax.all_gather(down_weight, ("dp", "ctx"), axis=0, tiled=True),
            lax.all_gather(biases, ("dp", "ctx"), axis=0, tiled=True),
            lax.all_gather(norms, ("dp", "ctx"), axis=0, tiled=True),
        ),
        model_width,
    )
    qkv_back, out_back, up_back, down_back, bias_back, norm_vec = back
    gain_one_b = norm_vec[:model_width]
    shift_one_b = norm_vec[model_width : 2 * model_width]
    gain_two_b = norm_vec[2 * model_width : 3 * model_width]
    shift_two_b = norm_vec[3 * model_width :]
    upstream = cotangent[0].astype(jnp.float32)
    grad_mlp = upstream.astype(jnp.bfloat16)
    grad_down_loc = jnp.einsum("ta,tb->ab", activated, grad_mlp, preferred_element_type=jnp.float32)
    grad_act = jnp.einsum("tb,ab->ta", grad_mlp, down_back, preferred_element_type=jnp.float32)
    _, gelu_pull = jax.vjp(gelu_exact, pre_act)
    grad_pre = gelu_pull(grad_act)[0].astype(jnp.bfloat16)
    grad_up_loc = jnp.einsum("ta,tb->ab", second_in, grad_pre, preferred_element_type=jnp.float32)
    grad_second = jnp.einsum("tb,ab->ta", grad_pre, up_back, preferred_element_type=jnp.float32)
    grad_after_part, grad_gain_two, grad_shift_two = norm_back(
        after_attn, gain_two_b, shift_two_b, grad_second
    )
    grad_after = upstream + grad_after_part
    grad_attn = grad_after.astype(jnp.bfloat16)
    grad_out_loc = jnp.einsum("ta,tb->ab", mixed_b, grad_attn, preferred_element_type=jnp.float32)
    grad_mixed = jnp.einsum(
        "tb,ab->ta", grad_attn, out_back, preferred_element_type=jnp.float32
    ).astype(jnp.bfloat16)
    grad_heads = grad_mixed.reshape(seq_rows, HEADS, head_dim)
    delta_rows = jnp.sum(
        grad_heads.astype(jnp.float32) * mixed_f.reshape(seq_rows, HEADS, head_dim), axis=-1
    )
    delta_heads = delta_rows.T
    stats = jnp.concatenate([log_sum.T, delta_rows], axis=1)
    all_stats = lax.all_gather(stats, "ctx", axis=0, tiled=True)
    zero_heads = jnp.zeros((HEADS, seq_rows, head_dim), jnp.float32)
    shard = (
        lax.all_gather(key_rows, "ctx", axis=0, tiled=True),
        lax.all_gather(value_rows, "ctx", axis=0, tiled=True),
    )
    shard_rows = shard[0].shape[0]
    query_block_len, query_block_count, (query_key_blocks, query_value_blocks) = to_blocks(
        shard, shard_rows
    )

    def query_one_block(total, block_in):
        key_block, value_block, position = block_in
        key_pos = position * query_block_len + jnp.arange(query_block_len, dtype=jnp.int32)
        term = query_terms(
            query_heads,
            grad_heads,
            log_sum,
            delta_heads,
            query_pos,
            query_flag,
            key_block,
            value_block,
            key_pos,
            factor,
        )
        return (total + term, None)

    def query_compute(total):
        return lax.scan(
            query_one_block,
            total,
            (query_key_blocks, query_value_blocks, jnp.arange(query_block_count, dtype=jnp.int32)),
        )[0]

    grad_q = lax.cond(jnp.int32(0) <= last_row, query_compute, keep_state, zero_heads)
    shard = (
        lax.all_gather(queries, "ctx", axis=0, tiled=True),
        lax.all_gather(grad_mixed, "ctx", axis=0, tiled=True),
    )
    shard_rows = shard[0].shape[0]
    key_block_len, key_block_count, (query_blocks, grad_blocks) = to_blocks(shard, shard_rows)

    def key_one_block(totals, block_in):
        query_block, grad_block, position = block_in
        begin = position * key_block_len
        remote_pos = begin + jnp.arange(key_block_len, dtype=jnp.int32)
        remote_flag = piece_flags(remote_pos, starts_row)
        stats_block = lax.dynamic_slice_in_dim(all_stats, begin, key_block_len, 0)
        lse_block = stats_block[:, :HEADS].T
        delta_block = stats_block[:, HEADS:].T
        grad_keys, grad_values = key_terms(
            query_block,
            grad_block,
            lse_block,
            delta_block,
            remote_pos,
            remote_flag,
            key_heads,
            value_heads,
            query_pos,
            factor,
        )
        return ((totals[0] + grad_keys, totals[1] + grad_values), None)

    def key_compute(totals):
        return lax.scan(
            key_one_block,
            totals,
            (query_blocks, grad_blocks, jnp.arange(key_block_count, dtype=jnp.int32)),
        )[0]

    grad_k, grad_v = lax.cond(
        jnp.int32(0) + shard_rows - 1 >= first_row,
        key_compute,
        keep_state,
        (zero_heads, zero_heads),
    )

    def merge_heads(grad_part):
        return (
            jnp.transpose(grad_part, (1, 0, 2)).reshape(seq_rows, model_width).astype(jnp.bfloat16)
        )

    grad_qkv_rows = jnp.concatenate(
        [merge_heads(grad_q), merge_heads(grad_k), merge_heads(grad_v)], axis=1
    )
    grad_qkv_loc = jnp.einsum(
        "ta,tb->ab", first_in, grad_qkv_rows, preferred_element_type=jnp.float32
    )
    grad_first = jnp.einsum(
        "tb,ab->ta", grad_qkv_rows, qkv_back, preferred_element_type=jnp.float32
    )
    grad_in_part, grad_gain_one, grad_shift_one = norm_back(
        inputs, gain_one_b, shift_one_b, grad_first
    )
    grad_tokens = (grad_after + grad_in_part)[None]
    grad_bias_loc = jnp.concatenate(
        [
            column_sum(grad_qkv_rows[:, :model_width]),
            column_sum(grad_qkv_rows[:, 2 * model_width :]),
            column_sum(grad_attn),
            column_sum(grad_pre),
            column_sum(grad_mlp),
        ]
    )
    grad_norm_loc = jnp.concatenate([grad_gain_one, grad_shift_one, grad_gain_two, grad_shift_two])
    summed = (
        lax.psum_scatter(grad_qkv_loc.reshape(-1), ("dp", "ctx"), scatter_dimension=0, tiled=True),
        lax.psum_scatter(grad_out_loc.reshape(-1), ("dp", "ctx"), scatter_dimension=0, tiled=True),
        lax.psum_scatter(grad_up_loc.reshape(-1), ("dp", "ctx"), scatter_dimension=0, tiled=True),
        lax.psum_scatter(grad_down_loc.reshape(-1), ("dp", "ctx"), scatter_dimension=0, tiled=True),
        lax.psum_scatter(grad_bias_loc, ("dp", "ctx"), scatter_dimension=0, tiled=True),
        lax.psum_scatter(grad_norm_loc, ("dp", "ctx"), scatter_dimension=0, tiled=True),
    )
    return (output, grad_tokens, summed[0], summed[1], summed[2], summed[3], summed[4], summed[5])


MESH = pl.DeviceIdType.MESH
BF16 = jnp.bfloat16
F32 = jnp.float32
VMEM_SPEC = pl.BlockSpec(memory_space=pltpu.VMEM)
SMEM_SPEC = pl.BlockSpec(memory_space=pltpu.SMEM)
ANY_SPEC = pl.BlockSpec(memory_space=pl.ANY)
HALF = 64
NT = (((1,), (1,)), ((), ()))
TN = (((0,), (0,)), ((), ()))
VMEM_LIMIT = 60 << 20


def params(cid=None):
    if cid is None:
        return pltpu.CompilerParams(vmem_limit_bytes=VMEM_LIMIT)
    return pltpu.CompilerParams(
        collective_id=cid, has_side_effects=True, vmem_limit_bytes=VMEM_LIMIT
    )


def place():
    dp = lax.axis_index("dp")
    ctx = lax.axis_index("ctx")
    return dp // 2, dp % 2, ctx // 2, ctx % 2


def device(x, core, z, y):
    return (x * 2 + core, z * 2 + y)


def greet(peers):
    barrier = pltpu.get_barrier_semaphore()
    for peer in peers:
        pl.semaphore_signal(barrier, inc=1, device_id=peer, device_id_type=MESH)
    pl.semaphore_wait(barrier, len(peers))


def remote(src, dst, send, recv, peer):
    return pltpu.make_async_remote_copy(
        src_ref=src,
        dst_ref=dst,
        send_sem=send,
        recv_sem=recv,
        device_id=peer,
        device_id_type=MESH,
    )


def mm(a, b, dims=None):
    if dims is None:
        return jnp.dot(a, b, preferred_element_type=F32)
    return lax.dot_general(a, b, dims, preferred_element_type=F32)


def swap_halves(v):
    return jnp.concatenate([v[:, HALF:], v[:, :HALF]], axis=1)


def left_lanes(rows):
    return lax.broadcasted_iota(jnp.int32, (rows, 2 * HALF), 1) < HALF


def diagonal_mask(size, flags, first, transposed):
    row = lax.broadcasted_iota(jnp.int32, (size, size), 0)
    col = lax.broadcasted_iota(jnp.int32, (size, size), 1)
    key, query = (row, col) if transposed else (col, row)
    allowed = key <= query
    same = (key // PIECE) == (query // PIECE)
    for t in range(size // PIECE):
        inside = jnp.logical_and(same, (query // PIECE) == t)
        allowed = jnp.logical_or(allowed, jnp.logical_and(inside, flags[first + t] > 0))
    return allowed


def xor8(a, b):
    return (
        (a // 4 + b // 4) % 2 * 4 + (a // 2 % 2 + b // 2 % 2) % 2 * 2 + (a % 2 + b % 2) % 2
    )


def unflatten(flat_ref, stage, rows, groups):
    count = rows * groups
    stage[pl.ds(0, count), :] = flat_ref[...].astype(F32)
    return [stage[pl.ds(j, rows, stride=groups), :] for j in range(groups)]


def reduce_buffers(rows, width, wire):
    vmem = pltpu.VMEM
    return [
        vmem((2, 2, rows, width), wire),
        vmem((2, 2, rows, width), wire),
        vmem((2, 2, rows, width), wire),
        vmem((2, 2, rows, width), wire),
        vmem((2, 2, rows, width), wire),
        vmem((2, 2, rows, width), wire),
        vmem((4, rows, width), wire),
        vmem((3, rows, width), wire),
        vmem((4, rows, width), F32),
    ]


REDUCE_BUFFERS = 9
REDUCE_COPIES = 7


def reducer(acc, bufs, send, recv, first):
    to_wire_x, from_x, to_wire_y, from_y, to_two, from_two, to_three, from_three, total = bufs
    wire = to_wire_x.dtype
    x, core, z, y = place()
    ox, oy = 1 - x, 1 - y
    to_x = device(ox, core, z, y)
    to_y = device(x, core, z, oy)
    others = [(z + j) % 4 for j in range(1, 4)]

    def copies(stage):
        def make(n, src, dst, peer):
            return remote(src, dst, send.at[first + n], recv.at[first + n], peer)

        if stage == 1:
            return [make(0, to_wire_x, from_x, to_x), make(1, to_wire_y, from_y, to_y)]
        if stage == 2:
            return [
                make(2, to_two.at[0], from_two.at[0], to_y),
                make(3, to_two.at[1], from_two.at[1], to_x),
            ]
        return [
            make(4 + j, to_three.at[other], from_three.at[j], device(x, core, other, y))
            for j, other in enumerate(others)
        ]

    def launch(stage):
        if stage == 1:
            to_wire_x[...] = acc[ox, pl.ds(0, 2)].astype(wire)
            for n in range(2):
                to_wire_y[n] = acc[n, pl.ds(2, 2), oy].astype(wire)
        elif stage == 2:
            to_two[0] = (acc[x, pl.ds(0, 2), oy] + from_x[:, oy].astype(F32)).astype(wire)
            to_two[1] = (acc[ox, pl.ds(2, 2), y] + from_y[ox].astype(F32)).astype(wire)
        else:
            low = acc[x, pl.ds(0, 2), y] + from_x[:, y].astype(F32) + from_two[0].astype(F32)
            high = acc[x, pl.ds(2, 2), y] + from_y[x].astype(F32) + from_two[1].astype(F32)
            total[pl.ds(0, 2)] = low
            total[pl.ds(2, 2)] = high
            to_three[pl.ds(0, 2)] = low.astype(wire)
            to_three[pl.ds(2, 2)] = high.astype(wire)
        for copy in copies(stage):
            copy.start()

    def finish(stage):
        for copy in copies(stage):
            copy.wait()

    def result():
        value = total[z]
        for j in range(3):
            value = value + from_three[j].astype(F32)
        return value

    return launch, finish, result


def digits(values):
    return sum(v * 4**n for n, v in enumerate(values))


TILES = (
    (
        digits((0, 1, 1, 2, 2, 2, 3, 3, 3, 3)),
        digits((0, 1, 0, 0, 1, 2, 0, 1, 2, 3)),
        digits((1, 0, 1, 0, 0, 1, 0, 0, 0, 1)),
    ),
    (
        digits((2, 3, 3, 2, 3, 0, 2, 3, 1, 1)),
        digits((2, 3, 2, 0, 0, 0, 1, 1, 0, 1)),
        digits((0, 0, 0, 0, 0, 1, 1, 1, 0, 1)),
    ),
)


def forward_phase(r):
    flags = r.flags
    tokens = r.tokens
    qkv_flat = r.qkv_flat
    out_flat = r.out_flat
    up_flat = r.up_flat
    down_flat = r.down_flat
    a1_ref = r.a1
    got = r.got
    mix = r.mix
    o_ref = r.o_heads
    lse_ref = r.lse
    vec_ref = r.vec
    qkv_all = r.qkv_all
    ou_all = r.ou_all
    down_all = r.down_all
    stage = r.stage
    qkv_own = r.qkv_own
    ou_own = r.ou_own
    down_own = r.down_own
    norm_s = r.n2_s
    packed = r.packed
    q_s = r.q_s
    k_s = r.k_s
    v_s = r.v_s
    m_s = r.m_s
    acc_s = r.acc_s
    o2_s = r.o2_s
    g_own = r.g_own
    g_send = r.g_send
    g_recv = r.g_recv
    f_send = r.f_send
    f_recv = r.f_recv
    x_send = r.x_send
    x_recv = r.x_recv
    o_send = r.o_send
    o_recv = r.o_recv
    x, core, z, y = place()
    ox, oc, oy = 1 - x, 1 - core, 1 - y
    me = z * 2 + y
    width = tokens.shape[1]
    rows = tokens.shape[0]
    half = rows // 2
    tile = 2 * rows
    groups = width // 128
    group = 3 * width // 2
    scale = math.log2(math.e) * HALF**-0.5
    left = left_lanes(rows)
    left_half = left_lanes(half)
    to_x = device(ox, core, z, y)
    to_y = device(x, core, z, oy)
    to_core = device(x, oc, z, y)
    others = [(z + j) % 4 for j in range(1, 4)]

    qkv = unflatten(qkv_flat, stage, 16, 3 * groups)
    left16 = left_lanes(16)
    for j in range(groups):
        k_pair, v_pair = qkv[groups + j], qkv[2 * groups + j]
        own = qkv_own.at[j // 2]
        at = (j % 2) * 128
        own[:, at : at + 128] = qkv[j].astype(BF16)
        at = 256 + (j % 2) * 256
        own[:, at : at + 128] = jnp.where(left16, k_pair, swap_halves(v_pair)).astype(BF16)
        at += 128
        own[:, at : at + 128] = jnp.where(left16, swap_halves(k_pair), v_pair).astype(BF16)
    norm_row = jnp.concatenate(
        [r.norms[...].astype(F32), jnp.zeros((1, 128 - r.norms.shape[1]), F32)], axis=1
    )
    block = jnp.concatenate(
        [r.biases[...].astype(F32), norm_row, jnp.zeros((14, 128), F32)], axis=0
    )
    for g in range(2):
        qkv_own[g, :, group:] = block.astype(BF16)
    for t in range(flags.shape[0]):
        found = jnp.int32(0)
        for j in range(r.starts.shape[1]):
            found = found + (r.starts[0, j] == t * PIECE).astype(jnp.int32)
        flags[t] = found
    greet(
        [device(x, core, (z + c) % 4, (y + d) % 2) for c in range(4) for d in range(2)][1:]
        + [to_x, to_core]
    )
    arrays = ((qkv_own, qkv_all), (ou_own, ou_all), (down_own, down_all))

    def moves(phase, a):
        own, full = arrays[a]
        if phase == 1:
            mine = full.at[x, core, z, y]
            return [(own, mine, device(x, core, o, y), j) for j, o in enumerate(others)]
        if phase == 2:
            part = full.at[x, core, :, y]
            return [(part, part, to_x, 3), (part, part, to_y, 4), (part, part, to_core, 5)]
        if phase == 3:
            low = full.at[x, core, pl.ds(0, 2), oy]
            high = full.at[ox, core, pl.ds(2, 2), y]
            from_x = full.at[ox, core, :, y]
            from_y = full.at[x, core, :, oy]
            return [
                (low, low, to_x, 6),
                (high, high, to_y, 7),
                (from_x, from_x, to_core, 8),
                (from_y, from_y, to_core, 9),
            ]
        part = full.at[ox, core, :, oy]
        return [(part, part, to_core, 10)]

    def phase_copies(phase, a):
        copies = [
            remote(src, dst, g_send.at[a * 11 + n], g_recv.at[a * 11 + n], peer)
            for src, dst, peer, n in moves(phase, a)
        ]
        if phase == 1:
            own, full = arrays[a]
            copies.append(pltpu.make_async_copy(own, full.at[x, core, z, y], g_own.at[a]))
        return copies

    def launch(phase, a):
        for copy in phase_copies(phase, a):
            copy.start()

    def finish(phase, a):
        for copy in phase_copies(phase, a):
            copy.wait()

    hz = z // 2

    def picked(position, half_z):
        return half_z * (1 - position) + (1 - half_z) * position

    def hop(src, dst, peer, g, n):
        return remote(src, dst, f_send.at[20 * g + n], f_recv.at[20 * g + n], peer)

    def to_xy(g, c):
        part = qkv_all.at[g, x, core, c, y]
        return hop(part, part, to_x, g, 4 + c), hop(part, part, to_y, g, 8 + c)

    def corner(g, c, over_x):
        if over_x:
            part = qkv_all.at[g, x, core, c, oy]
            return hop(part, part, to_x, g, 12 + c)
        part = qkv_all.at[g, ox, core, c, y]
        return hop(part, part, to_y, g, 12 + c)

    def to_sibling(g, n):
        part = (
            qkv_all.at[g, x, core, :, y],
            qkv_all.at[g, ox, core, :, y],
            qkv_all.at[g, x, core, :, oy],
            qkv_all.at[g, ox, core, :, oy],
        )[n]
        return hop(part, part, to_core, g, 16 + n)

    def along(g, n):
        return hop(
            qkv_own.at[g], qkv_all.at[g, x, core, z, y], device(x, core, others[n], y), g, n
        )

    own_first = pltpu.make_async_copy(qkv_own, qkv_all.at[:, x, core, z, y], g_own.at[0])
    own_first.start()
    for position in range(2):
        for n, other in enumerate(others):
            along(picked(position, other // 2), n).start()
        g = picked(position, hz)
        own = qkv_all.at[g, x, core, z, y]
        hop(qkv_own.at[g], own, to_x, g, 4 + z).start()
        hop(qkv_own.at[g], own, to_y, g, 8 + z).start()
    out_parts = unflatten(out_flat, stage, 16, groups)
    for j in range(groups):
        ou_own[:, 128 * j : 128 * (j + 1)] = out_parts[j].astype(BF16)
    up_groups = up_flat.shape[0] // 16
    up_parts = unflatten(up_flat, stage, 16, up_groups)
    for j in range(up_groups):
        at = width + 128 * j
        ou_own[:, at : at + 128] = up_parts[j].astype(BF16)
    down_rows = down_flat.shape[0] // groups
    down_parts = unflatten(down_flat, stage, down_rows, groups)
    for j in range(groups):
        down_own[:, 128 * j : 128 * (j + 1)] = down_parts[j].astype(BF16)
    launch(1, 1)
    launch(1, 2)
    own_first.wait()
    one, two = picked(0, hz), picked(1, hz)
    for g in (one, two):
        for n in range(3):
            along(g, n).wait_recv()
            for copy in to_xy(g, (z + 3 - n) % 4):
                copy.start()
        to_sibling(g, 0).start()
    value = tokens[...].astype(F32)
    center = jnp.mean(value, axis=1, keepdims=True)
    offset = value - center
    spread = jnp.mean(offset * offset, axis=1, keepdims=True)
    norm_s[...] = offset * lax.rsqrt(spread + eps_norm)

    def meet(g):
        for c in [z] + others:
            over_x, over_y = to_xy(g, c)
            over_x.wait_recv()
            over_y.wait_recv()

            @pl.when(c < 2)
            def _():
                corner(g, c, True).start()

            @pl.when(c >= 2)
            def _():
                corner(g, c, False).start()

        to_sibling(g, 1).start()
        to_sibling(g, 2).start()

    def turn(g):
        for c in range(4):
            corner(g, c, c < 2).wait()
        to_sibling(g, 3).start()

    def close(g):
        for n in range(4):
            to_sibling(g, n).wait()

    meet(one)
    meet(two)
    turn(one)
    turn(two)
    close(one)

    vec_ref[...] = jnp.zeros_like(vec_ref)
    devices = [(a, b, c, d) for a in range(2) for b in range(2) for c in range(4) for d in range(2)]
    base = 128 * len(devices)

    def bias_rows(begin, end):
        for n in range(begin, end):
            piece = qkv_all[(one,) + devices[n] + (slice(None), pl.ds(group, 128))].astype(F32)
            vec_ref[0:1, 128 * n : 128 * (n + 1)] = piece[0:1]

    def norm_rows(begin, end):
        for n in range(begin, end):
            pair = [
                qkv_all[(one,) + devices[2 * n + d] + (slice(None), pl.ds(group, 128))].astype(F32)
                for d in range(2)
            ]
            joined = jnp.concatenate([pair[0][1:2, :HALF], pair[1][1:2, :HALF]], axis=1)
            vec_ref[0:1, base + 128 * n : base + 128 * (n + 1)] = joined

    bias_rows(0, 2 * groups)
    norm_rows(0, 2 * groups)
    gain = vec_ref[0:1, base : base + width]
    shift = vec_ref[0:1, base + width : base + 2 * width]
    a1_ref[...] = (norm_s[...] * gain + shift).astype(BF16)

    def part_of(is_query):
        return pl.ds(rows, half) if is_query else pl.ds(0, rows)

    def send_part(tz, mark, is_query):
        for step in range(2):
            ty = (y + step) % 2
            index = mark + step
            src = packed.at[2 * tz + ty, part_of(is_query)]
            dst = got.at[me, part_of(is_query)]
            n = index + 8 * is_query
            if index == 0:
                pltpu.make_async_copy(src, dst, x_recv.at[n]).start()
            else:
                remote(src, dst, x_send.at[n], x_recv.at[n], device(x, core, tz, ty)).start()

    order = (
        hz * 2 + 1 - z % 2,
        z,
        (1 - hz) * 2 + z % 2,
        (1 - hz) * 2 + 1 - z % 2,
    )
    marks = (2, 0, 4, 6)
    left1 = left_lanes(1)
    for place_of, (tz, mark) in enumerate(zip(order, marks)):
        if place_of == 2:
            close(two)
        g = one if place_of < 2 else two
        a1 = a1_ref[...]
        at = pl.multiple_of(tz % 2 * 128, 128)
        w_q = qkv_all[g, :, :, :, :, :, pl.ds(at, 128)].reshape(width, 128)
        q = (mm(a1, w_q) + vec_ref[0:1, pl.ds(pl.multiple_of(128 * tz, 128), 128)]).astype(BF16)
        at_kv = pl.multiple_of(256 + tz % 2 * 256, 128)
        w_kv = qkv_all[g, :, :, :, :, :, pl.ds(at_kv, 256)].reshape(width, 256)
        bias = vec_ref[0:1, pl.ds(pl.multiple_of(width + 128 * tz, 128), 128)]
        kv = mm(a1, w_kv)
        even = kv[:, :128] + jnp.where(left1, 0.0, swap_halves(bias))
        odd = kv[:, 128:] + jnp.where(left1, 0.0, bias)
        packed[2 * tz, :rows] = even.astype(BF16)
        packed[2 * tz + 1, :rows] = odd.astype(BF16)
        top, low = q[:half], q[half:]
        packed[2 * tz, rows:] = jnp.where(left_half, top, swap_halves(low))
        packed[2 * tz + 1, rows:] = jnp.where(left_half, swap_halves(top), low)
        if mark < 4:
            send_part(tz, mark, False)
            send_part(tz, mark, True)

    def send_cross():
        def send_all(is_query):
            for tz, mark in zip(order[2:], marks[2:]):
                send_part(tz, mark, is_query)

        pl.when(hz == 1)(lambda: send_all(True))
        send_all(False)
        pl.when(hz == 0)(lambda: send_all(True))

    send_cross()
    finish(1, 1)
    finish(1, 2)
    launch(2, 1)
    launch(2, 2)
    bias_rows(2 * groups, len(devices))
    norm_rows(2 * groups, len(devices) // 2)

    def block_wait(sems, index, view):
        pltpu.make_async_copy(view, view, sems.at[index]).wait()

    def arrive(part, is_query):
        for t in range(2):
            b = 2 * part + t
            block_wait(x_recv, xor8(b, me) + 8 * is_query, got.at[b, part_of(is_query)])
            at = pl.multiple_of(b * rows, rows)
            if is_query:
                both = got[b, rows:]
                q_s[pl.ds(at, half), :] = jnp.where(left_half, both, 0).astype(BF16)
                q_s[pl.ds(at + half, half), :] = jnp.where(
                    left_half, swap_halves(both), 0
                ).astype(BF16)
            else:
                pair = got[b, :rows]
                k_s[pl.ds(at, rows), :] = jnp.where(left, pair, 0).astype(BF16)
                v_s[pl.ds(at, rows), :] = jnp.where(left, 1, pair).astype(BF16)

    low = 1 - hz
    queries = low * TILES[0][0] + hz * TILES[1][0]
    keys = low * TILES[0][1] + hz * TILES[1][1]
    ends = low * TILES[0][2] + hz * TILES[1][2]
    m_s[...] = jnp.full(m_s.shape, masked_score, F32)
    acc_s[...] = jnp.zeros(acc_s.shape, F32)
    for n in range(2):
        arrive(2 * hz + n, False)
        arrive(2 * hz + n, True)

    def step(n, carry):
        q_left, k_left, e_left = carry
        i, j, done = q_left % 4, k_left % 4, e_left % 4

        @pl.when(n == 3)
        def _():
            for a in (1, 2):
                finish(2, a)
                launch(3, a)

        @pl.when(n == 6)
        def _():
            for a in (1, 2):
                finish(3, a)
                launch(4, a)

        for when, part, is_query in ((3, 2, 1), (5, 2, 0), (6, 3, 1), (9, 3, 0)):
            pl.when(n == when + 16 * hz)(lambda: arrive(part, is_query))
        for when, part, is_query in ((3, 0, 0), (5, 0, 1), (6, 1, 0), (8, 1, 1)):
            pl.when(n == when + 16 * low)(lambda: arrive(part, is_query))

        at = pl.multiple_of(i * tile, tile)
        begin = pl.multiple_of(j * tile, tile)

        def update(diagonal):
            s = mm(q_s[pl.ds(at, tile), :], k_s[pl.ds(begin, tile), :], NT)
            if diagonal:
                allowed = diagonal_mask(tile, flags, i * (tile // PIECE), False)
                s = jnp.where(allowed, s, masked_score)
            old = m_s[pl.ds(at, tile), :]
            new = jnp.maximum(old, jnp.max(s, axis=1, keepdims=True) * scale)
            p = jnp.exp2(s * scale - new[:, :1])
            m_s[pl.ds(at, tile), :] = new
            acc_s[pl.ds(at, tile), :] = acc_s[pl.ds(at, tile), :] * jnp.exp2(old - new) + mm(
                p.astype(BF16), v_s[pl.ds(begin, tile), :]
            )

        pl.when(i == j)(lambda: update(True))
        pl.when(i != j)(lambda: update(False))

        @pl.when(done == 1)
        def _():
            acc = acc_s[pl.ds(at, tile), :]
            total = jnp.broadcast_to(acc[:, :1], acc.shape)
            o = acc / total
            o_ref[pl.ds(at, tile), :] = o
            lse = m_s[pl.ds(at, tile), :] + jnp.log2(total)
            lse_ref[:, pl.ds(at, tile)] = jnp.transpose(lse)[:8]
            for t in range(2):
                b = 2 * i + t
                top = o[t * rows : t * rows + half]
                bottom = o[t * rows + half : (t + 1) * rows]
                o2_s[b] = jnp.where(left_half, swap_halves(top), bottom).astype(BF16)
                index = xor8(b, me)

                @pl.when(b == me)
                def _():
                    pltpu.make_async_copy(o2_s.at[b], mix.at[me], o_recv.at[0]).start()

                @pl.when(b != me)
                def _():
                    remote(
                        o2_s.at[b],
                        mix.at[me],
                        o_send.at[index],
                        o_recv.at[index],
                        device(x, core, i, t),
                    ).start()

        return q_left // 4, k_left // 4, e_left // 4

    lax.fori_loop(0, 10, step, (queries, keys, ends))
    for a in (1, 2):
        finish(4, a)
    for g in range(2):
        for n in range(3):
            along(g, n).wait_send()
        for c in range(4):
            for copy in to_xy(g, c):
                copy.wait_send()
    for index in range(8):
        block_wait(o_recv, index, mix.at[0])
        if index:
            block_wait(x_send, index, packed.at[0, part_of(False)])
            block_wait(x_send, index + 8, packed.at[0, part_of(True)])
            block_wait(o_send, index, o2_s.at[0])


def middle_phase(r):
    tokens = r.tokens
    cot = r.cot
    mix = r.mix
    vec = r.vec
    ou_all = r.ou_all
    down_all = r.down_all
    out_ref = r.out_ref
    dx_ref = r.n2_s
    do2_ref = r.do2
    acc_ou = r.acc_ou
    acc_down = r.acc_down
    sums_ref = r.sums
    o_s = r.o_s
    x1_s = r.x1_s
    n2_s = r.n2_s
    a2_s = r.a2_s
    gl_s = r.gl_s
    du_s = r.du_s
    dh_s = r.dh_s
    da_s = r.da_s
    r_s = r.r_s
    send2 = r.o2_s
    core_ou = r.core_ou
    core_down = r.core_down
    got_ou = r.got_ou
    got_down = r.got_down
    x_send = r.d_send
    x_recv = r.d_recv
    c_send = r.c_send
    c_recv = r.c_recv
    x, core, z, y = place()
    oc, oy = 1 - core, 1 - y
    me = z * 2 + y
    rows, width = tokens.shape
    half = rows // 2
    hidden = ou_all.shape[-1] - width
    left_half = left_lanes(half)
    to_core = device(x, oc, z, y)
    bias_o = vec[0:1, 2 * width : 3 * width]
    bias_down = vec[0:1, 3 * width + hidden : 4 * width + hidden]
    base = 4 * width + hidden
    gain = vec[0:1, base + 2 * width : base + 3 * width]
    shift = vec[0:1, base + 3 * width : base + 4 * width]

    for j in range(HEADS // 2):
        even, odd = mix[2 * j], mix[2 * j + 1]
        at = 128 * j
        o_s[:half, at : at + 128] = jnp.where(left_half, even, swap_halves(odd))
        o_s[half:, at : at + 128] = jnp.where(left_half, swap_halves(even), odd)
    w_out = ou_all[:, :, :, :, :, :width].reshape(width, width)
    x1 = tokens[...].astype(F32) + mm(o_s[...], w_out) + bias_o
    x1_s[...] = x1
    center = jnp.mean(x1, axis=1, keepdims=True)
    offset = x1 - center
    spread = jnp.mean(offset * offset, axis=1, keepdims=True)
    inverse = lax.rsqrt(spread + eps_norm)
    r_s[...] = jnp.broadcast_to(inverse, r_s.shape)
    n2 = offset * inverse
    n2_s[...] = n2
    a2_s[...] = (n2 * gain + shift).astype(BF16)
    sums_ref[...] = jnp.zeros_like(sums_ref)

    @pl.loop(0, hidden // width, unroll=True)
    def _(j):
        at = pl.multiple_of(j * width, width)
        w_up = ou_all[:, :, :, :, :, pl.ds(pl.multiple_of(width + at, width), width)].reshape(
            width, width
        )
        b_up = vec[0:1, pl.ds(pl.multiple_of(3 * width + at, width), width)]
        w_down = down_all[j // 2, j % 2].reshape(width, width)
        u = mm(a2_s[...], w_up) + b_up
        phi = 0.5 * (1.0 + lax.erf(u * (0.5**0.5)))
        slope = phi + u * jnp.exp(-0.5 * u * u) * (1.0 / math.sqrt(2.0 * math.pi))
        gl_s[:, pl.ds(at, width)] = (u * phi).astype(BF16)
        grad = mm(cot[...], w_down, NT)
        du = (grad * slope).astype(BF16)
        du_s[:, pl.ds(at, width)] = du
        sums_ref[0:1, pl.ds(pl.multiple_of(3 * width + at, width), width)] = jnp.sum(
            du.astype(F32), axis=0, keepdims=True
        )
        part = mm(du, w_up, NT)

        @pl.when(j == 0)
        def _():
            dh_s[...] = part

        @pl.when(j > 0)
        def _():
            dh_s[...] += part

    dh2 = dh_s[...]
    n2 = n2_s[...]
    sums_ref[0:1, base + 2 * width : base + 3 * width] = jnp.sum(dh2 * n2, axis=0, keepdims=True)
    sums_ref[0:1, base + 3 * width : base + 4 * width] = jnp.sum(dh2, axis=0, keepdims=True)
    e = dh2 * gain
    mean_e = jnp.mean(e, axis=1, keepdims=True)
    mean_en = jnp.mean(e * n2, axis=1, keepdims=True)
    dx = cot[...].astype(F32) + r_s[:, :1] * (e - mean_e - n2 * mean_en)
    dx_ref[...] = dx
    da = dx.astype(BF16)
    da_s[...] = da
    w_out = ou_all[:, :, :, :, :, :width].reshape(width, width)
    grad_o = mm(da, w_out, NT).astype(BF16)
    for j in range(HEADS // 2):
        group = grad_o[:, 128 * j : 128 * (j + 1)]
        top, low = group[:half], group[half:]
        send2[2 * j] = jnp.where(left_half, top, swap_halves(low))
        send2[2 * j + 1] = jnp.where(left_half, swap_halves(top), low)
    hz = z // 2
    order = (hz * 2 + 1 - z % 2, z, (1 - hz) * 2 + z % 2, (1 - hz) * 2 + 1 - z % 2)
    for tz, mark in zip(order, (2, 0, 4, 6)):
        for step in range(2):
            ty = (y + step) % 2
            index = mark + step
            src = send2.at[2 * tz + ty]
            if index == 0:
                pltpu.make_async_copy(src, do2_ref.at[me], x_recv.at[0]).start()
            else:
                remote(
                    src,
                    do2_ref.at[me],
                    x_send.at[index],
                    x_recv.at[index],
                    device(x, core, tz, ty),
                ).start()

    def grads(c, n):
        dp = 2 * n + c
        at = pl.multiple_of(dp * 128, 128)
        down_at = pl.multiple_of(dp * width, width)
        d_down = mm(gl_s[:, pl.ds(down_at, width)], cot[...], TN)
        d_up = mm(a2_s[:, pl.ds(at, 128)], du_s[...], TN)
        d_out = mm(o_s[:, pl.ds(at, 128)], da_s[...], TN)
        return (
            d_down.reshape(4, 2, width // 8, width),
            d_up.reshape(4, 2, 16, hidden),
            d_out.reshape(4, 2, 16, width),
        )

    for n in range(2):
        d_down, d_up, d_out = grads(oc, n)
        core_down[n] = d_down.astype(BF16)
        core_ou[n, :, :, :, width:] = d_up.astype(BF16)
        core_ou[n, :, :, :, :width] = d_out.astype(BF16)
    to_ou = remote(core_ou, got_ou, c_send.at[0], c_recv.at[0], to_core)
    to_down = remote(core_down, got_down, c_send.at[1], c_recv.at[1], to_core)
    to_ou.start()
    to_down.start()
    sums_ref[0:1, 2 * width : 3 * width] = jnp.sum(da_s[...].astype(F32), axis=0, keepdims=True)
    sums_ref[0:1, 3 * width + hidden : 4 * width + hidden] = jnp.sum(
        cot[...].astype(F32), axis=0, keepdims=True
    )
    result = x1_s[...] + mm(gl_s[...], down_all[...].reshape(hidden, width)) + bias_down
    out_ref[...] = result.astype(BF16)
    for n in range(2):
        d_down, d_up, d_out = grads(core, n)
        acc_down[n] = d_down
        acc_ou[n, :, :, :, width:] = d_up
        acc_ou[n, :, :, :, :width] = d_out
    to_ou.wait()
    to_down.wait()
    acc_ou[...] += got_ou[...].astype(F32)
    acc_down[...] += got_down[...].astype(F32)


def lanes_of(ref, r, g):
    group = r.tokens.shape[1] * 3 // 2
    return ref.at[:, :, :, :, pl.ds(pl.multiple_of(g * group, 128), group)]


def reducer_of(r, name, first, at=None):
    bufs = [getattr(r, f"{name}{n}") for n in range(REDUCE_BUFFERS)]
    if at is not None:
        return reducer(lanes_of(r.acc_ou, r, at), [b.at[at] for b in bufs], r.r_send, r.r_recv, first)
    acc = getattr(r, f"acc_{name}")
    return reducer(acc, bufs, r.r_send, r.r_recv, first)


def backward_phase(r):
    got, do2, o_heads, lse, grads, packed = r.got, r.do2, r.o_heads, r.lse, r.grads, r.packed
    qd_s, k_s, v_s, delta_s, dq_s, dkv_s = r.q_s, r.k_s, r.v_s, r.delta_s, r.acc_s, r.m_s
    flags = r.flags
    x, core, z, y = place()
    me = z * 2 + y
    hz = z // 2
    low = 1 - hz
    blocks = got.shape[0]
    rows = got.shape[1] // 3 * 2
    half = rows // 2
    quarter = blocks // 2
    scale = math.log2(math.e) * HALF**-0.5
    factor = HALF**-0.5
    left = left_lanes(rows)
    left_half = left_lanes(half)
    sums = (reducer_of(r, "ou", 0), reducer_of(r, "down", REDUCE_COPIES))
    for launch, _, _ in sums:
        launch(1)

    def enter(b):
        at = pl.multiple_of(b * rows, rows)
        pltpu.make_async_copy(do2.at[b], do2.at[b], r.d_recv.at[xor8(b, me)]).wait()
        v_s[pl.ds(at, rows), :] = jnp.where(left, 0, v_s[pl.ds(at, rows), :]).astype(BF16)
        grad = do2[b]
        for part, begin in ((swap_halves(grad), 0), (grad, half)):
            rows_at = pl.ds(at + begin, half)
            qd_s[rows_at, :] = jnp.where(left_half, qd_s[rows_at, :], part)
            product = jnp.where(left_half, 0.0, part.astype(F32) * o_heads[rows_at, :])
            delta = jnp.sum(jnp.transpose(product), axis=0, keepdims=True)
            delta_s[:, rows_at] = jnp.broadcast_to(delta, (8, half))
        dq_s[pl.ds(at, rows), :] = jnp.zeros((rows, 2 * HALF), F32)
        dkv_s[pl.ds(at, rows), :] = jnp.zeros((rows, 2 * HALF), F32)

    def tile(kj, qi, diagonal):
        k0 = pl.multiple_of(kj * rows, rows)
        q0 = pl.multiple_of(qi * rows, rows)
        k = k_s[pl.ds(k0, rows), :]
        v = v_s[pl.ds(k0, rows), :]
        qd = qd_s[pl.ds(q0, rows), :]
        scores = mm(k, qd, NT)
        dprobs = mm(v, qd, NT)
        p = jnp.exp2(scores * scale - lse[:1, pl.ds(q0, rows)])
        if diagonal:
            allowed = diagonal_mask(rows, flags, kj * (rows // PIECE), True)
            p = jnp.where(allowed, p, 0.0)
        ds = (p * (dprobs - delta_s[:1, pl.ds(q0, rows)])).astype(BF16)
        dkv_s[pl.ds(k0, rows), :] += jnp.where(left, mm(ds, qd), mm(p.astype(BF16), qd))
        dq_s[pl.ds(q0, rows), :] += mm(ds, k, TN)

    def part_of(is_query):
        return pl.ds(rows, half) if is_query else pl.ds(0, rows)

    def leave(a, is_query):
        at = pl.multiple_of(a * rows, rows)
        if is_query:
            top = dq_s[pl.ds(at, half), :]
            bottom = dq_s[pl.ds(at + half, half), :]
            packed[a, rows:] = (
                jnp.where(left_half, top, swap_halves(bottom)) * factor
            ).astype(BF16)
        else:
            block = dkv_s[pl.ds(at, rows), :]
            packed[a, :rows] = jnp.where(left, block * factor, block).astype(BF16)
        index = xor8(a, me) + 8 * is_query
        src = packed.at[a, part_of(is_query)]
        dst = grads.at[me, part_of(is_query)]

        @pl.when(a == me)
        def _():
            pltpu.make_async_copy(src, dst, r.b_recv.at[index]).start()

        @pl.when(a != me)
        def _():
            remote(
                src, dst, r.b_send.at[index], r.b_recv.at[index], device(x, core, a // 2, a % 2)
            ).start()

    for n in range(quarter):
        enter(hz * quarter + n)

    @pl.loop(0, 12)
    def _(row):
        seg = (row + 3) // 4
        last = seg // 3
        first = (3 - seg) // 3
        square = seg // 2 - last
        cross = seg % 2 - last
        own = first + last
        i = (row + 3) % 4 + last - 3 * first

        @pl.when(row == 8)
        def _():
            for _, finish, _ in sums:
                finish(1)
            for launch, _, _ in sums:
                launch(2)

        a_low = own * (3 - i) + (1 - own) * (7 - i)
        a_high = own * (4 + i) + (1 - own) * i
        a = low * a_low + hz * a_high
        count = own * (3 - i) + cross * i + square * 4

        @pl.when(cross == 1)
        def _():
            enter(a)


        @pl.when(square == 0)
        def _():
            tile(a, a, True)

        @pl.loop(0, count)
        def _(u):
            k_low = (own + square) * u + cross * a_low
            q_low = (own + square) * a_low + cross * (7 - u)
            k_high = (own + square) * a_high + cross * u
            q_high = own * (5 + i + u) + cross * a_high + square * (4 + u)
            tile(low * k_low + hz * k_high, low * q_low + hz * q_high, False)

        @pl.when(cross * hz + square * low + last > 0)
        def _():
            leave(a, 1)

        @pl.when(cross * low + square * hz + last > 0)
        def _():
            leave(a, 0)

        @pl.when(row == 8)
        def _():
            begin = low * 3 + hz * 4
            leave(begin, 1)
            leave(begin, 0)


def last_phase(r):
    grads, a1, tokens, dx, qkv_all, vec, sums = (
        r.grads,
        r.a1,
        r.tokens,
        r.n2_s,
        r.qkv_all,
        r.vec,
        r.sums,
    )
    dqkv_s, got_q = r.gl_s, r.got_q
    core_small, got_small, acc_small = r.core_small, r.got_small, r.acc_small
    x, core, z, y = place()
    me = z * 2 + y
    hz = z // 2
    oc = 1 - core
    to_core = device(x, oc, z, y)
    rows, width = tokens.shape
    half = rows // 2
    group = 3 * width // 2
    left_half = left_lanes(half)
    left1 = left_lanes(1)
    base = vec.shape[1] - 4 * width

    def columns_of(g):
        return pl.ds(pl.multiple_of(g * group, 128), group)

    def enter(g):
        for n in range(HEADS // 2):
            h = g * (HEADS // 2) + n
            for is_query in range(2):
                view = grads.at[h, pl.ds(rows, half) if is_query else pl.ds(0, rows)]
                pltpu.make_async_copy(view, view, r.b_recv.at[xor8(h, me) + 8 * is_query]).wait()
        begin = g * group
        for j in range(HEADS // 4):
            h = g * (HEADS // 2) + 2 * j
            even, odd = grads[h, rows:], grads[h + 1, rows:]
            at = pl.ds(pl.multiple_of(begin + 128 * j, 128), 128)
            dqkv_s[:half, at] = jnp.where(left_half, even, swap_halves(odd))
            dqkv_s[half:, at] = jnp.where(left_half, swap_halves(even), odd)
        for n in range(HEADS // 2):
            at = pl.ds(pl.multiple_of(begin + 256 + 128 * n, 128), 128)
            dqkv_s[:, at] = grads[g * (HEADS // 2) + n, :rows]

    def weight_grad(c, n, g):
        at = pl.multiple_of((2 * n + c) * 128, 128)
        return mm(a1[:, pl.ds(at, 128)], dqkv_s[:, columns_of(g)], TN).reshape(4, 2, 16, group)

    def over(g):
        return remote(lanes_of(r.core_ou, r, g), got_q.at[g], r.e_send.at[g], r.e_recv.at[g], to_core)

    parts = []
    for position, g in enumerate((1 - hz, hz)):
        enter(g)
        if position == 0:
            for early in (reducer_of(r, "ou", 0), reducer_of(r, "down", REDUCE_COPIES)):
                early[1](2)
                early[0](3)
        for n in range(2):
            lanes_of(r.core_ou, r, g)[n] = weight_grad(oc, n, g).astype(BF16)
        over(g).start()
        w = qkv_all[g, :, :, :, :, :, :group].reshape(width, group)
        part = mm(dqkv_s[:, columns_of(g)], w, NT)
        if position:
            r.dh_s[...] += part
        else:
            r.dh_s[...] = part
        for n in range(2):
            lanes_of(r.acc_ou, r, g)[n] = weight_grad(core, n, g)
        over(g).wait()
        acc_q = lanes_of(r.acc_ou, r, g)
        acc_q[...] = acc_q[...] + got_q[g].astype(F32)
        parts.append(reducer_of(r, "q", (2 + g) * REDUCE_COPIES, g))
        parts[-1][0](1)

    columns = jnp.sum(dqkv_s[:, : 3 * width].astype(F32), axis=0, keepdims=True)
    for j in range(HEADS // 2):
        at = (j // 2) * group + (j % 2) * 128
        sums[0:1, 128 * j : 128 * (j + 1)] = columns[:, at : at + 128]
        at = (j // 2) * group + 256 + (j % 2) * 256
        pair = jnp.where(
            left1, swap_halves(columns[:, at : at + 128]), columns[:, at + 128 : at + 256]
        )
        sums[0:1, width + 128 * j : width + 128 * (j + 1)] = pair
    dh = r.dh_s[...]
    gain = vec[0:1, base : base + width]
    value = tokens[...].astype(F32)
    center = jnp.mean(value, axis=1, keepdims=True)
    offset = value - center
    spread = jnp.mean(offset * offset, axis=1, keepdims=True)
    inverse = lax.rsqrt(spread + eps_norm)
    norm = offset * inverse
    sums[0:1, base : base + width] = jnp.sum(dh * norm, axis=0, keepdims=True)
    sums[0:1, base + width : base + 2 * width] = jnp.sum(dh, axis=0, keepdims=True)

    def small_block(a, b, c, d):
        n = (a * 2 + b) * 8 + c * 2 + d
        piece = sums[0:1, pl.ds(pl.multiple_of(128 * n, 128), 128)]
        pair = sums[0:1, pl.ds(pl.multiple_of(base + 128 * (n // 2), 128), 128)]
        own = pair if d == 0 else swap_halves(pair)
        return jnp.concatenate([piece, own, jnp.zeros((6, 128), F32)], axis=0)

    for a in range(2):
        for c in range(4):
            for d in range(2):
                core_small[a, c, d] = small_block(a, oc, c, d)
                acc_small[a, c, d] = small_block(a, core, c, d)
    over_small = remote(core_small, got_small, r.e_send.at[2], r.e_recv.at[2], to_core)
    over_small.start()
    parts[0][1](1)
    parts[0][0](2)
    over_small.wait()
    acc_small[...] += got_small[...]
    parts.append(reducer_of(r, "small", 4 * REDUCE_COPIES))
    parts[2][0](1)
    e = dh * gain
    mean_e = jnp.mean(e, axis=1, keepdims=True)
    mean_en = jnp.mean(e * norm, axis=1, keepdims=True)
    r.grad_tokens[...] = dx[...] + inverse * (e - mean_e - norm * mean_en)
    parts[1][1](1)
    parts[1][0](2)
    parts[0][1](2)
    parts[0][0](3)
    parts[2][1](1)
    parts[2][0](2)
    parts[1][1](2)
    parts[1][0](3)
    parts[2][1](2)
    parts[2][0](3)
    for part in (reducer_of(r, "ou", 0), reducer_of(r, "down", REDUCE_COPIES)):
        part[1](3)
    r.sum_ou[...] = reducer_of(r, "ou", 0)[2]()
    r.sum_down[...] = reducer_of(r, "down", REDUCE_COPIES)[2]()
    for _, finish, _ in parts:
        finish(3)
    for g, part in zip((1 - hz, hz), parts):
        r.sum_qkv[g] = part[2]()
    r.sum_small[...] = parts[2][2]()
    for index in range(HEADS):
        if index:
            for is_query, count in ((0, rows), (1, half)):
                view = r.packed.at[0, pl.ds(rows * is_query, count)]
                pltpu.make_async_copy(view, view, r.b_send.at[index + 8 * is_query]).wait()
            view = r.o2_s.at[0]
            pltpu.make_async_copy(view, view, r.d_send.at[index]).wait()


def layer_kernel(names, *refs):
    r = types.SimpleNamespace(**dict(zip(names, refs)))
    forward_phase(r)
    middle_phase(r)
    backward_phase(r)
    last_phase(r)


def layer(inputs, cid):
    rows, width = inputs["tokens"].shape
    length = rows * HEADS
    lanes = 2 * HALF
    hidden = inputs["up_flat"].shape[0] * 128 // 16
    down_rows = inputs["down_flat"].shape[0] * 128 // width
    group = 3 * width // 2
    every = (2, 2, 4, 2)
    mine = (2, 4, 2)
    row = (8, 4096 + 4 * width)
    vmem = pltpu.VMEM
    dma = pltpu.SemaphoreType.DMA
    outputs = {
        "out_ref": jax.ShapeDtypeStruct((rows, width), BF16),
        "grad_tokens": jax.ShapeDtypeStruct((rows, width), F32),
        "sum_qkv": jax.ShapeDtypeStruct((2, 16, group), F32),
        "sum_ou": jax.ShapeDtypeStruct((16, width + hidden), F32),
        "sum_down": jax.ShapeDtypeStruct((down_rows, width), F32),
        "sum_small": jax.ShapeDtypeStruct((8, 128), F32),
    }
    scratch = {
        "flags": pltpu.SMEM((length // PIECE,), jnp.int32),
        "a1": vmem((rows, width), BF16),
        "got": vmem((HEADS, rows + rows // 2, lanes), BF16),
        "mix": vmem((HEADS, rows // 2, lanes), BF16),
        "o_heads": vmem((length, lanes), F32),
        "lse": vmem((8, length), F32),
        "vec": vmem(row, F32),
        "qkv_all": vmem((2,) + every + (16, group + 128), BF16),
        "ou_all": vmem(every + (16, width + hidden), BF16),
        "down_all": vmem(every + (down_rows, width), BF16),
        "stage": vmem((256, 128), F32),
        "qkv_own": vmem((2, 16, group + 128), BF16),
        "ou_own": vmem((16, width + hidden), BF16),
        "down_own": vmem((down_rows, width), BF16),
        "packed": vmem((HEADS, rows + rows // 2, lanes), BF16),
        "q_s": vmem((length, lanes), BF16),
        "k_s": vmem((length, lanes), BF16),
        "v_s": vmem((length, lanes), BF16),
        "m_s": vmem((length, lanes), F32),
        "acc_s": vmem((length, lanes), F32),
        "o2_s": vmem((HEADS, rows // 2, lanes), BF16),
        "do2": vmem((HEADS, rows // 2, lanes), BF16),
        "acc_ou": vmem(mine + (16, width + hidden), F32),
        "acc_down": vmem(mine + (down_rows, width), F32),
        "sums": vmem(row, F32),
        "o_s": vmem((rows, width), BF16),
        "x1_s": vmem((rows, width), F32),
        "n2_s": vmem((rows, width), F32),
        "a2_s": vmem((rows, width), BF16),
        "gl_s": vmem((rows, hidden), BF16),
        "du_s": vmem((rows, hidden), BF16),
        "dh_s": vmem((rows, width), F32),
        "da_s": vmem((rows, width), BF16),
        "r_s": vmem((rows, lanes), F32),
        "core_ou": vmem(mine + (16, width + hidden), BF16),
        "core_down": vmem(mine + (down_rows, width), BF16),
        "got_ou": vmem(mine + (16, width + hidden), BF16),
        "got_down": vmem(mine + (down_rows, width), BF16),
        "delta_s": vmem((8, length), F32),
        "grads": vmem((HEADS, rows + rows // 2, lanes), BF16),
        "got_q": vmem((2,) + mine + (16, group), BF16),
        "core_small": vmem(mine + (8, 128), F32),
        "got_small": vmem(mine + (8, 128), F32),
        "acc_small": vmem(mine + (8, 128), F32),
    }
    for name, lead, r, w, wire in (
        ("ou", (), 16, width + hidden, BF16),
        ("down", (), down_rows, width, BF16),
        ("q", (2,), 16, group, BF16),
        ("small", (), 8, 128, F32),
    ):
        for n, buf in enumerate(reduce_buffers(r, w, wire)):
            scratch[f"{name}{n}"] = vmem(lead + buf.shape, buf.dtype)
    for name, count in (
        ("g_own", 3),
        ("g_send", 33),
        ("g_recv", 33),
        ("f_send", 40),
        ("f_recv", 40),
        ("x_send", 16),
        ("x_recv", 16),
        ("o_send", 8),
        ("o_recv", 8),
        ("d_send", 8),
        ("d_recv", 8),
        ("c_send", 2),
        ("c_recv", 2),
        ("r_send", 5 * REDUCE_COPIES),
        ("r_recv", 5 * REDUCE_COPIES),
        ("b_send", 16),
        ("b_recv", 16),
        ("e_send", 3),
        ("e_recv", 3),
    ):
        scratch[name] = dma((count,))
    names = tuple(inputs) + tuple(outputs) + tuple(scratch)

    def kernel(*refs):
        layer_kernel(names, *refs)

    return pl.pallas_call(
        kernel,
        out_shape=list(outputs.values()),
        in_specs=[SMEM_SPEC if n == "starts" else VMEM_SPEC for n in inputs],
        out_specs=[VMEM_SPEC] * len(outputs),
        scratch_shapes=list(scratch.values()),
        compiler_params=params(cid),
    )(*inputs.values())


def flatten_kernel(
    output,
    grad_tokens,
    sum_qkv,
    sum_ou,
    sum_down,
    sum_small,
    output_o,
    tokens_o,
    qkv_o,
    out_o,
    up_o,
    down_o,
    bias_o,
    norm_o,
):
    output_o[...] = output[...]
    tokens_o[...] = grad_tokens[...]
    groups = sum_down.shape[1] // 128
    left = left_lanes(16)

    def group(ref, j):
        return ref[:, 128 * j : 128 * (j + 1)]

    for j in range(groups):
        part = sum_qkv.at[j // 2]
        pair = j % 2
        qkv_o[pl.ds(j, 16, stride=3 * groups), :] = group(part, pair)
        even, odd = group(part, 2 + 2 * pair), group(part, 3 + 2 * pair)
        qkv_o[pl.ds(groups + j, 16, stride=3 * groups), :] = jnp.where(
            left, even, swap_halves(odd)
        )
        qkv_o[pl.ds(2 * groups + j, 16, stride=3 * groups), :] = jnp.where(
            left, swap_halves(even), odd
        )
        out_o[pl.ds(j, 16, stride=groups), :] = group(sum_ou, j)
        down_o[pl.ds(j, sum_down.shape[0], stride=groups), :] = group(sum_down, j)
    ups = sum_ou.shape[1] // 128 - groups
    for j in range(ups):
        up_o[pl.ds(j, 16, stride=ups), :] = group(sum_ou, groups + j)
    bias_o[...] = sum_small[0:1]
    norm_o[...] = sum_small[1:2, : norm_o.shape[1]]


def flatten(output, grad_tokens, sum_qkv, sum_ou, sum_down, sum_small, norm_len):
    width = sum_down.shape[1]
    sizes = (
        sum_qkv.size // 128,
        width * 16 // 128,
        (sum_ou.shape[1] - width) * 16 // 128,
        sum_down.size // 128,
    )
    return pl.pallas_call(
        flatten_kernel,
        out_shape=[
            jax.ShapeDtypeStruct(output.shape, output.dtype),
            jax.ShapeDtypeStruct(grad_tokens.shape, grad_tokens.dtype),
        ]
        + [jax.ShapeDtypeStruct((n, 128), F32) for n in sizes]
        + [jax.ShapeDtypeStruct((1, 128), F32), jax.ShapeDtypeStruct((1, norm_len), F32)],
        in_specs=[VMEM_SPEC] * 6,
        out_specs=[VMEM_SPEC] * 8,
        compiler_params=params(),
    )(output, grad_tokens, sum_qkv, sum_ou, sum_down, sum_small)


def fast_device(
    tokens, piece_starts, qkv_weight, out_weight, up_weight, down_weight, biases, norms, cotangent
):
    output, grad_tokens, sum_qkv, sum_ou, sum_down, sum_small = layer(
        {
            "starts": piece_starts,
            "tokens": tokens[0],
            "cot": cotangent[0],
            "biases": biases.reshape(1, -1),
            "norms": norms.reshape(1, -1),
            "qkv_flat": qkv_weight.reshape(-1, 128),
            "out_flat": out_weight.reshape(-1, 128),
            "up_flat": up_weight.reshape(-1, 128),
            "down_flat": down_weight.reshape(-1, 128),
        },
        1,
    )
    output, grad_tokens, *flats = flatten(
        output, grad_tokens, sum_qkv, sum_ou, sum_down, sum_small, norms.shape[0]
    )
    return (output[None], grad_tokens[None]) + tuple(f.reshape(-1) for f in flats)


def solution(mesh):
    flat = P(("dp", "ctx"))
    rows = P("dp", "ctx", None)
    fast = mesh.shape["dp"] == 4 and mesh.shape["ctx"] == HEADS
    return jax.shard_map(
        fast_device if fast else general_device,
        mesh=mesh,
        in_specs=(rows, P("dp", None), flat, flat, flat, flat, flat, flat, rows),
        out_specs=(rows, rows, flat, flat, flat, flat, flat, flat),
        check_vma=False,
    )
```
